256 devices in a mesh: sec: 32 (over z, y), blk: 8 (over x, core).
Axes of the slice: x: 4, y: 4, z: 8, core: 2. Of those that a mesh axis runs over, the one named last changes fastest.
Arguments:
- state_now: float32 [128, 65536], P(None, ('sec', 'blk')), may hold values from -5 to 5
- source: float32 [128, 65536], P(None, ('sec', 'blk')), may hold values from -6 to 6
- fan_gain: float32 [65536], P(('sec', 'blk')), may hold values from 0.5 to 12
- section_block: bfloat16 [65536, 2048], P(('sec', 'blk')), may hold values from -1 to 7
- block_inverse: bfloat16 [65536, 2048], P(('sec', 'blk')), may hold values from -1 to 1
- back_panel: bfloat16 [65536, 128], P(('sec', 'blk')), may hold values from -6 to 6
- ahead_panel: bfloat16 [65536, 128], P(('sec', 'blk')), may hold values from -0.0625 to 0.0625
- interface: int32 [32, 128], P('sec'), may hold values from 0 to 2047, as said below
Outputs:
- new_state: float32 [128, 65536], P(None, ('sec', 'blk'))
The draws below stay inside these ranges and needn't reach their ends.
Inputs may be any that keep to these rules, and one draw needn't show every extreme that they name: `interface`: entries of one section are distinct; entry p lies in [p * 16, (p + 1) * 16).
All inputs are finite; a program needn't handle non-finite values.
Results may differ from the reference program's by a relative error of at most 0.0063.
Values may be sent and summed in bfloat16 or wider, within the bound.
A program may use at most 64 MiB of HBM per device.

```python
import math
import jax
import jax.numpy as jnp
from jax import lax

CASES = 128
PANEL = 128
KRYLOV = 3
SECTION = 2048
SECTIONS = 32
NODES = 65536


def block_diagonal(key):
    diag_key = jax.random.fold_in(key, 11)
    diagonal = jax.random.uniform(diag_key, (SECTIONS, SECTION), jnp.float32, 2.0, 4.0)
    return diagonal


def block_noise(key):
    noise_key = jax.random.fold_in(key, 12)
    spread = 0.6 / SECTION ** 0.5
    return jnp.clip(jax.random.normal(noise_key, (SECTIONS, SECTION, SECTION), jnp.float32), -4.0, 4.0) * spread


def interface_table(key):
    table_key = jax.random.fold_in(key, 21)
    stride = SECTION // PANEL
    offsets = jax.random.randint(table_key, (SECTIONS, PANEL), 0, stride)
    panel_idx = jnp.arange(PANEL)[None, :]
    section_idx = jnp.arange(SECTIONS)[:, None]
    offsets = jnp.where((section_idx == 0) & (panel_idx == PANEL - 1), stride - 1, offsets)
    offsets = jnp.where((section_idx == 0) & (panel_idx == 0), 0, offsets)
    return (panel_idx * stride + offsets).astype(jnp.int32)


def draw_section_block(key, part):
    diagonal = block_diagonal(key)
    noise = block_noise(key)
    eye_mask = jnp.eye(SECTION, dtype=jnp.float32)[None]
    whole = noise + eye_mask * diagonal[:, :, None]
    return whole.reshape(SECTIONS * SECTION, SECTION).astype(jnp.bfloat16)


def draw_block_inverse(key, part):
    diagonal = block_diagonal(key)
    noise = block_noise(key)
    eye_mask = jnp.eye(SECTION, dtype=jnp.float32)[None]
    whole = eye_mask / diagonal[:, :, None] - noise / (diagonal[:, :, None] * diagonal[:, None, :])
    return whole.reshape(SECTIONS * SECTION, SECTION).astype(jnp.bfloat16)


def draw_interface(key, part):
    return interface_table(key)


def draw_back_panel(key, part):
    diagonal = block_diagonal(key)
    indices = interface_table(key)
    carry_gain = 0.85
    coupling_scale = carry_gain / PANEL ** 0.5
    small_scale = (4.0 * (SECTION + PANEL)) ** (-0.5)
    section_idx = jnp.arange(SECTIONS)[:, None]
    picked = diagonal[section_idx, indices]
    row_scale = jnp.full((SECTIONS, SECTION), small_scale, jnp.float32)
    row_scale = row_scale.at[section_idx, indices].set(picked * coupling_scale)
    values = jnp.clip(jax.random.normal(jax.random.fold_in(key, 31), (SECTIONS, SECTION, PANEL), jnp.float32), -4.0, 4.0)
    whole = values * row_scale[:, :, None]
    return whole.reshape(SECTIONS * SECTION, PANEL).astype(jnp.bfloat16)


def levels(own_key, dims, shards, least, largest):
    def one(dim, blocks):
        draws = jax.random.uniform(jax.random.fold_in(jax.random.fold_in(own_key, 6), dim), (blocks,), jnp.float32, least / len(shards), largest / len(shards))
        return jnp.repeat(jnp.exp(draws), dims[dim] // blocks).reshape((-1,) + (1,) * (len(dims) - dim - 1))

    factor_of = one(*shards[0])
    for cut in shards[1:]:
        factor_of = factor_of * one(*cut)
    return factor_of


def bell_draw(own_key, extent, deviation, limit, cuts=(), kind=jnp.bfloat16):
    level = levels(own_key, extent, cuts, -0.22, 0.18) if cuts else 1.0
    values = jax.random.normal(own_key, extent, jnp.float32) * deviation * level
    return jnp.minimum(jnp.maximum(values, -limit), limit).astype(kind)


def setup_inputs(seed: int = 0) -> dict:
    splits = jax.random.split(jax.random.key(seed), 9)
    state_now = bell_draw(splits[0], (CASES, NODES), 1.0, 5.0, ((1, 256),), jnp.float32)
    source = bell_draw(splits[1], (CASES, NODES), 1.0, 6.0, ((1, 256),), jnp.float32)
    fan_gain = jnp.clip(jnp.exp(math.log(12.0) - 3.1780538 * jax.random.uniform(splits[2], (NODES,), jnp.float32) ** levels(splits[2], (NODES,), ((0, 256),), -0.2, 0.2)), 0.5, 12.0)
    section_block = draw_section_block(jax.random.fold_in(splits[8], 71), 0)
    block_inverse = draw_block_inverse(jax.random.fold_in(splits[8], 71), 0)
    back_panel = draw_back_panel(jax.random.fold_in(splits[8], 71), 0)
    ahead_panel = bell_draw(splits[6], (NODES, PANEL), (4 * (SECTION + PANEL)) ** -0.5, 0.0625, ((0, 256),))
    interface = draw_interface(jax.random.fold_in(splits[8], 71), 0)
    return dict(state_now=state_now, source=source, fan_gain=fan_gain, section_block=section_block, block_inverse=block_inverse, back_panel=back_panel, ahead_panel=ahead_panel, interface=interface)


epsilon = 1e-06

def section_products(rounded, blocks):

    def section_product(pair):
        values, matrix = pair
        return jnp.dot(values, matrix.T, preferred_element_type=jnp.float32)
    result = lax.map(section_product, (jnp.swapaxes(rounded, 0, 1), blocks))
    return jnp.swapaxes(result, 0, 1)

def least_squares(hessen, beta):
    cases = hessen.shape[0]
    depth = hessen.shape[2]
    rhs = jnp.zeros((cases, depth + 1), jnp.float32).at[:, 0].set(beta)
    upper = hessen
    for column in range(depth):
        upper_row = upper[:, column, :]
        lower_row = upper[:, column + 1, :]
        radius = jnp.sqrt(upper_row[:, column] ** 2 + lower_row[:, column] ** 2)
        cosine = upper_row[:, column] / radius
        sine_term = lower_row[:, column] / radius
        upper = upper.at[:, column, :].set(cosine[:, None] * upper_row + sine_term[:, None] * lower_row)
        upper = upper.at[:, column + 1, :].set(-sine_term[:, None] * upper_row + cosine[:, None] * lower_row)
        first_rhs = rhs[:, column]
        second_rhs = rhs[:, column + 1]
        rhs = rhs.at[:, column].set(cosine * first_rhs + sine_term * second_rhs)
        rhs = rhs.at[:, column + 1].set(-sine_term * first_rhs + cosine * second_rhs)
    weights = jnp.zeros((cases, depth), jnp.float32)
    for column in reversed(range(depth)):
        remain = rhs[:, column] - lax.optimization_barrier(jnp.sum(upper[:, column, column + 1:] * weights[:, column + 1:], axis=1))
        weights = weights.at[:, column].set(remain / upper[:, column, column])
    return weights

def reference(state_now, source, fan_gain, section_block, block_inverse, back_panel, ahead_panel, interface):
    cases = state_now.shape[0]
    blocks = section_block.reshape(SECTIONS, SECTION, SECTION)
    inverses = block_inverse.reshape(SECTIONS, SECTION, SECTION)
    backs = back_panel.reshape(SECTIONS, SECTION, PANEL)
    aheads = ahead_panel.reshape(SECTIONS, SECTION, PANEL)
    indices = interface.astype(jnp.int32)
    picks = jnp.broadcast_to(indices[None], (cases, SECTIONS, PANEL))

    def operator(vector):
        rounded = vector.astype(jnp.bfloat16).reshape(cases, SECTIONS, SECTION)
        dense_part = section_products(rounded, blocks)
        behind_vals = jnp.take_along_axis(rounded, picks, axis=2)
        previous = jnp.concatenate([jnp.zeros_like(behind_vals[:, :1]), behind_vals[:, :-1]], axis=1)
        lower_term = jnp.einsum('csp,snp->csn', previous.astype(jnp.float32), backs.astype(jnp.float32))
        upward = jnp.einsum('csn,snp->csp', rounded.astype(jnp.float32), aheads.astype(jnp.float32))
        ahead_term = jnp.concatenate([upward[:, 1:], jnp.zeros_like(upward[:, :1])], axis=1)
        upper_term = jnp.zeros((cases, SECTIONS, SECTION), jnp.float32)
        upper_term = upper_term.at[:, jnp.arange(SECTIONS)[:, None], indices].add(ahead_term)
        return (dense_part + lower_term + upper_term).reshape(cases, NODES)

    def panel_product(pair):
        inverse, back = pair
        return jnp.dot(inverse, back, preferred_element_type=jnp.float32)
    gain_panel = lax.map(panel_product, (inverses, backs))
    row_picks = jnp.broadcast_to(indices[:, :, None], (SECTIONS, PANEL, PANEL))
    panel_maps = -jnp.take_along_axis(gain_panel, row_picks, axis=1)

    def precondition(vector):
        rounded = vector.astype(jnp.bfloat16).reshape(cases, SECTIONS, SECTION)
        spread = section_products(rounded, inverses)
        values = jnp.take_along_axis(spread, picks, axis=2)

        def advance(carried, inputs):
            local_value, local_map = inputs
            updated = local_value + jnp.dot(carried, local_map.T, precision=lax.Precision.HIGHEST)
            return (updated, carried)
        _, before = lax.scan(advance, jnp.zeros((cases, PANEL), jnp.float32), (jnp.swapaxes(values, 0, 1), panel_maps))
        result = spread - jnp.einsum('scp,snp->csn', before, gain_panel, precision=lax.Precision.HIGHEST)
        return result.reshape(cases, NODES)
    bent = jnp.tanh(state_now)
    residual = source - operator(state_now) - fan_gain[None, :] * bent
    jac_diag = fan_gain[None, :] * (1.0 - bent * bent)
    beta = jnp.sqrt(lax.optimization_barrier(jnp.sum(residual * residual, axis=1)) + epsilon)
    basis = [residual / beta[:, None]]
    directions = []
    hessen = jnp.zeros((cases, KRYLOV + 1, KRYLOV), jnp.float32)
    for column in range(KRYLOV):
        direction = precondition(basis[column])
        product = operator(direction) + jac_diag * direction
        stacked = jnp.stack(basis)
        projections = lax.optimization_barrier(jnp.sum(product[None] * stacked, axis=2))
        product = product - lax.optimization_barrier(jnp.sum(projections[:, :, None] * stacked, axis=0))
        length = jnp.sqrt(lax.optimization_barrier(jnp.sum(product * product, axis=1)) + epsilon)
        hessen = hessen.at[:, :column + 1, column].set(projections.T)
        hessen = hessen.at[:, column + 1, column].set(length)
        basis.append(product / length[:, None])
        directions.append(direction)
    weights = least_squares(hessen, beta)
    update = jnp.zeros_like(state_now)
    for column in range(KRYLOV):
        update = update + weights[:, column:column + 1] * directions[column]
    return state_now + update
```

```python
import functools

import jax
import jax.numpy as jnp
from jax import lax
from jax.experimental import pallas as pl
from jax.experimental.pallas import tpu as pltpu
from jax.sharding import PartitionSpec as P

MESH = pl.DeviceIdType.MESH

KRYLOV = 3


epsilon = 1e-06


def extended(x, sides, width):
    for axis, dim in sides:
        size, length = (lax.axis_size(axis), x.shape[dim])
        up = [(i, (i + 1) % size) for i in range(size - 1)]
        down = [(j, i) for i, j in up]
        last = lax.slice_in_dim(x, length - width, length, axis=dim)
        first = lax.slice_in_dim(x, 0, width, axis=dim)
        before = lax.ppermute(last, axis, up)
        after = lax.ppermute(first, axis, down)
        x = jnp.concatenate([before, x, after], axis=dim)
    return x


def entering(value, axis, join, neutral):
    count, mine = (lax.axis_size(axis), lax.axis_index(axis))
    pieces = jax.tree.map(lambda part: lax.all_gather(part, axis), value)
    so_far = jax.tree.map(
        lambda part, zero: jnp.full_like(part, 0) + jnp.asarray(zero, part.dtype), value, neutral
    )

    def step(position, so_far):
        longer = join(so_far, jax.tree.map(lambda part: part[position], pieces))
        return jax.tree.map(lambda new, old: jnp.where(position < mine, new, old), longer, so_far)

    return lax.fori_loop(0, count - 1, step, so_far)


def _reduce_kernel(stages, x_ref, o_ref, *scratch):
    count = len(stages)
    slots = scratch[:count]
    partial = scratch[count]
    sends = scratch[count + 1 : 2 * count + 1]
    recvs = scratch[2 * count + 1 :]
    barrier = pltpu.get_barrier_semaphore()
    peers = 0
    for axis, n in stages:
        mine = lax.axis_index(axis)
        for k in range(1, n):
            pl.semaphore_signal(
                barrier, inc=1, device_id={axis: lax.rem(mine + k, n)}, device_id_type=MESH
            )
            peers += 1
    pl.semaphore_wait(barrier, peers)
    source = x_ref
    for stage, (axis, n) in enumerate(stages):
        mine = lax.axis_index(axis)
        copies = []
        for k in range(1, n):
            copy = pltpu.make_async_remote_copy(
                src_ref=source,
                dst_ref=slots[stage].at[mine],
                send_sem=sends[stage].at[k],
                recv_sem=recvs[stage].at[mine],
                device_id={axis: lax.rem(mine + k, n)},
                device_id_type=MESH,
            )
            copy.start()
            copies.append(copy)
        slots[stage][mine] = source[...]
        for k in range(1, n):
            sender = lax.rem(mine + k, n)
            pltpu.make_async_remote_copy(
                src_ref=source,
                dst_ref=slots[stage].at[sender],
                send_sem=sends[stage].at[k],
                recv_sem=recvs[stage].at[sender],
                device_id={axis: sender},
                device_id_type=MESH,
            ).wait_recv()
        for copy in copies:
            copy.wait_send()
        total = slots[stage][0]
        for j in range(1, n):
            total = total + slots[stage][j]
        if stage == count - 1:
            o_ref[...] = total
        else:
            partial[...] = total
            source = partial


def all_sum(x, axes, mesh_shape, collective):
    stages = tuple((axis, mesh_shape[axis]) for axis in axes if mesh_shape[axis] > 1)
    rows, cols = x.shape
    scratch = [pltpu.VMEM((n, rows, cols), jnp.float32) for _, n in stages]
    scratch.append(pltpu.VMEM((rows, cols), jnp.float32))
    scratch += [pltpu.SemaphoreType.DMA((n,)) for _, n in stages]
    scratch += [pltpu.SemaphoreType.DMA((n,)) for _, n in stages]
    return pl.pallas_call(
        functools.partial(_reduce_kernel, stages),
        out_shape=jax.ShapeDtypeStruct((rows, cols), jnp.float32),
        in_specs=[pl.BlockSpec(memory_space=pltpu.VMEM)],
        out_specs=pl.BlockSpec(memory_space=pltpu.VMEM),
        scratch_shapes=scratch,
        compiler_params=pltpu.CompilerParams(collective_id=collective, has_side_effects=True),
    )(x.astype(jnp.float32))


def global_sum(rows_of_sums, mesh_shape):
    count = rows_of_sums.shape[0]
    padded = jnp.zeros((8, rows_of_sums.shape[1]), jnp.float32).at[:count].set(rows_of_sums)
    return all_sum(padded, ("blk", "sec"), mesh_shape, 0)[:count]


def least_squares(hessen, beta):
    cases = hessen.shape[0]
    depth = hessen.shape[2]
    rhs = jnp.zeros((cases, depth + 1), jnp.float32).at[:, 0].set(beta)
    upper = hessen
    for column in range(depth):
        upper_row = upper[:, column, :]
        lower_row = upper[:, column + 1, :]
        radius = jnp.sqrt(upper_row[:, column] ** 2 + lower_row[:, column] ** 2)
        cosine = upper_row[:, column] / radius
        sine_term = lower_row[:, column] / radius
        upper = upper.at[:, column, :].set(
            cosine[:, None] * upper_row + sine_term[:, None] * lower_row
        )
        upper = upper.at[:, column + 1, :].set(
            -sine_term[:, None] * upper_row + cosine[:, None] * lower_row
        )
        first_rhs = rhs[:, column]
        second_rhs = rhs[:, column + 1]
        rhs = rhs.at[:, column].set(cosine * first_rhs + sine_term * second_rhs)
        rhs = rhs.at[:, column + 1].set(-sine_term * first_rhs + cosine * second_rhs)
    weights = jnp.zeros((cases, depth), jnp.float32)
    for column in reversed(range(depth)):
        remain = rhs[:, column] - jnp.sum(
            upper[:, column, column + 1 :] * weights[:, column + 1 :], axis=1
        )
        weights = weights.at[:, column].set(remain / upper[:, column, column])
    return weights


def local(
    mesh_shape,
    state_now, source, fan_gain, section_block, block_inverse, back_panel, ahead_panel, interface
):
    highest = lax.Precision.HIGHEST
    cases, node_rows = state_now.shape
    panel_width = back_panel.shape[1]
    indices = interface[0]
    first_row = lax.axis_index("blk") * node_rows
    selector = (indices[None, :] == first_row + jnp.arange(node_rows)[:, None]).astype(jnp.float32)
    contract = (((1,), (1,)), ((), ()))
    gain_panel = jnp.dot(
        block_inverse,
        lax.all_gather(back_panel, "blk", axis=0, tiled=True),
        preferred_element_type=jnp.float32,
    )
    panel_maps = -all_sum(jnp.dot(selector.T, gain_panel, precision=highest), ("blk",), mesh_shape, 1)

    def section_terms(dense_part, behind_vals, piece):
        width = piece.shape[1]
        dense_part = lax.dot_general(
            piece, section_block, contract, preferred_element_type=jnp.float32
        )
        picker = (indices[None, :] == jnp.arange(width)[:, None]).astype(jnp.bfloat16)
        behind_vals = jnp.dot(piece, picker, preferred_element_type=jnp.float32)
        return (dense_part, behind_vals)

    def fold_section(carry, piece):
        return section_terms(carry[0], carry[1], piece)

    def operator(vector):
        rounded = vector.astype(jnp.bfloat16)
        empty_dense = jnp.zeros((cases, node_rows), jnp.float32)
        empty_panel = jnp.zeros((cases, panel_width), jnp.float32)
        start_carry = (empty_dense, empty_panel)
        folded = fold_section(start_carry, lax.all_gather(rounded, "blk", axis=1, tiled=True))
        dense_part, behind_vals = folded
        upward = all_sum(
            jnp.dot(rounded, ahead_panel, preferred_element_type=jnp.float32), ("blk",), mesh_shape, 1
        )
        framed = extended(jnp.stack([behind_vals, upward])[None], (("sec", 0),), 1)
        behind = framed[0, 0].astype(jnp.bfloat16)
        ahead_term = framed[2, 1]
        lower_term = lax.dot_general(
            behind, back_panel, contract, preferred_element_type=jnp.float32
        )
        upper_term = jnp.dot(ahead_term, selector.T, precision=highest)
        return dense_part + lower_term + upper_term

    def compose(earlier, later):
        first_map, first_value = earlier
        second_map, second_value = later
        joined_map = jnp.dot(second_map, first_map, precision=highest)
        joined_value = jnp.dot(first_value, second_map.T, precision=highest) + second_value
        return (joined_map, joined_value)

    def lengths(vector):
        return jnp.sqrt(global_sum(jnp.sum(vector * vector, axis=1)[None], mesh_shape)[0] + epsilon)

    bent = jnp.tanh(state_now)
    residual = source - operator(state_now) - fan_gain[None, :] * bent
    jac_diag = fan_gain[None, :] * (1.0 - bent * bent)
    beta = lengths(residual)
    basis = [residual / beta[:, None]]
    directions = []
    hessen = jnp.zeros((cases, KRYLOV + 1, KRYLOV), jnp.float32)
    for column in range(KRYLOV):
        precondition_rounded = basis[column].astype(jnp.bfloat16)
        precondition_folded = lax.dot_general(
            lax.all_gather(precondition_rounded, "blk", axis=1, tiled=True),
            block_inverse,
            contract,
            preferred_element_type=jnp.float32,
        )
        values = all_sum(
            jnp.dot(precondition_folded, selector, precision=highest), ("blk",), mesh_shape, 1
        )
        identity = (
            jnp.eye(panel_width, dtype=jnp.float32),
            jnp.zeros((cases, panel_width), jnp.float32),
        )
        _, before = entering((panel_maps, values), "sec", compose, identity)
        direction = precondition_folded - lax.dot_general(
            before, gain_panel, contract, precision=highest
        )
        product = operator(direction) + jac_diag * direction
        stacked = jnp.stack(basis)
        projections = global_sum(jnp.sum(product[None] * stacked, axis=2), mesh_shape)
        product = product - jnp.sum(projections[:, :, None] * stacked, axis=0)
        length = lengths(product)
        hessen = hessen.at[:, : column + 1, column].set(projections.T)
        hessen = hessen.at[:, column + 1, column].set(length)
        basis.append(product / length[:, None])
        directions.append(direction)
    weights = least_squares(hessen, beta)
    update = jnp.zeros_like(state_now)
    for column in range(KRYLOV):
        update = update + weights[:, column : column + 1] * directions[column]
    return state_now + update


def solution(mesh):
    in_specs = (
        P(None, ("sec", "blk")),
        P(None, ("sec", "blk")),
        P(("sec", "blk")),
        P(("sec", "blk"), None),
        P(("sec", "blk"), None),
        P(("sec", "blk"), None),
        P(("sec", "blk"), None),
        P("sec", None),
    )
    out_specs = P(None, ("sec", "blk"))
    return jax.shard_map(functools.partial(local, dict(mesh.shape)), mesh=mesh, in_specs=in_specs, out_specs=out_specs, check_vma=False)
```

```python
import functools

import jax
import jax.numpy as jnp
from jax import lax
from jax.experimental import pallas as pl
from jax.experimental.pallas import tpu as pltpu
from jax.sharding import PartitionSpec as P

MESH = pl.DeviceIdType.MESH

KRYLOV = 3


epsilon = 1e-06


def extended(x, sides, width):
    for axis, dim in sides:
        size, length = (lax.axis_size(axis), x.shape[dim])
        up = [(i, (i + 1) % size) for i in range(size - 1)]
        down = [(j, i) for i, j in up]
        last = lax.slice_in_dim(x, length - width, length, axis=dim)
        first = lax.slice_in_dim(x, 0, width, axis=dim)
        before = lax.ppermute(last, axis, up)
        after = lax.ppermute(first, axis, down)
        x = jnp.concatenate([before, x, after], axis=dim)
    return x


def entering(value, axis, join, neutral):
    count, mine = (lax.axis_size(axis), lax.axis_index(axis))
    pieces = jax.tree.map(lambda part: lax.all_gather(part, axis), value)
    so_far = jax.tree.map(
        lambda part, zero: jnp.full_like(part, 0) + jnp.asarray(zero, part.dtype), value, neutral
    )

    def step(position, so_far):
        longer = join(so_far, jax.tree.map(lambda part: part[position], pieces))
        return jax.tree.map(lambda new, old: jnp.where(position < mine, new, old), longer, so_far)

    return lax.fori_loop(0, count - 1, step, so_far)


def _reduce_kernel(stages, x_ref, o_ref, *scratch):
    count = len(stages)
    slots = scratch[:count]
    partial = scratch[count]
    sends = scratch[count + 1 : 2 * count + 1]
    recvs = scratch[2 * count + 1 :]
    barrier = pltpu.get_barrier_semaphore()
    peers = 0
    for axis, n in stages:
        mine = lax.axis_index(axis)
        for k in range(1, n):
            pl.semaphore_signal(
                barrier, inc=1, device_id={axis: lax.rem(mine + k, n)}, device_id_type=MESH
            )
            peers += 1
    pl.semaphore_wait(barrier, peers)
    source = x_ref
    for stage, (axis, n) in enumerate(stages):
        mine = lax.axis_index(axis)
        copies = []
        for k in range(1, n):
            copy = pltpu.make_async_remote_copy(
                src_ref=source,
                dst_ref=slots[stage].at[mine],
                send_sem=sends[stage].at[k],
                recv_sem=recvs[stage].at[mine],
                device_id={axis: lax.rem(mine + k, n)},
                device_id_type=MESH,
            )
            copy.start()
            copies.append(copy)
        slots[stage][mine] = source[...]
        for k in range(1, n):
            sender = lax.rem(mine + k, n)
            pltpu.make_async_remote_copy(
                src_ref=source,
                dst_ref=slots[stage].at[sender],
                send_sem=sends[stage].at[k],
                recv_sem=recvs[stage].at[sender],
                device_id={axis: sender},
                device_id_type=MESH,
            ).wait_recv()
        for copy in copies:
            copy.wait_send()
        total = slots[stage][0]
        for j in range(1, n):
            total = total + slots[stage][j]
        if stage == count - 1:
            o_ref[...] = total
        else:
            partial[...] = total
            source = partial


def all_sum(x, axes, mesh_shape, collective):
    stages = tuple((axis, mesh_shape[axis]) for axis in axes if mesh_shape[axis] > 1)
    rows, cols = x.shape
    scratch = [pltpu.VMEM((n, rows, cols), jnp.float32) for _, n in stages]
    scratch.append(pltpu.VMEM((rows, cols), jnp.float32))
    scratch += [pltpu.SemaphoreType.DMA((n,)) for _, n in stages]
    scratch += [pltpu.SemaphoreType.DMA((n,)) for _, n in stages]
    return pl.pallas_call(
        functools.partial(_reduce_kernel, stages),
        out_shape=jax.ShapeDtypeStruct((rows, cols), jnp.float32),
        in_specs=[pl.BlockSpec(memory_space=pltpu.VMEM)],
        out_specs=pl.BlockSpec(memory_space=pltpu.VMEM),
        scratch_shapes=scratch,
        compiler_params=pltpu.CompilerParams(collective_id=collective, has_side_effects=True),
    )(x.astype(jnp.float32))


def global_sum(rows_of_sums, mesh_shape):
    count = rows_of_sums.shape[0]
    padded = jnp.zeros((8, rows_of_sums.shape[1]), jnp.float32).at[:count].set(rows_of_sums)
    return all_sum(padded, ("blk", "sec"), mesh_shape, 0)[:count]


def _doubling(n):
    distances, d = [], 1
    while d < n:
        distances.append(d)
        d *= 2
    return tuple(distances)


def _greet(n, distances):
    barrier = pltpu.get_barrier_semaphore()
    mine = lax.axis_index("sec")
    for d in distances:
        for peer in (lax.rem(mine + d, n), lax.rem(mine + n - d, n)):
            pl.semaphore_signal(barrier, inc=1, device_id={"sec": peer}, device_id_type=MESH)
    pl.semaphore_wait(barrier, 2 * len(distances))


def _hop(n, d, source, slot, send_sem, recv_sem):
    mine = lax.axis_index("sec")
    copy = pltpu.make_async_remote_copy(
        src_ref=source,
        dst_ref=slot,
        send_sem=send_sem,
        recv_sem=recv_sem,
        device_id={"sec": lax.rem(mine + d, n)},
        device_id_type=MESH,
    )
    copy.start()
    copy.wait_recv()
    copy.wait_send()


def _maps_kernel(n, distances, e_ref, t_ref, slots, sends, recvs):
    mine = lax.axis_index("sec")
    _greet(n, distances)
    t_ref[0] = e_ref[...]
    for k, d in enumerate(distances[:-1]):
        _hop(n, d, t_ref.at[k], slots.at[k], sends.at[k], recvs.at[k])
        joined = jnp.dot(
            slots[k], t_ref[k], precision=lax.Precision.HIGHEST, preferred_element_type=jnp.float32
        )
        t_ref[k + 1] = jnp.where(mine >= d, joined, t_ref[k])


def _sweep_kernel(n, distances, f_ref, t_ref, o_ref, carry, slots, sends, recvs):
    mine = lax.axis_index("sec")
    _greet(n, distances)
    carry[0] = f_ref[...]
    for k, d in enumerate(distances):
        _hop(n, d, carry.at[k], slots.at[k], sends.at[k], recvs.at[k])
        joined = carry[k] + jnp.dot(
            slots[k], t_ref[k], precision=lax.Precision.HIGHEST, preferred_element_type=jnp.float32
        )
        carry[k + 1] = jnp.where(mine >= d, joined, carry[k])
    last = len(distances)
    _hop(n, 1, carry.at[last], slots.at[last], sends.at[last], recvs.at[last])
    o_ref[...] = jnp.where(mine >= 1, slots[last], jnp.zeros_like(o_ref))


def scan_maps(maps_t, n):
    distances = _doubling(n)
    rounds, width = len(distances), maps_t.shape[0]
    return pl.pallas_call(
        functools.partial(_maps_kernel, n, distances),
        out_shape=jax.ShapeDtypeStruct((rounds, width, width), jnp.float32),
        in_specs=[pl.BlockSpec(memory_space=pltpu.VMEM)],
        out_specs=pl.BlockSpec(memory_space=pltpu.VMEM),
        scratch_shapes=[
            pltpu.VMEM((rounds, width, width), jnp.float32),
            pltpu.SemaphoreType.DMA((rounds,)),
            pltpu.SemaphoreType.DMA((rounds,)),
        ],
        compiler_params=pltpu.CompilerParams(collective_id=2, has_side_effects=True),
    )(maps_t)


def sweep(values, chain, n):
    distances = _doubling(n)
    rounds = len(distances)
    return pl.pallas_call(
        functools.partial(_sweep_kernel, n, distances),
        out_shape=jax.ShapeDtypeStruct(values.shape, jnp.float32),
        in_specs=[pl.BlockSpec(memory_space=pltpu.VMEM)] * 2,
        out_specs=pl.BlockSpec(memory_space=pltpu.VMEM),
        scratch_shapes=[
            pltpu.VMEM((rounds + 1,) + values.shape, jnp.float32),
            pltpu.VMEM((rounds + 1,) + values.shape, jnp.float32),
            pltpu.SemaphoreType.DMA((rounds + 1,)),
            pltpu.SemaphoreType.DMA((rounds + 1,)),
        ],
        compiler_params=pltpu.CompilerParams(collective_id=3, has_side_effects=True),
    )(values, chain)


def least_squares(hessen, beta):
    cases = hessen.shape[0]
    depth = hessen.shape[2]
    rhs = jnp.zeros((cases, depth + 1), jnp.float32).at[:, 0].set(beta)
    upper = hessen
    for column in range(depth):
        upper_row = upper[:, column, :]
        lower_row = upper[:, column + 1, :]
        radius = jnp.sqrt(upper_row[:, column] ** 2 + lower_row[:, column] ** 2)
        cosine = upper_row[:, column] / radius
        sine_term = lower_row[:, column] / radius
        upper = upper.at[:, column, :].set(
            cosine[:, None] * upper_row + sine_term[:, None] * lower_row
        )
        upper = upper.at[:, column + 1, :].set(
            -sine_term[:, None] * upper_row + cosine[:, None] * lower_row
        )
        first_rhs = rhs[:, column]
        second_rhs = rhs[:, column + 1]
        rhs = rhs.at[:, column].set(cosine * first_rhs + sine_term * second_rhs)
        rhs = rhs.at[:, column + 1].set(-sine_term * first_rhs + cosine * second_rhs)
    weights = jnp.zeros((cases, depth), jnp.float32)
    for column in reversed(range(depth)):
        remain = rhs[:, column] - jnp.sum(
            upper[:, column, column + 1 :] * weights[:, column + 1 :], axis=1
        )
        weights = weights.at[:, column].set(remain / upper[:, column, column])
    return weights


def local(
    mesh_shape,
    state_now, source, fan_gain, section_block, block_inverse, back_panel, ahead_panel, interface
):
    highest = lax.Precision.HIGHEST
    cases, node_rows = state_now.shape
    panel_width = back_panel.shape[1]
    indices = interface[0]
    first_row = lax.axis_index("blk") * node_rows
    selector = (indices[None, :] == first_row + jnp.arange(node_rows)[:, None]).astype(jnp.float32)
    contract = (((1,), (1,)), ((), ()))
    gain_panel = jnp.dot(
        block_inverse,
        lax.all_gather(back_panel, "blk", axis=0, tiled=True),
        preferred_element_type=jnp.float32,
    )
    panel_maps = -all_sum(jnp.dot(selector.T, gain_panel, precision=highest), ("blk",), mesh_shape, 1)

    chain = scan_maps(panel_maps.T, mesh_shape["sec"])

    def section_terms(dense_part, behind_vals, piece):
        width = piece.shape[1]
        dense_part = lax.dot_general(
            piece, section_block, contract, preferred_element_type=jnp.float32
        )
        picker = (indices[None, :] == jnp.arange(width)[:, None]).astype(jnp.bfloat16)
        behind_vals = jnp.dot(piece, picker, preferred_element_type=jnp.float32)
        return (dense_part, behind_vals)

    def fold_section(carry, piece):
        return section_terms(carry[0], carry[1], piece)

    def operator(vector):
        rounded = vector.astype(jnp.bfloat16)
        empty_dense = jnp.zeros((cases, node_rows), jnp.float32)
        empty_panel = jnp.zeros((cases, panel_width), jnp.float32)
        start_carry = (empty_dense, empty_panel)
        folded = fold_section(start_carry, lax.all_gather(rounded, "blk", axis=1, tiled=True))
        dense_part, behind_vals = folded
        upward = all_sum(
            jnp.dot(rounded, ahead_panel, preferred_element_type=jnp.float32), ("blk",), mesh_shape, 1
        )
        framed = extended(jnp.stack([behind_vals, upward])[None], (("sec", 0),), 1)
        behind = framed[0, 0].astype(jnp.bfloat16)
        ahead_term = framed[2, 1]
        lower_term = lax.dot_general(
            behind, back_panel, contract, preferred_element_type=jnp.float32
        )
        upper_term = jnp.dot(ahead_term, selector.T, precision=highest)
        return dense_part + lower_term + upper_term

    def compose(earlier, later):
        first_map, first_value = earlier
        second_map, second_value = later
        joined_map = jnp.dot(second_map, first_map, precision=highest)
        joined_value = jnp.dot(first_value, second_map.T, precision=highest) + second_value
        return (joined_map, joined_value)

    def lengths(vector):
        return jnp.sqrt(global_sum(jnp.sum(vector * vector, axis=1)[None], mesh_shape)[0] + epsilon)

    bent = jnp.tanh(state_now)
    residual = source - operator(state_now) - fan_gain[None, :] * bent
    jac_diag = fan_gain[None, :] * (1.0 - bent * bent)
    beta = lengths(residual)
    basis = [residual / beta[:, None]]
    directions = []
    hessen = jnp.zeros((cases, KRYLOV + 1, KRYLOV), jnp.float32)
    for column in range(KRYLOV):
        precondition_rounded = basis[column].astype(jnp.bfloat16)
        precondition_folded = lax.dot_general(
            lax.all_gather(precondition_rounded, "blk", axis=1, tiled=True),
            block_inverse,
            contract,
            preferred_element_type=jnp.float32,
        )
        values = all_sum(
            jnp.dot(precondition_folded, selector, precision=highest), ("blk",), mesh_shape, 1
        )
        before = sweep(values, chain, mesh_shape["sec"])
        direction = precondition_folded - lax.dot_general(
            before, gain_panel, contract, precision=highest
        )
        product = operator(direction) + jac_diag * direction
        stacked = jnp.stack(basis)
        projections = global_sum(jnp.sum(product[None] * stacked, axis=2), mesh_shape)
        product = product - jnp.sum(projections[:, :, None] * stacked, axis=0)
        length = lengths(product)
        hessen = hessen.at[:, : column + 1, column].set(projections.T)
        hessen = hessen.at[:, column + 1, column].set(length)
        basis.append(product / length[:, None])
        directions.append(direction)
    weights = least_squares(hessen, beta)
    update = jnp.zeros_like(state_now)
    for column in range(KRYLOV):
        update = update + weights[:, column : column + 1] * directions[column]
    return state_now + update


def solution(mesh):
    in_specs = (
        P(None, ("sec", "blk")),
        P(None, ("sec", "blk")),
        P(("sec", "blk")),
        P(("sec", "blk"), None),
        P(("sec", "blk"), None),
        P(("sec", "blk"), None),
        P(("sec", "blk"), None),
        P("sec", None),
    )
    out_specs = P(None, ("sec", "blk"))
    return jax.shard_map(functools.partial(local, dict(mesh.shape)), mesh=mesh, in_specs=in_specs, out_specs=out_specs, check_vma=False)
```

```python
import functools

import jax
import jax.numpy as jnp
from jax import lax
from jax.experimental import pallas as pl
from jax.experimental.pallas import tpu as pltpu
from jax.sharding import PartitionSpec as P

MESH = pl.DeviceIdType.MESH

KRYLOV = 3


epsilon = 1e-06


def extended(x, sides, width):
    for axis, dim in sides:
        size, length = (lax.axis_size(axis), x.shape[dim])
        up = [(i, (i + 1) % size) for i in range(size - 1)]
        down = [(j, i) for i, j in up]
        last = lax.slice_in_dim(x, length - width, length, axis=dim)
        first = lax.slice_in_dim(x, 0, width, axis=dim)
        before = lax.ppermute(last, axis, up)
        after = lax.ppermute(first, axis, down)
        x = jnp.concatenate([before, x, after], axis=dim)
    return x


def entering(value, axis, join, neutral):
    count, mine = (lax.axis_size(axis), lax.axis_index(axis))
    pieces = jax.tree.map(lambda part: lax.all_gather(part, axis), value)
    so_far = jax.tree.map(
        lambda part, zero: jnp.full_like(part, 0) + jnp.asarray(zero, part.dtype), value, neutral
    )

    def step(position, so_far):
        longer = join(so_far, jax.tree.map(lambda part: part[position], pieces))
        return jax.tree.map(lambda new, old: jnp.where(position < mine, new, old), longer, so_far)

    return lax.fori_loop(0, count - 1, step, so_far)


def _reduce_kernel(stages, x_ref, o_ref, *scratch):
    count = len(stages)
    slots = scratch[:count]
    partial = scratch[count]
    sends = scratch[count + 1 : 2 * count + 1]
    recvs = scratch[2 * count + 1 :]
    barrier = pltpu.get_barrier_semaphore()
    peers = 0
    for axis, n in stages:
        mine = lax.axis_index(axis)
        for k in range(1, n):
            pl.semaphore_signal(
                barrier, inc=1, device_id={axis: lax.rem(mine + k, n)}, device_id_type=MESH
            )
            peers += 1
    pl.semaphore_wait(barrier, peers)
    source = x_ref
    for stage, (axis, n) in enumerate(stages):
        mine = lax.axis_index(axis)
        copies = []
        for k in range(1, n):
            copy = pltpu.make_async_remote_copy(
                src_ref=source,
                dst_ref=slots[stage].at[mine],
                send_sem=sends[stage].at[k],
                recv_sem=recvs[stage].at[mine],
                device_id={axis: lax.rem(mine + k, n)},
                device_id_type=MESH,
            )
            copy.start()
            copies.append(copy)
        slots[stage][mine] = source[...]
        for k in range(1, n):
            sender = lax.rem(mine + k, n)
            pltpu.make_async_remote_copy(
                src_ref=source,
                dst_ref=slots[stage].at[sender],
                send_sem=sends[stage].at[k],
                recv_sem=recvs[stage].at[sender],
                device_id={axis: sender},
                device_id_type=MESH,
            ).wait_recv()
        for copy in copies:
            copy.wait_send()
        total = slots[stage][0]
        for j in range(1, n):
            total = total + slots[stage][j]
        if stage == count - 1:
            o_ref[...] = total
        else:
            partial[...] = total
            source = partial


def all_sum(x, axes, mesh_shape, collective):
    stages = tuple((axis, mesh_shape[axis]) for axis in axes if mesh_shape[axis] > 1)
    rows, cols = x.shape
    scratch = [pltpu.VMEM((n, rows, cols), jnp.float32) for _, n in stages]
    scratch.append(pltpu.VMEM((rows, cols), jnp.float32))
    scratch += [pltpu.SemaphoreType.DMA((n,)) for _, n in stages]
    scratch += [pltpu.SemaphoreType.DMA((n,)) for _, n in stages]
    return pl.pallas_call(
        functools.partial(_reduce_kernel, stages),
        out_shape=jax.ShapeDtypeStruct((rows, cols), jnp.float32),
        in_specs=[pl.BlockSpec(memory_space=pltpu.VMEM)],
        out_specs=pl.BlockSpec(memory_space=pltpu.VMEM),
        scratch_shapes=scratch,
        compiler_params=pltpu.CompilerParams(collective_id=collective, has_side_effects=True),
    )(x.astype(jnp.float32))


def global_sum(rows_of_sums, mesh_shape):
    count = rows_of_sums.shape[0]
    padded = jnp.zeros((8, rows_of_sums.shape[1]), jnp.float32).at[:count].set(rows_of_sums)
    return all_sum(padded, ("blk", "sec"), mesh_shape, 0)[:count]


def _doubling(n):
    distances, d = [], 1
    while d < n:
        distances.append(d)
        d *= 2
    return tuple(distances)


def _greet(n, distances):
    barrier = pltpu.get_barrier_semaphore()
    mine = lax.axis_index("sec")
    for d in distances:
        for peer in (lax.rem(mine + d, n), lax.rem(mine + n - d, n)):
            pl.semaphore_signal(barrier, inc=1, device_id={"sec": peer}, device_id_type=MESH)
    pl.semaphore_wait(barrier, 2 * len(distances))


def _hop(n, d, source, slot, send_sem, recv_sem):
    mine = lax.axis_index("sec")
    copy = pltpu.make_async_remote_copy(
        src_ref=source,
        dst_ref=slot,
        send_sem=send_sem,
        recv_sem=recv_sem,
        device_id={"sec": lax.rem(mine + d, n)},
        device_id_type=MESH,
    )
    copy.start()
    copy.wait_recv()
    copy.wait_send()


def _maps_kernel(n, distances, e_ref, t_ref, slots, sends, recvs):
    mine = lax.axis_index("sec")
    _greet(n, distances)
    t_ref[0] = e_ref[...]
    for k, d in enumerate(distances[:-1]):
        _hop(n, d, t_ref.at[k], slots.at[k], sends.at[k], recvs.at[k])
        joined = jnp.dot(
            slots[k], t_ref[k], precision=lax.Precision.HIGHEST, preferred_element_type=jnp.float32
        )
        t_ref[k + 1] = jnp.where(mine >= d, joined, t_ref[k])


def _sweep_kernel(n, distances, f_ref, t_ref, o_ref, carry, slots, sends, recvs):
    mine = lax.axis_index("sec")
    _greet(n, distances)
    carry[0] = f_ref[...]
    for k, d in enumerate(distances):
        _hop(n, d, carry.at[k], slots.at[k], sends.at[k], recvs.at[k])
        joined = carry[k] + jnp.dot(
            slots[k], t_ref[k], precision=lax.Precision.HIGHEST, preferred_element_type=jnp.float32
        )
        carry[k + 1] = jnp.where(mine >= d, joined, carry[k])
    last = len(distances)
    _hop(n, 1, carry.at[last], slots.at[last], sends.at[last], recvs.at[last])
    o_ref[...] = jnp.where(mine >= 1, slots[last], jnp.zeros_like(o_ref))


def scan_maps(maps_t, n):
    distances = _doubling(n)
    rounds, width = len(distances), maps_t.shape[0]
    return pl.pallas_call(
        functools.partial(_maps_kernel, n, distances),
        out_shape=jax.ShapeDtypeStruct((rounds, width, width), jnp.float32),
        in_specs=[pl.BlockSpec(memory_space=pltpu.VMEM)],
        out_specs=pl.BlockSpec(memory_space=pltpu.VMEM),
        scratch_shapes=[
            pltpu.VMEM((rounds, width, width), jnp.float32),
            pltpu.SemaphoreType.DMA((rounds,)),
            pltpu.SemaphoreType.DMA((rounds,)),
        ],
        compiler_params=pltpu.CompilerParams(collective_id=2, has_side_effects=True),
    )(maps_t)


def sweep(values, chain, n):
    distances = _doubling(n)
    rounds = len(distances)
    return pl.pallas_call(
        functools.partial(_sweep_kernel, n, distances),
        out_shape=jax.ShapeDtypeStruct(values.shape, jnp.float32),
        in_specs=[pl.BlockSpec(memory_space=pltpu.VMEM)] * 2,
        out_specs=pl.BlockSpec(memory_space=pltpu.VMEM),
        scratch_shapes=[
            pltpu.VMEM((rounds + 1,) + values.shape, jnp.float32),
            pltpu.VMEM((rounds + 1,) + values.shape, jnp.float32),
            pltpu.SemaphoreType.DMA((rounds + 1,)),
            pltpu.SemaphoreType.DMA((rounds + 1,)),
        ],
        compiler_params=pltpu.CompilerParams(collective_id=3, has_side_effects=True),
    )(values, chain)


def _gather_kernel(n, x_ref, o_ref, slots, sends, recvs):
    mine = lax.axis_index("blk")
    barrier = pltpu.get_barrier_semaphore()
    for k in range(1, n):
        pl.semaphore_signal(
            barrier, inc=1, device_id={"blk": lax.rem(mine + k, n)}, device_id_type=MESH
        )
    pl.semaphore_wait(barrier, n - 1)
    copies = []
    for k in range(1, n):
        copy = pltpu.make_async_remote_copy(
            src_ref=x_ref,
            dst_ref=slots.at[mine],
            send_sem=sends.at[k],
            recv_sem=recvs.at[mine],
            device_id={"blk": lax.rem(mine + k, n)},
            device_id_type=MESH,
        )
        copy.start()
        copies.append(copy)
    slots[mine] = x_ref[...]
    for k in range(1, n):
        sender = lax.rem(mine + k, n)
        pltpu.make_async_remote_copy(
            src_ref=x_ref,
            dst_ref=slots.at[sender],
            send_sem=sends.at[k],
            recv_sem=recvs.at[sender],
            device_id={"blk": sender},
            device_id_type=MESH,
        ).wait_recv()
    for copy in copies:
        copy.wait_send()
    width = x_ref.shape[1]
    for j in range(n):
        o_ref[:, j * width : (j + 1) * width] = slots[j]


def gather_blk(x, n):
    rows, width = x.shape
    return pl.pallas_call(
        functools.partial(_gather_kernel, n),
        out_shape=jax.ShapeDtypeStruct((rows, n * width), x.dtype),
        in_specs=[pl.BlockSpec(memory_space=pltpu.VMEM)],
        out_specs=pl.BlockSpec(memory_space=pltpu.VMEM),
        scratch_shapes=[
            pltpu.VMEM((n, rows, width), x.dtype),
            pltpu.SemaphoreType.DMA((n,)),
            pltpu.SemaphoreType.DMA((n,)),
        ],
        compiler_params=pltpu.CompilerParams(collective_id=4, has_side_effects=True),
    )(x)


def least_squares(hessen, beta):
    cases = hessen.shape[0]
    depth = hessen.shape[2]
    rhs = jnp.zeros((cases, depth + 1), jnp.float32).at[:, 0].set(beta)
    upper = hessen
    for column in range(depth):
        upper_row = upper[:, column, :]
        lower_row = upper[:, column + 1, :]
        radius = jnp.sqrt(upper_row[:, column] ** 2 + lower_row[:, column] ** 2)
        cosine = upper_row[:, column] / radius
        sine_term = lower_row[:, column] / radius
        upper = upper.at[:, column, :].set(
            cosine[:, None] * upper_row + sine_term[:, None] * lower_row
        )
        upper = upper.at[:, column + 1, :].set(
            -sine_term[:, None] * upper_row + cosine[:, None] * lower_row
        )
        first_rhs = rhs[:, column]
        second_rhs = rhs[:, column + 1]
        rhs = rhs.at[:, column].set(cosine * first_rhs + sine_term * second_rhs)
        rhs = rhs.at[:, column + 1].set(-sine_term * first_rhs + cosine * second_rhs)
    weights = jnp.zeros((cases, depth), jnp.float32)
    for column in reversed(range(depth)):
        remain = rhs[:, column] - jnp.sum(
            upper[:, column, column + 1 :] * weights[:, column + 1 :], axis=1
        )
        weights = weights.at[:, column].set(remain / upper[:, column, column])
    return weights


def local(
    mesh_shape,
    state_now, source, fan_gain, section_block, block_inverse, back_panel, ahead_panel, interface
):
    highest = lax.Precision.HIGHEST
    cases, node_rows = state_now.shape
    panel_width = back_panel.shape[1]
    indices = interface[0]
    first_row = lax.axis_index("blk") * node_rows
    selector = (indices[None, :] == first_row + jnp.arange(node_rows)[:, None]).astype(jnp.float32)
    contract = (((1,), (1,)), ((), ()))
    gain_panel = jnp.dot(
        block_inverse,
        lax.all_gather(back_panel, "blk", axis=0, tiled=True),
        preferred_element_type=jnp.float32,
    )
    panel_maps = -all_sum(jnp.dot(selector.T, gain_panel, precision=highest), ("blk",), mesh_shape, 1)

    chain = scan_maps(panel_maps.T, mesh_shape["sec"])

    def section_terms(dense_part, behind_vals, piece):
        width = piece.shape[1]
        dense_part = lax.dot_general(
            piece, section_block, contract, preferred_element_type=jnp.float32
        )
        picker = (indices[None, :] == jnp.arange(width)[:, None]).astype(jnp.bfloat16)
        behind_vals = jnp.dot(piece, picker, preferred_element_type=jnp.float32)
        return (dense_part, behind_vals)

    def fold_section(carry, piece):
        return section_terms(carry[0], carry[1], piece)

    def operator(vector):
        rounded = vector.astype(jnp.bfloat16)
        empty_dense = jnp.zeros((cases, node_rows), jnp.float32)
        empty_panel = jnp.zeros((cases, panel_width), jnp.float32)
        start_carry = (empty_dense, empty_panel)
        folded = fold_section(start_carry, gather_blk(rounded, mesh_shape["blk"]))
        dense_part, behind_vals = folded
        upward = all_sum(
            jnp.dot(rounded, ahead_panel, preferred_element_type=jnp.float32), ("blk",), mesh_shape, 1
        )
        framed = extended(jnp.stack([behind_vals, upward])[None], (("sec", 0),), 1)
        behind = framed[0, 0].astype(jnp.bfloat16)
        ahead_term = framed[2, 1]
        lower_term = lax.dot_general(
            behind, back_panel, contract, preferred_element_type=jnp.float32
        )
        upper_term = jnp.dot(ahead_term, selector.T, precision=highest)
        return dense_part + lower_term + upper_term

    def compose(earlier, later):
        first_map, first_value = earlier
        second_map, second_value = later
        joined_map = jnp.dot(second_map, first_map, precision=highest)
        joined_value = jnp.dot(first_value, second_map.T, precision=highest) + second_value
        return (joined_map, joined_value)

    def lengths(vector):
        return jnp.sqrt(global_sum(jnp.sum(vector * vector, axis=1)[None], mesh_shape)[0] + epsilon)

    bent = jnp.tanh(state_now)
    residual = source - operator(state_now) - fan_gain[None, :] * bent
    jac_diag = fan_gain[None, :] * (1.0 - bent * bent)
    beta = lengths(residual)
    basis = [residual / beta[:, None]]
    directions = []
    hessen = jnp.zeros((cases, KRYLOV + 1, KRYLOV), jnp.float32)
    for column in range(KRYLOV):
        precondition_rounded = basis[column].astype(jnp.bfloat16)
        precondition_folded = lax.dot_general(
            gather_blk(precondition_rounded, mesh_shape["blk"]),
            block_inverse,
            contract,
            preferred_element_type=jnp.float32,
        )
        values = all_sum(
            jnp.dot(precondition_folded, selector, precision=highest), ("blk",), mesh_shape, 1
        )
        before = sweep(values, chain, mesh_shape["sec"])
        direction = precondition_folded - lax.dot_general(
            before, gain_panel, contract, precision=highest
        )
        product = operator(direction) + jac_diag * direction
        stacked = jnp.stack(basis)
        projections = global_sum(jnp.sum(product[None] * stacked, axis=2), mesh_shape)
        product = product - jnp.sum(projections[:, :, None] * stacked, axis=0)
        length = lengths(product)
        hessen = hessen.at[:, : column + 1, column].set(projections.T)
        hessen = hessen.at[:, column + 1, column].set(length)
        basis.append(product / length[:, None])
        directions.append(direction)
    weights = least_squares(hessen, beta)
    update = jnp.zeros_like(state_now)
    for column in range(KRYLOV):
        update = update + weights[:, column : column + 1] * directions[column]
    return state_now + update


def solution(mesh):
    in_specs = (
        P(None, ("sec", "blk")),
        P(None, ("sec", "blk")),
        P(("sec", "blk")),
        P(("sec", "blk"), None),
        P(("sec", "blk"), None),
        P(("sec", "blk"), None),
        P(("sec", "blk"), None),
        P("sec", None),
    )
    out_specs = P(None, ("sec", "blk"))
    return jax.shard_map(functools.partial(local, dict(mesh.shape)), mesh=mesh, in_specs=in_specs, out_specs=out_specs, check_vma=False)
```

```python
import functools

import jax
import jax.numpy as jnp
from jax import lax
from jax.experimental import pallas as pl
from jax.experimental.pallas import tpu as pltpu
from jax.sharding import PartitionSpec as P

MESH = pl.DeviceIdType.MESH

KRYLOV = 3


epsilon = 1e-06


def extended(x, sides, width):
    for axis, dim in sides:
        size, length = (lax.axis_size(axis), x.shape[dim])
        up = [(i, (i + 1) % size) for i in range(size - 1)]
        down = [(j, i) for i, j in up]
        last = lax.slice_in_dim(x, length - width, length, axis=dim)
        first = lax.slice_in_dim(x, 0, width, axis=dim)
        before = lax.ppermute(last, axis, up)
        after = lax.ppermute(first, axis, down)
        x = jnp.concatenate([before, x, after], axis=dim)
    return x


def entering(value, axis, join, neutral):
    count, mine = (lax.axis_size(axis), lax.axis_index(axis))
    pieces = jax.tree.map(lambda part: lax.all_gather(part, axis), value)
    so_far = jax.tree.map(
        lambda part, zero: jnp.full_like(part, 0) + jnp.asarray(zero, part.dtype), value, neutral
    )

    def step(position, so_far):
        longer = join(so_far, jax.tree.map(lambda part: part[position], pieces))
        return jax.tree.map(lambda new, old: jnp.where(position < mine, new, old), longer, so_far)

    return lax.fori_loop(0, count - 1, step, so_far)


def _reduce_kernel(stages, x_ref, o_ref, *scratch):
    count = len(stages)
    slots = scratch[:count]
    partial = scratch[count]
    sends = scratch[count + 1 : 2 * count + 1]
    recvs = scratch[2 * count + 1 :]
    barrier = pltpu.get_barrier_semaphore()
    peers = 0
    for axis, n in stages:
        mine = lax.axis_index(axis)
        for k in range(1, n):
            pl.semaphore_signal(
                barrier, inc=1, device_id={axis: lax.rem(mine + k, n)}, device_id_type=MESH
            )
            peers += 1
    pl.semaphore_wait(barrier, peers)
    source = x_ref
    for stage, (axis, n) in enumerate(stages):
        mine = lax.axis_index(axis)
        copies = []
        for k in range(1, n):
            copy = pltpu.make_async_remote_copy(
                src_ref=source,
                dst_ref=slots[stage].at[mine],
                send_sem=sends[stage].at[k],
                recv_sem=recvs[stage].at[mine],
                device_id={axis: lax.rem(mine + k, n)},
                device_id_type=MESH,
            )
            copy.start()
            copies.append(copy)
        slots[stage][mine] = source[...]
        for k in range(1, n):
            sender = lax.rem(mine + k, n)
            pltpu.make_async_remote_copy(
                src_ref=source,
                dst_ref=slots[stage].at[sender],
                send_sem=sends[stage].at[k],
                recv_sem=recvs[stage].at[sender],
                device_id={axis: sender},
                device_id_type=MESH,
            ).wait_recv()
        for copy in copies:
            copy.wait_send()
        total = slots[stage][0]
        for j in range(1, n):
            total = total + slots[stage][j]
        if stage == count - 1:
            o_ref[...] = total
        else:
            partial[...] = total
            source = partial


def all_sum(x, axes, mesh_shape, collective):
    stages = tuple((axis, mesh_shape[axis]) for axis in axes if mesh_shape[axis] > 1)
    rows, cols = x.shape
    scratch = [pltpu.VMEM((n, rows, cols), jnp.float32) for _, n in stages]
    scratch.append(pltpu.VMEM((rows, cols), jnp.float32))
    scratch += [pltpu.SemaphoreType.DMA((n,)) for _, n in stages]
    scratch += [pltpu.SemaphoreType.DMA((n,)) for _, n in stages]
    return pl.pallas_call(
        functools.partial(_reduce_kernel, stages),
        out_shape=jax.ShapeDtypeStruct((rows, cols), jnp.float32),
        in_specs=[pl.BlockSpec(memory_space=pltpu.VMEM)],
        out_specs=pl.BlockSpec(memory_space=pltpu.VMEM),
        scratch_shapes=scratch,
        compiler_params=pltpu.CompilerParams(collective_id=collective, has_side_effects=True),
    )(x.astype(jnp.float32))


def global_sum(rows_of_sums, mesh_shape):
    count = rows_of_sums.shape[0]
    padded = jnp.zeros((8, rows_of_sums.shape[1]), jnp.float32).at[:count].set(rows_of_sums)
    return all_sum(padded, ("blk", "sec"), mesh_shape, 0)[:count]


def _doubling(n):
    distances, d = [], 1
    while d < n:
        distances.append(d)
        d *= 2
    return tuple(distances)


def _greet(n, distances):
    barrier = pltpu.get_barrier_semaphore()
    mine = lax.axis_index("sec")
    for d in distances:
        for peer in (lax.rem(mine + d, n), lax.rem(mine + n - d, n)):
            pl.semaphore_signal(barrier, inc=1, device_id={"sec": peer}, device_id_type=MESH)
    pl.semaphore_wait(barrier, 2 * len(distances))


def _hop(n, d, source, slot, send_sem, recv_sem):
    mine = lax.axis_index("sec")
    copy = pltpu.make_async_remote_copy(
        src_ref=source,
        dst_ref=slot,
        send_sem=send_sem,
        recv_sem=recv_sem,
        device_id={"sec": lax.rem(mine + d, n)},
        device_id_type=MESH,
    )
    copy.start()
    copy.wait_recv()
    copy.wait_send()


def _maps_kernel(n, distances, e_ref, t_ref, slots, sends, recvs):
    mine = lax.axis_index("sec")
    _greet(n, distances)
    t_ref[0] = e_ref[...]
    for k, d in enumerate(distances[:-1]):
        _hop(n, d, t_ref.at[k], slots.at[k], sends.at[k], recvs.at[k])
        joined = jnp.dot(
            slots[k], t_ref[k], precision=lax.Precision.HIGHEST, preferred_element_type=jnp.float32
        )
        t_ref[k + 1] = jnp.where(mine >= d, joined, t_ref[k])


def _sweep_kernel(n, distances, f_ref, t_ref, o_ref, carry, slots, sends, recvs):
    mine = lax.axis_index("sec")
    _greet(n, distances)
    carry[0] = f_ref[...]
    for k, d in enumerate(distances):
        _hop(n, d, carry.at[k], slots.at[k], sends.at[k], recvs.at[k])
        joined = carry[k] + jnp.dot(
            slots[k], t_ref[k], precision=lax.Precision.HIGHEST, preferred_element_type=jnp.float32
        )
        carry[k + 1] = jnp.where(mine >= d, joined, carry[k])
    last = len(distances)
    _hop(n, 1, carry.at[last], slots.at[last], sends.at[last], recvs.at[last])
    o_ref[...] = jnp.where(mine >= 1, slots[last], jnp.zeros_like(o_ref))


def scan_maps(maps_t, n):
    distances = _doubling(n)
    rounds, width = len(distances), maps_t.shape[0]
    return pl.pallas_call(
        functools.partial(_maps_kernel, n, distances),
        out_shape=jax.ShapeDtypeStruct((rounds, width, width), jnp.float32),
        in_specs=[pl.BlockSpec(memory_space=pltpu.VMEM)],
        out_specs=pl.BlockSpec(memory_space=pltpu.VMEM),
        scratch_shapes=[
            pltpu.VMEM((rounds, width, width), jnp.float32),
            pltpu.SemaphoreType.DMA((rounds,)),
            pltpu.SemaphoreType.DMA((rounds,)),
        ],
        compiler_params=pltpu.CompilerParams(collective_id=2, has_side_effects=True),
    )(maps_t)


def sweep(values, chain, n):
    distances = _doubling(n)
    rounds = len(distances)
    return pl.pallas_call(
        functools.partial(_sweep_kernel, n, distances),
        out_shape=jax.ShapeDtypeStruct(values.shape, jnp.float32),
        in_specs=[pl.BlockSpec(memory_space=pltpu.VMEM)] * 2,
        out_specs=pl.BlockSpec(memory_space=pltpu.VMEM),
        scratch_shapes=[
            pltpu.VMEM((rounds + 1,) + values.shape, jnp.float32),
            pltpu.VMEM((rounds + 1,) + values.shape, jnp.float32),
            pltpu.SemaphoreType.DMA((rounds + 1,)),
            pltpu.SemaphoreType.DMA((rounds + 1,)),
        ],
        compiler_params=pltpu.CompilerParams(collective_id=3, has_side_effects=True),
    )(values, chain)


def _gather_kernel(n, x_ref, o_ref, slots, sends, recvs):
    mine = lax.axis_index("blk")
    barrier = pltpu.get_barrier_semaphore()
    for k in range(1, n):
        pl.semaphore_signal(
            barrier, inc=1, device_id={"blk": lax.rem(mine + k, n)}, device_id_type=MESH
        )
    pl.semaphore_wait(barrier, n - 1)
    copies = []
    for k in range(1, n):
        copy = pltpu.make_async_remote_copy(
            src_ref=x_ref,
            dst_ref=slots.at[mine],
            send_sem=sends.at[k],
            recv_sem=recvs.at[mine],
            device_id={"blk": lax.rem(mine + k, n)},
            device_id_type=MESH,
        )
        copy.start()
        copies.append(copy)
    slots[mine] = x_ref[...]
    for k in range(1, n):
        sender = lax.rem(mine + k, n)
        pltpu.make_async_remote_copy(
            src_ref=x_ref,
            dst_ref=slots.at[sender],
            send_sem=sends.at[k],
            recv_sem=recvs.at[sender],
            device_id={"blk": sender},
            device_id_type=MESH,
        ).wait_recv()
    for copy in copies:
        copy.wait_send()
    width = x_ref.shape[1]
    for j in range(n):
        o_ref[:, j * width : (j + 1) * width] = slots[j]


def gather_blk(x, n):
    rows, width = x.shape
    return pl.pallas_call(
        functools.partial(_gather_kernel, n),
        out_shape=jax.ShapeDtypeStruct((rows, n * width), x.dtype),
        in_specs=[pl.BlockSpec(memory_space=pltpu.VMEM)],
        out_specs=pl.BlockSpec(memory_space=pltpu.VMEM),
        scratch_shapes=[
            pltpu.VMEM((n, rows, width), x.dtype),
            pltpu.SemaphoreType.DMA((n,)),
            pltpu.SemaphoreType.DMA((n,)),
        ],
        compiler_params=pltpu.CompilerParams(collective_id=4, has_side_effects=True),
    )(x)


def _operator_kernel(n_sec, n_blk, x_ref, up_ref, be_ref, g_ref, b_ref, a_ref, *scratch):
    gslots, bslots, aslots, gsend, grecv, bsend, brecv, asend, arecv = scratch
    sec, blk = lax.axis_index("sec"), lax.axis_index("blk")
    nxt, prv = lax.rem(sec + 1, n_sec), lax.rem(sec + n_sec - 1, n_sec)
    piece = bslots.shape[1]
    barrier = pltpu.get_barrier_semaphore()
    for k in range(1, n_blk):
        pl.semaphore_signal(
            barrier, inc=1, device_id={"blk": lax.rem(blk + k, n_blk)}, device_id_type=MESH
        )
    for j in range(n_blk):
        for other in (nxt, prv):
            pl.semaphore_signal(
                barrier, inc=1, device_id={"sec": other, "blk": j}, device_id_type=MESH
            )
    pl.semaphore_wait(barrier, 3 * n_blk - 1)
    copies = []
    for k in range(1, n_blk):
        copies.append(
            pltpu.make_async_remote_copy(
                src_ref=x_ref,
                dst_ref=gslots.at[blk],
                send_sem=gsend.at[k],
                recv_sem=grecv.at[blk],
                device_id={"blk": lax.rem(blk + k, n_blk)},
                device_id_type=MESH,
            )
        )
    mine = pl.ds(pl.multiple_of(blk * piece, 8), piece)
    for j in range(n_blk):
        copies.append(
            pltpu.make_async_remote_copy(
                src_ref=be_ref.at[mine],
                dst_ref=bslots.at[blk],
                send_sem=bsend.at[j],
                recv_sem=brecv.at[blk],
                device_id={"sec": nxt, "blk": j},
                device_id_type=MESH,
            )
        )
        copies.append(
            pltpu.make_async_remote_copy(
                src_ref=up_ref.at[pl.ds(j * piece, piece)],
                dst_ref=aslots.at[blk],
                send_sem=asend.at[j],
                recv_sem=arecv.at[blk],
                device_id={"sec": prv, "blk": j},
                device_id_type=MESH,
            )
        )
    for copy in copies:
        copy.start()
    gslots[blk] = x_ref[...]
    for k in range(1, n_blk):
        sender = lax.rem(blk + k, n_blk)
        pltpu.make_async_remote_copy(
            src_ref=x_ref,
            dst_ref=gslots.at[sender],
            send_sem=gsend.at[k],
            recv_sem=grecv.at[sender],
            device_id={"blk": sender},
            device_id_type=MESH,
        ).wait_recv()
    for j in range(n_blk):
        pltpu.make_async_remote_copy(
            src_ref=be_ref.at[mine],
            dst_ref=bslots.at[j],
            send_sem=bsend.at[j],
            recv_sem=brecv.at[j],
            device_id={"sec": prv, "blk": j},
            device_id_type=MESH,
        ).wait_recv()
        pltpu.make_async_remote_copy(
            src_ref=up_ref.at[pl.ds(j * piece, piece)],
            dst_ref=aslots.at[j],
            send_sem=asend.at[j],
            recv_sem=arecv.at[j],
            device_id={"sec": nxt, "blk": j},
            device_id_type=MESH,
        ).wait_recv()
    for copy in copies:
        copy.wait_send()
    width = x_ref.shape[1]
    for j in range(n_blk):
        g_ref[:, j * width : (j + 1) * width] = gslots[j]
        b_ref[j * piece : (j + 1) * piece, :] = jnp.where(
            sec >= 1, bslots[j], jnp.zeros_like(bslots[j])
        )
    total = aslots[0]
    for j in range(1, n_blk):
        total = total + aslots[j]
    a_ref[...] = jnp.where(sec <= n_sec - 2, total, jnp.zeros_like(total))


def operator_exchange(x, up_t, be_t, n_sec, n_blk):
    rows, width = x.shape
    panel, cases = up_t.shape
    piece = panel // n_blk
    return pl.pallas_call(
        functools.partial(_operator_kernel, n_sec, n_blk),
        out_shape=(
            jax.ShapeDtypeStruct((rows, n_blk * width), x.dtype),
            jax.ShapeDtypeStruct((panel, cases), jnp.float32),
            jax.ShapeDtypeStruct((piece, cases), jnp.float32),
        ),
        in_specs=[pl.BlockSpec(memory_space=pltpu.VMEM)] * 3,
        out_specs=[pl.BlockSpec(memory_space=pltpu.VMEM)] * 3,
        scratch_shapes=[
            pltpu.VMEM((n_blk, rows, width), x.dtype),
            pltpu.VMEM((n_blk, piece, cases), jnp.float32),
            pltpu.VMEM((n_blk, piece, cases), jnp.float32),
        ]
        + [pltpu.SemaphoreType.DMA((n_blk,))] * 6,
        compiler_params=pltpu.CompilerParams(collective_id=5, has_side_effects=True),
    )(x, up_t, be_t)


def least_squares(hessen, beta):
    cases = hessen.shape[0]
    depth = hessen.shape[2]
    rhs = jnp.zeros((cases, depth + 1), jnp.float32).at[:, 0].set(beta)
    upper = hessen
    for column in range(depth):
        upper_row = upper[:, column, :]
        lower_row = upper[:, column + 1, :]
        radius = jnp.sqrt(upper_row[:, column] ** 2 + lower_row[:, column] ** 2)
        cosine = upper_row[:, column] / radius
        sine_term = lower_row[:, column] / radius
        upper = upper.at[:, column, :].set(
            cosine[:, None] * upper_row + sine_term[:, None] * lower_row
        )
        upper = upper.at[:, column + 1, :].set(
            -sine_term[:, None] * upper_row + cosine[:, None] * lower_row
        )
        first_rhs = rhs[:, column]
        second_rhs = rhs[:, column + 1]
        rhs = rhs.at[:, column].set(cosine * first_rhs + sine_term * second_rhs)
        rhs = rhs.at[:, column + 1].set(-sine_term * first_rhs + cosine * second_rhs)
    weights = jnp.zeros((cases, depth), jnp.float32)
    for column in reversed(range(depth)):
        remain = rhs[:, column] - jnp.sum(
            upper[:, column, column + 1 :] * weights[:, column + 1 :], axis=1
        )
        weights = weights.at[:, column].set(remain / upper[:, column, column])
    return weights


def local(
    mesh_shape,
    state_now, source, fan_gain, section_block, block_inverse, back_panel, ahead_panel, interface
):
    highest = lax.Precision.HIGHEST
    cases, node_rows = state_now.shape
    panel_width = back_panel.shape[1]
    indices = interface[0]
    first_row = lax.axis_index("blk") * node_rows
    selector = (indices[None, :] == first_row + jnp.arange(node_rows)[:, None]).astype(jnp.float32)
    contract = (((1,), (1,)), ((), ()))
    gain_panel = jnp.dot(
        block_inverse,
        lax.all_gather(back_panel, "blk", axis=0, tiled=True),
        preferred_element_type=jnp.float32,
    )
    panel_maps = -all_sum(jnp.dot(selector.T, gain_panel, precision=highest), ("blk",), mesh_shape, 1)

    chain = scan_maps(panel_maps.T, mesh_shape["sec"])

    def section_terms(dense_part, behind_vals, piece):
        width = piece.shape[1]
        dense_part = lax.dot_general(
            piece, section_block, contract, preferred_element_type=jnp.float32
        )
        picker = (indices[None, :] == jnp.arange(width)[:, None]).astype(jnp.bfloat16)
        behind_vals = jnp.dot(piece, picker, preferred_element_type=jnp.float32)
        return (dense_part, behind_vals)

    def fold_section(carry, piece):
        return section_terms(carry[0], carry[1], piece)

    def operator(vector):
        rounded = vector.astype(jnp.bfloat16)
        n_sec, n_blk = mesh_shape["sec"], mesh_shape["blk"]
        piece = panel_width // n_blk
        up_t = lax.dot_general(
            ahead_panel, rounded, (((0,), (1,)), ((), ())), preferred_element_type=jnp.float32
        )
        be_t = lax.dot_general(
            selector.astype(jnp.bfloat16),
            rounded,
            (((0,), (1,)), ((), ())),
            preferred_element_type=jnp.float32,
        )
        gathered, behind_t, ahead_piece = operator_exchange(rounded, up_t, be_t, n_sec, n_blk)
        dense_part = lax.dot_general(
            gathered, section_block, contract, preferred_element_type=jnp.float32
        )
        lower_term = lax.dot_general(
            behind_t.astype(jnp.bfloat16),
            back_panel,
            (((0,), (1,)), ((), ())),
            preferred_element_type=jnp.float32,
        )
        local_picks = lax.dynamic_slice_in_dim(selector, lax.axis_index("blk") * piece, piece, 1)
        upper_term = lax.dot_general(
            ahead_piece, local_picks, (((0,), (1,)), ((), ())), precision=highest
        )
        return dense_part + lower_term + upper_term

    def compose(earlier, later):
        first_map, first_value = earlier
        second_map, second_value = later
        joined_map = jnp.dot(second_map, first_map, precision=highest)
        joined_value = jnp.dot(first_value, second_map.T, precision=highest) + second_value
        return (joined_map, joined_value)

    def lengths(vector):
        return jnp.sqrt(global_sum(jnp.sum(vector * vector, axis=1)[None], mesh_shape)[0] + epsilon)

    bent = jnp.tanh(state_now)
    residual = source - operator(state_now) - fan_gain[None, :] * bent
    jac_diag = fan_gain[None, :] * (1.0 - bent * bent)
    beta = lengths(residual)
    basis = [residual / beta[:, None]]
    directions = []
    hessen = jnp.zeros((cases, KRYLOV + 1, KRYLOV), jnp.float32)
    for column in range(KRYLOV):
        precondition_rounded = basis[column].astype(jnp.bfloat16)
        precondition_folded = lax.dot_general(
            gather_blk(precondition_rounded, mesh_shape["blk"]),
            block_inverse,
            contract,
            preferred_element_type=jnp.float32,
        )
        values = all_sum(
            jnp.dot(precondition_folded, selector, precision=highest), ("blk",), mesh_shape, 1
        )
        before = sweep(values, chain, mesh_shape["sec"])
        direction = precondition_folded - lax.dot_general(
            before, gain_panel, contract, precision=highest
        )
        product = operator(direction) + jac_diag * direction
        stacked = jnp.stack(basis)
        projections = global_sum(jnp.sum(product[None] * stacked, axis=2), mesh_shape)
        product = product - jnp.sum(projections[:, :, None] * stacked, axis=0)
        length = lengths(product)
        hessen = hessen.at[:, : column + 1, column].set(projections.T)
        hessen = hessen.at[:, column + 1, column].set(length)
        basis.append(product / length[:, None])
        directions.append(direction)
    weights = least_squares(hessen, beta)
    update = jnp.zeros_like(state_now)
    for column in range(KRYLOV):
        update = update + weights[:, column : column + 1] * directions[column]
    return state_now + update


def solution(mesh):
    in_specs = (
        P(None, ("sec", "blk")),
        P(None, ("sec", "blk")),
        P(("sec", "blk")),
        P(("sec", "blk"), None),
        P(("sec", "blk"), None),
        P(("sec", "blk"), None),
        P(("sec", "blk"), None),
        P("sec", None),
    )
    out_specs = P(None, ("sec", "blk"))
    return jax.shard_map(functools.partial(local, dict(mesh.shape)), mesh=mesh, in_specs=in_specs, out_specs=out_specs, check_vma=False)
```

```python
import functools

import jax
import jax.numpy as jnp
from jax import lax
from jax.experimental import pallas as pl
from jax.experimental.pallas import tpu as pltpu
from jax.sharding import PartitionSpec as P

MESH = pl.DeviceIdType.MESH

KRYLOV = 3


epsilon = 1e-06


def extended(x, sides, width):
    for axis, dim in sides:
        size, length = (lax.axis_size(axis), x.shape[dim])
        up = [(i, (i + 1) % size) for i in range(size - 1)]
        down = [(j, i) for i, j in up]
        last = lax.slice_in_dim(x, length - width, length, axis=dim)
        first = lax.slice_in_dim(x, 0, width, axis=dim)
        before = lax.ppermute(last, axis, up)
        after = lax.ppermute(first, axis, down)
        x = jnp.concatenate([before, x, after], axis=dim)
    return x


def entering(value, axis, join, neutral):
    count, mine = (lax.axis_size(axis), lax.axis_index(axis))
    pieces = jax.tree.map(lambda part: lax.all_gather(part, axis), value)
    so_far = jax.tree.map(
        lambda part, zero: jnp.full_like(part, 0) + jnp.asarray(zero, part.dtype), value, neutral
    )

    def step(position, so_far):
        longer = join(so_far, jax.tree.map(lambda part: part[position], pieces))
        return jax.tree.map(lambda new, old: jnp.where(position < mine, new, old), longer, so_far)

    return lax.fori_loop(0, count - 1, step, so_far)


def _reduce_kernel(stages, x_ref, o_ref, *scratch):
    count = len(stages)
    slots = scratch[:count]
    partial = scratch[count]
    sends = scratch[count + 1 : 2 * count + 1]
    recvs = scratch[2 * count + 1 :]
    barrier = pltpu.get_barrier_semaphore()
    peers = 0
    for axis, n in stages:
        mine = lax.axis_index(axis)
        for k in range(1, n):
            pl.semaphore_signal(
                barrier, inc=1, device_id={axis: lax.rem(mine + k, n)}, device_id_type=MESH
            )
            peers += 1
    pl.semaphore_wait(barrier, peers)
    source = x_ref
    for stage, (axis, n) in enumerate(stages):
        mine = lax.axis_index(axis)
        copies = []
        for k in range(1, n):
            copy = pltpu.make_async_remote_copy(
                src_ref=source,
                dst_ref=slots[stage].at[mine],
                send_sem=sends[stage].at[k],
                recv_sem=recvs[stage].at[mine],
                device_id={axis: lax.rem(mine + k, n)},
                device_id_type=MESH,
            )
            copy.start()
            copies.append(copy)
        slots[stage][mine] = source[...]
        for k in range(1, n):
            sender = lax.rem(mine + k, n)
            pltpu.make_async_remote_copy(
                src_ref=source,
                dst_ref=slots[stage].at[sender],
                send_sem=sends[stage].at[k],
                recv_sem=recvs[stage].at[sender],
                device_id={axis: sender},
                device_id_type=MESH,
            ).wait_recv()
        for copy in copies:
            copy.wait_send()
        total = slots[stage][0]
        for j in range(1, n):
            total = total + slots[stage][j]
        if stage == count - 1:
            o_ref[...] = total
        else:
            partial[...] = total
            source = partial


def all_sum(x, axes, mesh_shape, collective):
    stages = tuple((axis, mesh_shape[axis]) for axis in axes if mesh_shape[axis] > 1)
    rows, cols = x.shape
    scratch = [pltpu.VMEM((n, rows, cols), jnp.float32) for _, n in stages]
    scratch.append(pltpu.VMEM((rows, cols), jnp.float32))
    scratch += [pltpu.SemaphoreType.DMA((n,)) for _, n in stages]
    scratch += [pltpu.SemaphoreType.DMA((n,)) for _, n in stages]
    return pl.pallas_call(
        functools.partial(_reduce_kernel, stages),
        out_shape=jax.ShapeDtypeStruct((rows, cols), jnp.float32),
        in_specs=[pl.BlockSpec(memory_space=pltpu.VMEM)],
        out_specs=pl.BlockSpec(memory_space=pltpu.VMEM),
        scratch_shapes=scratch,
        compiler_params=pltpu.CompilerParams(collective_id=collective, has_side_effects=True),
    )(x.astype(jnp.float32))


def global_sum(rows_of_sums, mesh_shape):
    count = rows_of_sums.shape[0]
    padded = jnp.zeros((8, rows_of_sums.shape[1]), jnp.float32).at[:count].set(rows_of_sums)
    return all_sum(padded, ("blk", "sec"), mesh_shape, 0)[:count]


def _doubling(n):
    distances, d = [], 1
    while d < n:
        distances.append(d)
        d *= 2
    return tuple(distances)


def _greet(n, distances):
    barrier = pltpu.get_barrier_semaphore()
    mine = lax.axis_index("sec")
    for d in distances:
        for peer in (lax.rem(mine + d, n), lax.rem(mine + n - d, n)):
            pl.semaphore_signal(barrier, inc=1, device_id={"sec": peer}, device_id_type=MESH)
    pl.semaphore_wait(barrier, 2 * len(distances))


def _hop(n, d, source, slot, send_sem, recv_sem):
    mine = lax.axis_index("sec")
    copy = pltpu.make_async_remote_copy(
        src_ref=source,
        dst_ref=slot,
        send_sem=send_sem,
        recv_sem=recv_sem,
        device_id={"sec": lax.rem(mine + d, n)},
        device_id_type=MESH,
    )
    copy.start()
    copy.wait_recv()
    copy.wait_send()


def _maps_kernel(n, distances, e_ref, t_ref, slots, sends, recvs):
    mine = lax.axis_index("sec")
    _greet(n, distances)
    t_ref[0] = e_ref[...]
    for k, d in enumerate(distances[:-1]):
        _hop(n, d, t_ref.at[k], slots.at[k], sends.at[k], recvs.at[k])
        joined = jnp.dot(
            t_ref[k], slots[k], precision=lax.Precision.HIGHEST, preferred_element_type=jnp.float32
        )
        t_ref[k + 1] = jnp.where(mine >= d, joined, t_ref[k])


def _sweep_kernel(n, distances, f_ref, t_ref, o_ref, carry, slots, sends, recvs):
    mine = lax.axis_index("sec")
    _greet(n, distances)
    carry[0] = f_ref[...]
    for k, d in enumerate(distances):
        _hop(n, d, carry.at[k], slots.at[k], sends.at[k], recvs.at[k])
        joined = carry[k] + jnp.dot(
            slots[k], t_ref[k], precision=lax.Precision.HIGHEST, preferred_element_type=jnp.float32
        )
        carry[k + 1] = jnp.where(mine >= d, joined, carry[k])
    last = len(distances)
    _hop(n, 1, carry.at[last], slots.at[last], sends.at[last], recvs.at[last])
    o_ref[...] = jnp.where(mine >= 1, slots[last], jnp.zeros_like(o_ref))


def scan_maps(maps_t, n):
    distances = _doubling(n)
    rounds, width = len(distances), maps_t.shape[0]
    return pl.pallas_call(
        functools.partial(_maps_kernel, n, distances),
        out_shape=jax.ShapeDtypeStruct((rounds, width, width), jnp.float32),
        in_specs=[pl.BlockSpec(memory_space=pltpu.VMEM)],
        out_specs=pl.BlockSpec(memory_space=pltpu.VMEM),
        scratch_shapes=[
            pltpu.VMEM((rounds, width, width), jnp.float32),
            pltpu.SemaphoreType.DMA((rounds,)),
            pltpu.SemaphoreType.DMA((rounds,)),
        ],
        compiler_params=pltpu.CompilerParams(collective_id=2, has_side_effects=True),
    )(maps_t)


def sweep(values, chain, n):
    distances = _doubling(n)
    rounds = len(distances)
    return pl.pallas_call(
        functools.partial(_sweep_kernel, n, distances),
        out_shape=jax.ShapeDtypeStruct(values.shape, jnp.float32),
        in_specs=[pl.BlockSpec(memory_space=pltpu.VMEM)] * 2,
        out_specs=pl.BlockSpec(memory_space=pltpu.VMEM),
        scratch_shapes=[
            pltpu.VMEM((rounds + 1,) + values.shape, jnp.float32),
            pltpu.VMEM((rounds + 1,) + values.shape, jnp.float32),
            pltpu.SemaphoreType.DMA((rounds + 1,)),
            pltpu.SemaphoreType.DMA((rounds + 1,)),
        ],
        compiler_params=pltpu.CompilerParams(collective_id=3, has_side_effects=True),
    )(values, chain)


def _gather_kernel(n, x_ref, o_ref, slots, sends, recvs):
    mine = lax.axis_index("blk")
    barrier = pltpu.get_barrier_semaphore()
    for k in range(1, n):
        pl.semaphore_signal(
            barrier, inc=1, device_id={"blk": lax.rem(mine + k, n)}, device_id_type=MESH
        )
    pl.semaphore_wait(barrier, n - 1)
    copies = []
    for k in range(1, n):
        copy = pltpu.make_async_remote_copy(
            src_ref=x_ref,
            dst_ref=slots.at[mine],
            send_sem=sends.at[k],
            recv_sem=recvs.at[mine],
            device_id={"blk": lax.rem(mine + k, n)},
            device_id_type=MESH,
        )
        copy.start()
        copies.append(copy)
    slots[mine] = x_ref[...]
    for k in range(1, n):
        sender = lax.rem(mine + k, n)
        pltpu.make_async_remote_copy(
            src_ref=x_ref,
            dst_ref=slots.at[sender],
            send_sem=sends.at[k],
            recv_sem=recvs.at[sender],
            device_id={"blk": sender},
            device_id_type=MESH,
        ).wait_recv()
    for copy in copies:
        copy.wait_send()
    width = x_ref.shape[1]
    for j in range(n):
        o_ref[:, j * width : (j + 1) * width] = slots[j]


def gather_blk(x, n):
    rows, width = x.shape
    return pl.pallas_call(
        functools.partial(_gather_kernel, n),
        out_shape=jax.ShapeDtypeStruct((rows, n * width), x.dtype),
        in_specs=[pl.BlockSpec(memory_space=pltpu.VMEM)],
        out_specs=pl.BlockSpec(memory_space=pltpu.VMEM),
        scratch_shapes=[
            pltpu.VMEM((n, rows, width), x.dtype),
            pltpu.SemaphoreType.DMA((n,)),
            pltpu.SemaphoreType.DMA((n,)),
        ],
        compiler_params=pltpu.CompilerParams(collective_id=4, has_side_effects=True),
    )(x)


def _operator_kernel(n_sec, n_blk, x_ref, up_ref, be_ref, g_ref, b_ref, a_ref, *scratch):
    gslots, bslots, aslots, gsend, grecv, bsend, brecv, asend, arecv = scratch
    sec, blk = lax.axis_index("sec"), lax.axis_index("blk")
    nxt, prv = lax.rem(sec + 1, n_sec), lax.rem(sec + n_sec - 1, n_sec)
    piece = bslots.shape[1]
    barrier = pltpu.get_barrier_semaphore()
    for k in range(1, n_blk):
        pl.semaphore_signal(
            barrier, inc=1, device_id={"blk": lax.rem(blk + k, n_blk)}, device_id_type=MESH
        )
    for j in range(n_blk):
        for other in (nxt, prv):
            pl.semaphore_signal(
                barrier, inc=1, device_id={"sec": other, "blk": j}, device_id_type=MESH
            )
    pl.semaphore_wait(barrier, 3 * n_blk - 1)
    copies = []
    for k in range(1, n_blk):
        copies.append(
            pltpu.make_async_remote_copy(
                src_ref=x_ref,
                dst_ref=gslots.at[blk],
                send_sem=gsend.at[k],
                recv_sem=grecv.at[blk],
                device_id={"blk": lax.rem(blk + k, n_blk)},
                device_id_type=MESH,
            )
        )
    mine = pl.ds(pl.multiple_of(blk * piece, 8), piece)
    for j in range(n_blk):
        copies.append(
            pltpu.make_async_remote_copy(
                src_ref=be_ref.at[mine],
                dst_ref=bslots.at[blk],
                send_sem=bsend.at[j],
                recv_sem=brecv.at[blk],
                device_id={"sec": nxt, "blk": j},
                device_id_type=MESH,
            )
        )
        copies.append(
            pltpu.make_async_remote_copy(
                src_ref=up_ref.at[pl.ds(j * piece, piece)],
                dst_ref=aslots.at[blk],
                send_sem=asend.at[j],
                recv_sem=arecv.at[blk],
                device_id={"sec": prv, "blk": j},
                device_id_type=MESH,
            )
        )
    for copy in copies:
        copy.start()
    gslots[blk] = x_ref[...]
    for k in range(1, n_blk):
        sender = lax.rem(blk + k, n_blk)
        pltpu.make_async_remote_copy(
            src_ref=x_ref,
            dst_ref=gslots.at[sender],
            send_sem=gsend.at[k],
            recv_sem=grecv.at[sender],
            device_id={"blk": sender},
            device_id_type=MESH,
        ).wait_recv()
    for j in range(n_blk):
        pltpu.make_async_remote_copy(
            src_ref=be_ref.at[mine],
            dst_ref=bslots.at[j],
            send_sem=bsend.at[j],
            recv_sem=brecv.at[j],
            device_id={"sec": prv, "blk": j},
            device_id_type=MESH,
        ).wait_recv()
        pltpu.make_async_remote_copy(
            src_ref=up_ref.at[pl.ds(j * piece, piece)],
            dst_ref=aslots.at[j],
            send_sem=asend.at[j],
            recv_sem=arecv.at[j],
            device_id={"sec": nxt, "blk": j},
            device_id_type=MESH,
        ).wait_recv()
    for copy in copies:
        copy.wait_send()
    width = x_ref.shape[1]
    for j in range(n_blk):
        g_ref[:, j * width : (j + 1) * width] = gslots[j]
        b_ref[j * piece : (j + 1) * piece, :] = jnp.where(
            sec >= 1, bslots[j], jnp.zeros_like(bslots[j])
        )
    total = aslots[0]
    for j in range(1, n_blk):
        total = total + aslots[j]
    a_ref[...] = jnp.where(sec <= n_sec - 2, total, jnp.zeros_like(total))


def operator_exchange(x, up_t, be_t, n_sec, n_blk):
    rows, width = x.shape
    panel, cases = up_t.shape
    piece = panel // n_blk
    return pl.pallas_call(
        functools.partial(_operator_kernel, n_sec, n_blk),
        out_shape=(
            jax.ShapeDtypeStruct((rows, n_blk * width), x.dtype),
            jax.ShapeDtypeStruct((panel, cases), jnp.float32),
            jax.ShapeDtypeStruct((piece, cases), jnp.float32),
        ),
        in_specs=[pl.BlockSpec(memory_space=pltpu.VMEM)] * 3,
        out_specs=[pl.BlockSpec(memory_space=pltpu.VMEM)] * 3,
        scratch_shapes=[
            pltpu.VMEM((n_blk, rows, width), x.dtype),
            pltpu.VMEM((n_blk, piece, cases), jnp.float32),
            pltpu.VMEM((n_blk, piece, cases), jnp.float32),
        ]
        + [pltpu.SemaphoreType.DMA((n_blk,))] * 6,
        compiler_params=pltpu.CompilerParams(collective_id=5, has_side_effects=True),
    )(x, up_t, be_t)


def _precondition_kernel(n_sec, n_blk, distances, x_ref, inv_ref, pick_ref, u_ref, w_ref, o_ref, *scratch):
    gslots, fslots, carry, slots, gsend, grecv, fsend, frecv, ssend, srecv = scratch
    sec, blk = lax.axis_index("sec"), lax.axis_index("blk")
    barrier = pltpu.get_barrier_semaphore()
    for k in range(1, n_blk):
        pl.semaphore_signal(
            barrier, inc=1, device_id={"blk": lax.rem(blk + k, n_blk)}, device_id_type=MESH
        )
    for d in distances:
        for peer in (lax.rem(sec + d, n_sec), lax.rem(sec + n_sec - d, n_sec)):
            pl.semaphore_signal(barrier, inc=1, device_id={"sec": peer}, device_id_type=MESH)
    pl.semaphore_wait(barrier, n_blk - 1 + 2 * len(distances))

    def blk_copy(source, slot_ref, send, recv, k, target):
        return pltpu.make_async_remote_copy(
            src_ref=source,
            dst_ref=slot_ref.at[target[1]],
            send_sem=send.at[k],
            recv_sem=recv.at[target[1]],
            device_id={"blk": target[0]},
            device_id_type=MESH,
        )

    outgoing = [
        blk_copy(x_ref, gslots, gsend, grecv, k, (lax.rem(blk + k, n_blk), blk))
        for k in range(1, n_blk)
    ]
    for copy in outgoing:
        copy.start()
    gslots[blk] = x_ref[...]
    for k in range(1, n_blk):
        sender = lax.rem(blk + k, n_blk)
        blk_copy(x_ref, gslots, gsend, grecv, k, (sender, sender)).wait_recv()
    for copy in outgoing:
        copy.wait_send()
    width = x_ref.shape[1]
    contract = (((1,), (1,)), ((), ()))
    folded = lax.dot_general(
        gslots[0], inv_ref[:, 0:width], contract, preferred_element_type=jnp.float32
    )
    for j in range(1, n_blk):
        folded = folded + lax.dot_general(
            gslots[j],
            inv_ref[:, j * width : (j + 1) * width],
            contract,
            preferred_element_type=jnp.float32,
        )
    w_ref[...] = folded
    fslots[blk] = lax.dot_general(
        pick_ref[...], folded, contract, precision=lax.Precision.HIGHEST,
        preferred_element_type=jnp.float32,
    )
    outgoing = [
        blk_copy(fslots.at[blk], fslots, fsend, frecv, k, (lax.rem(blk + k, n_blk), blk))
        for k in range(1, n_blk)
    ]
    for copy in outgoing:
        copy.start()
    for k in range(1, n_blk):
        sender = lax.rem(blk + k, n_blk)
        blk_copy(fslots.at[blk], fslots, fsend, frecv, k, (sender, sender)).wait_recv()
    for copy in outgoing:
        copy.wait_send()
    piece = fslots.shape[1]
    for j in range(n_blk):
        carry[0, j * piece : (j + 1) * piece, :] = fslots[j]
    for k, d in enumerate(distances):
        _hop(n_sec, d, carry.at[k], slots.at[k], ssend.at[k], srecv.at[k])
        joined = carry[k] + jnp.dot(
            u_ref[k], slots[k], precision=lax.Precision.HIGHEST, preferred_element_type=jnp.float32
        )
        carry[k + 1] = jnp.where(sec >= d, joined, carry[k])
    last = len(distances)
    _hop(n_sec, 1, carry.at[last], slots.at[last], ssend.at[last], srecv.at[last])
    o_ref[...] = jnp.where(sec >= 1, slots[last], jnp.zeros_like(o_ref))


def precondition_sweep(x, inverse, picks, chain, n_sec, n_blk):
    cases, width = x.shape
    piece, _ = picks.shape
    panel = piece * n_blk
    distances = _doubling(n_sec)
    rounds = len(distances)
    return pl.pallas_call(
        functools.partial(_precondition_kernel, n_sec, n_blk, distances),
        out_shape=(
            jax.ShapeDtypeStruct((cases, width), jnp.float32),
            jax.ShapeDtypeStruct((panel, cases), jnp.float32),
        ),
        in_specs=[pl.BlockSpec(memory_space=pltpu.VMEM)] * 4,
        out_specs=[pl.BlockSpec(memory_space=pltpu.VMEM)] * 2,
        scratch_shapes=[
            pltpu.VMEM((n_blk, cases, width), x.dtype),
            pltpu.VMEM((n_blk, piece, cases), jnp.float32),
            pltpu.VMEM((rounds + 1, panel, cases), jnp.float32),
            pltpu.VMEM((rounds + 1, panel, cases), jnp.float32),
        ]
        + [pltpu.SemaphoreType.DMA((n_blk,))] * 4
        + [pltpu.SemaphoreType.DMA((rounds + 1,))] * 2,
        compiler_params=pltpu.CompilerParams(collective_id=6, has_side_effects=True),
    )(x, inverse, picks, chain)


def least_squares(hessen, beta):
    cases = hessen.shape[0]
    depth = hessen.shape[2]
    rhs = jnp.zeros((cases, depth + 1), jnp.float32).at[:, 0].set(beta)
    upper = hessen
    for column in range(depth):
        upper_row = upper[:, column, :]
        lower_row = upper[:, column + 1, :]
        radius = jnp.sqrt(upper_row[:, column] ** 2 + lower_row[:, column] ** 2)
        cosine = upper_row[:, column] / radius
        sine_term = lower_row[:, column] / radius
        upper = upper.at[:, column, :].set(
            cosine[:, None] * upper_row + sine_term[:, None] * lower_row
        )
        upper = upper.at[:, column + 1, :].set(
            -sine_term[:, None] * upper_row + cosine[:, None] * lower_row
        )
        first_rhs = rhs[:, column]
        second_rhs = rhs[:, column + 1]
        rhs = rhs.at[:, column].set(cosine * first_rhs + sine_term * second_rhs)
        rhs = rhs.at[:, column + 1].set(-sine_term * first_rhs + cosine * second_rhs)
    weights = jnp.zeros((cases, depth), jnp.float32)
    for column in reversed(range(depth)):
        remain = rhs[:, column] - jnp.sum(
            upper[:, column, column + 1 :] * weights[:, column + 1 :], axis=1
        )
        weights = weights.at[:, column].set(remain / upper[:, column, column])
    return weights


def local(
    mesh_shape,
    state_now, source, fan_gain, section_block, block_inverse, back_panel, ahead_panel, interface
):
    highest = lax.Precision.HIGHEST
    cases, node_rows = state_now.shape
    panel_width = back_panel.shape[1]
    indices = interface[0]
    first_row = lax.axis_index("blk") * node_rows
    selector = (indices[None, :] == first_row + jnp.arange(node_rows)[:, None]).astype(jnp.float32)
    contract = (((1,), (1,)), ((), ()))
    gain_panel = jnp.dot(
        block_inverse,
        lax.all_gather(back_panel, "blk", axis=0, tiled=True),
        preferred_element_type=jnp.float32,
    )
    panel_maps = -all_sum(jnp.dot(selector.T, gain_panel, precision=highest), ("blk",), mesh_shape, 1)

    chain = scan_maps(panel_maps, mesh_shape["sec"])
    own_piece = panel_width // mesh_shape["blk"]
    own_picks = lax.dynamic_slice_in_dim(selector, lax.axis_index("blk") * own_piece, own_piece, 1).T

    def section_terms(dense_part, behind_vals, piece):
        width = piece.shape[1]
        dense_part = lax.dot_general(
            piece, section_block, contract, preferred_element_type=jnp.float32
        )
        picker = (indices[None, :] == jnp.arange(width)[:, None]).astype(jnp.bfloat16)
        behind_vals = jnp.dot(piece, picker, preferred_element_type=jnp.float32)
        return (dense_part, behind_vals)

    def fold_section(carry, piece):
        return section_terms(carry[0], carry[1], piece)

    def operator(vector):
        rounded = vector.astype(jnp.bfloat16)
        n_sec, n_blk = mesh_shape["sec"], mesh_shape["blk"]
        piece = panel_width // n_blk
        up_t = lax.dot_general(
            ahead_panel, rounded, (((0,), (1,)), ((), ())), preferred_element_type=jnp.float32
        )
        be_t = lax.dot_general(
            selector.astype(jnp.bfloat16),
            rounded,
            (((0,), (1,)), ((), ())),
            preferred_element_type=jnp.float32,
        )
        gathered, behind_t, ahead_piece = operator_exchange(rounded, up_t, be_t, n_sec, n_blk)
        dense_part = lax.dot_general(
            gathered, section_block, contract, preferred_element_type=jnp.float32
        )
        lower_term = lax.dot_general(
            behind_t.astype(jnp.bfloat16),
            back_panel,
            (((0,), (1,)), ((), ())),
            preferred_element_type=jnp.float32,
        )
        local_picks = lax.dynamic_slice_in_dim(selector, lax.axis_index("blk") * piece, piece, 1)
        upper_term = lax.dot_general(
            ahead_piece, local_picks, (((0,), (1,)), ((), ())), precision=highest
        )
        return dense_part + lower_term + upper_term

    def compose(earlier, later):
        first_map, first_value = earlier
        second_map, second_value = later
        joined_map = jnp.dot(second_map, first_map, precision=highest)
        joined_value = jnp.dot(first_value, second_map.T, precision=highest) + second_value
        return (joined_map, joined_value)

    def lengths(vector):
        return jnp.sqrt(global_sum(jnp.sum(vector * vector, axis=1)[None], mesh_shape)[0] + epsilon)

    bent = jnp.tanh(state_now)
    residual = source - operator(state_now) - fan_gain[None, :] * bent
    jac_diag = fan_gain[None, :] * (1.0 - bent * bent)
    beta = lengths(residual)
    basis = [residual / beta[:, None]]
    directions = []
    hessen = jnp.zeros((cases, KRYLOV + 1, KRYLOV), jnp.float32)
    for column in range(KRYLOV):
        precondition_rounded = basis[column].astype(jnp.bfloat16)
        precondition_folded, before_t = precondition_sweep(
            precondition_rounded, block_inverse, own_picks, chain, mesh_shape["sec"], mesh_shape["blk"]
        )
        direction = precondition_folded - lax.dot_general(
            before_t, gain_panel, (((0,), (1,)), ((), ())), precision=highest
        )
        product = operator(direction) + jac_diag * direction
        stacked = jnp.stack(basis)
        projections = global_sum(jnp.sum(product[None] * stacked, axis=2), mesh_shape)
        product = product - jnp.sum(projections[:, :, None] * stacked, axis=0)
        length = lengths(product)
        hessen = hessen.at[:, : column + 1, column].set(projections.T)
        hessen = hessen.at[:, column + 1, column].set(length)
        basis.append(product / length[:, None])
        directions.append(direction)
    weights = least_squares(hessen, beta)
    update = jnp.zeros_like(state_now)
    for column in range(KRYLOV):
        update = update + weights[:, column : column + 1] * directions[column]
    return state_now + update


def solution(mesh):
    in_specs = (
        P(None, ("sec", "blk")),
        P(None, ("sec", "blk")),
        P(("sec", "blk")),
        P(("sec", "blk"), None),
        P(("sec", "blk"), None),
        P(("sec", "blk"), None),
        P(("sec", "blk"), None),
        P("sec", None),
    )
    out_specs = P(None, ("sec", "blk"))
    return jax.shard_map(functools.partial(local, dict(mesh.shape)), mesh=mesh, in_specs=in_specs, out_specs=out_specs, check_vma=False)
```

```python
import functools

import jax
import jax.numpy as jnp
from jax import lax
from jax.experimental import pallas as pl
from jax.experimental.pallas import tpu as pltpu
from jax.sharding import PartitionSpec as P

MESH = pl.DeviceIdType.MESH

KRYLOV = 3


epsilon = 1e-06


def extended(x, sides, width):
    for axis, dim in sides:
        size, length = (lax.axis_size(axis), x.shape[dim])
        up = [(i, (i + 1) % size) for i in range(size - 1)]
        down = [(j, i) for i, j in up]
        last = lax.slice_in_dim(x, length - width, length, axis=dim)
        first = lax.slice_in_dim(x, 0, width, axis=dim)
        before = lax.ppermute(last, axis, up)
        after = lax.ppermute(first, axis, down)
        x = jnp.concatenate([before, x, after], axis=dim)
    return x


def entering(value, axis, join, neutral):
    count, mine = (lax.axis_size(axis), lax.axis_index(axis))
    pieces = jax.tree.map(lambda part: lax.all_gather(part, axis), value)
    so_far = jax.tree.map(
        lambda part, zero: jnp.full_like(part, 0) + jnp.asarray(zero, part.dtype), value, neutral
    )

    def step(position, so_far):
        longer = join(so_far, jax.tree.map(lambda part: part[position], pieces))
        return jax.tree.map(lambda new, old: jnp.where(position < mine, new, old), longer, so_far)

    return lax.fori_loop(0, count - 1, step, so_far)


def _reduce_kernel(stages, x_ref, o_ref, *scratch):
    count = len(stages)
    slots = scratch[:count]
    partial = scratch[count]
    sends = scratch[count + 1 : 2 * count + 1]
    recvs = scratch[2 * count + 1 :]
    barrier = pltpu.get_barrier_semaphore()
    peers = 0
    for axis, n in stages:
        mine = lax.axis_index(axis)
        for k in range(1, n):
            pl.semaphore_signal(
                barrier, inc=1, device_id={axis: lax.rem(mine + k, n)}, device_id_type=MESH
            )
            peers += 1
    pl.semaphore_wait(barrier, peers)
    source = x_ref
    for stage, (axis, n) in enumerate(stages):
        mine = lax.axis_index(axis)
        copies = []
        for k in range(1, n):
            copy = pltpu.make_async_remote_copy(
                src_ref=source,
                dst_ref=slots[stage].at[mine],
                send_sem=sends[stage].at[k],
                recv_sem=recvs[stage].at[mine],
                device_id={axis: lax.rem(mine + k, n)},
                device_id_type=MESH,
            )
            copy.start()
            copies.append(copy)
        slots[stage][mine] = source[...]
        for k in range(1, n):
            sender = lax.rem(mine + k, n)
            pltpu.make_async_remote_copy(
                src_ref=source,
                dst_ref=slots[stage].at[sender],
                send_sem=sends[stage].at[k],
                recv_sem=recvs[stage].at[sender],
                device_id={axis: sender},
                device_id_type=MESH,
            ).wait_recv()
        for copy in copies:
            copy.wait_send()
        total = slots[stage][0]
        for j in range(1, n):
            total = total + slots[stage][j]
        if stage == count - 1:
            o_ref[...] = total
        else:
            partial[...] = total
            source = partial


def all_sum(x, axes, mesh_shape, collective):
    stages = tuple((axis, mesh_shape[axis]) for axis in axes if mesh_shape[axis] > 1)
    rows, cols = x.shape
    scratch = [pltpu.VMEM((n, rows, cols), jnp.float32) for _, n in stages]
    scratch.append(pltpu.VMEM((rows, cols), jnp.float32))
    scratch += [pltpu.SemaphoreType.DMA((n,)) for _, n in stages]
    scratch += [pltpu.SemaphoreType.DMA((n,)) for _, n in stages]
    return pl.pallas_call(
        functools.partial(_reduce_kernel, stages),
        out_shape=jax.ShapeDtypeStruct((rows, cols), jnp.float32),
        in_specs=[pl.BlockSpec(memory_space=pltpu.VMEM)],
        out_specs=pl.BlockSpec(memory_space=pltpu.VMEM),
        scratch_shapes=scratch,
        compiler_params=pltpu.CompilerParams(collective_id=collective, has_side_effects=True),
    )(x.astype(jnp.float32))


def global_sum(rows_of_sums, mesh_shape):
    count = rows_of_sums.shape[0]
    padded = jnp.zeros((8, rows_of_sums.shape[1]), jnp.float32).at[:count].set(rows_of_sums)
    return all_sum(padded, ("blk", "sec"), mesh_shape, 0)[:count]


def _doubling(n):
    distances, d = [], 1
    while d < n:
        distances.append(d)
        d *= 2
    return tuple(distances)


def _greet(n, distances):
    barrier = pltpu.get_barrier_semaphore()
    mine = lax.axis_index("sec")
    for d in distances:
        for peer in (lax.rem(mine + d, n), lax.rem(mine + n - d, n)):
            pl.semaphore_signal(barrier, inc=1, device_id={"sec": peer}, device_id_type=MESH)
    pl.semaphore_wait(barrier, 2 * len(distances))


def _hop(n, d, source, slot, send_sem, recv_sem):
    mine = lax.axis_index("sec")
    copy = pltpu.make_async_remote_copy(
        src_ref=source,
        dst_ref=slot,
        send_sem=send_sem,
        recv_sem=recv_sem,
        device_id={"sec": lax.rem(mine + d, n)},
        device_id_type=MESH,
    )
    copy.start()
    copy.wait_recv()
    copy.wait_send()


RADIX = 4


def _plan(n):
    rounds, d = [], 1
    while d < n:
        rounds.append((d, tuple(j for j in range(1, RADIX) if j * d < n)))
        d *= RADIX
    return tuple(rounds)


def _plan_peers(rounds):
    return tuple(sorted({j * d for d, js in rounds for j in js} | {1}))


def _send_all(n, sec, sources, slots, sends, recvs, flat, d, js):
    copies = []
    for i, j in enumerate(js):
        copy = pltpu.make_async_remote_copy(
            src_ref=sources,
            dst_ref=slots.at[flat + i],
            send_sem=sends.at[flat + i],
            recv_sem=recvs.at[flat + i],
            device_id={"sec": lax.rem(sec + j * d, n)},
            device_id_type=MESH,
        )
        copy.start()
        copies.append(copy)
    for copy in copies:
        copy.wait_recv()
    for copy in copies:
        copy.wait_send()


def _maps_kernel(n, rounds, e_ref, a_ref, current, slots, sends, recvs):
    sec = lax.axis_index("sec")
    _greet(n, _plan_peers(rounds))
    current[...] = e_ref[...]
    flat = 0
    for k, (d, js) in enumerate(rounds):
        onward = k < len(rounds) - 1
        if onward or len(js) > 1:
            _send_all(n, sec, current, slots, sends, recvs, flat, d, js)
        joined = current[...]
        for i, j in enumerate(js):
            a_ref[flat + i] = joined
            if onward or i < len(js) - 1:
                joined = jnp.dot(
                    joined, slots[flat + i], precision=lax.Precision.HIGHEST,
                    preferred_element_type=jnp.float32,
                )
        if onward:
            current[...] = joined
        flat += len(js)


def scan_maps(maps, n):
    rounds = _plan(n)
    total = sum(len(js) for _, js in rounds)
    width = maps.shape[0]
    return pl.pallas_call(
        functools.partial(_maps_kernel, n, rounds),
        out_shape=jax.ShapeDtypeStruct((total, width, width), jnp.float32),
        in_specs=[pl.BlockSpec(memory_space=pltpu.VMEM)],
        out_specs=pl.BlockSpec(memory_space=pltpu.VMEM),
        scratch_shapes=[
            pltpu.VMEM((width, width), jnp.float32),
            pltpu.VMEM((total, width, width), jnp.float32),
            pltpu.SemaphoreType.DMA((total,)),
            pltpu.SemaphoreType.DMA((total,)),
        ],
        compiler_params=pltpu.CompilerParams(collective_id=2, has_side_effects=True),
    )(maps)


def _gather_kernel(n, x_ref, o_ref, slots, sends, recvs):
    mine = lax.axis_index("blk")
    barrier = pltpu.get_barrier_semaphore()
    for k in range(1, n):
        pl.semaphore_signal(
            barrier, inc=1, device_id={"blk": lax.rem(mine + k, n)}, device_id_type=MESH
        )
    pl.semaphore_wait(barrier, n - 1)
    copies = []
    for k in range(1, n):
        copy = pltpu.make_async_remote_copy(
            src_ref=x_ref,
            dst_ref=slots.at[mine],
            send_sem=sends.at[k],
            recv_sem=recvs.at[mine],
            device_id={"blk": lax.rem(mine + k, n)},
            device_id_type=MESH,
        )
        copy.start()
        copies.append(copy)
    slots[mine] = x_ref[...]
    for k in range(1, n):
        sender = lax.rem(mine + k, n)
        pltpu.make_async_remote_copy(
            src_ref=x_ref,
            dst_ref=slots.at[sender],
            send_sem=sends.at[k],
            recv_sem=recvs.at[sender],
            device_id={"blk": sender},
            device_id_type=MESH,
        ).wait_recv()
    for copy in copies:
        copy.wait_send()
    width = x_ref.shape[1]
    for j in range(n):
        o_ref[:, j * width : (j + 1) * width] = slots[j]


def gather_blk(x, n):
    rows, width = x.shape
    return pl.pallas_call(
        functools.partial(_gather_kernel, n),
        out_shape=jax.ShapeDtypeStruct((rows, n * width), x.dtype),
        in_specs=[pl.BlockSpec(memory_space=pltpu.VMEM)],
        out_specs=pl.BlockSpec(memory_space=pltpu.VMEM),
        scratch_shapes=[
            pltpu.VMEM((n, rows, width), x.dtype),
            pltpu.SemaphoreType.DMA((n,)),
            pltpu.SemaphoreType.DMA((n,)),
        ],
        compiler_params=pltpu.CompilerParams(collective_id=4, has_side_effects=True),
    )(x)


def _operator_kernel(n_sec, n_blk, x_ref, up_ref, be_ref, g_ref, b_ref, a_ref, *scratch):
    gslots, bslots, aslots, gsend, grecv, bsend, brecv, asend, arecv = scratch
    sec, blk = lax.axis_index("sec"), lax.axis_index("blk")
    nxt, prv = lax.rem(sec + 1, n_sec), lax.rem(sec + n_sec - 1, n_sec)
    piece = bslots.shape[1]
    barrier = pltpu.get_barrier_semaphore()
    for k in range(1, n_blk):
        pl.semaphore_signal(
            barrier, inc=1, device_id={"blk": lax.rem(blk + k, n_blk)}, device_id_type=MESH
        )
    for j in range(n_blk):
        for other in (nxt, prv):
            pl.semaphore_signal(
                barrier, inc=1, device_id={"sec": other, "blk": j}, device_id_type=MESH
            )
    pl.semaphore_wait(barrier, 3 * n_blk - 1)
    copies = []
    for k in range(1, n_blk):
        copies.append(
            pltpu.make_async_remote_copy(
                src_ref=x_ref,
                dst_ref=gslots.at[blk],
                send_sem=gsend.at[k],
                recv_sem=grecv.at[blk],
                device_id={"blk": lax.rem(blk + k, n_blk)},
                device_id_type=MESH,
            )
        )
    mine = pl.ds(pl.multiple_of(blk * piece, 8), piece)
    for j in range(n_blk):
        copies.append(
            pltpu.make_async_remote_copy(
                src_ref=be_ref.at[mine],
                dst_ref=bslots.at[blk],
                send_sem=bsend.at[j],
                recv_sem=brecv.at[blk],
                device_id={"sec": nxt, "blk": j},
                device_id_type=MESH,
            )
        )
        copies.append(
            pltpu.make_async_remote_copy(
                src_ref=up_ref.at[pl.ds(j * piece, piece)],
                dst_ref=aslots.at[blk],
                send_sem=asend.at[j],
                recv_sem=arecv.at[blk],
                device_id={"sec": prv, "blk": j},
                device_id_type=MESH,
            )
        )
    for copy in copies:
        copy.start()
    gslots[blk] = x_ref[...]
    for k in range(1, n_blk):
        sender = lax.rem(blk + k, n_blk)
        pltpu.make_async_remote_copy(
            src_ref=x_ref,
            dst_ref=gslots.at[sender],
            send_sem=gsend.at[k],
            recv_sem=grecv.at[sender],
            device_id={"blk": sender},
            device_id_type=MESH,
        ).wait_recv()
    for j in range(n_blk):
        pltpu.make_async_remote_copy(
            src_ref=be_ref.at[mine],
            dst_ref=bslots.at[j],
            send_sem=bsend.at[j],
            recv_sem=brecv.at[j],
            device_id={"sec": prv, "blk": j},
            device_id_type=MESH,
        ).wait_recv()
        pltpu.make_async_remote_copy(
            src_ref=up_ref.at[pl.ds(j * piece, piece)],
            dst_ref=aslots.at[j],
            send_sem=asend.at[j],
            recv_sem=arecv.at[j],
            device_id={"sec": nxt, "blk": j},
            device_id_type=MESH,
        ).wait_recv()
    for copy in copies:
        copy.wait_send()
    width = x_ref.shape[1]
    for j in range(n_blk):
        g_ref[:, j * width : (j + 1) * width] = gslots[j]
        b_ref[j * piece : (j + 1) * piece, :] = jnp.where(
            sec >= 1, bslots[j], jnp.zeros_like(bslots[j])
        )
    total = aslots[0]
    for j in range(1, n_blk):
        total = total + aslots[j]
    a_ref[...] = jnp.where(sec <= n_sec - 2, total, jnp.zeros_like(total))


def operator_exchange(x, up_t, be_t, n_sec, n_blk):
    rows, width = x.shape
    panel, cases = up_t.shape
    piece = panel // n_blk
    return pl.pallas_call(
        functools.partial(_operator_kernel, n_sec, n_blk),
        out_shape=(
            jax.ShapeDtypeStruct((rows, n_blk * width), x.dtype),
            jax.ShapeDtypeStruct((panel, cases), jnp.float32),
            jax.ShapeDtypeStruct((piece, cases), jnp.float32),
        ),
        in_specs=[pl.BlockSpec(memory_space=pltpu.VMEM)] * 3,
        out_specs=[pl.BlockSpec(memory_space=pltpu.VMEM)] * 3,
        scratch_shapes=[
            pltpu.VMEM((n_blk, rows, width), x.dtype),
            pltpu.VMEM((n_blk, piece, cases), jnp.float32),
            pltpu.VMEM((n_blk, piece, cases), jnp.float32),
        ]
        + [pltpu.SemaphoreType.DMA((n_blk,))] * 6,
        compiler_params=pltpu.CompilerParams(collective_id=5, has_side_effects=True),
    )(x, up_t, be_t)


def _precondition_kernel(n_sec, n_blk, rounds, x_ref, inv_ref, pick_ref, u_ref, w_ref, o_ref, *scratch):
    gslots, fslots, carry, slots, gsend, grecv, fsend, frecv, ssend, srecv = scratch
    sec, blk = lax.axis_index("sec"), lax.axis_index("blk")
    barrier = pltpu.get_barrier_semaphore()
    for k in range(1, n_blk):
        pl.semaphore_signal(
            barrier, inc=1, device_id={"blk": lax.rem(blk + k, n_blk)}, device_id_type=MESH
        )
    distances = _plan_peers(rounds)
    for d in distances:
        for peer in (lax.rem(sec + d, n_sec), lax.rem(sec + n_sec - d, n_sec)):
            pl.semaphore_signal(barrier, inc=1, device_id={"sec": peer}, device_id_type=MESH)
    pl.semaphore_wait(barrier, n_blk - 1 + 2 * len(distances))

    def blk_copy(source, slot_ref, send, recv, k, target):
        return pltpu.make_async_remote_copy(
            src_ref=source,
            dst_ref=slot_ref.at[target[1]],
            send_sem=send.at[k],
            recv_sem=recv.at[target[1]],
            device_id={"blk": target[0]},
            device_id_type=MESH,
        )

    outgoing = [
        blk_copy(x_ref, gslots, gsend, grecv, k, (lax.rem(blk + k, n_blk), blk))
        for k in range(1, n_blk)
    ]
    for copy in outgoing:
        copy.start()
    gslots[blk] = x_ref[...]
    for k in range(1, n_blk):
        sender = lax.rem(blk + k, n_blk)
        blk_copy(x_ref, gslots, gsend, grecv, k, (sender, sender)).wait_recv()
    for copy in outgoing:
        copy.wait_send()
    width = x_ref.shape[1]
    contract = (((1,), (1,)), ((), ()))
    folded = lax.dot_general(
        gslots[0], inv_ref[:, 0:width], contract, preferred_element_type=jnp.float32
    )
    for j in range(1, n_blk):
        folded = folded + lax.dot_general(
            gslots[j],
            inv_ref[:, j * width : (j + 1) * width],
            contract,
            preferred_element_type=jnp.float32,
        )
    w_ref[...] = folded
    fslots[blk] = lax.dot_general(
        pick_ref[...], folded, contract, precision=lax.Precision.HIGHEST,
        preferred_element_type=jnp.float32,
    )
    outgoing = [
        blk_copy(fslots.at[blk], fslots, fsend, frecv, k, (lax.rem(blk + k, n_blk), blk))
        for k in range(1, n_blk)
    ]
    for copy in outgoing:
        copy.start()
    for k in range(1, n_blk):
        sender = lax.rem(blk + k, n_blk)
        blk_copy(fslots.at[blk], fslots, fsend, frecv, k, (sender, sender)).wait_recv()
    for copy in outgoing:
        copy.wait_send()
    piece = fslots.shape[1]
    for j in range(n_blk):
        carry[0, j * piece : (j + 1) * piece, :] = fslots[j]
    flat = 0
    for k, (d, js) in enumerate(rounds):
        _send_all(n_sec, sec, carry.at[k], slots, ssend, srecv, flat, d, js)
        joined = carry[k]
        for i, j in enumerate(js):
            term = jnp.dot(
                u_ref[flat + i], slots[flat + i], precision=lax.Precision.HIGHEST,
                preferred_element_type=jnp.float32,
            )
            joined = joined + jnp.where(sec >= j * d, term, jnp.zeros_like(term))
        carry[k + 1] = joined
        flat += len(js)
    last = len(rounds)
    _hop(n_sec, 1, carry.at[last], slots.at[flat], ssend.at[flat], srecv.at[flat])
    o_ref[...] = jnp.where(sec >= 1, slots[flat], jnp.zeros_like(o_ref))


def precondition_sweep(x, inverse, picks, chain, n_sec, n_blk):
    cases, width = x.shape
    piece, _ = picks.shape
    panel = piece * n_blk
    plan = _plan(n_sec)
    rounds = len(plan)
    total = sum(len(js) for _, js in plan) + 1
    return pl.pallas_call(
        functools.partial(_precondition_kernel, n_sec, n_blk, plan),
        out_shape=(
            jax.ShapeDtypeStruct((cases, width), jnp.float32),
            jax.ShapeDtypeStruct((panel, cases), jnp.float32),
        ),
        in_specs=[pl.BlockSpec(memory_space=pltpu.VMEM)] * 4,
        out_specs=[pl.BlockSpec(memory_space=pltpu.VMEM)] * 2,
        scratch_shapes=[
            pltpu.VMEM((n_blk, cases, width), x.dtype),
            pltpu.VMEM((n_blk, piece, cases), jnp.float32),
            pltpu.VMEM((rounds + 1, panel, cases), jnp.float32),
            pltpu.VMEM((total, panel, cases), jnp.float32),
        ]
        + [pltpu.SemaphoreType.DMA((n_blk,))] * 4
        + [pltpu.SemaphoreType.DMA((total,))] * 2,
        compiler_params=pltpu.CompilerParams(collective_id=6, has_side_effects=True),
    )(x, inverse, picks, chain)


def least_squares(hessen, beta):
    cases = hessen.shape[0]
    depth = hessen.shape[2]
    rhs = jnp.zeros((cases, depth + 1), jnp.float32).at[:, 0].set(beta)
    upper = hessen
    for column in range(depth):
        upper_row = upper[:, column, :]
        lower_row = upper[:, column + 1, :]
        radius = jnp.sqrt(upper_row[:, column] ** 2 + lower_row[:, column] ** 2)
        cosine = upper_row[:, column] / radius
        sine_term = lower_row[:, column] / radius
        upper = upper.at[:, column, :].set(
            cosine[:, None] * upper_row + sine_term[:, None] * lower_row
        )
        upper = upper.at[:, column + 1, :].set(
            -sine_term[:, None] * upper_row + cosine[:, None] * lower_row
        )
        first_rhs = rhs[:, column]
        second_rhs = rhs[:, column + 1]
        rhs = rhs.at[:, column].set(cosine * first_rhs + sine_term * second_rhs)
        rhs = rhs.at[:, column + 1].set(-sine_term * first_rhs + cosine * second_rhs)
    weights = jnp.zeros((cases, depth), jnp.float32)
    for column in reversed(range(depth)):
        remain = rhs[:, column] - jnp.sum(
            upper[:, column, column + 1 :] * weights[:, column + 1 :], axis=1
        )
        weights = weights.at[:, column].set(remain / upper[:, column, column])
    return weights


def local(
    mesh_shape,
    state_now, source, fan_gain, section_block, block_inverse, back_panel, ahead_panel, interface
):
    highest = lax.Precision.HIGHEST
    cases, node_rows = state_now.shape
    panel_width = back_panel.shape[1]
    indices = interface[0]
    first_row = lax.axis_index("blk") * node_rows
    selector = (indices[None, :] == first_row + jnp.arange(node_rows)[:, None]).astype(jnp.float32)
    contract = (((1,), (1,)), ((), ()))
    gain_panel = jnp.dot(
        block_inverse,
        lax.all_gather(back_panel, "blk", axis=0, tiled=True),
        preferred_element_type=jnp.float32,
    )
    panel_maps = -all_sum(jnp.dot(selector.T, gain_panel, precision=highest), ("blk",), mesh_shape, 1)

    chain = scan_maps(panel_maps, mesh_shape["sec"])
    own_piece = panel_width // mesh_shape["blk"]
    own_picks = lax.dynamic_slice_in_dim(selector, lax.axis_index("blk") * own_piece, own_piece, 1).T

    def section_terms(dense_part, behind_vals, piece):
        width = piece.shape[1]
        dense_part = lax.dot_general(
            piece, section_block, contract, preferred_element_type=jnp.float32
        )
        picker = (indices[None, :] == jnp.arange(width)[:, None]).astype(jnp.bfloat16)
        behind_vals = jnp.dot(piece, picker, preferred_element_type=jnp.float32)
        return (dense_part, behind_vals)

    def fold_section(carry, piece):
        return section_terms(carry[0], carry[1], piece)

    def operator(vector):
        rounded = vector.astype(jnp.bfloat16)
        n_sec, n_blk = mesh_shape["sec"], mesh_shape["blk"]
        piece = panel_width // n_blk
        up_t = lax.dot_general(
            ahead_panel, rounded, (((0,), (1,)), ((), ())), preferred_element_type=jnp.float32
        )
        be_t = lax.dot_general(
            selector.astype(jnp.bfloat16),
            rounded,
            (((0,), (1,)), ((), ())),
            preferred_element_type=jnp.float32,
        )
        gathered, behind_t, ahead_piece = operator_exchange(rounded, up_t, be_t, n_sec, n_blk)
        dense_part = lax.dot_general(
            gathered, section_block, contract, preferred_element_type=jnp.float32
        )
        lower_term = lax.dot_general(
            behind_t.astype(jnp.bfloat16),
            back_panel,
            (((0,), (1,)), ((), ())),
            preferred_element_type=jnp.float32,
        )
        local_picks = lax.dynamic_slice_in_dim(selector, lax.axis_index("blk") * piece, piece, 1)
        upper_term = lax.dot_general(
            ahead_piece, local_picks, (((0,), (1,)), ((), ())), precision=highest
        )
        return dense_part + lower_term + upper_term

    def compose(earlier, later):
        first_map, first_value = earlier
        second_map, second_value = later
        joined_map = jnp.dot(second_map, first_map, precision=highest)
        joined_value = jnp.dot(first_value, second_map.T, precision=highest) + second_value
        return (joined_map, joined_value)

    def lengths(vector):
        return jnp.sqrt(global_sum(jnp.sum(vector * vector, axis=1)[None], mesh_shape)[0] + epsilon)

    bent = jnp.tanh(state_now)
    residual = source - operator(state_now) - fan_gain[None, :] * bent
    jac_diag = fan_gain[None, :] * (1.0 - bent * bent)
    beta = lengths(residual)
    basis = [residual / beta[:, None]]
    directions = []
    hessen = jnp.zeros((cases, KRYLOV + 1, KRYLOV), jnp.float32)
    for column in range(KRYLOV):
        precondition_rounded = basis[column].astype(jnp.bfloat16)
        precondition_folded, before_t = precondition_sweep(
            precondition_rounded, block_inverse, own_picks, chain, mesh_shape["sec"], mesh_shape["blk"]
        )
        direction = precondition_folded - lax.dot_general(
            before_t, gain_panel, (((0,), (1,)), ((), ())), precision=highest
        )
        product = operator(direction) + jac_diag * direction
        stacked = jnp.stack(basis)
        projections = global_sum(jnp.sum(product[None] * stacked, axis=2), mesh_shape)
        product = product - jnp.sum(projections[:, :, None] * stacked, axis=0)
        length = lengths(product)
        hessen = hessen.at[:, : column + 1, column].set(projections.T)
        hessen = hessen.at[:, column + 1, column].set(length)
        basis.append(product / length[:, None])
        directions.append(direction)
    weights = least_squares(hessen, beta)
    update = jnp.zeros_like(state_now)
    for column in range(KRYLOV):
        update = update + weights[:, column : column + 1] * directions[column]
    return state_now + update


def solution(mesh):
    in_specs = (
        P(None, ("sec", "blk")),
        P(None, ("sec", "blk")),
        P(("sec", "blk")),
        P(("sec", "blk"), None),
        P(("sec", "blk"), None),
        P(("sec", "blk"), None),
        P(("sec", "blk"), None),
        P("sec", None),
    )
    out_specs = P(None, ("sec", "blk"))
    return jax.shard_map(functools.partial(local, dict(mesh.shape)), mesh=mesh, in_specs=in_specs, out_specs=out_specs, check_vma=False)
```

```python
import functools

import jax
import jax.numpy as jnp
from jax import lax
from jax.experimental import pallas as pl
from jax.experimental.pallas import tpu as pltpu
from jax.sharding import PartitionSpec as P

MESH = pl.DeviceIdType.MESH

KRYLOV = 3


epsilon = 1e-06


def extended(x, sides, width):
    for axis, dim in sides:
        size, length = (lax.axis_size(axis), x.shape[dim])
        up = [(i, (i + 1) % size) for i in range(size - 1)]
        down = [(j, i) for i, j in up]
        last = lax.slice_in_dim(x, length - width, length, axis=dim)
        first = lax.slice_in_dim(x, 0, width, axis=dim)
        before = lax.ppermute(last, axis, up)
        after = lax.ppermute(first, axis, down)
        x = jnp.concatenate([before, x, after], axis=dim)
    return x


def entering(value, axis, join, neutral):
    count, mine = (lax.axis_size(axis), lax.axis_index(axis))
    pieces = jax.tree.map(lambda part: lax.all_gather(part, axis), value)
    so_far = jax.tree.map(
        lambda part, zero: jnp.full_like(part, 0) + jnp.asarray(zero, part.dtype), value, neutral
    )

    def step(position, so_far):
        longer = join(so_far, jax.tree.map(lambda part: part[position], pieces))
        return jax.tree.map(lambda new, old: jnp.where(position < mine, new, old), longer, so_far)

    return lax.fori_loop(0, count - 1, step, so_far)


def _reduce_kernel(stages, x_ref, o_ref, *scratch):
    count = len(stages)
    slots = scratch[:count]
    partial = scratch[count]
    sends = scratch[count + 1 : 2 * count + 1]
    recvs = scratch[2 * count + 1 :]
    barrier = pltpu.get_barrier_semaphore()
    peers = 0
    for axis, n in stages:
        mine = lax.axis_index(axis)
        for k in range(1, n):
            pl.semaphore_signal(
                barrier, inc=1, device_id={axis: lax.rem(mine + k, n)}, device_id_type=MESH
            )
            peers += 1
    pl.semaphore_wait(barrier, peers)
    source = x_ref
    for stage, (axis, n) in enumerate(stages):
        mine = lax.axis_index(axis)
        copies = []
        for k in range(1, n):
            copy = pltpu.make_async_remote_copy(
                src_ref=source,
                dst_ref=slots[stage].at[mine],
                send_sem=sends[stage].at[k],
                recv_sem=recvs[stage].at[mine],
                device_id={axis: lax.rem(mine + k, n)},
                device_id_type=MESH,
            )
            copy.start()
            copies.append(copy)
        slots[stage][mine] = source[...]
        for k in range(1, n):
            sender = lax.rem(mine + k, n)
            pltpu.make_async_remote_copy(
                src_ref=source,
                dst_ref=slots[stage].at[sender],
                send_sem=sends[stage].at[k],
                recv_sem=recvs[stage].at[sender],
                device_id={axis: sender},
                device_id_type=MESH,
            ).wait_recv()
        for copy in copies:
            copy.wait_send()
        total = slots[stage][0]
        for j in range(1, n):
            total = total + slots[stage][j]
        if stage == count - 1:
            o_ref[...] = total
        else:
            partial[...] = total
            source = partial


def all_sum(x, axes, mesh_shape, collective):
    stages = tuple((axis, mesh_shape[axis]) for axis in axes if mesh_shape[axis] > 1)
    rows, cols = x.shape
    scratch = [pltpu.VMEM((n, rows, cols), jnp.float32) for _, n in stages]
    scratch.append(pltpu.VMEM((rows, cols), jnp.float32))
    scratch += [pltpu.SemaphoreType.DMA((n,)) for _, n in stages]
    scratch += [pltpu.SemaphoreType.DMA((n,)) for _, n in stages]
    return pl.pallas_call(
        functools.partial(_reduce_kernel, stages),
        out_shape=jax.ShapeDtypeStruct((rows, cols), jnp.float32),
        in_specs=[pl.BlockSpec(memory_space=pltpu.VMEM)],
        out_specs=pl.BlockSpec(memory_space=pltpu.VMEM),
        scratch_shapes=scratch,
        compiler_params=pltpu.CompilerParams(collective_id=collective, has_side_effects=True),
    )(x.astype(jnp.float32))


def global_sum(rows_of_sums, mesh_shape):
    count = rows_of_sums.shape[0]
    padded = jnp.zeros((8, rows_of_sums.shape[1]), jnp.float32).at[:count].set(rows_of_sums)
    return all_sum(padded, ("blk", "sec"), mesh_shape, 0)[:count]


def _doubling(n):
    distances, d = [], 1
    while d < n:
        distances.append(d)
        d *= 2
    return tuple(distances)


def _greet(n, distances):
    barrier = pltpu.get_barrier_semaphore()
    mine = lax.axis_index("sec")
    for d in distances:
        for peer in (lax.rem(mine + d, n), lax.rem(mine + n - d, n)):
            pl.semaphore_signal(barrier, inc=1, device_id={"sec": peer}, device_id_type=MESH)
    pl.semaphore_wait(barrier, 2 * len(distances))


def _hop(n, d, source, slot, send_sem, recv_sem):
    mine = lax.axis_index("sec")
    copy = pltpu.make_async_remote_copy(
        src_ref=source,
        dst_ref=slot,
        send_sem=send_sem,
        recv_sem=recv_sem,
        device_id={"sec": lax.rem(mine + d, n)},
        device_id_type=MESH,
    )
    copy.start()
    copy.wait_recv()
    copy.wait_send()


RADIX = 4


def _plan(n):
    rounds, d = [], 1
    while d < n:
        rounds.append((d, tuple(j for j in range(1, RADIX) if j * d < n)))
        d *= RADIX
    return tuple(rounds)


def _plan_peers(rounds):
    return tuple(sorted({j * d for d, js in rounds for j in js} | {1}))


def _send_all(n, sec, sources, slots, sends, recvs, flat, d, js):
    copies = []
    for i, j in enumerate(js):
        copy = pltpu.make_async_remote_copy(
            src_ref=sources,
            dst_ref=slots.at[flat + i],
            send_sem=sends.at[flat + i],
            recv_sem=recvs.at[flat + i],
            device_id={"sec": lax.rem(sec + j * d, n)},
            device_id_type=MESH,
        )
        copy.start()
        copies.append(copy)
    for copy in copies:
        copy.wait_recv()
    for copy in copies:
        copy.wait_send()


def _spread(n_sec, n_blk, offsets, piece_ref, slots, sends, recvs):
    sec, blk = lax.axis_index("sec"), lax.axis_index("blk")

    def copy(o, j, index):
        return pltpu.make_async_remote_copy(
            src_ref=piece_ref,
            dst_ref=slots.at[index],
            send_sem=sends.at[(o - 1) * n_blk + j],
            recv_sem=recvs.at[index],
            device_id={"sec": lax.rem(sec + o, n_sec), "blk": j},
            device_id_type=MESH,
        )

    outgoing = [
        copy(o, j, (o - 1) * n_blk + blk) for o in range(1, offsets + 1) for j in range(n_blk)
    ]
    for c in outgoing:
        c.start()
    for o in range(1, offsets + 1):
        for j in range(n_blk):
            copy(o, j, (o - 1) * n_blk + j).wait_recv()
    for c in outgoing:
        c.wait_send()


def _assemble(n_blk, offsets, slots, mats):
    piece = slots.shape[1]
    for o in range(offsets):
        for j in range(n_blk):
            mats[o, j * piece : (j + 1) * piece, :] = slots[o * n_blk + j]


def _greet_all(n_sec, n_blk, offsets, rounds, blk_peers):
    barrier = pltpu.get_barrier_semaphore()
    sec, blk = lax.axis_index("sec"), lax.axis_index("blk")
    count = 0
    if blk_peers:
        for k in range(1, n_blk):
            pl.semaphore_signal(
                barrier, inc=1, device_id={"blk": lax.rem(blk + k, n_blk)}, device_id_type=MESH
            )
            count += 1
    for o in range(1, offsets + 1):
        for j in range(n_blk):
            for peer in (lax.rem(sec + o, n_sec), lax.rem(sec + n_sec - o, n_sec)):
                pl.semaphore_signal(
                    barrier, inc=1, device_id={"sec": peer, "blk": j}, device_id_type=MESH
                )
                count += 1
    for d in sorted({j * d for d, js in rounds[1:] for j in js}):
        for peer in (lax.rem(sec + d, n_sec), lax.rem(sec + n_sec - d, n_sec)):
            pl.semaphore_signal(barrier, inc=1, device_id={"sec": peer}, device_id_type=MESH)
            count += 1
    pl.semaphore_wait(barrier, count)


def _maps_kernel(n, n_blk, rounds, e_ref, a_ref, eslots, emat, current, slots, esend, erecv, sends, recvs):
    sec = lax.axis_index("sec")
    first = rounds[0][1]
    offsets = len(first) + 1
    _greet_all(n, n_blk, offsets, rounds, False)
    _spread(n, n_blk, offsets, e_ref, eslots, esend, erecv)
    _assemble(n_blk, offsets, eslots, emat)
    joined = emat[0]
    for i, j in enumerate(first):
        a_ref[i] = joined
        joined = jnp.dot(
            joined, emat[j], precision=lax.Precision.HIGHEST, preferred_element_type=jnp.float32
        )
    current[...] = joined
    flat = len(first)
    for k in range(1, len(rounds)):
        d, js = rounds[k]
        onward = k < len(rounds) - 1
        if onward or len(js) > 1:
            _send_all(n, sec, current, slots, sends, recvs, flat, d, js)
        joined = current[...]
        for i, j in enumerate(js):
            a_ref[flat + i] = joined
            if onward or i < len(js) - 1:
                joined = jnp.dot(
                    joined, slots[flat + i], precision=lax.Precision.HIGHEST,
                    preferred_element_type=jnp.float32,
                )
        if onward:
            current[...] = joined
        flat += len(js)


def scan_maps(e_piece, n, n_blk):
    rounds = _plan(n)
    total = sum(len(js) for _, js in rounds)
    offsets = len(rounds[0][1]) + 1
    piece, width = e_piece.shape
    return pl.pallas_call(
        functools.partial(_maps_kernel, n, n_blk, rounds),
        out_shape=jax.ShapeDtypeStruct((total, width, width), jnp.float32),
        in_specs=[pl.BlockSpec(memory_space=pltpu.VMEM)],
        out_specs=pl.BlockSpec(memory_space=pltpu.VMEM),
        scratch_shapes=[
            pltpu.VMEM((offsets * n_blk, piece, width), jnp.float32),
            pltpu.VMEM((offsets, width, width), jnp.float32),
            pltpu.VMEM((width, width), jnp.float32),
            pltpu.VMEM((total, width, width), jnp.float32),
            pltpu.SemaphoreType.DMA((offsets * n_blk,)),
            pltpu.SemaphoreType.DMA((offsets * n_blk,)),
            pltpu.SemaphoreType.DMA((total,)),
            pltpu.SemaphoreType.DMA((total,)),
        ],
        compiler_params=pltpu.CompilerParams(collective_id=2, has_side_effects=True),
    )(e_piece)


def _gather_kernel(n, x_ref, o_ref, slots, sends, recvs):
    mine = lax.axis_index("blk")
    barrier = pltpu.get_barrier_semaphore()
    for k in range(1, n):
        pl.semaphore_signal(
            barrier, inc=1, device_id={"blk": lax.rem(mine + k, n)}, device_id_type=MESH
        )
    pl.semaphore_wait(barrier, n - 1)
    copies = []
    for k in range(1, n):
        copy = pltpu.make_async_remote_copy(
            src_ref=x_ref,
            dst_ref=slots.at[mine],
            send_sem=sends.at[k],
            recv_sem=recvs.at[mine],
            device_id={"blk": lax.rem(mine + k, n)},
            device_id_type=MESH,
        )
        copy.start()
        copies.append(copy)
    slots[mine] = x_ref[...]
    for k in range(1, n):
        sender = lax.rem(mine + k, n)
        pltpu.make_async_remote_copy(
            src_ref=x_ref,
            dst_ref=slots.at[sender],
            send_sem=sends.at[k],
            recv_sem=recvs.at[sender],
            device_id={"blk": sender},
            device_id_type=MESH,
        ).wait_recv()
    for copy in copies:
        copy.wait_send()
    width = x_ref.shape[1]
    for j in range(n):
        o_ref[:, j * width : (j + 1) * width] = slots[j]


def gather_blk(x, n):
    rows, width = x.shape
    return pl.pallas_call(
        functools.partial(_gather_kernel, n),
        out_shape=jax.ShapeDtypeStruct((rows, n * width), x.dtype),
        in_specs=[pl.BlockSpec(memory_space=pltpu.VMEM)],
        out_specs=pl.BlockSpec(memory_space=pltpu.VMEM),
        scratch_shapes=[
            pltpu.VMEM((n, rows, width), x.dtype),
            pltpu.SemaphoreType.DMA((n,)),
            pltpu.SemaphoreType.DMA((n,)),
        ],
        compiler_params=pltpu.CompilerParams(collective_id=4, has_side_effects=True),
    )(x)


def _operator_kernel(n_sec, n_blk, x_ref, up_ref, be_ref, g_ref, b_ref, a_ref, *scratch):
    gslots, bslots, aslots, gsend, grecv, bsend, brecv, asend, arecv = scratch
    sec, blk = lax.axis_index("sec"), lax.axis_index("blk")
    nxt, prv = lax.rem(sec + 1, n_sec), lax.rem(sec + n_sec - 1, n_sec)
    piece = bslots.shape[1]
    barrier = pltpu.get_barrier_semaphore()
    for k in range(1, n_blk):
        pl.semaphore_signal(
            barrier, inc=1, device_id={"blk": lax.rem(blk + k, n_blk)}, device_id_type=MESH
        )
    for j in range(n_blk):
        for other in (nxt, prv):
            pl.semaphore_signal(
                barrier, inc=1, device_id={"sec": other, "blk": j}, device_id_type=MESH
            )
    pl.semaphore_wait(barrier, 3 * n_blk - 1)
    copies = []
    for k in range(1, n_blk):
        copies.append(
            pltpu.make_async_remote_copy(
                src_ref=x_ref,
                dst_ref=gslots.at[blk],
                send_sem=gsend.at[k],
                recv_sem=grecv.at[blk],
                device_id={"blk": lax.rem(blk + k, n_blk)},
                device_id_type=MESH,
            )
        )
    mine = pl.ds(pl.multiple_of(blk * piece, 8), piece)
    for j in range(n_blk):
        copies.append(
            pltpu.make_async_remote_copy(
                src_ref=be_ref.at[mine],
                dst_ref=bslots.at[blk],
                send_sem=bsend.at[j],
                recv_sem=brecv.at[blk],
                device_id={"sec": nxt, "blk": j},
                device_id_type=MESH,
            )
        )
        copies.append(
            pltpu.make_async_remote_copy(
                src_ref=up_ref.at[pl.ds(j * piece, piece)],
                dst_ref=aslots.at[blk],
                send_sem=asend.at[j],
                recv_sem=arecv.at[blk],
                device_id={"sec": prv, "blk": j},
                device_id_type=MESH,
            )
        )
    for copy in copies:
        copy.start()
    gslots[blk] = x_ref[...]
    for k in range(1, n_blk):
        sender = lax.rem(blk + k, n_blk)
        pltpu.make_async_remote_copy(
            src_ref=x_ref,
            dst_ref=gslots.at[sender],
            send_sem=gsend.at[k],
            recv_sem=grecv.at[sender],
            device_id={"blk": sender},
            device_id_type=MESH,
        ).wait_recv()
    for j in range(n_blk):
        pltpu.make_async_remote_copy(
            src_ref=be_ref.at[mine],
            dst_ref=bslots.at[j],
            send_sem=bsend.at[j],
            recv_sem=brecv.at[j],
            device_id={"sec": prv, "blk": j},
            device_id_type=MESH,
        ).wait_recv()
        pltpu.make_async_remote_copy(
            src_ref=up_ref.at[pl.ds(j * piece, piece)],
            dst_ref=aslots.at[j],
            send_sem=asend.at[j],
            recv_sem=arecv.at[j],
            device_id={"sec": nxt, "blk": j},
            device_id_type=MESH,
        ).wait_recv()
    for copy in copies:
        copy.wait_send()
    width = x_ref.shape[1]
    for j in range(n_blk):
        g_ref[:, j * width : (j + 1) * width] = gslots[j]
        b_ref[j * piece : (j + 1) * piece, :] = jnp.where(
            sec >= 1, bslots[j], jnp.zeros_like(bslots[j])
        )
    total = aslots[0]
    for j in range(1, n_blk):
        total = total + aslots[j]
    a_ref[...] = jnp.where(sec <= n_sec - 2, total, jnp.zeros_like(total))


def operator_exchange(x, up_t, be_t, n_sec, n_blk):
    rows, width = x.shape
    panel, cases = up_t.shape
    piece = panel // n_blk
    return pl.pallas_call(
        functools.partial(_operator_kernel, n_sec, n_blk),
        out_shape=(
            jax.ShapeDtypeStruct((rows, n_blk * width), x.dtype),
            jax.ShapeDtypeStruct((panel, cases), jnp.float32),
            jax.ShapeDtypeStruct((piece, cases), jnp.float32),
        ),
        in_specs=[pl.BlockSpec(memory_space=pltpu.VMEM)] * 3,
        out_specs=[pl.BlockSpec(memory_space=pltpu.VMEM)] * 3,
        scratch_shapes=[
            pltpu.VMEM((n_blk, rows, width), x.dtype),
            pltpu.VMEM((n_blk, piece, cases), jnp.float32),
            pltpu.VMEM((n_blk, piece, cases), jnp.float32),
        ]
        + [pltpu.SemaphoreType.DMA((n_blk,))] * 6,
        compiler_params=pltpu.CompilerParams(collective_id=5, has_side_effects=True),
    )(x, up_t, be_t)


def _precondition_kernel(n_sec, n_blk, rounds, x_ref, inv_ref, pick_ref, u_ref, w_ref, o_ref, *scratch):
    gslots, fpiece, fslots, fmat, carry, slots, gsend, grecv, fsend, frecv, ssend, srecv = scratch
    sec, blk = lax.axis_index("sec"), lax.axis_index("blk")
    first = rounds[0][1]
    offsets = len(first) + 1
    _greet_all(n_sec, n_blk, offsets, rounds, True)

    def blk_copy(k, target, slot):
        return pltpu.make_async_remote_copy(
            src_ref=x_ref,
            dst_ref=gslots.at[slot],
            send_sem=gsend.at[k],
            recv_sem=grecv.at[slot],
            device_id={"blk": target},
            device_id_type=MESH,
        )

    outgoing = [blk_copy(k, lax.rem(blk + k, n_blk), blk) for k in range(1, n_blk)]
    for copy in outgoing:
        copy.start()
    gslots[blk] = x_ref[...]
    for k in range(1, n_blk):
        sender = lax.rem(blk + k, n_blk)
        blk_copy(k, sender, sender).wait_recv()
    for copy in outgoing:
        copy.wait_send()
    width = x_ref.shape[1]
    contract = (((1,), (1,)), ((), ()))
    folded = lax.dot_general(
        gslots[0], inv_ref[:, 0:width], contract, preferred_element_type=jnp.float32
    )
    for j in range(1, n_blk):
        folded = folded + lax.dot_general(
            gslots[j],
            inv_ref[:, j * width : (j + 1) * width],
            contract,
            preferred_element_type=jnp.float32,
        )
    w_ref[...] = folded
    fpiece[...] = lax.dot_general(
        pick_ref[...], folded, contract, precision=lax.Precision.HIGHEST,
        preferred_element_type=jnp.float32,
    )
    _spread(n_sec, n_blk, offsets, fpiece, fslots, fsend, frecv)
    _assemble(n_blk, offsets, fslots, fmat)
    joined = jnp.where(sec >= 1, fmat[0], jnp.zeros_like(fmat[0]))
    for i, j in enumerate(first):
        term = jnp.dot(
            u_ref[i], fmat[j], precision=lax.Precision.HIGHEST, preferred_element_type=jnp.float32
        )
        joined = joined + jnp.where(sec >= j + 1, term, jnp.zeros_like(term))
    carry[1] = joined
    flat = len(first)
    for k in range(1, len(rounds)):
        d, js = rounds[k]
        _send_all(n_sec, sec, carry.at[k], slots, ssend, srecv, flat, d, js)
        joined = carry[k]
        for i, j in enumerate(js):
            term = jnp.dot(
                u_ref[flat + i], slots[flat + i], precision=lax.Precision.HIGHEST,
                preferred_element_type=jnp.float32,
            )
            joined = joined + jnp.where(sec >= j * d, term, jnp.zeros_like(term))
        carry[k + 1] = joined
        flat += len(js)
    o_ref[...] = carry[len(rounds)]


def precondition_sweep(x, inverse, picks, chain, n_sec, n_blk):
    cases, width = x.shape
    piece, _ = picks.shape
    panel = piece * n_blk
    plan = _plan(n_sec)
    rounds = len(plan)
    total = sum(len(js) for _, js in plan)
    offsets = len(plan[0][1]) + 1
    return pl.pallas_call(
        functools.partial(_precondition_kernel, n_sec, n_blk, plan),
        out_shape=(
            jax.ShapeDtypeStruct((cases, width), jnp.float32),
            jax.ShapeDtypeStruct((panel, cases), jnp.float32),
        ),
        in_specs=[pl.BlockSpec(memory_space=pltpu.VMEM)] * 4,
        out_specs=[pl.BlockSpec(memory_space=pltpu.VMEM)] * 2,
        scratch_shapes=[
            pltpu.VMEM((n_blk, cases, width), x.dtype),
            pltpu.VMEM((piece, cases), jnp.float32),
            pltpu.VMEM((offsets * n_blk, piece, cases), jnp.float32),
            pltpu.VMEM((offsets, panel, cases), jnp.float32),
            pltpu.VMEM((rounds + 1, panel, cases), jnp.float32),
            pltpu.VMEM((total, panel, cases), jnp.float32),
            pltpu.SemaphoreType.DMA((n_blk,)),
            pltpu.SemaphoreType.DMA((n_blk,)),
            pltpu.SemaphoreType.DMA((offsets * n_blk,)),
            pltpu.SemaphoreType.DMA((offsets * n_blk,)),
            pltpu.SemaphoreType.DMA((total,)),
            pltpu.SemaphoreType.DMA((total,)),
        ],
        compiler_params=pltpu.CompilerParams(collective_id=6, has_side_effects=True),
    )(x, inverse, picks, chain)


def least_squares(hessen, beta):
    cases = hessen.shape[0]
    depth = hessen.shape[2]
    rhs = jnp.zeros((cases, depth + 1), jnp.float32).at[:, 0].set(beta)
    upper = hessen
    for column in range(depth):
        upper_row = upper[:, column, :]
        lower_row = upper[:, column + 1, :]
        radius = jnp.sqrt(upper_row[:, column] ** 2 + lower_row[:, column] ** 2)
        cosine = upper_row[:, column] / radius
        sine_term = lower_row[:, column] / radius
        upper = upper.at[:, column, :].set(
            cosine[:, None] * upper_row + sine_term[:, None] * lower_row
        )
        upper = upper.at[:, column + 1, :].set(
            -sine_term[:, None] * upper_row + cosine[:, None] * lower_row
        )
        first_rhs = rhs[:, column]
        second_rhs = rhs[:, column + 1]
        rhs = rhs.at[:, column].set(cosine * first_rhs + sine_term * second_rhs)
        rhs = rhs.at[:, column + 1].set(-sine_term * first_rhs + cosine * second_rhs)
    weights = jnp.zeros((cases, depth), jnp.float32)
    for column in reversed(range(depth)):
        remain = rhs[:, column] - jnp.sum(
            upper[:, column, column + 1 :] * weights[:, column + 1 :], axis=1
        )
        weights = weights.at[:, column].set(remain / upper[:, column, column])
    return weights


def local(
    mesh_shape,
    state_now, source, fan_gain, section_block, block_inverse, back_panel, ahead_panel, interface
):
    highest = lax.Precision.HIGHEST
    cases, node_rows = state_now.shape
    panel_width = back_panel.shape[1]
    indices = interface[0]
    first_row = lax.axis_index("blk") * node_rows
    selector = (indices[None, :] == first_row + jnp.arange(node_rows)[:, None]).astype(jnp.float32)
    contract = (((1,), (1,)), ((), ()))
    gain_panel = jnp.dot(
        block_inverse,
        lax.all_gather(back_panel, "blk", axis=0, tiled=True),
        preferred_element_type=jnp.float32,
    )

    own_piece = panel_width // mesh_shape["blk"]
    own_picks = lax.dynamic_slice_in_dim(selector, lax.axis_index("blk") * own_piece, own_piece, 1).T
    own_maps = -jnp.dot(own_picks, gain_panel, precision=highest)
    chain = scan_maps(own_maps, mesh_shape["sec"], mesh_shape["blk"])

    def section_terms(dense_part, behind_vals, piece):
        width = piece.shape[1]
        dense_part = lax.dot_general(
            piece, section_block, contract, preferred_element_type=jnp.float32
        )
        picker = (indices[None, :] == jnp.arange(width)[:, None]).astype(jnp.bfloat16)
        behind_vals = jnp.dot(piece, picker, preferred_element_type=jnp.float32)
        return (dense_part, behind_vals)

    def fold_section(carry, piece):
        return section_terms(carry[0], carry[1], piece)

    def operator(vector):
        rounded = vector.astype(jnp.bfloat16)
        n_sec, n_blk = mesh_shape["sec"], mesh_shape["blk"]
        piece = panel_width // n_blk
        up_t = lax.dot_general(
            ahead_panel, rounded, (((0,), (1,)), ((), ())), preferred_element_type=jnp.float32
        )
        be_t = lax.dot_general(
            selector.astype(jnp.bfloat16),
            rounded,
            (((0,), (1,)), ((), ())),
            preferred_element_type=jnp.float32,
        )
        gathered, behind_t, ahead_piece = operator_exchange(rounded, up_t, be_t, n_sec, n_blk)
        dense_part = lax.dot_general(
            gathered, section_block, contract, preferred_element_type=jnp.float32
        )
        lower_term = lax.dot_general(
            behind_t.astype(jnp.bfloat16),
            back_panel,
            (((0,), (1,)), ((), ())),
            preferred_element_type=jnp.float32,
        )
        local_picks = lax.dynamic_slice_in_dim(selector, lax.axis_index("blk") * piece, piece, 1)
        upper_term = lax.dot_general(
            ahead_piece, local_picks, (((0,), (1,)), ((), ())), precision=highest
        )
        return dense_part + lower_term + upper_term

    def compose(earlier, later):
        first_map, first_value = earlier
        second_map, second_value = later
        joined_map = jnp.dot(second_map, first_map, precision=highest)
        joined_value = jnp.dot(first_value, second_map.T, precision=highest) + second_value
        return (joined_map, joined_value)

    def lengths(vector):
        return jnp.sqrt(global_sum(jnp.sum(vector * vector, axis=1)[None], mesh_shape)[0] + epsilon)

    bent = jnp.tanh(state_now)
    residual = source - operator(state_now) - fan_gain[None, :] * bent
    jac_diag = fan_gain[None, :] * (1.0 - bent * bent)
    beta = lengths(residual)
    basis = [residual / beta[:, None]]
    directions = []
    hessen = jnp.zeros((cases, KRYLOV + 1, KRYLOV), jnp.float32)
    for column in range(KRYLOV):
        precondition_rounded = basis[column].astype(jnp.bfloat16)
        precondition_folded, before_t = precondition_sweep(
            precondition_rounded, block_inverse, own_picks, chain, mesh_shape["sec"], mesh_shape["blk"]
        )
        direction = precondition_folded - lax.dot_general(
            before_t, gain_panel, (((0,), (1,)), ((), ())), precision=highest
        )
        product = operator(direction) + jac_diag * direction
        stacked = jnp.stack(basis)
        projections = global_sum(jnp.sum(product[None] * stacked, axis=2), mesh_shape)
        product = product - jnp.sum(projections[:, :, None] * stacked, axis=0)
        length = lengths(product)
        hessen = hessen.at[:, : column + 1, column].set(projections.T)
        hessen = hessen.at[:, column + 1, column].set(length)
        basis.append(product / length[:, None])
        directions.append(direction)
    weights = least_squares(hessen, beta)
    update = jnp.zeros_like(state_now)
    for column in range(KRYLOV):
        update = update + weights[:, column : column + 1] * directions[column]
    return state_now + update


def solution(mesh):
    in_specs = (
        P(None, ("sec", "blk")),
        P(None, ("sec", "blk")),
        P(("sec", "blk")),
        P(("sec", "blk"), None),
        P(("sec", "blk"), None),
        P(("sec", "blk"), None),
        P(("sec", "blk"), None),
        P("sec", None),
    )
    out_specs = P(None, ("sec", "blk"))
    return jax.shard_map(functools.partial(local, dict(mesh.shape)), mesh=mesh, in_specs=in_specs, out_specs=out_specs, check_vma=False)
```

```python
import functools

import jax
import jax.numpy as jnp
from jax import lax
from jax.experimental import pallas as pl
from jax.experimental.pallas import tpu as pltpu
from jax.sharding import PartitionSpec as P

MESH = pl.DeviceIdType.MESH

KRYLOV = 3


epsilon = 1e-06


def extended(x, sides, width):
    for axis, dim in sides:
        size, length = (lax.axis_size(axis), x.shape[dim])
        up = [(i, (i + 1) % size) for i in range(size - 1)]
        down = [(j, i) for i, j in up]
        last = lax.slice_in_dim(x, length - width, length, axis=dim)
        first = lax.slice_in_dim(x, 0, width, axis=dim)
        before = lax.ppermute(last, axis, up)
        after = lax.ppermute(first, axis, down)
        x = jnp.concatenate([before, x, after], axis=dim)
    return x


def entering(value, axis, join, neutral):
    count, mine = (lax.axis_size(axis), lax.axis_index(axis))
    pieces = jax.tree.map(lambda part: lax.all_gather(part, axis), value)
    so_far = jax.tree.map(
        lambda part, zero: jnp.full_like(part, 0) + jnp.asarray(zero, part.dtype), value, neutral
    )

    def step(position, so_far):
        longer = join(so_far, jax.tree.map(lambda part: part[position], pieces))
        return jax.tree.map(lambda new, old: jnp.where(position < mine, new, old), longer, so_far)

    return lax.fori_loop(0, count - 1, step, so_far)


def _reduce_kernel(stages, x_ref, o_ref, *scratch):
    count = len(stages)
    slots = scratch[:count]
    partial = scratch[count]
    sends = scratch[count + 1 : 2 * count + 1]
    recvs = scratch[2 * count + 1 :]
    barrier = pltpu.get_barrier_semaphore()
    peers = 0
    for axis, n in stages:
        mine = lax.axis_index(axis)
        for k in range(1, n):
            pl.semaphore_signal(
                barrier, inc=1, device_id={axis: lax.rem(mine + k, n)}, device_id_type=MESH
            )
            peers += 1
    pl.semaphore_wait(barrier, peers)
    source = x_ref
    for stage, (axis, n) in enumerate(stages):
        mine = lax.axis_index(axis)
        copies = []
        for k in range(1, n):
            copy = pltpu.make_async_remote_copy(
                src_ref=source,
                dst_ref=slots[stage].at[mine],
                send_sem=sends[stage].at[k],
                recv_sem=recvs[stage].at[mine],
                device_id={axis: lax.rem(mine + k, n)},
                device_id_type=MESH,
            )
            copy.start()
            copies.append(copy)
        slots[stage][mine] = source[...]
        for k in range(1, n):
            sender = lax.rem(mine + k, n)
            pltpu.make_async_remote_copy(
                src_ref=source,
                dst_ref=slots[stage].at[sender],
                send_sem=sends[stage].at[k],
                recv_sem=recvs[stage].at[sender],
                device_id={axis: sender},
                device_id_type=MESH,
            ).wait_recv()
        for copy in copies:
            copy.wait_send()
        total = slots[stage][0]
        for j in range(1, n):
            total = total + slots[stage][j]
        if stage == count - 1:
            o_ref[...] = total
        else:
            partial[...] = total
            source = partial


def all_sum(x, axes, mesh_shape, collective):
    stages = tuple((axis, mesh_shape[axis]) for axis in axes if mesh_shape[axis] > 1)
    rows, cols = x.shape
    scratch = [pltpu.VMEM((n, rows, cols), jnp.float32) for _, n in stages]
    scratch.append(pltpu.VMEM((rows, cols), jnp.float32))
    scratch += [pltpu.SemaphoreType.DMA((n,)) for _, n in stages]
    scratch += [pltpu.SemaphoreType.DMA((n,)) for _, n in stages]
    return pl.pallas_call(
        functools.partial(_reduce_kernel, stages),
        out_shape=jax.ShapeDtypeStruct((rows, cols), jnp.float32),
        in_specs=[pl.BlockSpec(memory_space=pltpu.VMEM)],
        out_specs=pl.BlockSpec(memory_space=pltpu.VMEM),
        scratch_shapes=scratch,
        compiler_params=pltpu.CompilerParams(collective_id=collective, has_side_effects=True),
    )(x.astype(jnp.float32))


def global_sum(rows_of_sums, mesh_shape):
    count = rows_of_sums.shape[0]
    padded = jnp.zeros((8, rows_of_sums.shape[1]), jnp.float32).at[:count].set(rows_of_sums)
    return all_sum(padded, ("blk", "sec"), mesh_shape, 0)[:count]


def _doubling(n):
    distances, d = [], 1
    while d < n:
        distances.append(d)
        d *= 2
    return tuple(distances)


def _greet(n, distances):
    barrier = pltpu.get_barrier_semaphore()
    mine = lax.axis_index("sec")
    for d in distances:
        for peer in (lax.rem(mine + d, n), lax.rem(mine + n - d, n)):
            pl.semaphore_signal(barrier, inc=1, device_id={"sec": peer}, device_id_type=MESH)
    pl.semaphore_wait(barrier, 2 * len(distances))


def _hop(n, d, source, slot, send_sem, recv_sem):
    mine = lax.axis_index("sec")
    copy = pltpu.make_async_remote_copy(
        src_ref=source,
        dst_ref=slot,
        send_sem=send_sem,
        recv_sem=recv_sem,
        device_id={"sec": lax.rem(mine + d, n)},
        device_id_type=MESH,
    )
    copy.start()
    copy.wait_recv()
    copy.wait_send()


RADIX = 4


def _plan(n):
    rounds, d = [], 1
    while d < n:
        rounds.append((d, tuple(j for j in range(1, RADIX) if j * d < n)))
        d *= RADIX
    return tuple(rounds)


def _plan_peers(rounds):
    return tuple(sorted({j * d for d, js in rounds for j in js} | {1}))


def _send_all(n, sec, sources, slots, sends, recvs, flat, d, js):
    copies = []
    for i, j in enumerate(js):
        copy = pltpu.make_async_remote_copy(
            src_ref=sources,
            dst_ref=slots.at[flat + i],
            send_sem=sends.at[flat + i],
            recv_sem=recvs.at[flat + i],
            device_id={"sec": lax.rem(sec + j * d, n)},
            device_id_type=MESH,
        )
        copy.start()
        copies.append(copy)
    for copy in copies:
        copy.wait_recv()
    for copy in copies:
        copy.wait_send()


def _spread(n_sec, n_blk, offsets, piece_ref, slots, sends, recvs):
    sec, blk = lax.axis_index("sec"), lax.axis_index("blk")

    def copy(o, j, index):
        return pltpu.make_async_remote_copy(
            src_ref=piece_ref,
            dst_ref=slots.at[index],
            send_sem=sends.at[(o - 1) * n_blk + j],
            recv_sem=recvs.at[index],
            device_id={"sec": lax.rem(sec + o, n_sec), "blk": j},
            device_id_type=MESH,
        )

    outgoing = [
        copy(o, j, (o - 1) * n_blk + blk) for o in range(1, offsets + 1) for j in range(n_blk)
    ]
    for c in outgoing:
        c.start()
    for o in range(1, offsets + 1):
        for j in range(n_blk):
            copy(o, j, (o - 1) * n_blk + j).wait_recv()
    for c in outgoing:
        c.wait_send()


def _assemble(n_blk, offsets, slots, mats):
    piece = slots.shape[1]
    for o in range(offsets):
        for j in range(n_blk):
            mats[o, j * piece : (j + 1) * piece, :] = slots[o * n_blk + j]


def _greet_all(n_sec, n_blk, offsets, rounds, blk_peers):
    barrier = pltpu.get_barrier_semaphore()
    sec, blk = lax.axis_index("sec"), lax.axis_index("blk")
    count = 0
    if blk_peers:
        for k in range(1, n_blk):
            pl.semaphore_signal(
                barrier, inc=1, device_id={"blk": lax.rem(blk + k, n_blk)}, device_id_type=MESH
            )
            count += 1
    for o in range(1, offsets + 1):
        for j in range(n_blk):
            for peer in (lax.rem(sec + o, n_sec), lax.rem(sec + n_sec - o, n_sec)):
                pl.semaphore_signal(
                    barrier, inc=1, device_id={"sec": peer, "blk": j}, device_id_type=MESH
                )
                count += 1
    for d in sorted({j * d for d, js in rounds[1:] for j in js}):
        for peer in (lax.rem(sec + d, n_sec), lax.rem(sec + n_sec - d, n_sec)):
            pl.semaphore_signal(barrier, inc=1, device_id={"sec": peer}, device_id_type=MESH)
            count += 1
    pl.semaphore_wait(barrier, count)


def _maps_kernel(n, n_blk, rounds, e_ref, a_ref, eslots, emat, current, slots, esend, erecv, sends, recvs):
    sec = lax.axis_index("sec")
    first = rounds[0][1]
    offsets = len(first) + 1
    _greet_all(n, n_blk, offsets, rounds, False)
    _spread(n, n_blk, offsets, e_ref, eslots, esend, erecv)
    _assemble(n_blk, offsets, eslots, emat)
    joined = emat[0]
    for i, j in enumerate(first):
        a_ref[i] = joined
        joined = jnp.dot(
            joined, emat[j], precision=lax.Precision.HIGHEST, preferred_element_type=jnp.float32
        )
    current[...] = joined
    flat = len(first)
    for k in range(1, len(rounds)):
        d, js = rounds[k]
        onward = k < len(rounds) - 1
        if onward or len(js) > 1:
            _send_all(n, sec, current, slots, sends, recvs, flat, d, js)
        joined = current[...]
        for i, j in enumerate(js):
            a_ref[flat + i] = joined
            if onward or i < len(js) - 1:
                joined = jnp.dot(
                    joined, slots[flat + i], precision=lax.Precision.HIGHEST,
                    preferred_element_type=jnp.float32,
                )
        if onward:
            current[...] = joined
        flat += len(js)


def scan_maps(e_piece, n, n_blk):
    rounds = _plan(n)
    total = sum(len(js) for _, js in rounds)
    offsets = len(rounds[0][1]) + 1
    piece, width = e_piece.shape
    return pl.pallas_call(
        functools.partial(_maps_kernel, n, n_blk, rounds),
        out_shape=jax.ShapeDtypeStruct((total, width, width), jnp.float32),
        in_specs=[pl.BlockSpec(memory_space=pltpu.VMEM)],
        out_specs=pl.BlockSpec(memory_space=pltpu.VMEM),
        scratch_shapes=[
            pltpu.VMEM((offsets * n_blk, piece, width), jnp.float32),
            pltpu.VMEM((offsets, width, width), jnp.float32),
            pltpu.VMEM((width, width), jnp.float32),
            pltpu.VMEM((total, width, width), jnp.float32),
            pltpu.SemaphoreType.DMA((offsets * n_blk,)),
            pltpu.SemaphoreType.DMA((offsets * n_blk,)),
            pltpu.SemaphoreType.DMA((total,)),
            pltpu.SemaphoreType.DMA((total,)),
        ],
        compiler_params=pltpu.CompilerParams(collective_id=2, has_side_effects=True),
    )(e_piece)


def _gather_kernel(n, x_ref, o_ref, slots, sends, recvs):
    mine = lax.axis_index("blk")
    barrier = pltpu.get_barrier_semaphore()
    for k in range(1, n):
        pl.semaphore_signal(
            barrier, inc=1, device_id={"blk": lax.rem(mine + k, n)}, device_id_type=MESH
        )
    pl.semaphore_wait(barrier, n - 1)
    copies = []
    for k in range(1, n):
        copy = pltpu.make_async_remote_copy(
            src_ref=x_ref,
            dst_ref=slots.at[mine],
            send_sem=sends.at[k],
            recv_sem=recvs.at[mine],
            device_id={"blk": lax.rem(mine + k, n)},
            device_id_type=MESH,
        )
        copy.start()
        copies.append(copy)
    slots[mine] = x_ref[...]
    for k in range(1, n):
        sender = lax.rem(mine + k, n)
        pltpu.make_async_remote_copy(
            src_ref=x_ref,
            dst_ref=slots.at[sender],
            send_sem=sends.at[k],
            recv_sem=recvs.at[sender],
            device_id={"blk": sender},
            device_id_type=MESH,
        ).wait_recv()
    for copy in copies:
        copy.wait_send()
    width = x_ref.shape[1]
    for j in range(n):
        o_ref[:, j * width : (j + 1) * width] = slots[j]


def gather_blk(x, n):
    rows, width = x.shape
    return pl.pallas_call(
        functools.partial(_gather_kernel, n),
        out_shape=jax.ShapeDtypeStruct((rows, n * width), x.dtype),
        in_specs=[pl.BlockSpec(memory_space=pltpu.VMEM)],
        out_specs=pl.BlockSpec(memory_space=pltpu.VMEM),
        scratch_shapes=[
            pltpu.VMEM((n, rows, width), x.dtype),
            pltpu.SemaphoreType.DMA((n,)),
            pltpu.SemaphoreType.DMA((n,)),
        ],
        compiler_params=pltpu.CompilerParams(collective_id=4, has_side_effects=True),
    )(x)


def _operator_kernel(n_sec, n_blk, x_ref, up_ref, be_ref, g_ref, b_ref, a_ref, *scratch):
    gslots, bslots, aslots, gsend, grecv, bsend, brecv, asend, arecv = scratch
    sec, blk = lax.axis_index("sec"), lax.axis_index("blk")
    nxt, prv = lax.rem(sec + 1, n_sec), lax.rem(sec + n_sec - 1, n_sec)
    piece = bslots.shape[1]
    barrier = pltpu.get_barrier_semaphore()
    for k in range(1, n_blk):
        pl.semaphore_signal(
            barrier, inc=1, device_id={"blk": lax.rem(blk + k, n_blk)}, device_id_type=MESH
        )
    for j in range(n_blk):
        for other in (nxt, prv):
            pl.semaphore_signal(
                barrier, inc=1, device_id={"sec": other, "blk": j}, device_id_type=MESH
            )
    pl.semaphore_wait(barrier, 3 * n_blk - 1)
    copies = []
    for k in range(1, n_blk):
        copies.append(
            pltpu.make_async_remote_copy(
                src_ref=x_ref,
                dst_ref=gslots.at[blk],
                send_sem=gsend.at[k],
                recv_sem=grecv.at[blk],
                device_id={"blk": lax.rem(blk + k, n_blk)},
                device_id_type=MESH,
            )
        )
    mine = pl.ds(pl.multiple_of(blk * piece, 8), piece)
    for j in range(n_blk):
        copies.append(
            pltpu.make_async_remote_copy(
                src_ref=be_ref.at[mine],
                dst_ref=bslots.at[blk],
                send_sem=bsend.at[j],
                recv_sem=brecv.at[blk],
                device_id={"sec": nxt, "blk": j},
                device_id_type=MESH,
            )
        )
        copies.append(
            pltpu.make_async_remote_copy(
                src_ref=up_ref.at[pl.ds(j * piece, piece)],
                dst_ref=aslots.at[blk],
                send_sem=asend.at[j],
                recv_sem=arecv.at[blk],
                device_id={"sec": prv, "blk": j},
                device_id_type=MESH,
            )
        )
    for copy in copies:
        copy.start()
    gslots[blk] = x_ref[...]
    for k in range(1, n_blk):
        sender = lax.rem(blk + k, n_blk)
        pltpu.make_async_remote_copy(
            src_ref=x_ref,
            dst_ref=gslots.at[sender],
            send_sem=gsend.at[k],
            recv_sem=grecv.at[sender],
            device_id={"blk": sender},
            device_id_type=MESH,
        ).wait_recv()
    for j in range(n_blk):
        pltpu.make_async_remote_copy(
            src_ref=be_ref.at[mine],
            dst_ref=bslots.at[j],
            send_sem=bsend.at[j],
            recv_sem=brecv.at[j],
            device_id={"sec": prv, "blk": j},
            device_id_type=MESH,
        ).wait_recv()
        pltpu.make_async_remote_copy(
            src_ref=up_ref.at[pl.ds(j * piece, piece)],
            dst_ref=aslots.at[j],
            send_sem=asend.at[j],
            recv_sem=arecv.at[j],
            device_id={"sec": nxt, "blk": j},
            device_id_type=MESH,
        ).wait_recv()
    for copy in copies:
        copy.wait_send()
    width = x_ref.shape[1]
    for j in range(n_blk):
        g_ref[:, j * width : (j + 1) * width] = gslots[j]
        b_ref[j * piece : (j + 1) * piece, :] = jnp.where(
            sec >= 1, bslots[j], jnp.zeros_like(bslots[j])
        )
    total = aslots[0]
    for j in range(1, n_blk):
        total = total + aslots[j]
    a_ref[...] = jnp.where(sec <= n_sec - 2, total, jnp.zeros_like(total))


def operator_exchange(x, up_t, be_t, n_sec, n_blk):
    rows, width = x.shape
    panel, cases = up_t.shape
    piece = panel // n_blk
    return pl.pallas_call(
        functools.partial(_operator_kernel, n_sec, n_blk),
        out_shape=(
            jax.ShapeDtypeStruct((rows, n_blk * width), x.dtype),
            jax.ShapeDtypeStruct((panel, cases), jnp.float32),
            jax.ShapeDtypeStruct((piece, cases), jnp.float32),
        ),
        in_specs=[pl.BlockSpec(memory_space=pltpu.VMEM)] * 3,
        out_specs=[pl.BlockSpec(memory_space=pltpu.VMEM)] * 3,
        scratch_shapes=[
            pltpu.VMEM((n_blk, rows, width), x.dtype),
            pltpu.VMEM((n_blk, piece, cases), jnp.float32),
            pltpu.VMEM((n_blk, piece, cases), jnp.float32),
        ]
        + [pltpu.SemaphoreType.DMA((n_blk,))] * 6,
        compiler_params=pltpu.CompilerParams(collective_id=5, has_side_effects=True),
    )(x, up_t, be_t)


def _precondition_kernel(n_sec, n_blk, rounds, x_ref, inv_ref, pick_ref, u_ref, w_ref, o_ref, *scratch):
    gslots, fpiece, fslots, fmat, carry, slots, gsend, grecv, fsend, frecv, ssend, srecv = scratch
    sec, blk = lax.axis_index("sec"), lax.axis_index("blk")
    first = rounds[0][1]
    offsets = len(first) + 1
    _greet_all(n_sec, n_blk, offsets, rounds, True)

    def blk_copy(k, target, slot):
        return pltpu.make_async_remote_copy(
            src_ref=x_ref,
            dst_ref=gslots.at[slot],
            send_sem=gsend.at[k],
            recv_sem=grecv.at[slot],
            device_id={"blk": target},
            device_id_type=MESH,
        )

    outgoing = [blk_copy(k, lax.rem(blk + k, n_blk), blk) for k in range(1, n_blk)]
    for copy in outgoing:
        copy.start()
    gslots[blk] = x_ref[...]
    for k in range(1, n_blk):
        sender = lax.rem(blk + k, n_blk)
        blk_copy(k, sender, sender).wait_recv()
    for copy in outgoing:
        copy.wait_send()
    width = x_ref.shape[1]
    contract = (((1,), (1,)), ((), ()))
    folded = lax.dot_general(
        gslots[0], inv_ref[:, 0:width], contract, preferred_element_type=jnp.float32
    )
    for j in range(1, n_blk):
        folded = folded + lax.dot_general(
            gslots[j],
            inv_ref[:, j * width : (j + 1) * width],
            contract,
            preferred_element_type=jnp.float32,
        )
    w_ref[...] = folded
    fpiece[...] = lax.dot_general(
        pick_ref[...], folded, contract, precision=lax.Precision.HIGHEST,
        preferred_element_type=jnp.float32,
    )
    _spread(n_sec, n_blk, offsets, fpiece, fslots, fsend, frecv)
    _assemble(n_blk, offsets, fslots, fmat)
    joined = jnp.where(sec >= 1, fmat[0], jnp.zeros_like(fmat[0]))
    for i, j in enumerate(first):
        term = jnp.dot(
            u_ref[i], fmat[j], precision=lax.Precision.HIGHEST, preferred_element_type=jnp.float32
        )
        joined = joined + jnp.where(sec >= j + 1, term, jnp.zeros_like(term))
    carry[1] = joined
    flat = len(first)
    for k in range(1, len(rounds)):
        d, js = rounds[k]
        _send_all(n_sec, sec, carry.at[k], slots, ssend, srecv, flat, d, js)
        joined = carry[k]
        for i, j in enumerate(js):
            term = jnp.dot(
                u_ref[flat + i], slots[flat + i], precision=lax.Precision.HIGHEST,
                preferred_element_type=jnp.float32,
            )
            joined = joined + jnp.where(sec >= j * d, term, jnp.zeros_like(term))
        carry[k + 1] = joined
        flat += len(js)
    o_ref[...] = carry[len(rounds)]


def precondition_sweep(x, inverse, picks, chain, n_sec, n_blk):
    cases, width = x.shape
    piece, _ = picks.shape
    panel = piece * n_blk
    plan = _plan(n_sec)
    rounds = len(plan)
    total = sum(len(js) for _, js in plan)
    offsets = len(plan[0][1]) + 1
    return pl.pallas_call(
        functools.partial(_precondition_kernel, n_sec, n_blk, plan),
        out_shape=(
            jax.ShapeDtypeStruct((cases, width), jnp.float32),
            jax.ShapeDtypeStruct((panel, cases), jnp.float32),
        ),
        in_specs=[pl.BlockSpec(memory_space=pltpu.VMEM)] * 4,
        out_specs=[pl.BlockSpec(memory_space=pltpu.VMEM)] * 2,
        scratch_shapes=[
            pltpu.VMEM((n_blk, cases, width), x.dtype),
            pltpu.VMEM((piece, cases), jnp.float32),
            pltpu.VMEM((offsets * n_blk, piece, cases), jnp.float32),
            pltpu.VMEM((offsets, panel, cases), jnp.float32),
            pltpu.VMEM((rounds + 1, panel, cases), jnp.float32),
            pltpu.VMEM((total, panel, cases), jnp.float32),
            pltpu.SemaphoreType.DMA((n_blk,)),
            pltpu.SemaphoreType.DMA((n_blk,)),
            pltpu.SemaphoreType.DMA((offsets * n_blk,)),
            pltpu.SemaphoreType.DMA((offsets * n_blk,)),
            pltpu.SemaphoreType.DMA((total,)),
            pltpu.SemaphoreType.DMA((total,)),
        ],
        compiler_params=pltpu.CompilerParams(collective_id=6, has_side_effects=True),
    )(x, inverse, picks, chain)


def _exchange_sum(stages, source, slots, partial, sends, recvs, out):
    count = len(stages)
    for stage, (axis, n) in enumerate(stages):
        mine = lax.axis_index(axis)
        copies = []
        for k in range(1, n):
            copy = pltpu.make_async_remote_copy(
                src_ref=source,
                dst_ref=slots[stage].at[mine],
                send_sem=sends[stage].at[k],
                recv_sem=recvs[stage].at[mine],
                device_id={axis: lax.rem(mine + k, n)},
                device_id_type=MESH,
            )
            copy.start()
            copies.append(copy)
        slots[stage][mine] = source[...]
        for k in range(1, n):
            sender = lax.rem(mine + k, n)
            pltpu.make_async_remote_copy(
                src_ref=source,
                dst_ref=slots[stage].at[sender],
                send_sem=sends[stage].at[k],
                recv_sem=recvs[stage].at[sender],
                device_id={axis: sender},
                device_id_type=MESH,
            ).wait_recv()
        for copy in copies:
            copy.wait_send()
        total = slots[stage][0]
        for j in range(1, n):
            total = total + slots[stage][j]
        if stage == count - 1:
            out[...] = total
        else:
            partial[...] = total
            source = partial


def _project_kernel(stages, depth, basis_ref, image_ref, h_ref, next_ref, *scratch):
    count = len(stages)
    first, second = scratch[: 3 * count + 1], scratch[3 * count + 1 : 6 * count + 2]
    rows, work = scratch[6 * count + 2 :]
    barrier = pltpu.get_barrier_semaphore()
    peers = 0
    for axis, n in stages:
        mine = lax.axis_index(axis)
        for k in range(1, n):
            pl.semaphore_signal(
                barrier, inc=1, device_id={axis: lax.rem(mine + k, n)}, device_id_type=MESH
            )
            peers += 1
    pl.semaphore_wait(barrier, peers)
    highest = lax.Precision.HIGHEST
    contract = (((1,), (1,)), ((), ()))
    image = image_ref[...]
    ones = jnp.ones((8, image.shape[1]), jnp.float32)
    eye = (
        lax.broadcasted_iota(jnp.int32, (image.shape[0],) * 2, 0)
        == lax.broadcasted_iota(jnp.int32, (image.shape[0],) * 2, 1)
    ).astype(jnp.float32)
    rows[...] = jnp.zeros_like(rows)
    for i in range(depth):
        summed = lax.dot_general(
            ones, image * basis_ref[i], contract, precision=highest,
            preferred_element_type=jnp.float32,
        )
        rows[i : i + 1, :] = summed[0:1, :]

    def run(buffers, source, out):
        slots = buffers[:count]
        partial = buffers[count]
        sends = buffers[count + 1 : 2 * count + 1]
        recvs = buffers[2 * count + 1 :]
        _exchange_sum(stages, source, slots, partial, sends, recvs, out)

    run(first, rows, h_ref)
    columns = lax.dot_general(
        eye, h_ref[...], contract, precision=highest, preferred_element_type=jnp.float32
    )
    for i in range(depth):
        image = image - columns[:, i : i + 1] * basis_ref[i]
    work[...] = lax.dot_general(
        ones, image * image, contract, precision=highest, preferred_element_type=jnp.float32
    )
    run(second, work, rows)
    length = jnp.sqrt(rows[...] + epsilon)
    h_ref[depth : depth + 1, :] = length[0:1, :]
    scale = lax.dot_general(
        eye, length, contract, precision=highest, preferred_element_type=jnp.float32
    )
    next_ref[...] = image / scale[:, 0:1]


def project(stacked, image, mesh_shape):
    depth, cases, width = stacked.shape
    stages = tuple((axis, mesh_shape[axis]) for axis in ("blk", "sec") if mesh_shape[axis] > 1)

    def buffers():
        out = [pltpu.VMEM((n, 8, cases), jnp.float32) for _, n in stages]
        out.append(pltpu.VMEM((8, cases), jnp.float32))
        out += [pltpu.SemaphoreType.DMA((n,)) for _, n in stages]
        out += [pltpu.SemaphoreType.DMA((n,)) for _, n in stages]
        return out

    return pl.pallas_call(
        functools.partial(_project_kernel, stages, depth),
        out_shape=(
            jax.ShapeDtypeStruct((8, cases), jnp.float32),
            jax.ShapeDtypeStruct((cases, width), jnp.float32),
        ),
        in_specs=[pl.BlockSpec(memory_space=pltpu.VMEM)] * 2,
        out_specs=[pl.BlockSpec(memory_space=pltpu.VMEM)] * 2,
        scratch_shapes=buffers()
        + buffers()
        + [pltpu.VMEM((8, cases), jnp.float32), pltpu.VMEM((8, cases), jnp.float32)],
        compiler_params=pltpu.CompilerParams(collective_id=6 + depth, has_side_effects=True),
    )(stacked, image)


def least_squares(hessen, beta):
    cases = hessen.shape[0]
    depth = hessen.shape[2]
    rhs = jnp.zeros((cases, depth + 1), jnp.float32).at[:, 0].set(beta)
    upper = hessen
    for column in range(depth):
        upper_row = upper[:, column, :]
        lower_row = upper[:, column + 1, :]
        radius = jnp.sqrt(upper_row[:, column] ** 2 + lower_row[:, column] ** 2)
        cosine = upper_row[:, column] / radius
        sine_term = lower_row[:, column] / radius
        upper = upper.at[:, column, :].set(
            cosine[:, None] * upper_row + sine_term[:, None] * lower_row
        )
        upper = upper.at[:, column + 1, :].set(
            -sine_term[:, None] * upper_row + cosine[:, None] * lower_row
        )
        first_rhs = rhs[:, column]
        second_rhs = rhs[:, column + 1]
        rhs = rhs.at[:, column].set(cosine * first_rhs + sine_term * second_rhs)
        rhs = rhs.at[:, column + 1].set(-sine_term * first_rhs + cosine * second_rhs)
    weights = jnp.zeros((cases, depth), jnp.float32)
    for column in reversed(range(depth)):
        remain = rhs[:, column] - jnp.sum(
            upper[:, column, column + 1 :] * weights[:, column + 1 :], axis=1
        )
        weights = weights.at[:, column].set(remain / upper[:, column, column])
    return weights


def local(
    mesh_shape,
    state_now, source, fan_gain, section_block, block_inverse, back_panel, ahead_panel, interface
):
    highest = lax.Precision.HIGHEST
    cases, node_rows = state_now.shape
    panel_width = back_panel.shape[1]
    indices = interface[0]
    first_row = lax.axis_index("blk") * node_rows
    selector = (indices[None, :] == first_row + jnp.arange(node_rows)[:, None]).astype(jnp.float32)
    contract = (((1,), (1,)), ((), ()))
    gain_panel = jnp.dot(
        block_inverse,
        lax.all_gather(back_panel, "blk", axis=0, tiled=True),
        preferred_element_type=jnp.float32,
    )

    own_piece = panel_width // mesh_shape["blk"]
    own_picks = lax.dynamic_slice_in_dim(selector, lax.axis_index("blk") * own_piece, own_piece, 1).T
    own_maps = -jnp.dot(own_picks, gain_panel, precision=highest)
    chain = scan_maps(own_maps, mesh_shape["sec"], mesh_shape["blk"])

    def section_terms(dense_part, behind_vals, piece):
        width = piece.shape[1]
        dense_part = lax.dot_general(
            piece, section_block, contract, preferred_element_type=jnp.float32
        )
        picker = (indices[None, :] == jnp.arange(width)[:, None]).astype(jnp.bfloat16)
        behind_vals = jnp.dot(piece, picker, preferred_element_type=jnp.float32)
        return (dense_part, behind_vals)

    def fold_section(carry, piece):
        return section_terms(carry[0], carry[1], piece)

    def operator(vector):
        rounded = vector.astype(jnp.bfloat16)
        n_sec, n_blk = mesh_shape["sec"], mesh_shape["blk"]
        piece = panel_width // n_blk
        up_t = lax.dot_general(
            ahead_panel, rounded, (((0,), (1,)), ((), ())), preferred_element_type=jnp.float32
        )
        be_t = lax.dot_general(
            selector.astype(jnp.bfloat16),
            rounded,
            (((0,), (1,)), ((), ())),
            preferred_element_type=jnp.float32,
        )
        gathered, behind_t, ahead_piece = operator_exchange(rounded, up_t, be_t, n_sec, n_blk)
        dense_part = lax.dot_general(
            gathered, section_block, contract, preferred_element_type=jnp.float32
        )
        lower_term = lax.dot_general(
            behind_t.astype(jnp.bfloat16),
            back_panel,
            (((0,), (1,)), ((), ())),
            preferred_element_type=jnp.float32,
        )
        local_picks = lax.dynamic_slice_in_dim(selector, lax.axis_index("blk") * piece, piece, 1)
        upper_term = lax.dot_general(
            ahead_piece, local_picks, (((0,), (1,)), ((), ())), precision=highest
        )
        return dense_part + lower_term + upper_term

    def compose(earlier, later):
        first_map, first_value = earlier
        second_map, second_value = later
        joined_map = jnp.dot(second_map, first_map, precision=highest)
        joined_value = jnp.dot(first_value, second_map.T, precision=highest) + second_value
        return (joined_map, joined_value)

    def lengths(vector):
        return jnp.sqrt(global_sum(jnp.sum(vector * vector, axis=1)[None], mesh_shape)[0] + epsilon)

    bent = jnp.tanh(state_now)
    residual = source - operator(state_now) - fan_gain[None, :] * bent
    jac_diag = fan_gain[None, :] * (1.0 - bent * bent)
    beta = lengths(residual)
    basis = [residual / beta[:, None]]
    directions = []
    hessen = jnp.zeros((cases, KRYLOV + 1, KRYLOV), jnp.float32)
    for column in range(KRYLOV):
        precondition_rounded = basis[column].astype(jnp.bfloat16)
        precondition_folded, before_t = precondition_sweep(
            precondition_rounded, block_inverse, own_picks, chain, mesh_shape["sec"], mesh_shape["blk"]
        )
        direction = precondition_folded - lax.dot_general(
            before_t, gain_panel, (((0,), (1,)), ((), ())), precision=highest
        )
        product = operator(direction) + jac_diag * direction
        stacked = jnp.stack(basis)
        sums, following = project(stacked, product, mesh_shape)
        hessen = hessen.at[:, : column + 2, column].set(sums[: column + 2].T)
        basis.append(following)
        directions.append(direction)
    weights = least_squares(hessen, beta)
    update = jnp.zeros_like(state_now)
    for column in range(KRYLOV):
        update = update + weights[:, column : column + 1] * directions[column]
    return state_now + update


def solution(mesh):
    in_specs = (
        P(None, ("sec", "blk")),
        P(None, ("sec", "blk")),
        P(("sec", "blk")),
        P(("sec", "blk"), None),
        P(("sec", "blk"), None),
        P(("sec", "blk"), None),
        P(("sec", "blk"), None),
        P("sec", None),
    )
    out_specs = P(None, ("sec", "blk"))
    return jax.shard_map(functools.partial(local, dict(mesh.shape)), mesh=mesh, in_specs=in_specs, out_specs=out_specs, check_vma=False)
```

```python
import functools

import jax
import jax.numpy as jnp
from jax import lax
from jax.experimental import pallas as pl
from jax.experimental.pallas import tpu as pltpu
from jax.sharding import PartitionSpec as P

MESH = pl.DeviceIdType.MESH

KRYLOV = 3


epsilon = 1e-06


def extended(x, sides, width):
    for axis, dim in sides:
        size, length = (lax.axis_size(axis), x.shape[dim])
        up = [(i, (i + 1) % size) for i in range(size - 1)]
        down = [(j, i) for i, j in up]
        last = lax.slice_in_dim(x, length - width, length, axis=dim)
        first = lax.slice_in_dim(x, 0, width, axis=dim)
        before = lax.ppermute(last, axis, up)
        after = lax.ppermute(first, axis, down)
        x = jnp.concatenate([before, x, after], axis=dim)
    return x


def entering(value, axis, join, neutral):
    count, mine = (lax.axis_size(axis), lax.axis_index(axis))
    pieces = jax.tree.map(lambda part: lax.all_gather(part, axis), value)
    so_far = jax.tree.map(
        lambda part, zero: jnp.full_like(part, 0) + jnp.asarray(zero, part.dtype), value, neutral
    )

    def step(position, so_far):
        longer = join(so_far, jax.tree.map(lambda part: part[position], pieces))
        return jax.tree.map(lambda new, old: jnp.where(position < mine, new, old), longer, so_far)

    return lax.fori_loop(0, count - 1, step, so_far)


def _reduce_kernel(stages, x_ref, o_ref, *scratch):
    count = len(stages)
    slots = scratch[:count]
    partial = scratch[count]
    sends = scratch[count + 1 : 2 * count + 1]
    recvs = scratch[2 * count + 1 :]
    barrier = pltpu.get_barrier_semaphore()
    peers = 0
    for axis, n in stages:
        mine = lax.axis_index(axis)
        for k in range(1, n):
            pl.semaphore_signal(
                barrier, inc=1, device_id={axis: lax.rem(mine + k, n)}, device_id_type=MESH
            )
            peers += 1
    pl.semaphore_wait(barrier, peers)
    source = x_ref
    for stage, (axis, n) in enumerate(stages):
        mine = lax.axis_index(axis)
        copies = []
        for k in range(1, n):
            copy = pltpu.make_async_remote_copy(
                src_ref=source,
                dst_ref=slots[stage].at[mine],
                send_sem=sends[stage].at[k],
                recv_sem=recvs[stage].at[mine],
                device_id={axis: lax.rem(mine + k, n)},
                device_id_type=MESH,
            )
            copy.start()
            copies.append(copy)
        slots[stage][mine] = source[...]
        for k in range(1, n):
            sender = lax.rem(mine + k, n)
            pltpu.make_async_remote_copy(
                src_ref=source,
                dst_ref=slots[stage].at[sender],
                send_sem=sends[stage].at[k],
                recv_sem=recvs[stage].at[sender],
                device_id={axis: sender},
                device_id_type=MESH,
            ).wait_recv()
        for copy in copies:
            copy.wait_send()
        total = slots[stage][0]
        for j in range(1, n):
            total = total + slots[stage][j]
        if stage == count - 1:
            o_ref[...] = total
        else:
            partial[...] = total
            source = partial


def all_sum(x, axes, mesh_shape, collective):
    stages = tuple((axis, mesh_shape[axis]) for axis in axes if mesh_shape[axis] > 1)
    rows, cols = x.shape
    scratch = [pltpu.VMEM((n, rows, cols), jnp.float32) for _, n in stages]
    scratch.append(pltpu.VMEM((rows, cols), jnp.float32))
    scratch += [pltpu.SemaphoreType.DMA((n,)) for _, n in stages]
    scratch += [pltpu.SemaphoreType.DMA((n,)) for _, n in stages]
    return pl.pallas_call(
        functools.partial(_reduce_kernel, stages),
        out_shape=jax.ShapeDtypeStruct((rows, cols), jnp.float32),
        in_specs=[pl.BlockSpec(memory_space=pltpu.VMEM)],
        out_specs=pl.BlockSpec(memory_space=pltpu.VMEM),
        scratch_shapes=scratch,
        compiler_params=pltpu.CompilerParams(collective_id=collective, has_side_effects=True),
    )(x.astype(jnp.float32))


def global_sum(rows_of_sums, mesh_shape):
    count = rows_of_sums.shape[0]
    padded = jnp.zeros((8, rows_of_sums.shape[1]), jnp.float32).at[:count].set(rows_of_sums)
    return all_sum(padded, ("blk", "sec"), mesh_shape, 0)[:count]


def _doubling(n):
    distances, d = [], 1
    while d < n:
        distances.append(d)
        d *= 2
    return tuple(distances)


def _greet(n, distances):
    barrier = pltpu.get_barrier_semaphore()
    mine = lax.axis_index("sec")
    for d in distances:
        for peer in (lax.rem(mine + d, n), lax.rem(mine + n - d, n)):
            pl.semaphore_signal(barrier, inc=1, device_id={"sec": peer}, device_id_type=MESH)
    pl.semaphore_wait(barrier, 2 * len(distances))


def _hop(n, d, source, slot, send_sem, recv_sem):
    mine = lax.axis_index("sec")
    copy = pltpu.make_async_remote_copy(
        src_ref=source,
        dst_ref=slot,
        send_sem=send_sem,
        recv_sem=recv_sem,
        device_id={"sec": lax.rem(mine + d, n)},
        device_id_type=MESH,
    )
    copy.start()
    copy.wait_recv()
    copy.wait_send()


RADIX = 4


def _plan(n):
    rounds, d = [], 1
    while d < n:
        rounds.append((d, tuple(j for j in range(1, RADIX) if j * d < n)))
        d *= RADIX
    return tuple(rounds)


def _plan_peers(rounds):
    return tuple(sorted({j * d for d, js in rounds for j in js} | {1}))


def _send_all(n, sec, sources, slots, sends, recvs, flat, d, js):
    copies = []
    for i, j in enumerate(js):
        copy = pltpu.make_async_remote_copy(
            src_ref=sources,
            dst_ref=slots.at[flat + i],
            send_sem=sends.at[flat + i],
            recv_sem=recvs.at[flat + i],
            device_id={"sec": lax.rem(sec + j * d, n)},
            device_id_type=MESH,
        )
        copy.start()
        copies.append(copy)
    for copy in copies:
        copy.wait_recv()
    for copy in copies:
        copy.wait_send()


def _spread(n_sec, n_blk, offsets, piece_ref, slots, sends, recvs):
    sec, blk = lax.axis_index("sec"), lax.axis_index("blk")

    def copy(o, j, index):
        return pltpu.make_async_remote_copy(
            src_ref=piece_ref,
            dst_ref=slots.at[index],
            send_sem=sends.at[(o - 1) * n_blk + j],
            recv_sem=recvs.at[index],
            device_id={"sec": lax.rem(sec + o, n_sec), "blk": j},
            device_id_type=MESH,
        )

    outgoing = [
        copy(o, j, (o - 1) * n_blk + blk) for o in range(1, offsets + 1) for j in range(n_blk)
    ]
    for c in outgoing:
        c.start()
    for o in range(1, offsets + 1):
        for j in range(n_blk):
            copy(o, j, (o - 1) * n_blk + j).wait_recv()
    for c in outgoing:
        c.wait_send()


def _assemble(n_blk, offsets, slots, mats):
    piece = slots.shape[1]
    for o in range(offsets):
        for j in range(n_blk):
            mats[o, j * piece : (j + 1) * piece, :] = slots[o * n_blk + j]


def _greet_all(n_sec, n_blk, offsets, rounds, blk_peers):
    barrier = pltpu.get_barrier_semaphore()
    sec, blk = lax.axis_index("sec"), lax.axis_index("blk")
    count = 0
    if blk_peers:
        for k in range(1, n_blk):
            pl.semaphore_signal(
                barrier, inc=1, device_id={"blk": lax.rem(blk + k, n_blk)}, device_id_type=MESH
            )
            count += 1
    for o in range(1, offsets + 1):
        for j in range(n_blk):
            for peer in (lax.rem(sec + o, n_sec), lax.rem(sec + n_sec - o, n_sec)):
                pl.semaphore_signal(
                    barrier, inc=1, device_id={"sec": peer, "blk": j}, device_id_type=MESH
                )
                count += 1
    for d in sorted({j * d for d, js in rounds[1:] for j in js}):
        for peer in (lax.rem(sec + d, n_sec), lax.rem(sec + n_sec - d, n_sec)):
            pl.semaphore_signal(barrier, inc=1, device_id={"sec": peer}, device_id_type=MESH)
            count += 1
    pl.semaphore_wait(barrier, count)


def _maps_kernel(n, n_blk, rounds, e_ref, a_ref, eslots, emat, current, slots, esend, erecv, sends, recvs):
    sec = lax.axis_index("sec")
    first = rounds[0][1]
    offsets = len(first) + 1
    _greet_all(n, n_blk, offsets, rounds, False)
    _spread(n, n_blk, offsets, e_ref, eslots, esend, erecv)
    _assemble(n_blk, offsets, eslots, emat)
    joined = emat[0]
    for i, j in enumerate(first):
        a_ref[i] = joined
        joined = jnp.dot(
            joined, emat[j], precision=lax.Precision.HIGHEST, preferred_element_type=jnp.float32
        )
    current[...] = joined
    flat = len(first)
    for k in range(1, len(rounds)):
        d, js = rounds[k]
        onward = k < len(rounds) - 1
        if onward or len(js) > 1:
            _send_all(n, sec, current, slots, sends, recvs, flat, d, js)
        joined = current[...]
        for i, j in enumerate(js):
            a_ref[flat + i] = joined
            if onward or i < len(js) - 1:
                joined = jnp.dot(
                    joined, slots[flat + i], precision=lax.Precision.HIGHEST,
                    preferred_element_type=jnp.float32,
                )
        if onward:
            current[...] = joined
        flat += len(js)


def scan_maps(e_piece, n, n_blk):
    rounds = _plan(n)
    total = sum(len(js) for _, js in rounds)
    offsets = len(rounds[0][1]) + 1
    piece, width = e_piece.shape
    return pl.pallas_call(
        functools.partial(_maps_kernel, n, n_blk, rounds),
        out_shape=jax.ShapeDtypeStruct((total, width, width), jnp.float32),
        in_specs=[pl.BlockSpec(memory_space=pltpu.VMEM)],
        out_specs=pl.BlockSpec(memory_space=pltpu.VMEM),
        scratch_shapes=[
            pltpu.VMEM((offsets * n_blk, piece, width), jnp.float32),
            pltpu.VMEM((offsets, width, width), jnp.float32),
            pltpu.VMEM((width, width), jnp.float32),
            pltpu.VMEM((total, width, width), jnp.float32),
            pltpu.SemaphoreType.DMA((offsets * n_blk,)),
            pltpu.SemaphoreType.DMA((offsets * n_blk,)),
            pltpu.SemaphoreType.DMA((total,)),
            pltpu.SemaphoreType.DMA((total,)),
        ],
        compiler_params=pltpu.CompilerParams(collective_id=2, has_side_effects=True),
    )(e_piece)


def _gather_kernel(n, x_ref, o_ref, slots, sends, recvs):
    mine = lax.axis_index("blk")
    barrier = pltpu.get_barrier_semaphore()
    for k in range(1, n):
        pl.semaphore_signal(
            barrier, inc=1, device_id={"blk": lax.rem(mine + k, n)}, device_id_type=MESH
        )
    pl.semaphore_wait(barrier, n - 1)
    copies = []
    for k in range(1, n):
        copy = pltpu.make_async_remote_copy(
            src_ref=x_ref,
            dst_ref=slots.at[mine],
            send_sem=sends.at[k],
            recv_sem=recvs.at[mine],
            device_id={"blk": lax.rem(mine + k, n)},
            device_id_type=MESH,
        )
        copy.start()
        copies.append(copy)
    slots[mine] = x_ref[...]
    for k in range(1, n):
        sender = lax.rem(mine + k, n)
        pltpu.make_async_remote_copy(
            src_ref=x_ref,
            dst_ref=slots.at[sender],
            send_sem=sends.at[k],
            recv_sem=recvs.at[sender],
            device_id={"blk": sender},
            device_id_type=MESH,
        ).wait_recv()
    for copy in copies:
        copy.wait_send()
    width = x_ref.shape[1]
    for j in range(n):
        o_ref[:, j * width : (j + 1) * width] = slots[j]


def gather_blk(x, n):
    rows, width = x.shape
    return pl.pallas_call(
        functools.partial(_gather_kernel, n),
        out_shape=jax.ShapeDtypeStruct((rows, n * width), x.dtype),
        in_specs=[pl.BlockSpec(memory_space=pltpu.VMEM)],
        out_specs=pl.BlockSpec(memory_space=pltpu.VMEM),
        scratch_shapes=[
            pltpu.VMEM((n, rows, width), x.dtype),
            pltpu.SemaphoreType.DMA((n,)),
            pltpu.SemaphoreType.DMA((n,)),
        ],
        compiler_params=pltpu.CompilerParams(collective_id=4, has_side_effects=True),
    )(x)


def _operator_phase(n_sec, n_blk, x_ref, up_ref, piece_ref, g_ref, b_ref, a_ref, scratch):
    gslots, bslots, aslots, gsend, grecv, bsend, brecv, asend, arecv = scratch
    sec, blk = lax.axis_index("sec"), lax.axis_index("blk")
    nxt, prv = lax.rem(sec + 1, n_sec), lax.rem(sec + n_sec - 1, n_sec)
    piece = bslots.shape[1]
    copies = []
    for k in range(1, n_blk):
        copies.append(
            pltpu.make_async_remote_copy(
                src_ref=x_ref,
                dst_ref=gslots.at[blk],
                send_sem=gsend.at[k],
                recv_sem=grecv.at[blk],
                device_id={"blk": lax.rem(blk + k, n_blk)},
                device_id_type=MESH,
            )
        )
    for j in range(n_blk):
        copies.append(
            pltpu.make_async_remote_copy(
                src_ref=piece_ref,
                dst_ref=bslots.at[blk],
                send_sem=bsend.at[j],
                recv_sem=brecv.at[blk],
                device_id={"sec": nxt, "blk": j},
                device_id_type=MESH,
            )
        )
        copies.append(
            pltpu.make_async_remote_copy(
                src_ref=up_ref.at[pl.ds(j * piece, piece)],
                dst_ref=aslots.at[blk],
                send_sem=asend.at[j],
                recv_sem=arecv.at[blk],
                device_id={"sec": prv, "blk": j},
                device_id_type=MESH,
            )
        )
    for copy in copies:
        copy.start()
    gslots[blk] = x_ref[...]
    for k in range(1, n_blk):
        sender = lax.rem(blk + k, n_blk)
        pltpu.make_async_remote_copy(
            src_ref=x_ref,
            dst_ref=gslots.at[sender],
            send_sem=gsend.at[k],
            recv_sem=grecv.at[sender],
            device_id={"blk": sender},
            device_id_type=MESH,
        ).wait_recv()
    for j in range(n_blk):
        pltpu.make_async_remote_copy(
            src_ref=piece_ref,
            dst_ref=bslots.at[j],
            send_sem=bsend.at[j],
            recv_sem=brecv.at[j],
            device_id={"sec": prv, "blk": j},
            device_id_type=MESH,
        ).wait_recv()
        pltpu.make_async_remote_copy(
            src_ref=up_ref.at[pl.ds(j * piece, piece)],
            dst_ref=aslots.at[j],
            send_sem=asend.at[j],
            recv_sem=arecv.at[j],
            device_id={"sec": nxt, "blk": j},
            device_id_type=MESH,
        ).wait_recv()
    for copy in copies:
        copy.wait_send()
    width = x_ref.shape[1]
    for j in range(n_blk):
        g_ref[:, j * width : (j + 1) * width] = gslots[j]
        b_ref[j * piece : (j + 1) * piece, :] = jnp.where(
            sec >= 1, bslots[j], jnp.zeros_like(bslots[j])
        )
    total = aslots[0]
    for j in range(1, n_blk):
        total = total + aslots[j]
    a_ref[...] = jnp.where(sec <= n_sec - 2, total, jnp.zeros_like(total))


def _operator_scratch(n_blk, rows, width, dtype, piece, cases):
    return [
        pltpu.VMEM((n_blk, rows, width), dtype),
        pltpu.VMEM((n_blk, piece, cases), jnp.float32),
        pltpu.VMEM((n_blk, piece, cases), jnp.float32),
    ] + [pltpu.SemaphoreType.DMA((n_blk,))] * 6


def _operator_kernel(n_sec, n_blk, x_ref, up_ref, be_ref, g_ref, b_ref, a_ref, *scratch):
    sec, blk = lax.axis_index("sec"), lax.axis_index("blk")
    nxt, prv = lax.rem(sec + 1, n_sec), lax.rem(sec + n_sec - 1, n_sec)
    piece = scratch[1].shape[1]
    barrier = pltpu.get_barrier_semaphore()
    for k in range(1, n_blk):
        pl.semaphore_signal(
            barrier, inc=1, device_id={"blk": lax.rem(blk + k, n_blk)}, device_id_type=MESH
        )
    for j in range(n_blk):
        for other in (nxt, prv):
            pl.semaphore_signal(
                barrier, inc=1, device_id={"sec": other, "blk": j}, device_id_type=MESH
            )
    pl.semaphore_wait(barrier, 3 * n_blk - 1)
    mine = be_ref.at[pl.ds(pl.multiple_of(blk * piece, 8), piece)]
    _operator_phase(n_sec, n_blk, x_ref, up_ref, mine, g_ref, b_ref, a_ref, scratch)


def operator_exchange(x, up_t, be_t, n_sec, n_blk):
    rows, width = x.shape
    panel, cases = up_t.shape
    piece = panel // n_blk
    return pl.pallas_call(
        functools.partial(_operator_kernel, n_sec, n_blk),
        out_shape=(
            jax.ShapeDtypeStruct((rows, n_blk * width), x.dtype),
            jax.ShapeDtypeStruct((panel, cases), jnp.float32),
            jax.ShapeDtypeStruct((piece, cases), jnp.float32),
        ),
        in_specs=[pl.BlockSpec(memory_space=pltpu.VMEM)] * 3,
        out_specs=[pl.BlockSpec(memory_space=pltpu.VMEM)] * 3,
        scratch_shapes=_operator_scratch(n_blk, rows, width, x.dtype, piece, cases),
        compiler_params=pltpu.CompilerParams(collective_id=5, has_side_effects=True),
    )(x, up_t, be_t)


def _precondition_kernel(
    n_sec, n_blk, rounds, x_ref, inv_ref, pick_ref, u_ref, gain_ref, ahead_ref,
    d_ref, g_ref, b_ref, a_ref, *scratch
):
    gslots, fpiece, fslots, fmat, carry, slots, gsend, grecv, fsend, frecv, ssend, srecv = scratch[:12]
    rounded, upward, own_piece = scratch[12:15]
    phase_scratch = scratch[15:]
    sec, blk = lax.axis_index("sec"), lax.axis_index("blk")
    first = rounds[0][1]
    offsets = len(first) + 1
    _greet_all(n_sec, n_blk, offsets, rounds, True)

    def blk_copy(k, target, slot):
        return pltpu.make_async_remote_copy(
            src_ref=x_ref,
            dst_ref=gslots.at[slot],
            send_sem=gsend.at[k],
            recv_sem=grecv.at[slot],
            device_id={"blk": target},
            device_id_type=MESH,
        )

    outgoing = [blk_copy(k, lax.rem(blk + k, n_blk), blk) for k in range(1, n_blk)]
    for copy in outgoing:
        copy.start()
    gslots[blk] = x_ref[...]
    for k in range(1, n_blk):
        sender = lax.rem(blk + k, n_blk)
        blk_copy(k, sender, sender).wait_recv()
    for copy in outgoing:
        copy.wait_send()
    width = x_ref.shape[1]
    contract = (((1,), (1,)), ((), ()))
    folded = lax.dot_general(
        gslots[0], inv_ref[:, 0:width], contract, preferred_element_type=jnp.float32
    )
    for j in range(1, n_blk):
        folded = folded + lax.dot_general(
            gslots[j],
            inv_ref[:, j * width : (j + 1) * width],
            contract,
            preferred_element_type=jnp.float32,
        )
    fpiece[...] = lax.dot_general(
        pick_ref[...], folded, contract, precision=lax.Precision.HIGHEST,
        preferred_element_type=jnp.float32,
    )
    _spread(n_sec, n_blk, offsets, fpiece, fslots, fsend, frecv)
    _assemble(n_blk, offsets, fslots, fmat)
    joined = jnp.where(sec >= 1, fmat[0], jnp.zeros_like(fmat[0]))
    for i, j in enumerate(first):
        term = jnp.dot(
            u_ref[i], fmat[j], precision=lax.Precision.HIGHEST, preferred_element_type=jnp.float32
        )
        joined = joined + jnp.where(sec >= j + 1, term, jnp.zeros_like(term))
    carry[1] = joined
    flat = len(first)
    for k in range(1, len(rounds)):
        d, js = rounds[k]
        _send_all(n_sec, sec, carry.at[k], slots, ssend, srecv, flat, d, js)
        joined = carry[k]
        for i, j in enumerate(js):
            term = jnp.dot(
                u_ref[flat + i], slots[flat + i], precision=lax.Precision.HIGHEST,
                preferred_element_type=jnp.float32,
            )
            joined = joined + jnp.where(sec >= j * d, term, jnp.zeros_like(term))
        carry[k + 1] = joined
        flat += len(js)
    before = carry[len(rounds)].T
    direction = folded - lax.dot_general(
        before, gain_ref[...], contract, precision=lax.Precision.HIGHEST,
        preferred_element_type=jnp.float32,
    )
    d_ref[...] = direction
    rounded[...] = direction.astype(rounded.dtype)
    upward[...] = jnp.dot(
        rounded[...], ahead_ref[...], preferred_element_type=jnp.float32
    ).T
    own_piece[...] = lax.dot_general(
        pick_ref[...], rounded[...].astype(jnp.float32), contract,
        precision=lax.Precision.HIGHEST, preferred_element_type=jnp.float32,
    )
    _operator_phase(n_sec, n_blk, rounded, upward, own_piece, g_ref, b_ref, a_ref, phase_scratch)


def precondition_sweep(x, inverse, picks, chain, gain, ahead, n_sec, n_blk):
    cases, width = x.shape
    piece, _ = picks.shape
    panel = piece * n_blk
    plan = _plan(n_sec)
    rounds = len(plan)
    total = sum(len(js) for _, js in plan)
    offsets = len(plan[0][1]) + 1
    return pl.pallas_call(
        functools.partial(_precondition_kernel, n_sec, n_blk, plan),
        out_shape=(
            jax.ShapeDtypeStruct((cases, width), jnp.float32),
            jax.ShapeDtypeStruct((cases, n_blk * width), x.dtype),
            jax.ShapeDtypeStruct((panel, cases), jnp.float32),
            jax.ShapeDtypeStruct((piece, cases), jnp.float32),
        ),
        in_specs=[pl.BlockSpec(memory_space=pltpu.VMEM)] * 6,
        out_specs=[pl.BlockSpec(memory_space=pltpu.VMEM)] * 4,
        scratch_shapes=[
            pltpu.VMEM((n_blk, cases, width), x.dtype),
            pltpu.VMEM((piece, cases), jnp.float32),
            pltpu.VMEM((offsets * n_blk, piece, cases), jnp.float32),
            pltpu.VMEM((offsets, panel, cases), jnp.float32),
            pltpu.VMEM((rounds + 1, panel, cases), jnp.float32),
            pltpu.VMEM((total, panel, cases), jnp.float32),
            pltpu.SemaphoreType.DMA((n_blk,)),
            pltpu.SemaphoreType.DMA((n_blk,)),
            pltpu.SemaphoreType.DMA((offsets * n_blk,)),
            pltpu.SemaphoreType.DMA((offsets * n_blk,)),
            pltpu.SemaphoreType.DMA((total,)),
            pltpu.SemaphoreType.DMA((total,)),
            pltpu.VMEM((cases, width), x.dtype),
            pltpu.VMEM((panel, cases), jnp.float32),
            pltpu.VMEM((piece, cases), jnp.float32),
        ]
        + _operator_scratch(n_blk, cases, width, x.dtype, piece, cases),
        compiler_params=pltpu.CompilerParams(collective_id=6, has_side_effects=True),
    )(x, inverse, picks, chain, gain, ahead)


def _exchange_sum(stages, source, slots, partial, sends, recvs, out):
    count = len(stages)
    for stage, (axis, n) in enumerate(stages):
        mine = lax.axis_index(axis)
        copies = []
        for k in range(1, n):
            copy = pltpu.make_async_remote_copy(
                src_ref=source,
                dst_ref=slots[stage].at[mine],
                send_sem=sends[stage].at[k],
                recv_sem=recvs[stage].at[mine],
                device_id={axis: lax.rem(mine + k, n)},
                device_id_type=MESH,
            )
            copy.start()
            copies.append(copy)
        slots[stage][mine] = source[...]
        for k in range(1, n):
            sender = lax.rem(mine + k, n)
            pltpu.make_async_remote_copy(
                src_ref=source,
                dst_ref=slots[stage].at[sender],
                send_sem=sends[stage].at[k],
                recv_sem=recvs[stage].at[sender],
                device_id={axis: sender},
                device_id_type=MESH,
            ).wait_recv()
        for copy in copies:
            copy.wait_send()
        total = slots[stage][0]
        for j in range(1, n):
            total = total + slots[stage][j]
        if stage == count - 1:
            out[...] = total
        else:
            partial[...] = total
            source = partial


def _project_kernel(stages, depth, basis_ref, image_ref, h_ref, next_ref, *scratch):
    count = len(stages)
    first, second = scratch[: 3 * count + 1], scratch[3 * count + 1 : 6 * count + 2]
    rows, work = scratch[6 * count + 2 :]
    barrier = pltpu.get_barrier_semaphore()
    peers = 0
    for axis, n in stages:
        mine = lax.axis_index(axis)
        for k in range(1, n):
            pl.semaphore_signal(
                barrier, inc=1, device_id={axis: lax.rem(mine + k, n)}, device_id_type=MESH
            )
            peers += 1
    pl.semaphore_wait(barrier, peers)
    highest = lax.Precision.HIGHEST
    contract = (((1,), (1,)), ((), ()))
    image = image_ref[...]
    ones = jnp.ones((8, image.shape[1]), jnp.float32)
    eye = (
        lax.broadcasted_iota(jnp.int32, (image.shape[0],) * 2, 0)
        == lax.broadcasted_iota(jnp.int32, (image.shape[0],) * 2, 1)
    ).astype(jnp.float32)
    rows[...] = jnp.zeros_like(rows)
    for i in range(depth):
        summed = lax.dot_general(
            ones, image * basis_ref[i], contract, precision=highest,
            preferred_element_type=jnp.float32,
        )
        rows[i : i + 1, :] = summed[0:1, :]

    def run(buffers, source, out):
        slots = buffers[:count]
        partial = buffers[count]
        sends = buffers[count + 1 : 2 * count + 1]
        recvs = buffers[2 * count + 1 :]
        _exchange_sum(stages, source, slots, partial, sends, recvs, out)

    run(first, rows, h_ref)
    columns = lax.dot_general(
        eye, h_ref[...], contract, precision=highest, preferred_element_type=jnp.float32
    )
    for i in range(depth):
        image = image - columns[:, i : i + 1] * basis_ref[i]
    work[...] = lax.dot_general(
        ones, image * image, contract, precision=highest, preferred_element_type=jnp.float32
    )
    run(second, work, rows)
    length = jnp.sqrt(rows[...] + epsilon)
    h_ref[depth : depth + 1, :] = length[0:1, :]
    scale = lax.dot_general(
        eye, length, contract, precision=highest, preferred_element_type=jnp.float32
    )
    next_ref[...] = image / scale[:, 0:1]


def project(stacked, image, mesh_shape):
    depth, cases, width = stacked.shape
    stages = tuple((axis, mesh_shape[axis]) for axis in ("blk", "sec") if mesh_shape[axis] > 1)

    def buffers():
        out = [pltpu.VMEM((n, 8, cases), jnp.float32) for _, n in stages]
        out.append(pltpu.VMEM((8, cases), jnp.float32))
        out += [pltpu.SemaphoreType.DMA((n,)) for _, n in stages]
        out += [pltpu.SemaphoreType.DMA((n,)) for _, n in stages]
        return out

    return pl.pallas_call(
        functools.partial(_project_kernel, stages, depth),
        out_shape=(
            jax.ShapeDtypeStruct((8, cases), jnp.float32),
            jax.ShapeDtypeStruct((cases, width), jnp.float32),
        ),
        in_specs=[pl.BlockSpec(memory_space=pltpu.VMEM)] * 2,
        out_specs=[pl.BlockSpec(memory_space=pltpu.VMEM)] * 2,
        scratch_shapes=buffers()
        + buffers()
        + [pltpu.VMEM((8, cases), jnp.float32), pltpu.VMEM((8, cases), jnp.float32)],
        compiler_params=pltpu.CompilerParams(collective_id=6 + depth, has_side_effects=True),
    )(stacked, image)


def least_squares(hessen, beta):
    cases = hessen.shape[0]
    depth = hessen.shape[2]
    rhs = jnp.zeros((cases, depth + 1), jnp.float32).at[:, 0].set(beta)
    upper = hessen
    for column in range(depth):
        upper_row = upper[:, column, :]
        lower_row = upper[:, column + 1, :]
        radius = jnp.sqrt(upper_row[:, column] ** 2 + lower_row[:, column] ** 2)
        cosine = upper_row[:, column] / radius
        sine_term = lower_row[:, column] / radius
        upper = upper.at[:, column, :].set(
            cosine[:, None] * upper_row + sine_term[:, None] * lower_row
        )
        upper = upper.at[:, column + 1, :].set(
            -sine_term[:, None] * upper_row + cosine[:, None] * lower_row
        )
        first_rhs = rhs[:, column]
        second_rhs = rhs[:, column + 1]
        rhs = rhs.at[:, column].set(cosine * first_rhs + sine_term * second_rhs)
        rhs = rhs.at[:, column + 1].set(-sine_term * first_rhs + cosine * second_rhs)
    weights = jnp.zeros((cases, depth), jnp.float32)
    for column in reversed(range(depth)):
        remain = rhs[:, column] - jnp.sum(
            upper[:, column, column + 1 :] * weights[:, column + 1 :], axis=1
        )
        weights = weights.at[:, column].set(remain / upper[:, column, column])
    return weights


def local(
    mesh_shape,
    state_now, source, fan_gain, section_block, block_inverse, back_panel, ahead_panel, interface
):
    highest = lax.Precision.HIGHEST
    cases, node_rows = state_now.shape
    panel_width = back_panel.shape[1]
    indices = interface[0]
    first_row = lax.axis_index("blk") * node_rows
    selector = (indices[None, :] == first_row + jnp.arange(node_rows)[:, None]).astype(jnp.float32)
    contract = (((1,), (1,)), ((), ()))
    gain_panel = jnp.dot(
        block_inverse,
        lax.all_gather(back_panel, "blk", axis=0, tiled=True),
        preferred_element_type=jnp.float32,
    )

    own_piece = panel_width // mesh_shape["blk"]
    own_picks = lax.dynamic_slice_in_dim(selector, lax.axis_index("blk") * own_piece, own_piece, 1).T
    own_maps = -jnp.dot(own_picks, gain_panel, precision=highest)
    chain = scan_maps(own_maps, mesh_shape["sec"], mesh_shape["blk"])

    def section_terms(dense_part, behind_vals, piece):
        width = piece.shape[1]
        dense_part = lax.dot_general(
            piece, section_block, contract, preferred_element_type=jnp.float32
        )
        picker = (indices[None, :] == jnp.arange(width)[:, None]).astype(jnp.bfloat16)
        behind_vals = jnp.dot(piece, picker, preferred_element_type=jnp.float32)
        return (dense_part, behind_vals)

    def fold_section(carry, piece):
        return section_terms(carry[0], carry[1], piece)

    n_sec, n_blk = mesh_shape["sec"], mesh_shape["blk"]
    piece = panel_width // n_blk
    local_picks = lax.dynamic_slice_in_dim(selector, lax.axis_index("blk") * piece, piece, 1)

    def finish(gathered, behind_t, ahead_piece):
        dense_part = lax.dot_general(
            gathered, section_block, contract, preferred_element_type=jnp.float32
        )
        lower_term = lax.dot_general(
            behind_t.astype(jnp.bfloat16),
            back_panel,
            (((0,), (1,)), ((), ())),
            preferred_element_type=jnp.float32,
        )
        upper_term = lax.dot_general(
            ahead_piece, local_picks, (((0,), (1,)), ((), ())), precision=highest
        )
        return dense_part + lower_term + upper_term

    def operator(vector):
        rounded = vector.astype(jnp.bfloat16)
        up_t = lax.dot_general(
            ahead_panel, rounded, (((0,), (1,)), ((), ())), preferred_element_type=jnp.float32
        )
        be_t = lax.dot_general(
            selector.astype(jnp.bfloat16),
            rounded,
            (((0,), (1,)), ((), ())),
            preferred_element_type=jnp.float32,
        )
        return finish(*operator_exchange(rounded, up_t, be_t, n_sec, n_blk))

    def compose(earlier, later):
        first_map, first_value = earlier
        second_map, second_value = later
        joined_map = jnp.dot(second_map, first_map, precision=highest)
        joined_value = jnp.dot(first_value, second_map.T, precision=highest) + second_value
        return (joined_map, joined_value)

    def lengths(vector):
        return jnp.sqrt(global_sum(jnp.sum(vector * vector, axis=1)[None], mesh_shape)[0] + epsilon)

    bent = jnp.tanh(state_now)
    residual = source - operator(state_now) - fan_gain[None, :] * bent
    jac_diag = fan_gain[None, :] * (1.0 - bent * bent)
    beta = lengths(residual)
    basis = [residual / beta[:, None]]
    directions = []
    hessen = jnp.zeros((cases, KRYLOV + 1, KRYLOV), jnp.float32)
    for column in range(KRYLOV):
        precondition_rounded = basis[column].astype(jnp.bfloat16)
        direction, gathered, behind_t, ahead_piece = precondition_sweep(
            precondition_rounded, block_inverse, own_picks, chain, gain_panel, ahead_panel,
            n_sec, n_blk,
        )
        product = finish(gathered, behind_t, ahead_piece) + jac_diag * direction
        stacked = jnp.stack(basis)
        sums, following = project(stacked, product, mesh_shape)
        hessen = hessen.at[:, : column + 2, column].set(sums[: column + 2].T)
        basis.append(following)
        directions.append(direction)
    weights = least_squares(hessen, beta)
    update = jnp.zeros_like(state_now)
    for column in range(KRYLOV):
        update = update + weights[:, column : column + 1] * directions[column]
    return state_now + update


def solution(mesh):
    in_specs = (
        P(None, ("sec", "blk")),
        P(None, ("sec", "blk")),
        P(("sec", "blk")),
        P(("sec", "blk"), None),
        P(("sec", "blk"), None),
        P(("sec", "blk"), None),
        P(("sec", "blk"), None),
        P("sec", None),
    )
    out_specs = P(None, ("sec", "blk"))
    return jax.shard_map(functools.partial(local, dict(mesh.shape)), mesh=mesh, in_specs=in_specs, out_specs=out_specs, check_vma=False)
```

```python
import functools

import jax
import jax.numpy as jnp
from jax import lax
from jax.experimental import pallas as pl
from jax.experimental.pallas import tpu as pltpu
from jax.sharding import PartitionSpec as P

MESH = pl.DeviceIdType.MESH

KRYLOV = 3


epsilon = 1e-06


def extended(x, sides, width):
    for axis, dim in sides:
        size, length = (lax.axis_size(axis), x.shape[dim])
        up = [(i, (i + 1) % size) for i in range(size - 1)]
        down = [(j, i) for i, j in up]
        last = lax.slice_in_dim(x, length - width, length, axis=dim)
        first = lax.slice_in_dim(x, 0, width, axis=dim)
        before = lax.ppermute(last, axis, up)
        after = lax.ppermute(first, axis, down)
        x = jnp.concatenate([before, x, after], axis=dim)
    return x


def entering(value, axis, join, neutral):
    count, mine = (lax.axis_size(axis), lax.axis_index(axis))
    pieces = jax.tree.map(lambda part: lax.all_gather(part, axis), value)
    so_far = jax.tree.map(
        lambda part, zero: jnp.full_like(part, 0) + jnp.asarray(zero, part.dtype), value, neutral
    )

    def step(position, so_far):
        longer = join(so_far, jax.tree.map(lambda part: part[position], pieces))
        return jax.tree.map(lambda new, old: jnp.where(position < mine, new, old), longer, so_far)

    return lax.fori_loop(0, count - 1, step, so_far)


def _reduce_kernel(stages, x_ref, o_ref, *scratch):
    count = len(stages)
    slots = scratch[:count]
    partial = scratch[count]
    sends = scratch[count + 1 : 2 * count + 1]
    recvs = scratch[2 * count + 1 :]
    barrier = pltpu.get_barrier_semaphore()
    peers = 0
    for axis, n in stages:
        mine = lax.axis_index(axis)
        for k in range(1, n):
            pl.semaphore_signal(
                barrier, inc=1, device_id={axis: lax.rem(mine + k, n)}, device_id_type=MESH
            )
            peers += 1
    pl.semaphore_wait(barrier, peers)
    source = x_ref
    for stage, (axis, n) in enumerate(stages):
        mine = lax.axis_index(axis)
        copies = []
        for k in range(1, n):
            copy = pltpu.make_async_remote_copy(
                src_ref=source,
                dst_ref=slots[stage].at[mine],
                send_sem=sends[stage].at[k],
                recv_sem=recvs[stage].at[mine],
                device_id={axis: lax.rem(mine + k, n)},
                device_id_type=MESH,
            )
            copy.start()
            copies.append(copy)
        slots[stage][mine] = source[...]
        for k in range(1, n):
            sender = lax.rem(mine + k, n)
            pltpu.make_async_remote_copy(
                src_ref=source,
                dst_ref=slots[stage].at[sender],
                send_sem=sends[stage].at[k],
                recv_sem=recvs[stage].at[sender],
                device_id={axis: sender},
                device_id_type=MESH,
            ).wait_recv()
        for copy in copies:
            copy.wait_send()
        total = slots[stage][0]
        for j in range(1, n):
            total = total + slots[stage][j]
        if stage == count - 1:
            o_ref[...] = total
        else:
            partial[...] = total
            source = partial


def all_sum(x, axes, mesh_shape, collective):
    stages = tuple((axis, mesh_shape[axis]) for axis in axes if mesh_shape[axis] > 1)
    rows, cols = x.shape
    scratch = [pltpu.VMEM((n, rows, cols), jnp.float32) for _, n in stages]
    scratch.append(pltpu.VMEM((rows, cols), jnp.float32))
    scratch += [pltpu.SemaphoreType.DMA((n,)) for _, n in stages]
    scratch += [pltpu.SemaphoreType.DMA((n,)) for _, n in stages]
    return pl.pallas_call(
        functools.partial(_reduce_kernel, stages),
        out_shape=jax.ShapeDtypeStruct((rows, cols), jnp.float32),
        in_specs=[pl.BlockSpec(memory_space=pltpu.VMEM)],
        out_specs=pl.BlockSpec(memory_space=pltpu.VMEM),
        scratch_shapes=scratch,
        compiler_params=pltpu.CompilerParams(collective_id=collective, has_side_effects=True),
    )(x.astype(jnp.float32))


def global_sum(rows_of_sums, mesh_shape):
    count = rows_of_sums.shape[0]
    padded = jnp.zeros((8, rows_of_sums.shape[1]), jnp.float32).at[:count].set(rows_of_sums)
    return all_sum(padded, ("blk", "sec"), mesh_shape, 0)[:count]


def _doubling(n):
    distances, d = [], 1
    while d < n:
        distances.append(d)
        d *= 2
    return tuple(distances)


def _greet(n, distances):
    barrier = pltpu.get_barrier_semaphore()
    mine = lax.axis_index("sec")
    for d in distances:
        for peer in (lax.rem(mine + d, n), lax.rem(mine + n - d, n)):
            pl.semaphore_signal(barrier, inc=1, device_id={"sec": peer}, device_id_type=MESH)
    pl.semaphore_wait(barrier, 2 * len(distances))


def _hop(n, d, source, slot, send_sem, recv_sem):
    mine = lax.axis_index("sec")
    copy = pltpu.make_async_remote_copy(
        src_ref=source,
        dst_ref=slot,
        send_sem=send_sem,
        recv_sem=recv_sem,
        device_id={"sec": lax.rem(mine + d, n)},
        device_id_type=MESH,
    )
    copy.start()
    copy.wait_recv()
    copy.wait_send()


RADIX = 4


def _plan(n):
    rounds, d = [], 1
    while d < n:
        rounds.append((d, tuple(j for j in range(1, RADIX) if j * d < n)))
        d *= RADIX
    return tuple(rounds)


def _plan_peers(rounds):
    return tuple(sorted({j * d for d, js in rounds for j in js} | {1}))


def _send_all(n, sec, sources, slots, sends, recvs, flat, d, js):
    copies = []
    for i, j in enumerate(js):
        copy = pltpu.make_async_remote_copy(
            src_ref=sources,
            dst_ref=slots.at[flat + i],
            send_sem=sends.at[flat + i],
            recv_sem=recvs.at[flat + i],
            device_id={"sec": lax.rem(sec + j * d, n)},
            device_id_type=MESH,
        )
        copy.start()
        copies.append(copy)
    for copy in copies:
        copy.wait_recv()
    for copy in copies:
        copy.wait_send()


def _spread(n_sec, n_blk, offsets, piece_ref, slots, sends, recvs):
    sec, blk = lax.axis_index("sec"), lax.axis_index("blk")

    def copy(o, j, index):
        return pltpu.make_async_remote_copy(
            src_ref=piece_ref,
            dst_ref=slots.at[index],
            send_sem=sends.at[(o - 1) * n_blk + j],
            recv_sem=recvs.at[index],
            device_id={"sec": lax.rem(sec + o, n_sec), "blk": j},
            device_id_type=MESH,
        )

    outgoing = [
        copy(o, j, (o - 1) * n_blk + blk) for o in range(1, offsets + 1) for j in range(n_blk)
    ]
    for c in outgoing:
        c.start()
    for o in range(1, offsets + 1):
        for j in range(n_blk):
            copy(o, j, (o - 1) * n_blk + j).wait_recv()
    for c in outgoing:
        c.wait_send()


def _assemble(n_blk, offsets, slots, mats):
    piece = slots.shape[1]
    for o in range(offsets):
        for j in range(n_blk):
            mats[o, j * piece : (j + 1) * piece, :] = slots[o * n_blk + j]


def _greet_all(n_sec, n_blk, offsets, rounds, blk_peers, stages=()):
    barrier = pltpu.get_barrier_semaphore()
    sec, blk = lax.axis_index("sec"), lax.axis_index("blk")
    count = _signal_stages(barrier, stages)
    if blk_peers:
        for k in range(1, n_blk):
            pl.semaphore_signal(
                barrier, inc=1, device_id={"blk": lax.rem(blk + k, n_blk)}, device_id_type=MESH
            )
            count += 1
    for o in range(1, offsets + 1):
        for j in range(n_blk):
            for peer in (lax.rem(sec + o, n_sec), lax.rem(sec + n_sec - o, n_sec)):
                pl.semaphore_signal(
                    barrier, inc=1, device_id={"sec": peer, "blk": j}, device_id_type=MESH
                )
                count += 1
    for d in sorted({j * d for d, js in rounds[1:] for j in js}):
        for peer in (lax.rem(sec + d, n_sec), lax.rem(sec + n_sec - d, n_sec)):
            pl.semaphore_signal(barrier, inc=1, device_id={"sec": peer}, device_id_type=MESH)
            count += 1
    pl.semaphore_wait(barrier, count)


def _maps_kernel(n, n_blk, rounds, e_ref, a_ref, eslots, emat, current, slots, esend, erecv, sends, recvs):
    sec = lax.axis_index("sec")
    first = rounds[0][1]
    offsets = len(first) + 1
    _greet_all(n, n_blk, offsets, rounds, False)
    _spread(n, n_blk, offsets, e_ref, eslots, esend, erecv)
    _assemble(n_blk, offsets, eslots, emat)
    joined = emat[0]
    for i, j in enumerate(first):
        a_ref[i] = joined
        joined = jnp.dot(
            joined, emat[j], precision=lax.Precision.HIGHEST, preferred_element_type=jnp.float32
        )
    current[...] = joined
    flat = len(first)
    for k in range(1, len(rounds)):
        d, js = rounds[k]
        onward = k < len(rounds) - 1
        if onward or len(js) > 1:
            _send_all(n, sec, current, slots, sends, recvs, flat, d, js)
        joined = current[...]
        for i, j in enumerate(js):
            a_ref[flat + i] = joined
            if onward or i < len(js) - 1:
                joined = jnp.dot(
                    joined, slots[flat + i], precision=lax.Precision.HIGHEST,
                    preferred_element_type=jnp.float32,
                )
        if onward:
            current[...] = joined
        flat += len(js)


def scan_maps(e_piece, n, n_blk):
    rounds = _plan(n)
    total = sum(len(js) for _, js in rounds)
    offsets = len(rounds[0][1]) + 1
    piece, width = e_piece.shape
    return pl.pallas_call(
        functools.partial(_maps_kernel, n, n_blk, rounds),
        out_shape=jax.ShapeDtypeStruct((total, width, width), jnp.float32),
        in_specs=[pl.BlockSpec(memory_space=pltpu.VMEM)],
        out_specs=pl.BlockSpec(memory_space=pltpu.VMEM),
        scratch_shapes=[
            pltpu.VMEM((offsets * n_blk, piece, width), jnp.float32),
            pltpu.VMEM((offsets, width, width), jnp.float32),
            pltpu.VMEM((width, width), jnp.float32),
            pltpu.VMEM((total, width, width), jnp.float32),
            pltpu.SemaphoreType.DMA((offsets * n_blk,)),
            pltpu.SemaphoreType.DMA((offsets * n_blk,)),
            pltpu.SemaphoreType.DMA((total,)),
            pltpu.SemaphoreType.DMA((total,)),
        ],
        compiler_params=pltpu.CompilerParams(collective_id=2, has_side_effects=True),
    )(e_piece)


def _gather_kernel(n, x_ref, o_ref, slots, sends, recvs):
    mine = lax.axis_index("blk")
    barrier = pltpu.get_barrier_semaphore()
    for k in range(1, n):
        pl.semaphore_signal(
            barrier, inc=1, device_id={"blk": lax.rem(mine + k, n)}, device_id_type=MESH
        )
    pl.semaphore_wait(barrier, n - 1)
    copies = []
    for k in range(1, n):
        copy = pltpu.make_async_remote_copy(
            src_ref=x_ref,
            dst_ref=slots.at[mine],
            send_sem=sends.at[k],
            recv_sem=recvs.at[mine],
            device_id={"blk": lax.rem(mine + k, n)},
            device_id_type=MESH,
        )
        copy.start()
        copies.append(copy)
    slots[mine] = x_ref[...]
    for k in range(1, n):
        sender = lax.rem(mine + k, n)
        pltpu.make_async_remote_copy(
            src_ref=x_ref,
            dst_ref=slots.at[sender],
            send_sem=sends.at[k],
            recv_sem=recvs.at[sender],
            device_id={"blk": sender},
            device_id_type=MESH,
        ).wait_recv()
    for copy in copies:
        copy.wait_send()
    width = x_ref.shape[1]
    for j in range(n):
        o_ref[:, j * width : (j + 1) * width] = slots[j]


def gather_blk(x, n):
    rows, width = x.shape
    return pl.pallas_call(
        functools.partial(_gather_kernel, n),
        out_shape=jax.ShapeDtypeStruct((rows, n * width), x.dtype),
        in_specs=[pl.BlockSpec(memory_space=pltpu.VMEM)],
        out_specs=pl.BlockSpec(memory_space=pltpu.VMEM),
        scratch_shapes=[
            pltpu.VMEM((n, rows, width), x.dtype),
            pltpu.SemaphoreType.DMA((n,)),
            pltpu.SemaphoreType.DMA((n,)),
        ],
        compiler_params=pltpu.CompilerParams(collective_id=4, has_side_effects=True),
    )(x)


def _operator_phase(n_sec, n_blk, x_ref, up_ref, piece_ref, g_ref, b_ref, a_ref, scratch):
    gslots, bslots, aslots, gsend, grecv, bsend, brecv, asend, arecv = scratch
    sec, blk = lax.axis_index("sec"), lax.axis_index("blk")
    nxt, prv = lax.rem(sec + 1, n_sec), lax.rem(sec + n_sec - 1, n_sec)
    piece = bslots.shape[1]
    copies = []
    for k in range(1, n_blk):
        copies.append(
            pltpu.make_async_remote_copy(
                src_ref=x_ref,
                dst_ref=gslots.at[blk],
                send_sem=gsend.at[k],
                recv_sem=grecv.at[blk],
                device_id={"blk": lax.rem(blk + k, n_blk)},
                device_id_type=MESH,
            )
        )
    for j in range(n_blk):
        copies.append(
            pltpu.make_async_remote_copy(
                src_ref=piece_ref,
                dst_ref=bslots.at[blk],
                send_sem=bsend.at[j],
                recv_sem=brecv.at[blk],
                device_id={"sec": nxt, "blk": j},
                device_id_type=MESH,
            )
        )
        copies.append(
            pltpu.make_async_remote_copy(
                src_ref=up_ref.at[pl.ds(j * piece, piece)],
                dst_ref=aslots.at[blk],
                send_sem=asend.at[j],
                recv_sem=arecv.at[blk],
                device_id={"sec": prv, "blk": j},
                device_id_type=MESH,
            )
        )
    for copy in copies:
        copy.start()
    gslots[blk] = x_ref[...]
    for k in range(1, n_blk):
        sender = lax.rem(blk + k, n_blk)
        pltpu.make_async_remote_copy(
            src_ref=x_ref,
            dst_ref=gslots.at[sender],
            send_sem=gsend.at[k],
            recv_sem=grecv.at[sender],
            device_id={"blk": sender},
            device_id_type=MESH,
        ).wait_recv()
    for j in range(n_blk):
        pltpu.make_async_remote_copy(
            src_ref=piece_ref,
            dst_ref=bslots.at[j],
            send_sem=bsend.at[j],
            recv_sem=brecv.at[j],
            device_id={"sec": prv, "blk": j},
            device_id_type=MESH,
        ).wait_recv()
        pltpu.make_async_remote_copy(
            src_ref=up_ref.at[pl.ds(j * piece, piece)],
            dst_ref=aslots.at[j],
            send_sem=asend.at[j],
            recv_sem=arecv.at[j],
            device_id={"sec": nxt, "blk": j},
            device_id_type=MESH,
        ).wait_recv()
    for copy in copies:
        copy.wait_send()
    width = x_ref.shape[1]
    for j in range(n_blk):
        g_ref[:, j * width : (j + 1) * width] = gslots[j]
        b_ref[j * piece : (j + 1) * piece, :] = jnp.where(
            sec >= 1, bslots[j], jnp.zeros_like(bslots[j])
        )
    total = aslots[0]
    for j in range(1, n_blk):
        total = total + aslots[j]
    a_ref[...] = jnp.where(sec <= n_sec - 2, total, jnp.zeros_like(total))


def _operator_scratch(n_blk, rows, width, dtype, piece, cases):
    return [
        pltpu.VMEM((n_blk, rows, width), dtype),
        pltpu.VMEM((n_blk, piece, cases), jnp.float32),
        pltpu.VMEM((n_blk, piece, cases), jnp.float32),
    ] + [pltpu.SemaphoreType.DMA((n_blk,))] * 6


def _operator_kernel(n_sec, n_blk, x_ref, up_ref, be_ref, g_ref, b_ref, a_ref, *scratch):
    sec, blk = lax.axis_index("sec"), lax.axis_index("blk")
    nxt, prv = lax.rem(sec + 1, n_sec), lax.rem(sec + n_sec - 1, n_sec)
    piece = scratch[1].shape[1]
    barrier = pltpu.get_barrier_semaphore()
    for k in range(1, n_blk):
        pl.semaphore_signal(
            barrier, inc=1, device_id={"blk": lax.rem(blk + k, n_blk)}, device_id_type=MESH
        )
    for j in range(n_blk):
        for other in (nxt, prv):
            pl.semaphore_signal(
                barrier, inc=1, device_id={"sec": other, "blk": j}, device_id_type=MESH
            )
    pl.semaphore_wait(barrier, 3 * n_blk - 1)
    mine = be_ref.at[pl.ds(pl.multiple_of(blk * piece, 8), piece)]
    _operator_phase(n_sec, n_blk, x_ref, up_ref, mine, g_ref, b_ref, a_ref, scratch)


def operator_exchange(x, up_t, be_t, n_sec, n_blk):
    rows, width = x.shape
    panel, cases = up_t.shape
    piece = panel // n_blk
    return pl.pallas_call(
        functools.partial(_operator_kernel, n_sec, n_blk),
        out_shape=(
            jax.ShapeDtypeStruct((rows, n_blk * width), x.dtype),
            jax.ShapeDtypeStruct((panel, cases), jnp.float32),
            jax.ShapeDtypeStruct((piece, cases), jnp.float32),
        ),
        in_specs=[pl.BlockSpec(memory_space=pltpu.VMEM)] * 3,
        out_specs=[pl.BlockSpec(memory_space=pltpu.VMEM)] * 3,
        scratch_shapes=_operator_scratch(n_blk, rows, width, x.dtype, piece, cases),
        compiler_params=pltpu.CompilerParams(collective_id=5, has_side_effects=True),
    )(x, up_t, be_t)


def _precondition_kernel(
    n_sec, n_blk, rounds, stages, depth, basis_ref, image_ref, inv_ref, pick_ref, u_ref,
    gain_ref, ahead_ref, h_ref, next_ref, d_ref, g_ref, b_ref, a_ref, *scratch
):
    gslots, fpiece, fslots, fmat, carry, slots, gsend, grecv, fsend, frecv, ssend, srecv = scratch[:12]
    rounded, upward, own_piece, x_ref = scratch[12:16]
    phase_scratch = scratch[16:25]
    project_scratch = scratch[25:]
    sec, blk = lax.axis_index("sec"), lax.axis_index("blk")
    first = rounds[0][1]
    offsets = len(first) + 1
    _greet_all(n_sec, n_blk, offsets, rounds, True, stages)
    _project_body(stages, depth, basis_ref, image_ref, h_ref, next_ref, project_scratch)
    x_ref[...] = next_ref[...].astype(x_ref.dtype)

    def blk_copy(k, target, slot):
        return pltpu.make_async_remote_copy(
            src_ref=x_ref,
            dst_ref=gslots.at[slot],
            send_sem=gsend.at[k],
            recv_sem=grecv.at[slot],
            device_id={"blk": target},
            device_id_type=MESH,
        )

    outgoing = [blk_copy(k, lax.rem(blk + k, n_blk), blk) for k in range(1, n_blk)]
    for copy in outgoing:
        copy.start()
    gslots[blk] = x_ref[...]
    for k in range(1, n_blk):
        sender = lax.rem(blk + k, n_blk)
        blk_copy(k, sender, sender).wait_recv()
    for copy in outgoing:
        copy.wait_send()
    width = x_ref.shape[1]
    contract = (((1,), (1,)), ((), ()))
    folded = lax.dot_general(
        gslots[0], inv_ref[:, 0:width], contract, preferred_element_type=jnp.float32
    )
    for j in range(1, n_blk):
        folded = folded + lax.dot_general(
            gslots[j],
            inv_ref[:, j * width : (j + 1) * width],
            contract,
            preferred_element_type=jnp.float32,
        )
    fpiece[...] = lax.dot_general(
        pick_ref[...], folded, contract, precision=lax.Precision.HIGHEST,
        preferred_element_type=jnp.float32,
    )
    _spread(n_sec, n_blk, offsets, fpiece, fslots, fsend, frecv)
    _assemble(n_blk, offsets, fslots, fmat)
    joined = jnp.where(sec >= 1, fmat[0], jnp.zeros_like(fmat[0]))
    for i, j in enumerate(first):
        term = jnp.dot(
            u_ref[i], fmat[j], precision=lax.Precision.HIGHEST, preferred_element_type=jnp.float32
        )
        joined = joined + jnp.where(sec >= j + 1, term, jnp.zeros_like(term))
    carry[1] = joined
    flat = len(first)
    for k in range(1, len(rounds)):
        d, js = rounds[k]
        _send_all(n_sec, sec, carry.at[k], slots, ssend, srecv, flat, d, js)
        joined = carry[k]
        for i, j in enumerate(js):
            term = jnp.dot(
                u_ref[flat + i], slots[flat + i], precision=lax.Precision.HIGHEST,
                preferred_element_type=jnp.float32,
            )
            joined = joined + jnp.where(sec >= j * d, term, jnp.zeros_like(term))
        carry[k + 1] = joined
        flat += len(js)
    before = carry[len(rounds)].T
    direction = folded - lax.dot_general(
        before, gain_ref[...], contract, precision=lax.Precision.HIGHEST,
        preferred_element_type=jnp.float32,
    )
    d_ref[...] = direction
    rounded[...] = direction.astype(rounded.dtype)
    upward[...] = jnp.dot(
        rounded[...], ahead_ref[...], preferred_element_type=jnp.float32
    ).T
    own_piece[...] = lax.dot_general(
        pick_ref[...], rounded[...].astype(jnp.float32), contract,
        precision=lax.Precision.HIGHEST, preferred_element_type=jnp.float32,
    )
    _operator_phase(n_sec, n_blk, rounded, upward, own_piece, g_ref, b_ref, a_ref, phase_scratch)


def precondition_sweep(basis, image, inverse, picks, chain, gain, ahead, mesh_shape, depth):
    n_sec, n_blk = mesh_shape["sec"], mesh_shape["blk"]
    stages = _global_stages(mesh_shape)
    cases, width = image.shape
    piece, _ = picks.shape
    panel = piece * n_blk
    plan = _plan(n_sec)
    rounds = len(plan)
    total = sum(len(js) for _, js in plan)
    offsets = len(plan[0][1]) + 1
    dtype = jnp.bfloat16
    return pl.pallas_call(
        functools.partial(_precondition_kernel, n_sec, n_blk, plan, stages, depth),
        out_shape=(
            jax.ShapeDtypeStruct((8, cases), jnp.float32),
            jax.ShapeDtypeStruct((cases, width), jnp.float32),
            jax.ShapeDtypeStruct((cases, width), jnp.float32),
            jax.ShapeDtypeStruct((cases, n_blk * width), dtype),
            jax.ShapeDtypeStruct((panel, cases), jnp.float32),
            jax.ShapeDtypeStruct((piece, cases), jnp.float32),
        ),
        in_specs=[pl.BlockSpec(memory_space=pltpu.VMEM)] * 7,
        out_specs=[pl.BlockSpec(memory_space=pltpu.VMEM)] * 6,
        scratch_shapes=[
            pltpu.VMEM((n_blk, cases, width), dtype),
            pltpu.VMEM((piece, cases), jnp.float32),
            pltpu.VMEM((offsets * n_blk, piece, cases), jnp.float32),
            pltpu.VMEM((offsets, panel, cases), jnp.float32),
            pltpu.VMEM((rounds + 1, panel, cases), jnp.float32),
            pltpu.VMEM((total, panel, cases), jnp.float32),
            pltpu.SemaphoreType.DMA((n_blk,)),
            pltpu.SemaphoreType.DMA((n_blk,)),
            pltpu.SemaphoreType.DMA((offsets * n_blk,)),
            pltpu.SemaphoreType.DMA((offsets * n_blk,)),
            pltpu.SemaphoreType.DMA((total,)),
            pltpu.SemaphoreType.DMA((total,)),
            pltpu.VMEM((cases, width), dtype),
            pltpu.VMEM((panel, cases), jnp.float32),
            pltpu.VMEM((piece, cases), jnp.float32),
            pltpu.VMEM((cases, width), dtype),
        ]
        + _operator_scratch(n_blk, cases, width, dtype, piece, cases)
        + _project_scratch(stages, cases),
        compiler_params=pltpu.CompilerParams(collective_id=10 + depth, has_side_effects=True),
    )(basis, image, inverse, picks, chain, gain, ahead)


def _exchange_sum(stages, source, slots, partial, sends, recvs, out):
    count = len(stages)
    for stage, (axis, n) in enumerate(stages):
        mine = lax.axis_index(axis)
        copies = []
        for k in range(1, n):
            copy = pltpu.make_async_remote_copy(
                src_ref=source,
                dst_ref=slots[stage].at[mine],
                send_sem=sends[stage].at[k],
                recv_sem=recvs[stage].at[mine],
                device_id={axis: lax.rem(mine + k, n)},
                device_id_type=MESH,
            )
            copy.start()
            copies.append(copy)
        slots[stage][mine] = source[...]
        for k in range(1, n):
            sender = lax.rem(mine + k, n)
            pltpu.make_async_remote_copy(
                src_ref=source,
                dst_ref=slots[stage].at[sender],
                send_sem=sends[stage].at[k],
                recv_sem=recvs[stage].at[sender],
                device_id={axis: sender},
                device_id_type=MESH,
            ).wait_recv()
        for copy in copies:
            copy.wait_send()
        total = slots[stage][0]
        for j in range(1, n):
            total = total + slots[stage][j]
        if stage == count - 1:
            out[...] = total
        else:
            partial[...] = total
            source = partial


def _project_scratch(stages, cases):
    def buffers():
        out = [pltpu.VMEM((n, 8, cases), jnp.float32) for _, n in stages]
        out.append(pltpu.VMEM((8, cases), jnp.float32))
        out += [pltpu.SemaphoreType.DMA((n,)) for _, n in stages]
        out += [pltpu.SemaphoreType.DMA((n,)) for _, n in stages]
        return out

    return buffers() + buffers() + [pltpu.VMEM((8, cases), jnp.float32)] * 2


def _project_body(stages, depth, basis_ref, image_ref, h_ref, next_ref, scratch):
    count = len(stages)
    first, second = scratch[: 3 * count + 1], scratch[3 * count + 1 : 6 * count + 2]
    rows, work = scratch[6 * count + 2 : 6 * count + 4]
    highest = lax.Precision.HIGHEST
    contract = (((1,), (1,)), ((), ()))
    image = image_ref[...]
    ones = jnp.ones((8, image.shape[1]), jnp.float32)
    eye = (
        lax.broadcasted_iota(jnp.int32, (image.shape[0],) * 2, 0)
        == lax.broadcasted_iota(jnp.int32, (image.shape[0],) * 2, 1)
    ).astype(jnp.float32)

    def run(buffers, source, out):
        slots = buffers[:count]
        partial = buffers[count]
        sends = buffers[count + 1 : 2 * count + 1]
        recvs = buffers[2 * count + 1 :]
        _exchange_sum(stages, source, slots, partial, sends, recvs, out)

    if depth > 0:
        rows[...] = jnp.zeros_like(rows)
        for i in range(depth):
            summed = lax.dot_general(
                ones, image * basis_ref[i], contract, precision=highest,
                preferred_element_type=jnp.float32,
            )
            rows[i : i + 1, :] = summed[0:1, :]
        run(first, rows, h_ref)
        columns = lax.dot_general(
            eye, h_ref[...], contract, precision=highest, preferred_element_type=jnp.float32
        )
        for i in range(depth):
            image = image - columns[:, i : i + 1] * basis_ref[i]
    else:
        h_ref[...] = jnp.zeros_like(h_ref)
    work[...] = lax.dot_general(
        ones, image * image, contract, precision=highest, preferred_element_type=jnp.float32
    )
    run(second, work, rows)
    length = jnp.sqrt(rows[...] + epsilon)
    h_ref[depth : depth + 1, :] = length[0:1, :]
    scale = lax.dot_general(
        eye, length, contract, precision=highest, preferred_element_type=jnp.float32
    )
    next_ref[...] = image / scale[:, 0:1]


def _signal_stages(barrier, stages):
    peers = 0
    for axis, n in stages:
        mine = lax.axis_index(axis)
        for k in range(1, n):
            pl.semaphore_signal(
                barrier, inc=1, device_id={axis: lax.rem(mine + k, n)}, device_id_type=MESH
            )
            peers += 1
    return peers


def _project_kernel(stages, depth, basis_ref, image_ref, h_ref, next_ref, *scratch):
    barrier = pltpu.get_barrier_semaphore()
    pl.semaphore_wait(barrier, _signal_stages(barrier, stages))
    _project_body(stages, depth, basis_ref, image_ref, h_ref, next_ref, scratch)


def _global_stages(mesh_shape):
    return tuple((axis, mesh_shape[axis]) for axis in ("blk", "sec") if mesh_shape[axis] > 1)


def project(stacked, image, mesh_shape):
    depth, cases, width = stacked.shape
    stages = _global_stages(mesh_shape)
    return pl.pallas_call(
        functools.partial(_project_kernel, stages, depth),
        out_shape=(
            jax.ShapeDtypeStruct((8, cases), jnp.float32),
            jax.ShapeDtypeStruct((cases, width), jnp.float32),
        ),
        in_specs=[pl.BlockSpec(memory_space=pltpu.VMEM)] * 2,
        out_specs=[pl.BlockSpec(memory_space=pltpu.VMEM)] * 2,
        scratch_shapes=_project_scratch(stages, cases),
        compiler_params=pltpu.CompilerParams(collective_id=6 + depth, has_side_effects=True),
    )(stacked, image)


def least_squares(hessen, beta):
    cases = hessen.shape[0]
    depth = hessen.shape[2]
    rhs = jnp.zeros((cases, depth + 1), jnp.float32).at[:, 0].set(beta)
    upper = hessen
    for column in range(depth):
        upper_row = upper[:, column, :]
        lower_row = upper[:, column + 1, :]
        radius = jnp.sqrt(upper_row[:, column] ** 2 + lower_row[:, column] ** 2)
        cosine = upper_row[:, column] / radius
        sine_term = lower_row[:, column] / radius
        upper = upper.at[:, column, :].set(
            cosine[:, None] * upper_row + sine_term[:, None] * lower_row
        )
        upper = upper.at[:, column + 1, :].set(
            -sine_term[:, None] * upper_row + cosine[:, None] * lower_row
        )
        first_rhs = rhs[:, column]
        second_rhs = rhs[:, column + 1]
        rhs = rhs.at[:, column].set(cosine * first_rhs + sine_term * second_rhs)
        rhs = rhs.at[:, column + 1].set(-sine_term * first_rhs + cosine * second_rhs)
    weights = jnp.zeros((cases, depth), jnp.float32)
    for column in reversed(range(depth)):
        remain = rhs[:, column] - jnp.sum(
            upper[:, column, column + 1 :] * weights[:, column + 1 :], axis=1
        )
        weights = weights.at[:, column].set(remain / upper[:, column, column])
    return weights


def local(
    mesh_shape,
    state_now, source, fan_gain, section_block, block_inverse, back_panel, ahead_panel, interface
):
    highest = lax.Precision.HIGHEST
    cases, node_rows = state_now.shape
    panel_width = back_panel.shape[1]
    indices = interface[0]
    first_row = lax.axis_index("blk") * node_rows
    selector = (indices[None, :] == first_row + jnp.arange(node_rows)[:, None]).astype(jnp.float32)
    contract = (((1,), (1,)), ((), ()))
    gain_panel = jnp.dot(
        block_inverse,
        lax.all_gather(back_panel, "blk", axis=0, tiled=True),
        preferred_element_type=jnp.float32,
    )

    own_piece = panel_width // mesh_shape["blk"]
    own_picks = lax.dynamic_slice_in_dim(selector, lax.axis_index("blk") * own_piece, own_piece, 1).T
    own_maps = -jnp.dot(own_picks, gain_panel, precision=highest)
    chain = scan_maps(own_maps, mesh_shape["sec"], mesh_shape["blk"])

    def section_terms(dense_part, behind_vals, piece):
        width = piece.shape[1]
        dense_part = lax.dot_general(
            piece, section_block, contract, preferred_element_type=jnp.float32
        )
        picker = (indices[None, :] == jnp.arange(width)[:, None]).astype(jnp.bfloat16)
        behind_vals = jnp.dot(piece, picker, preferred_element_type=jnp.float32)
        return (dense_part, behind_vals)

    def fold_section(carry, piece):
        return section_terms(carry[0], carry[1], piece)

    n_sec, n_blk = mesh_shape["sec"], mesh_shape["blk"]
    piece = panel_width // n_blk
    local_picks = lax.dynamic_slice_in_dim(selector, lax.axis_index("blk") * piece, piece, 1)

    def finish(gathered, behind_t, ahead_piece):
        dense_part = lax.dot_general(
            gathered, section_block, contract, preferred_element_type=jnp.float32
        )
        lower_term = lax.dot_general(
            behind_t.astype(jnp.bfloat16),
            back_panel,
            (((0,), (1,)), ((), ())),
            preferred_element_type=jnp.float32,
        )
        upper_term = lax.dot_general(
            ahead_piece, local_picks, (((0,), (1,)), ((), ())), precision=highest
        )
        return dense_part + lower_term + upper_term

    def operator(vector):
        rounded = vector.astype(jnp.bfloat16)
        up_t = lax.dot_general(
            ahead_panel, rounded, (((0,), (1,)), ((), ())), preferred_element_type=jnp.float32
        )
        be_t = lax.dot_general(
            selector.astype(jnp.bfloat16),
            rounded,
            (((0,), (1,)), ((), ())),
            preferred_element_type=jnp.float32,
        )
        return finish(*operator_exchange(rounded, up_t, be_t, n_sec, n_blk))

    def compose(earlier, later):
        first_map, first_value = earlier
        second_map, second_value = later
        joined_map = jnp.dot(second_map, first_map, precision=highest)
        joined_value = jnp.dot(first_value, second_map.T, precision=highest) + second_value
        return (joined_map, joined_value)

    def lengths(vector):
        return jnp.sqrt(global_sum(jnp.sum(vector * vector, axis=1)[None], mesh_shape)[0] + epsilon)

    bent = jnp.tanh(state_now)
    residual = source - operator(state_now) - fan_gain[None, :] * bent
    jac_diag = fan_gain[None, :] * (1.0 - bent * bent)
    hessen = jnp.zeros((cases, KRYLOV + 1, KRYLOV), jnp.float32)
    basis = []
    directions = []
    product = residual
    beta = None
    for column in range(KRYLOV):
        stacked = jnp.stack(basis) if basis else residual[None]
        sums, following, direction, gathered, behind_t, ahead_piece = precondition_sweep(
            stacked, product, block_inverse, own_picks, chain, gain_panel, ahead_panel,
            mesh_shape, len(basis),
        )
        if column == 0:
            beta = sums[0]
        else:
            hessen = hessen.at[:, : column + 1, column - 1].set(sums[: column + 1].T)
        basis.append(following)
        directions.append(direction)
        product = finish(gathered, behind_t, ahead_piece) + jac_diag * direction
    sums, _ = project(jnp.stack(basis), product, mesh_shape)
    hessen = hessen.at[:, : KRYLOV + 1, KRYLOV - 1].set(sums[: KRYLOV + 1].T)
    weights = least_squares(hessen, beta)
    update = jnp.zeros_like(state_now)
    for column in range(KRYLOV):
        update = update + weights[:, column : column + 1] * directions[column]
    return state_now + update


def solution(mesh):
    in_specs = (
        P(None, ("sec", "blk")),
        P(None, ("sec", "blk")),
        P(("sec", "blk")),
        P(("sec", "blk"), None),
        P(("sec", "blk"), None),
        P(("sec", "blk"), None),
        P(("sec", "blk"), None),
        P("sec", None),
    )
    out_specs = P(None, ("sec", "blk"))
    return jax.shard_map(functools.partial(local, dict(mesh.shape)), mesh=mesh, in_specs=in_specs, out_specs=out_specs, check_vma=False)
```

```python
import functools

import jax
import jax.numpy as jnp
from jax import lax
from jax.experimental import pallas as pl
from jax.experimental.pallas import tpu as pltpu
from jax.sharding import PartitionSpec as P

MESH = pl.DeviceIdType.MESH

KRYLOV = 3


epsilon = 1e-06


def extended(x, sides, width):
    for axis, dim in sides:
        size, length = (lax.axis_size(axis), x.shape[dim])
        up = [(i, (i + 1) % size) for i in range(size - 1)]
        down = [(j, i) for i, j in up]
        last = lax.slice_in_dim(x, length - width, length, axis=dim)
        first = lax.slice_in_dim(x, 0, width, axis=dim)
        before = lax.ppermute(last, axis, up)
        after = lax.ppermute(first, axis, down)
        x = jnp.concatenate([before, x, after], axis=dim)
    return x


def entering(value, axis, join, neutral):
    count, mine = (lax.axis_size(axis), lax.axis_index(axis))
    pieces = jax.tree.map(lambda part: lax.all_gather(part, axis), value)
    so_far = jax.tree.map(
        lambda part, zero: jnp.full_like(part, 0) + jnp.asarray(zero, part.dtype), value, neutral
    )

    def step(position, so_far):
        longer = join(so_far, jax.tree.map(lambda part: part[position], pieces))
        return jax.tree.map(lambda new, old: jnp.where(position < mine, new, old), longer, so_far)

    return lax.fori_loop(0, count - 1, step, so_far)


def _reduce_kernel(stages, x_ref, o_ref, *scratch):
    count = len(stages)
    slots = scratch[:count]
    partial = scratch[count]
    sends = scratch[count + 1 : 2 * count + 1]
    recvs = scratch[2 * count + 1 :]
    barrier = pltpu.get_barrier_semaphore()
    peers = 0
    for axis, n in stages:
        mine = lax.axis_index(axis)
        for k in range(1, n):
            pl.semaphore_signal(
                barrier, inc=1, device_id={axis: lax.rem(mine + k, n)}, device_id_type=MESH
            )
            peers += 1
    pl.semaphore_wait(barrier, peers)
    source = x_ref
    for stage, (axis, n) in enumerate(stages):
        mine = lax.axis_index(axis)
        copies = []
        for k in range(1, n):
            copy = pltpu.make_async_remote_copy(
                src_ref=source,
                dst_ref=slots[stage].at[mine],
                send_sem=sends[stage].at[k],
                recv_sem=recvs[stage].at[mine],
                device_id={axis: lax.rem(mine + k, n)},
                device_id_type=MESH,
            )
            copy.start()
            copies.append(copy)
        slots[stage][mine] = source[...]
        for k in range(1, n):
            sender = lax.rem(mine + k, n)
            pltpu.make_async_remote_copy(
                src_ref=source,
                dst_ref=slots[stage].at[sender],
                send_sem=sends[stage].at[k],
                recv_sem=recvs[stage].at[sender],
                device_id={axis: sender},
                device_id_type=MESH,
            ).wait_recv()
        for copy in copies:
            copy.wait_send()
        total = slots[stage][0]
        for j in range(1, n):
            total = total + slots[stage][j]
        if stage == count - 1:
            o_ref[...] = total
        else:
            partial[...] = total
            source = partial


def all_sum(x, axes, mesh_shape, collective):
    stages = tuple((axis, mesh_shape[axis]) for axis in axes if mesh_shape[axis] > 1)
    rows, cols = x.shape
    scratch = [pltpu.VMEM((n, rows, cols), jnp.float32) for _, n in stages]
    scratch.append(pltpu.VMEM((rows, cols), jnp.float32))
    scratch += [pltpu.SemaphoreType.DMA((n,)) for _, n in stages]
    scratch += [pltpu.SemaphoreType.DMA((n,)) for _, n in stages]
    return pl.pallas_call(
        functools.partial(_reduce_kernel, stages),
        out_shape=jax.ShapeDtypeStruct((rows, cols), jnp.float32),
        in_specs=[pl.BlockSpec(memory_space=pltpu.VMEM)],
        out_specs=pl.BlockSpec(memory_space=pltpu.VMEM),
        scratch_shapes=scratch,
        compiler_params=pltpu.CompilerParams(collective_id=collective, has_side_effects=True),
    )(x.astype(jnp.float32))


def global_sum(rows_of_sums, mesh_shape):
    count = rows_of_sums.shape[0]
    padded = jnp.zeros((8, rows_of_sums.shape[1]), jnp.float32).at[:count].set(rows_of_sums)
    return all_sum(padded, ("blk", "sec"), mesh_shape, 0)[:count]


def _doubling(n):
    distances, d = [], 1
    while d < n:
        distances.append(d)
        d *= 2
    return tuple(distances)


def _greet(n, distances):
    barrier = pltpu.get_barrier_semaphore()
    mine = lax.axis_index("sec")
    for d in distances:
        for peer in (lax.rem(mine + d, n), lax.rem(mine + n - d, n)):
            pl.semaphore_signal(barrier, inc=1, device_id={"sec": peer}, device_id_type=MESH)
    pl.semaphore_wait(barrier, 2 * len(distances))


def _hop(n, d, source, slot, send_sem, recv_sem):
    mine = lax.axis_index("sec")
    copy = pltpu.make_async_remote_copy(
        src_ref=source,
        dst_ref=slot,
        send_sem=send_sem,
        recv_sem=recv_sem,
        device_id={"sec": lax.rem(mine + d, n)},
        device_id_type=MESH,
    )
    copy.start()
    copy.wait_recv()
    copy.wait_send()


RADIX = 4


def _plan(n):
    rounds, d = [], 1
    while d < n:
        rounds.append((d, tuple(j for j in range(1, RADIX) if j * d < n)))
        d *= RADIX
    return tuple(rounds)


def _plan_peers(rounds):
    return tuple(sorted({j * d for d, js in rounds for j in js} | {1}))


def _send_all(n, sec, sources, slots, sends, recvs, flat, d, js):
    copies = []
    for i, j in enumerate(js):
        copy = pltpu.make_async_remote_copy(
            src_ref=sources,
            dst_ref=slots.at[flat + i],
            send_sem=sends.at[flat + i],
            recv_sem=recvs.at[flat + i],
            device_id={"sec": lax.rem(sec + j * d, n)},
            device_id_type=MESH,
        )
        copy.start()
        copies.append(copy)
    for copy in copies:
        copy.wait_recv()
    for copy in copies:
        copy.wait_send()


def _spread(n_sec, n_blk, offsets, piece_ref, slots, sends, recvs):
    sec, blk = lax.axis_index("sec"), lax.axis_index("blk")

    def copy(o, j, index):
        return pltpu.make_async_remote_copy(
            src_ref=piece_ref,
            dst_ref=slots.at[index],
            send_sem=sends.at[(o - 1) * n_blk + j],
            recv_sem=recvs.at[index],
            device_id={"sec": lax.rem(sec + o, n_sec), "blk": j},
            device_id_type=MESH,
        )

    outgoing = [
        copy(o, j, (o - 1) * n_blk + blk) for o in range(1, offsets + 1) for j in range(n_blk)
    ]
    for c in outgoing:
        c.start()
    for o in range(1, offsets + 1):
        for j in range(n_blk):
            copy(o, j, (o - 1) * n_blk + j).wait_recv()
    for c in outgoing:
        c.wait_send()


def _assemble(n_blk, offsets, slots, mats):
    piece = slots.shape[1]
    for o in range(offsets):
        for j in range(n_blk):
            mats[o, j * piece : (j + 1) * piece, :] = slots[o * n_blk + j]


def _greet_all(n_sec, n_blk, offsets, rounds, blk_peers, stages=()):
    barrier = pltpu.get_barrier_semaphore()
    sec, blk = lax.axis_index("sec"), lax.axis_index("blk")
    count = _signal_stages(barrier, stages)
    if blk_peers:
        for k in range(1, n_blk):
            pl.semaphore_signal(
                barrier, inc=1, device_id={"blk": lax.rem(blk + k, n_blk)}, device_id_type=MESH
            )
            count += 1
    for o in range(1, offsets + 1):
        for j in range(n_blk):
            for peer in (lax.rem(sec + o, n_sec), lax.rem(sec + n_sec - o, n_sec)):
                pl.semaphore_signal(
                    barrier, inc=1, device_id={"sec": peer, "blk": j}, device_id_type=MESH
                )
                count += 1
    for d in sorted({j * d for d, js in rounds[1:] for j in js}):
        for peer in (lax.rem(sec + d, n_sec), lax.rem(sec + n_sec - d, n_sec)):
            pl.semaphore_signal(barrier, inc=1, device_id={"sec": peer}, device_id_type=MESH)
            count += 1
    pl.semaphore_wait(barrier, count)


def _maps_body(n, n_blk, rounds, e_ref, a_ref, eslots, emat, current, slots, esend, erecv, sends, recvs):
    sec = lax.axis_index("sec")
    first = rounds[0][1]
    offsets = len(first) + 1
    _spread(n, n_blk, offsets, e_ref, eslots, esend, erecv)
    _assemble(n_blk, offsets, eslots, emat)
    joined = emat[0]
    for i, j in enumerate(first):
        a_ref[i] = joined
        joined = jnp.dot(
            joined, emat[j], precision=lax.Precision.HIGHEST, preferred_element_type=jnp.float32
        )
    current[...] = joined
    flat = len(first)
    for k in range(1, len(rounds)):
        d, js = rounds[k]
        onward = k < len(rounds) - 1
        if onward or len(js) > 1:
            _send_all(n, sec, current, slots, sends, recvs, flat, d, js)
        joined = current[...]
        for i, j in enumerate(js):
            a_ref[flat + i] = joined
            if onward or i < len(js) - 1:
                joined = jnp.dot(
                    joined, slots[flat + i], precision=lax.Precision.HIGHEST,
                    preferred_element_type=jnp.float32,
                )
        if onward:
            current[...] = joined
        flat += len(js)


def _setup_kernel(
    n_sec, n_blk, rounds, x_ref, up_ref, be_ref, back_ref, inv_ref, pick_ref,
    g_ref, b_ref, a_ref, gain_ref, chain_ref, *scratch
):
    phase_scratch = scratch[:9]
    pslots, psend, precv, epiece = scratch[9:13]
    maps_scratch = scratch[13:]
    sec, blk = lax.axis_index("sec"), lax.axis_index("blk")
    offsets = len(rounds[0][1]) + 1
    _greet_all(n_sec, n_blk, offsets, rounds, True)
    piece = epiece.shape[0]
    mine = be_ref.at[pl.ds(pl.multiple_of(blk * piece, 8), piece)]
    _operator_phase(n_sec, n_blk, x_ref, up_ref, mine, g_ref, b_ref, a_ref, phase_scratch)

    def blk_copy(k, target, slot):
        return pltpu.make_async_remote_copy(
            src_ref=back_ref,
            dst_ref=pslots.at[slot],
            send_sem=psend.at[k],
            recv_sem=precv.at[slot],
            device_id={"blk": target},
            device_id_type=MESH,
        )

    outgoing = [blk_copy(k, lax.rem(blk + k, n_blk), blk) for k in range(1, n_blk)]
    for copy in outgoing:
        copy.start()
    pslots[blk] = back_ref[...]
    for k in range(1, n_blk):
        sender = lax.rem(blk + k, n_blk)
        blk_copy(k, sender, sender).wait_recv()
    for copy in outgoing:
        copy.wait_send()
    rows = back_ref.shape[0]
    gain = jnp.dot(inv_ref[:, 0:rows], pslots[0], preferred_element_type=jnp.float32)
    for j in range(1, n_blk):
        gain = gain + jnp.dot(
            inv_ref[:, j * rows : (j + 1) * rows], pslots[j], preferred_element_type=jnp.float32
        )
    gain_ref[...] = gain
    epiece[...] = -jnp.dot(
        pick_ref[...], gain, precision=lax.Precision.HIGHEST, preferred_element_type=jnp.float32
    )
    _maps_body(n_sec, n_blk, rounds, epiece, chain_ref, *maps_scratch)


def setup_exchange(x, up_t, be_t, back, inverse, picks, n_sec, n_blk):
    cases, width = x.shape
    panel, _ = up_t.shape
    piece = panel // n_blk
    rows, panel_width = back.shape
    rounds = _plan(n_sec)
    total = sum(len(js) for _, js in rounds)
    offsets = len(rounds[0][1]) + 1
    return pl.pallas_call(
        functools.partial(_setup_kernel, n_sec, n_blk, rounds),
        out_shape=(
            jax.ShapeDtypeStruct((cases, n_blk * width), x.dtype),
            jax.ShapeDtypeStruct((panel, cases), jnp.float32),
            jax.ShapeDtypeStruct((piece, cases), jnp.float32),
            jax.ShapeDtypeStruct((rows, panel_width), jnp.float32),
            jax.ShapeDtypeStruct((total, panel_width, panel_width), jnp.float32),
        ),
        in_specs=[pl.BlockSpec(memory_space=pltpu.VMEM)] * 6,
        out_specs=[pl.BlockSpec(memory_space=pltpu.VMEM)] * 5,
        scratch_shapes=_operator_scratch(n_blk, cases, width, x.dtype, piece, cases)
        + [
            pltpu.VMEM((n_blk, rows, panel_width), back.dtype),
            pltpu.SemaphoreType.DMA((n_blk,)),
            pltpu.SemaphoreType.DMA((n_blk,)),
            pltpu.VMEM((piece, panel_width), jnp.float32),
            pltpu.VMEM((offsets * n_blk, piece, panel_width), jnp.float32),
            pltpu.VMEM((offsets, panel_width, panel_width), jnp.float32),
            pltpu.VMEM((panel_width, panel_width), jnp.float32),
            pltpu.VMEM((total, panel_width, panel_width), jnp.float32),
            pltpu.SemaphoreType.DMA((offsets * n_blk,)),
            pltpu.SemaphoreType.DMA((offsets * n_blk,)),
            pltpu.SemaphoreType.DMA((total,)),
            pltpu.SemaphoreType.DMA((total,)),
        ],
        compiler_params=pltpu.CompilerParams(collective_id=3, has_side_effects=True),
    )(x, up_t, be_t, back, inverse, picks)


def _gather_kernel(n, x_ref, o_ref, slots, sends, recvs):
    mine = lax.axis_index("blk")
    barrier = pltpu.get_barrier_semaphore()
    for k in range(1, n):
        pl.semaphore_signal(
            barrier, inc=1, device_id={"blk": lax.rem(mine + k, n)}, device_id_type=MESH
        )
    pl.semaphore_wait(barrier, n - 1)
    copies = []
    for k in range(1, n):
        copy = pltpu.make_async_remote_copy(
            src_ref=x_ref,
            dst_ref=slots.at[mine],
            send_sem=sends.at[k],
            recv_sem=recvs.at[mine],
            device_id={"blk": lax.rem(mine + k, n)},
            device_id_type=MESH,
        )
        copy.start()
        copies.append(copy)
    slots[mine] = x_ref[...]
    for k in range(1, n):
        sender = lax.rem(mine + k, n)
        pltpu.make_async_remote_copy(
            src_ref=x_ref,
            dst_ref=slots.at[sender],
            send_sem=sends.at[k],
            recv_sem=recvs.at[sender],
            device_id={"blk": sender},
            device_id_type=MESH,
        ).wait_recv()
    for copy in copies:
        copy.wait_send()
    width = x_ref.shape[1]
    for j in range(n):
        o_ref[:, j * width : (j + 1) * width] = slots[j]


def gather_blk(x, n):
    rows, width = x.shape
    return pl.pallas_call(
        functools.partial(_gather_kernel, n),
        out_shape=jax.ShapeDtypeStruct((rows, n * width), x.dtype),
        in_specs=[pl.BlockSpec(memory_space=pltpu.VMEM)],
        out_specs=pl.BlockSpec(memory_space=pltpu.VMEM),
        scratch_shapes=[
            pltpu.VMEM((n, rows, width), x.dtype),
            pltpu.SemaphoreType.DMA((n,)),
            pltpu.SemaphoreType.DMA((n,)),
        ],
        compiler_params=pltpu.CompilerParams(collective_id=4, has_side_effects=True),
    )(x)


def _operator_phase(n_sec, n_blk, x_ref, up_ref, piece_ref, g_ref, b_ref, a_ref, scratch):
    gslots, bslots, aslots, gsend, grecv, bsend, brecv, asend, arecv = scratch
    sec, blk = lax.axis_index("sec"), lax.axis_index("blk")
    nxt, prv = lax.rem(sec + 1, n_sec), lax.rem(sec + n_sec - 1, n_sec)
    piece = bslots.shape[1]
    copies = []
    for k in range(1, n_blk):
        copies.append(
            pltpu.make_async_remote_copy(
                src_ref=x_ref,
                dst_ref=gslots.at[blk],
                send_sem=gsend.at[k],
                recv_sem=grecv.at[blk],
                device_id={"blk": lax.rem(blk + k, n_blk)},
                device_id_type=MESH,
            )
        )
    for j in range(n_blk):
        copies.append(
            pltpu.make_async_remote_copy(
                src_ref=piece_ref,
                dst_ref=bslots.at[blk],
                send_sem=bsend.at[j],
                recv_sem=brecv.at[blk],
                device_id={"sec": nxt, "blk": j},
                device_id_type=MESH,
            )
        )
        copies.append(
            pltpu.make_async_remote_copy(
                src_ref=up_ref.at[pl.ds(j * piece, piece)],
                dst_ref=aslots.at[blk],
                send_sem=asend.at[j],
                recv_sem=arecv.at[blk],
                device_id={"sec": prv, "blk": j},
                device_id_type=MESH,
            )
        )
    for copy in copies:
        copy.start()
    gslots[blk] = x_ref[...]
    for k in range(1, n_blk):
        sender = lax.rem(blk + k, n_blk)
        pltpu.make_async_remote_copy(
            src_ref=x_ref,
            dst_ref=gslots.at[sender],
            send_sem=gsend.at[k],
            recv_sem=grecv.at[sender],
            device_id={"blk": sender},
            device_id_type=MESH,
        ).wait_recv()
    for j in range(n_blk):
        pltpu.make_async_remote_copy(
            src_ref=piece_ref,
            dst_ref=bslots.at[j],
            send_sem=bsend.at[j],
            recv_sem=brecv.at[j],
            device_id={"sec": prv, "blk": j},
            device_id_type=MESH,
        ).wait_recv()
        pltpu.make_async_remote_copy(
            src_ref=up_ref.at[pl.ds(j * piece, piece)],
            dst_ref=aslots.at[j],
            send_sem=asend.at[j],
            recv_sem=arecv.at[j],
            device_id={"sec": nxt, "blk": j},
            device_id_type=MESH,
        ).wait_recv()
    for copy in copies:
        copy.wait_send()
    width = x_ref.shape[1]
    for j in range(n_blk):
        g_ref[:, j * width : (j + 1) * width] = gslots[j]
        b_ref[j * piece : (j + 1) * piece, :] = jnp.where(
            sec >= 1, bslots[j], jnp.zeros_like(bslots[j])
        )
    total = aslots[0]
    for j in range(1, n_blk):
        total = total + aslots[j]
    a_ref[...] = jnp.where(sec <= n_sec - 2, total, jnp.zeros_like(total))


def _operator_scratch(n_blk, rows, width, dtype, piece, cases):
    return [
        pltpu.VMEM((n_blk, rows, width), dtype),
        pltpu.VMEM((n_blk, piece, cases), jnp.float32),
        pltpu.VMEM((n_blk, piece, cases), jnp.float32),
    ] + [pltpu.SemaphoreType.DMA((n_blk,))] * 6


def _operator_kernel(n_sec, n_blk, x_ref, up_ref, be_ref, g_ref, b_ref, a_ref, *scratch):
    sec, blk = lax.axis_index("sec"), lax.axis_index("blk")
    nxt, prv = lax.rem(sec + 1, n_sec), lax.rem(sec + n_sec - 1, n_sec)
    piece = scratch[1].shape[1]
    barrier = pltpu.get_barrier_semaphore()
    for k in range(1, n_blk):
        pl.semaphore_signal(
            barrier, inc=1, device_id={"blk": lax.rem(blk + k, n_blk)}, device_id_type=MESH
        )
    for j in range(n_blk):
        for other in (nxt, prv):
            pl.semaphore_signal(
                barrier, inc=1, device_id={"sec": other, "blk": j}, device_id_type=MESH
            )
    pl.semaphore_wait(barrier, 3 * n_blk - 1)
    mine = be_ref.at[pl.ds(pl.multiple_of(blk * piece, 8), piece)]
    _operator_phase(n_sec, n_blk, x_ref, up_ref, mine, g_ref, b_ref, a_ref, scratch)


def operator_exchange(x, up_t, be_t, n_sec, n_blk):
    rows, width = x.shape
    panel, cases = up_t.shape
    piece = panel // n_blk
    return pl.pallas_call(
        functools.partial(_operator_kernel, n_sec, n_blk),
        out_shape=(
            jax.ShapeDtypeStruct((rows, n_blk * width), x.dtype),
            jax.ShapeDtypeStruct((panel, cases), jnp.float32),
            jax.ShapeDtypeStruct((piece, cases), jnp.float32),
        ),
        in_specs=[pl.BlockSpec(memory_space=pltpu.VMEM)] * 3,
        out_specs=[pl.BlockSpec(memory_space=pltpu.VMEM)] * 3,
        scratch_shapes=_operator_scratch(n_blk, rows, width, x.dtype, piece, cases),
        compiler_params=pltpu.CompilerParams(collective_id=5, has_side_effects=True),
    )(x, up_t, be_t)


def _precondition_kernel(
    n_sec, n_blk, rounds, stages, depth, basis_ref, image_ref, inv_ref, pick_ref, u_ref,
    gain_ref, ahead_ref, h_ref, next_ref, d_ref, g_ref, b_ref, a_ref, *scratch
):
    gslots, fpiece, fslots, fmat, carry, slots, gsend, grecv, fsend, frecv, ssend, srecv = scratch[:12]
    rounded, upward, own_piece, x_ref = scratch[12:16]
    phase_scratch = scratch[16:25]
    project_scratch = scratch[25:]
    sec, blk = lax.axis_index("sec"), lax.axis_index("blk")
    first = rounds[0][1]
    offsets = len(first) + 1
    _greet_all(n_sec, n_blk, offsets, rounds, True, stages)
    _project_body(stages, depth, basis_ref, image_ref, h_ref, next_ref, project_scratch)
    x_ref[...] = next_ref[...].astype(x_ref.dtype)

    def blk_copy(k, target, slot):
        return pltpu.make_async_remote_copy(
            src_ref=x_ref,
            dst_ref=gslots.at[slot],
            send_sem=gsend.at[k],
            recv_sem=grecv.at[slot],
            device_id={"blk": target},
            device_id_type=MESH,
        )

    outgoing = [blk_copy(k, lax.rem(blk + k, n_blk), blk) for k in range(1, n_blk)]
    for copy in outgoing:
        copy.start()
    gslots[blk] = x_ref[...]
    for k in range(1, n_blk):
        sender = lax.rem(blk + k, n_blk)
        blk_copy(k, sender, sender).wait_recv()
    for copy in outgoing:
        copy.wait_send()
    width = x_ref.shape[1]
    contract = (((1,), (1,)), ((), ()))
    folded = lax.dot_general(
        gslots[0], inv_ref[:, 0:width], contract, preferred_element_type=jnp.float32
    )
    for j in range(1, n_blk):
        folded = folded + lax.dot_general(
            gslots[j],
            inv_ref[:, j * width : (j + 1) * width],
            contract,
            preferred_element_type=jnp.float32,
        )
    fpiece[...] = lax.dot_general(
        pick_ref[...], folded, contract, precision=lax.Precision.HIGHEST,
        preferred_element_type=jnp.float32,
    )
    _spread(n_sec, n_blk, offsets, fpiece, fslots, fsend, frecv)
    _assemble(n_blk, offsets, fslots, fmat)
    joined = jnp.where(sec >= 1, fmat[0], jnp.zeros_like(fmat[0]))
    for i, j in enumerate(first):
        term = jnp.dot(
            u_ref[i], fmat[j], precision=lax.Precision.HIGHEST, preferred_element_type=jnp.float32
        )
        joined = joined + jnp.where(sec >= j + 1, term, jnp.zeros_like(term))
    carry[1] = joined
    flat = len(first)
    for k in range(1, len(rounds)):
        d, js = rounds[k]
        _send_all(n_sec, sec, carry.at[k], slots, ssend, srecv, flat, d, js)
        joined = carry[k]
        for i, j in enumerate(js):
            term = jnp.dot(
                u_ref[flat + i], slots[flat + i], precision=lax.Precision.HIGHEST,
                preferred_element_type=jnp.float32,
            )
            joined = joined + jnp.where(sec >= j * d, term, jnp.zeros_like(term))
        carry[k + 1] = joined
        flat += len(js)
    before = carry[len(rounds)].T
    direction = folded - lax.dot_general(
        before, gain_ref[...], contract, precision=lax.Precision.HIGHEST,
        preferred_element_type=jnp.float32,
    )
    d_ref[...] = direction
    rounded[...] = direction.astype(rounded.dtype)
    upward[...] = jnp.dot(
        rounded[...], ahead_ref[...], preferred_element_type=jnp.float32
    ).T
    own_piece[...] = lax.dot_general(
        pick_ref[...], rounded[...].astype(jnp.float32), contract,
        precision=lax.Precision.HIGHEST, preferred_element_type=jnp.float32,
    )
    _operator_phase(n_sec, n_blk, rounded, upward, own_piece, g_ref, b_ref, a_ref, phase_scratch)


def precondition_sweep(basis, image, inverse, picks, chain, gain, ahead, mesh_shape, depth):
    n_sec, n_blk = mesh_shape["sec"], mesh_shape["blk"]
    stages = _global_stages(mesh_shape)
    cases, width = image.shape
    piece, _ = picks.shape
    panel = piece * n_blk
    plan = _plan(n_sec)
    rounds = len(plan)
    total = sum(len(js) for _, js in plan)
    offsets = len(plan[0][1]) + 1
    dtype = jnp.bfloat16
    return pl.pallas_call(
        functools.partial(_precondition_kernel, n_sec, n_blk, plan, stages, depth),
        out_shape=(
            jax.ShapeDtypeStruct((8, cases), jnp.float32),
            jax.ShapeDtypeStruct((cases, width), jnp.float32),
            jax.ShapeDtypeStruct((cases, width), jnp.float32),
            jax.ShapeDtypeStruct((cases, n_blk * width), dtype),
            jax.ShapeDtypeStruct((panel, cases), jnp.float32),
            jax.ShapeDtypeStruct((piece, cases), jnp.float32),
        ),
        in_specs=[pl.BlockSpec(memory_space=pltpu.VMEM)] * 7,
        out_specs=[pl.BlockSpec(memory_space=pltpu.VMEM)] * 6,
        scratch_shapes=[
            pltpu.VMEM((n_blk, cases, width), dtype),
            pltpu.VMEM((piece, cases), jnp.float32),
            pltpu.VMEM((offsets * n_blk, piece, cases), jnp.float32),
            pltpu.VMEM((offsets, panel, cases), jnp.float32),
            pltpu.VMEM((rounds + 1, panel, cases), jnp.float32),
            pltpu.VMEM((total, panel, cases), jnp.float32),
            pltpu.SemaphoreType.DMA((n_blk,)),
            pltpu.SemaphoreType.DMA((n_blk,)),
            pltpu.SemaphoreType.DMA((offsets * n_blk,)),
            pltpu.SemaphoreType.DMA((offsets * n_blk,)),
            pltpu.SemaphoreType.DMA((total,)),
            pltpu.SemaphoreType.DMA((total,)),
            pltpu.VMEM((cases, width), dtype),
            pltpu.VMEM((panel, cases), jnp.float32),
            pltpu.VMEM((piece, cases), jnp.float32),
            pltpu.VMEM((cases, width), dtype),
        ]
        + _operator_scratch(n_blk, cases, width, dtype, piece, cases)
        + _project_scratch(stages, cases),
        compiler_params=pltpu.CompilerParams(collective_id=10 + depth, has_side_effects=True),
    )(basis, image, inverse, picks, chain, gain, ahead)


def _exchange_sum(stages, source, slots, partial, sends, recvs, out):
    count = len(stages)
    for stage, (axis, n) in enumerate(stages):
        mine = lax.axis_index(axis)
        copies = []
        for k in range(1, n):
            copy = pltpu.make_async_remote_copy(
                src_ref=source,
                dst_ref=slots[stage].at[mine],
                send_sem=sends[stage].at[k],
                recv_sem=recvs[stage].at[mine],
                device_id={axis: lax.rem(mine + k, n)},
                device_id_type=MESH,
            )
            copy.start()
            copies.append(copy)
        slots[stage][mine] = source[...]
        for k in range(1, n):
            sender = lax.rem(mine + k, n)
            pltpu.make_async_remote_copy(
                src_ref=source,
                dst_ref=slots[stage].at[sender],
                send_sem=sends[stage].at[k],
                recv_sem=recvs[stage].at[sender],
                device_id={axis: sender},
                device_id_type=MESH,
            ).wait_recv()
        for copy in copies:
            copy.wait_send()
        total = slots[stage][0]
        for j in range(1, n):
            total = total + slots[stage][j]
        if stage == count - 1:
            out[...] = total
        else:
            partial[...] = total
            source = partial


def _project_scratch(stages, cases):
    def buffers():
        out = [pltpu.VMEM((n, 8, cases), jnp.float32) for _, n in stages]
        out.append(pltpu.VMEM((8, cases), jnp.float32))
        out += [pltpu.SemaphoreType.DMA((n,)) for _, n in stages]
        out += [pltpu.SemaphoreType.DMA((n,)) for _, n in stages]
        return out

    return buffers() + buffers() + [pltpu.VMEM((8, cases), jnp.float32)] * 2


def _project_body(stages, depth, basis_ref, image_ref, h_ref, next_ref, scratch):
    count = len(stages)
    first, second = scratch[: 3 * count + 1], scratch[3 * count + 1 : 6 * count + 2]
    rows, work = scratch[6 * count + 2 : 6 * count + 4]
    highest = lax.Precision.HIGHEST
    contract = (((1,), (1,)), ((), ()))
    image = image_ref[...]
    ones = jnp.ones((8, image.shape[1]), jnp.float32)
    eye = (
        lax.broadcasted_iota(jnp.int32, (image.shape[0],) * 2, 0)
        == lax.broadcasted_iota(jnp.int32, (image.shape[0],) * 2, 1)
    ).astype(jnp.float32)

    def run(buffers, source, out):
        slots = buffers[:count]
        partial = buffers[count]
        sends = buffers[count + 1 : 2 * count + 1]
        recvs = buffers[2 * count + 1 :]
        _exchange_sum(stages, source, slots, partial, sends, recvs, out)

    if depth > 0:
        rows[...] = jnp.zeros_like(rows)
        for i in range(depth):
            summed = lax.dot_general(
                ones, image * basis_ref[i], contract, precision=highest,
                preferred_element_type=jnp.float32,
            )
            rows[i : i + 1, :] = summed[0:1, :]
        run(first, rows, h_ref)
        columns = lax.dot_general(
            eye, h_ref[...], contract, precision=highest, preferred_element_type=jnp.float32
        )
        for i in range(depth):
            image = image - columns[:, i : i + 1] * basis_ref[i]
    else:
        h_ref[...] = jnp.zeros_like(h_ref)
    work[...] = lax.dot_general(
        ones, image * image, contract, precision=highest, preferred_element_type=jnp.float32
    )
    run(second, work, rows)
    length = jnp.sqrt(rows[...] + epsilon)
    h_ref[depth : depth + 1, :] = length[0:1, :]
    scale = lax.dot_general(
        eye, length, contract, precision=highest, preferred_element_type=jnp.float32
    )
    next_ref[...] = image / scale[:, 0:1]


def _signal_stages(barrier, stages):
    peers = 0
    for axis, n in stages:
        mine = lax.axis_index(axis)
        for k in range(1, n):
            pl.semaphore_signal(
                barrier, inc=1, device_id={axis: lax.rem(mine + k, n)}, device_id_type=MESH
            )
            peers += 1
    return peers


def _project_kernel(stages, depth, basis_ref, image_ref, h_ref, next_ref, *scratch):
    barrier = pltpu.get_barrier_semaphore()
    pl.semaphore_wait(barrier, _signal_stages(barrier, stages))
    _project_body(stages, depth, basis_ref, image_ref, h_ref, next_ref, scratch)


def _global_stages(mesh_shape):
    return tuple((axis, mesh_shape[axis]) for axis in ("blk", "sec") if mesh_shape[axis] > 1)


def project(stacked, image, mesh_shape):
    depth, cases, width = stacked.shape
    stages = _global_stages(mesh_shape)
    return pl.pallas_call(
        functools.partial(_project_kernel, stages, depth),
        out_shape=(
            jax.ShapeDtypeStruct((8, cases), jnp.float32),
            jax.ShapeDtypeStruct((cases, width), jnp.float32),
        ),
        in_specs=[pl.BlockSpec(memory_space=pltpu.VMEM)] * 2,
        out_specs=[pl.BlockSpec(memory_space=pltpu.VMEM)] * 2,
        scratch_shapes=_project_scratch(stages, cases),
        compiler_params=pltpu.CompilerParams(collective_id=6 + depth, has_side_effects=True),
    )(stacked, image)


def least_squares(hessen, beta):
    cases = hessen.shape[0]
    depth = hessen.shape[2]
    rhs = jnp.zeros((cases, depth + 1), jnp.float32).at[:, 0].set(beta)
    upper = hessen
    for column in range(depth):
        upper_row = upper[:, column, :]
        lower_row = upper[:, column + 1, :]
        radius = jnp.sqrt(upper_row[:, column] ** 2 + lower_row[:, column] ** 2)
        cosine = upper_row[:, column] / radius
        sine_term = lower_row[:, column] / radius
        upper = upper.at[:, column, :].set(
            cosine[:, None] * upper_row + sine_term[:, None] * lower_row
        )
        upper = upper.at[:, column + 1, :].set(
            -sine_term[:, None] * upper_row + cosine[:, None] * lower_row
        )
        first_rhs = rhs[:, column]
        second_rhs = rhs[:, column + 1]
        rhs = rhs.at[:, column].set(cosine * first_rhs + sine_term * second_rhs)
        rhs = rhs.at[:, column + 1].set(-sine_term * first_rhs + cosine * second_rhs)
    weights = jnp.zeros((cases, depth), jnp.float32)
    for column in reversed(range(depth)):
        remain = rhs[:, column] - jnp.sum(
            upper[:, column, column + 1 :] * weights[:, column + 1 :], axis=1
        )
        weights = weights.at[:, column].set(remain / upper[:, column, column])
    return weights


def local(
    mesh_shape,
    state_now, source, fan_gain, section_block, block_inverse, back_panel, ahead_panel, interface
):
    highest = lax.Precision.HIGHEST
    cases, node_rows = state_now.shape
    panel_width = back_panel.shape[1]
    indices = interface[0]
    first_row = lax.axis_index("blk") * node_rows
    selector = (indices[None, :] == first_row + jnp.arange(node_rows)[:, None]).astype(jnp.float32)
    contract = (((1,), (1,)), ((), ()))

    own_piece = panel_width // mesh_shape["blk"]
    own_picks = lax.dynamic_slice_in_dim(selector, lax.axis_index("blk") * own_piece, own_piece, 1).T

    def section_terms(dense_part, behind_vals, piece):
        width = piece.shape[1]
        dense_part = lax.dot_general(
            piece, section_block, contract, preferred_element_type=jnp.float32
        )
        picker = (indices[None, :] == jnp.arange(width)[:, None]).astype(jnp.bfloat16)
        behind_vals = jnp.dot(piece, picker, preferred_element_type=jnp.float32)
        return (dense_part, behind_vals)

    def fold_section(carry, piece):
        return section_terms(carry[0], carry[1], piece)

    n_sec, n_blk = mesh_shape["sec"], mesh_shape["blk"]
    piece = panel_width // n_blk
    local_picks = lax.dynamic_slice_in_dim(selector, lax.axis_index("blk") * piece, piece, 1)

    def finish(gathered, behind_t, ahead_piece):
        dense_part = lax.dot_general(
            gathered, section_block, contract, preferred_element_type=jnp.float32
        )
        lower_term = lax.dot_general(
            behind_t.astype(jnp.bfloat16),
            back_panel,
            (((0,), (1,)), ((), ())),
            preferred_element_type=jnp.float32,
        )
        upper_term = lax.dot_general(
            ahead_piece, local_picks, (((0,), (1,)), ((), ())), precision=highest
        )
        return dense_part + lower_term + upper_term

    def operator(vector):
        rounded = vector.astype(jnp.bfloat16)
        up_t = lax.dot_general(
            ahead_panel, rounded, (((0,), (1,)), ((), ())), preferred_element_type=jnp.float32
        )
        be_t = lax.dot_general(
            selector.astype(jnp.bfloat16),
            rounded,
            (((0,), (1,)), ((), ())),
            preferred_element_type=jnp.float32,
        )
        return finish(*operator_exchange(rounded, up_t, be_t, n_sec, n_blk))

    def compose(earlier, later):
        first_map, first_value = earlier
        second_map, second_value = later
        joined_map = jnp.dot(second_map, first_map, precision=highest)
        joined_value = jnp.dot(first_value, second_map.T, precision=highest) + second_value
        return (joined_map, joined_value)

    def lengths(vector):
        return jnp.sqrt(global_sum(jnp.sum(vector * vector, axis=1)[None], mesh_shape)[0] + epsilon)

    bent = jnp.tanh(state_now)
    state_rounded = state_now.astype(jnp.bfloat16)
    gathered, behind_t, ahead_piece, gain_panel, chain = setup_exchange(
        state_rounded,
        lax.dot_general(
            ahead_panel, state_rounded, (((0,), (1,)), ((), ())), preferred_element_type=jnp.float32
        ),
        lax.dot_general(
            selector.astype(jnp.bfloat16),
            state_rounded,
            (((0,), (1,)), ((), ())),
            preferred_element_type=jnp.float32,
        ),
        back_panel,
        block_inverse,
        own_picks,
        n_sec,
        n_blk,
    )
    residual = source - finish(gathered, behind_t, ahead_piece) - fan_gain[None, :] * bent
    jac_diag = fan_gain[None, :] * (1.0 - bent * bent)
    hessen = jnp.zeros((cases, KRYLOV + 1, KRYLOV), jnp.float32)
    basis = []
    directions = []
    product = residual
    beta = None
    for column in range(KRYLOV):
        stacked = jnp.stack(basis) if basis else residual[None]
        sums, following, direction, gathered, behind_t, ahead_piece = precondition_sweep(
            stacked, product, block_inverse, own_picks, chain, gain_panel, ahead_panel,
            mesh_shape, len(basis),
        )
        if column == 0:
            beta = sums[0]
        else:
            hessen = hessen.at[:, : column + 1, column - 1].set(sums[: column + 1].T)
        basis.append(following)
        directions.append(direction)
        product = finish(gathered, behind_t, ahead_piece) + jac_diag * direction
    sums, _ = project(jnp.stack(basis), product, mesh_shape)
    hessen = hessen.at[:, : KRYLOV + 1, KRYLOV - 1].set(sums[: KRYLOV + 1].T)
    weights = least_squares(hessen, beta)
    update = jnp.zeros_like(state_now)
    for column in range(KRYLOV):
        update = update + weights[:, column : column + 1] * directions[column]
    return state_now + update


def solution(mesh):
    in_specs = (
        P(None, ("sec", "blk")),
        P(None, ("sec", "blk")),
        P(("sec", "blk")),
        P(("sec", "blk"), None),
        P(("sec", "blk"), None),
        P(("sec", "blk"), None),
        P(("sec", "blk"), None),
        P("sec", None),
    )
    out_specs = P(None, ("sec", "blk"))
    return jax.shard_map(functools.partial(local, dict(mesh.shape)), mesh=mesh, in_specs=in_specs, out_specs=out_specs, check_vma=False)
```

```python
import functools

import jax
import jax.numpy as jnp
from jax import lax
from jax.experimental import pallas as pl
from jax.experimental.pallas import tpu as pltpu
from jax.sharding import PartitionSpec as P

MESH = pl.DeviceIdType.MESH

KRYLOV = 3


epsilon = 1e-06


def extended(x, sides, width):
    for axis, dim in sides:
        size, length = (lax.axis_size(axis), x.shape[dim])
        up = [(i, (i + 1) % size) for i in range(size - 1)]
        down = [(j, i) for i, j in up]
        last = lax.slice_in_dim(x, length - width, length, axis=dim)
        first = lax.slice_in_dim(x, 0, width, axis=dim)
        before = lax.ppermute(last, axis, up)
        after = lax.ppermute(first, axis, down)
        x = jnp.concatenate([before, x, after], axis=dim)
    return x


def entering(value, axis, join, neutral):
    count, mine = (lax.axis_size(axis), lax.axis_index(axis))
    pieces = jax.tree.map(lambda part: lax.all_gather(part, axis), value)
    so_far = jax.tree.map(
        lambda part, zero: jnp.full_like(part, 0) + jnp.asarray(zero, part.dtype), value, neutral
    )

    def step(position, so_far):
        longer = join(so_far, jax.tree.map(lambda part: part[position], pieces))
        return jax.tree.map(lambda new, old: jnp.where(position < mine, new, old), longer, so_far)

    return lax.fori_loop(0, count - 1, step, so_far)


def _reduce_kernel(stages, x_ref, o_ref, *scratch):
    count = len(stages)
    slots = scratch[:count]
    partial = scratch[count]
    sends = scratch[count + 1 : 2 * count + 1]
    recvs = scratch[2 * count + 1 :]
    barrier = pltpu.get_barrier_semaphore()
    peers = 0
    for axis, n in stages:
        mine = lax.axis_index(axis)
        for k in range(1, n):
            pl.semaphore_signal(
                barrier, inc=1, device_id={axis: lax.rem(mine + k, n)}, device_id_type=MESH
            )
            peers += 1
    pl.semaphore_wait(barrier, peers)
    source = x_ref
    for stage, (axis, n) in enumerate(stages):
        mine = lax.axis_index(axis)
        copies = []
        for k in range(1, n):
            copy = pltpu.make_async_remote_copy(
                src_ref=source,
                dst_ref=slots[stage].at[mine],
                send_sem=sends[stage].at[k],
                recv_sem=recvs[stage].at[mine],
                device_id={axis: lax.rem(mine + k, n)},
                device_id_type=MESH,
            )
            copy.start()
            copies.append(copy)
        slots[stage][mine] = source[...]
        for k in range(1, n):
            sender = lax.rem(mine + k, n)
            pltpu.make_async_remote_copy(
                src_ref=source,
                dst_ref=slots[stage].at[sender],
                send_sem=sends[stage].at[k],
                recv_sem=recvs[stage].at[sender],
                device_id={axis: sender},
                device_id_type=MESH,
            ).wait_recv()
        for copy in copies:
            copy.wait_send()
        total = slots[stage][0]
        for j in range(1, n):
            total = total + slots[stage][j]
        if stage == count - 1:
            o_ref[...] = total
        else:
            partial[...] = total
            source = partial


def all_sum(x, axes, mesh_shape, collective):
    stages = tuple((axis, mesh_shape[axis]) for axis in axes if mesh_shape[axis] > 1)
    rows, cols = x.shape
    scratch = [pltpu.VMEM((n, rows, cols), jnp.float32) for _, n in stages]
    scratch.append(pltpu.VMEM((rows, cols), jnp.float32))
    scratch += [pltpu.SemaphoreType.DMA((n,)) for _, n in stages]
    scratch += [pltpu.SemaphoreType.DMA((n,)) for _, n in stages]
    return pl.pallas_call(
        functools.partial(_reduce_kernel, stages),
        out_shape=jax.ShapeDtypeStruct((rows, cols), jnp.float32),
        in_specs=[pl.BlockSpec(memory_space=pltpu.VMEM)],
        out_specs=pl.BlockSpec(memory_space=pltpu.VMEM),
        scratch_shapes=scratch,
        compiler_params=pltpu.CompilerParams(collective_id=collective, has_side_effects=True),
    )(x.astype(jnp.float32))


def global_sum(rows_of_sums, mesh_shape):
    count = rows_of_sums.shape[0]
    padded = jnp.zeros((8, rows_of_sums.shape[1]), jnp.float32).at[:count].set(rows_of_sums)
    return all_sum(padded, ("blk", "sec"), mesh_shape, 0)[:count]


def _doubling(n):
    distances, d = [], 1
    while d < n:
        distances.append(d)
        d *= 2
    return tuple(distances)


def _greet(n, distances):
    barrier = pltpu.get_barrier_semaphore()
    mine = lax.axis_index("sec")
    for d in distances:
        for peer in (lax.rem(mine + d, n), lax.rem(mine + n - d, n)):
            pl.semaphore_signal(barrier, inc=1, device_id={"sec": peer}, device_id_type=MESH)
    pl.semaphore_wait(barrier, 2 * len(distances))


def _hop(n, d, source, slot, send_sem, recv_sem):
    mine = lax.axis_index("sec")
    copy = pltpu.make_async_remote_copy(
        src_ref=source,
        dst_ref=slot,
        send_sem=send_sem,
        recv_sem=recv_sem,
        device_id={"sec": lax.rem(mine + d, n)},
        device_id_type=MESH,
    )
    copy.start()
    copy.wait_recv()
    copy.wait_send()


RADIX = 4


def _plan(n):
    rounds, d = [], 1
    while d < n:
        rounds.append((d, tuple(j for j in range(1, RADIX) if j * d < n)))
        d *= RADIX
    return tuple(rounds)


def _plan_peers(rounds):
    return tuple(sorted({j * d for d, js in rounds for j in js} | {1}))


def _send_all(n, sec, sources, slots, sends, recvs, flat, d, js):
    copies = []
    for i, j in enumerate(js):
        copy = pltpu.make_async_remote_copy(
            src_ref=sources,
            dst_ref=slots.at[flat + i],
            send_sem=sends.at[flat + i],
            recv_sem=recvs.at[flat + i],
            device_id={"sec": lax.rem(sec + j * d, n)},
            device_id_type=MESH,
        )
        copy.start()
        copies.append(copy)
    for copy in copies:
        copy.wait_recv()
    for copy in copies:
        copy.wait_send()


def _spread(n_sec, n_blk, offsets, piece_ref, slots, sends, recvs):
    sec, blk = lax.axis_index("sec"), lax.axis_index("blk")

    def copy(o, j, index):
        return pltpu.make_async_remote_copy(
            src_ref=piece_ref,
            dst_ref=slots.at[index],
            send_sem=sends.at[(o - 1) * n_blk + j],
            recv_sem=recvs.at[index],
            device_id={"sec": lax.rem(sec + o, n_sec), "blk": j},
            device_id_type=MESH,
        )

    outgoing = [
        copy(o, j, (o - 1) * n_blk + blk) for o in range(1, offsets + 1) for j in range(n_blk)
    ]
    for c in outgoing:
        c.start()
    for o in range(1, offsets + 1):
        for j in range(n_blk):
            copy(o, j, (o - 1) * n_blk + j).wait_recv()
    for c in outgoing:
        c.wait_send()


def _assemble(n_blk, offsets, slots, mats):
    piece = slots.shape[1]
    for o in range(offsets):
        for j in range(n_blk):
            mats[o, j * piece : (j + 1) * piece, :] = slots[o * n_blk + j]


def _greet_all(n_sec, n_blk, offsets, rounds, blk_peers, stages=()):
    barrier = pltpu.get_barrier_semaphore()
    sec, blk = lax.axis_index("sec"), lax.axis_index("blk")
    count = _signal_stages(barrier, stages)
    if blk_peers:
        for k in range(1, n_blk):
            pl.semaphore_signal(
                barrier, inc=1, device_id={"blk": lax.rem(blk + k, n_blk)}, device_id_type=MESH
            )
            count += 1
    for o in range(1, offsets + 1):
        for j in range(n_blk):
            for peer in (lax.rem(sec + o, n_sec), lax.rem(sec + n_sec - o, n_sec)):
                pl.semaphore_signal(
                    barrier, inc=1, device_id={"sec": peer, "blk": j}, device_id_type=MESH
                )
                count += 1
    for d in sorted({j * d for d, js in rounds[1:] for j in js}):
        for peer in (lax.rem(sec + d, n_sec), lax.rem(sec + n_sec - d, n_sec)):
            pl.semaphore_signal(barrier, inc=1, device_id={"sec": peer}, device_id_type=MESH)
            count += 1
    pl.semaphore_wait(barrier, count)


def _maps_body(n, n_blk, rounds, e_ref, a_ref, eslots, emat, current, slots, esend, erecv, sends, recvs):
    sec = lax.axis_index("sec")
    first = rounds[0][1]
    offsets = len(first) + 1
    _spread(n, n_blk, offsets, e_ref, eslots, esend, erecv)
    _assemble(n_blk, offsets, eslots, emat)
    joined = emat[0]
    for i, j in enumerate(first):
        a_ref[i] = joined
        joined = jnp.dot(
            joined, emat[j], precision=lax.Precision.HIGHEST, preferred_element_type=jnp.float32
        )
    current[...] = joined
    flat = len(first)
    for k in range(1, len(rounds)):
        d, js = rounds[k]
        onward = k < len(rounds) - 1
        if onward or len(js) > 1:
            _send_all(n, sec, current, slots, sends, recvs, flat, d, js)
        joined = current[...]
        for i, j in enumerate(js):
            a_ref[flat + i] = joined
            if onward or i < len(js) - 1:
                joined = jnp.dot(
                    joined, slots[flat + i], precision=lax.Precision.HIGHEST,
                    preferred_element_type=jnp.float32,
                )
        if onward:
            current[...] = joined
        flat += len(js)


def _setup_kernel(
    n_sec, n_blk, rounds, x_ref, up_ref, be_ref, back_ref, inv_ref, pick_ref,
    g_ref, b_ref, a_ref, gain_ref, chain_ref, *scratch
):
    phase_scratch = scratch[:9]
    pslots, psend, precv, epiece = scratch[9:13]
    maps_scratch = scratch[13:]
    sec, blk = lax.axis_index("sec"), lax.axis_index("blk")
    offsets = len(rounds[0][1]) + 1
    _greet_all(n_sec, n_blk, offsets, rounds, True)
    piece = epiece.shape[0]
    mine = be_ref.at[pl.ds(pl.multiple_of(blk * piece, 8), piece)]
    _operator_phase(n_sec, n_blk, x_ref, up_ref, mine, g_ref, b_ref, a_ref, phase_scratch)

    def blk_copy(k, target, slot):
        return pltpu.make_async_remote_copy(
            src_ref=back_ref,
            dst_ref=pslots.at[slot],
            send_sem=psend.at[k],
            recv_sem=precv.at[slot],
            device_id={"blk": target},
            device_id_type=MESH,
        )

    outgoing = [blk_copy(k, lax.rem(blk + k, n_blk), blk) for k in range(1, n_blk)]
    for copy in outgoing:
        copy.start()
    pslots[blk] = back_ref[...]
    for k in range(1, n_blk):
        sender = lax.rem(blk + k, n_blk)
        blk_copy(k, sender, sender).wait_recv()
    for copy in outgoing:
        copy.wait_send()
    rows = back_ref.shape[0]
    gain = jnp.dot(inv_ref[:, 0:rows], pslots[0], preferred_element_type=jnp.float32)
    for j in range(1, n_blk):
        gain = gain + jnp.dot(
            inv_ref[:, j * rows : (j + 1) * rows], pslots[j], preferred_element_type=jnp.float32
        )
    gain_ref[...] = gain
    epiece[...] = -jnp.dot(
        pick_ref[...], gain, precision=lax.Precision.HIGHEST, preferred_element_type=jnp.float32
    )
    _maps_body(n_sec, n_blk, rounds, epiece, chain_ref, *maps_scratch)


def setup_exchange(x, up_t, be_t, back, inverse, picks, n_sec, n_blk):
    cases, width = x.shape
    panel, _ = up_t.shape
    piece = panel // n_blk
    rows, panel_width = back.shape
    rounds = _plan(n_sec)
    total = sum(len(js) for _, js in rounds)
    offsets = len(rounds[0][1]) + 1
    return pl.pallas_call(
        functools.partial(_setup_kernel, n_sec, n_blk, rounds),
        out_shape=(
            jax.ShapeDtypeStruct((cases, n_blk * width), x.dtype),
            jax.ShapeDtypeStruct((panel, cases), jnp.float32),
            jax.ShapeDtypeStruct((piece, cases), jnp.float32),
            jax.ShapeDtypeStruct((rows, panel_width), jnp.float32),
            jax.ShapeDtypeStruct((total, panel_width, panel_width), jnp.float32),
        ),
        in_specs=[pl.BlockSpec(memory_space=pltpu.VMEM)] * 6,
        out_specs=[pl.BlockSpec(memory_space=pltpu.VMEM)] * 5,
        scratch_shapes=_operator_scratch(n_blk, cases, width, x.dtype, piece, cases)
        + [
            pltpu.VMEM((n_blk, rows, panel_width), back.dtype),
            pltpu.SemaphoreType.DMA((n_blk,)),
            pltpu.SemaphoreType.DMA((n_blk,)),
            pltpu.VMEM((piece, panel_width), jnp.float32),
            pltpu.VMEM((offsets * n_blk, piece, panel_width), jnp.float32),
            pltpu.VMEM((offsets, panel_width, panel_width), jnp.float32),
            pltpu.VMEM((panel_width, panel_width), jnp.float32),
            pltpu.VMEM((total, panel_width, panel_width), jnp.float32),
            pltpu.SemaphoreType.DMA((offsets * n_blk,)),
            pltpu.SemaphoreType.DMA((offsets * n_blk,)),
            pltpu.SemaphoreType.DMA((total,)),
            pltpu.SemaphoreType.DMA((total,)),
        ],
        compiler_params=pltpu.CompilerParams(collective_id=3, has_side_effects=True),
    )(x, up_t, be_t, back, inverse, picks)


def _gather_kernel(n, x_ref, o_ref, slots, sends, recvs):
    mine = lax.axis_index("blk")
    barrier = pltpu.get_barrier_semaphore()
    for k in range(1, n):
        pl.semaphore_signal(
            barrier, inc=1, device_id={"blk": lax.rem(mine + k, n)}, device_id_type=MESH
        )
    pl.semaphore_wait(barrier, n - 1)
    copies = []
    for k in range(1, n):
        copy = pltpu.make_async_remote_copy(
            src_ref=x_ref,
            dst_ref=slots.at[mine],
            send_sem=sends.at[k],
            recv_sem=recvs.at[mine],
            device_id={"blk": lax.rem(mine + k, n)},
            device_id_type=MESH,
        )
        copy.start()
        copies.append(copy)
    slots[mine] = x_ref[...]
    for k in range(1, n):
        sender = lax.rem(mine + k, n)
        pltpu.make_async_remote_copy(
            src_ref=x_ref,
            dst_ref=slots.at[sender],
            send_sem=sends.at[k],
            recv_sem=recvs.at[sender],
            device_id={"blk": sender},
            device_id_type=MESH,
        ).wait_recv()
    for copy in copies:
        copy.wait_send()
    width = x_ref.shape[1]
    for j in range(n):
        o_ref[:, j * width : (j + 1) * width] = slots[j]


def gather_blk(x, n):
    rows, width = x.shape
    return pl.pallas_call(
        functools.partial(_gather_kernel, n),
        out_shape=jax.ShapeDtypeStruct((rows, n * width), x.dtype),
        in_specs=[pl.BlockSpec(memory_space=pltpu.VMEM)],
        out_specs=pl.BlockSpec(memory_space=pltpu.VMEM),
        scratch_shapes=[
            pltpu.VMEM((n, rows, width), x.dtype),
            pltpu.SemaphoreType.DMA((n,)),
            pltpu.SemaphoreType.DMA((n,)),
        ],
        compiler_params=pltpu.CompilerParams(collective_id=4, has_side_effects=True),
    )(x)


def _operator_phase(n_sec, n_blk, x_ref, up_ref, piece_ref, g_ref, b_ref, a_ref, scratch):
    gslots, bslots, aslots, gsend, grecv, bsend, brecv, asend, arecv = scratch
    sec, blk = lax.axis_index("sec"), lax.axis_index("blk")
    nxt, prv = lax.rem(sec + 1, n_sec), lax.rem(sec + n_sec - 1, n_sec)
    piece = bslots.shape[1]
    copies = []
    for k in range(1, n_blk):
        copies.append(
            pltpu.make_async_remote_copy(
                src_ref=x_ref,
                dst_ref=gslots.at[blk],
                send_sem=gsend.at[k],
                recv_sem=grecv.at[blk],
                device_id={"blk": lax.rem(blk + k, n_blk)},
                device_id_type=MESH,
            )
        )
    for j in range(n_blk):
        copies.append(
            pltpu.make_async_remote_copy(
                src_ref=piece_ref,
                dst_ref=bslots.at[blk],
                send_sem=bsend.at[j],
                recv_sem=brecv.at[blk],
                device_id={"sec": nxt, "blk": j},
                device_id_type=MESH,
            )
        )
        copies.append(
            pltpu.make_async_remote_copy(
                src_ref=up_ref.at[pl.ds(j * piece, piece)],
                dst_ref=aslots.at[blk],
                send_sem=asend.at[j],
                recv_sem=arecv.at[blk],
                device_id={"sec": prv, "blk": j},
                device_id_type=MESH,
            )
        )
    for copy in copies:
        copy.start()
    gslots[blk] = x_ref[...]
    for k in range(1, n_blk):
        sender = lax.rem(blk + k, n_blk)
        pltpu.make_async_remote_copy(
            src_ref=x_ref,
            dst_ref=gslots.at[sender],
            send_sem=gsend.at[k],
            recv_sem=grecv.at[sender],
            device_id={"blk": sender},
            device_id_type=MESH,
        ).wait_recv()
    for j in range(n_blk):
        pltpu.make_async_remote_copy(
            src_ref=piece_ref,
            dst_ref=bslots.at[j],
            send_sem=bsend.at[j],
            recv_sem=brecv.at[j],
            device_id={"sec": prv, "blk": j},
            device_id_type=MESH,
        ).wait_recv()
        pltpu.make_async_remote_copy(
            src_ref=up_ref.at[pl.ds(j * piece, piece)],
            dst_ref=aslots.at[j],
            send_sem=asend.at[j],
            recv_sem=arecv.at[j],
            device_id={"sec": nxt, "blk": j},
            device_id_type=MESH,
        ).wait_recv()
    for copy in copies:
        copy.wait_send()
    width = x_ref.shape[1]
    for j in range(n_blk):
        g_ref[:, j * width : (j + 1) * width] = gslots[j]
        b_ref[j * piece : (j + 1) * piece, :] = jnp.where(
            sec >= 1, bslots[j], jnp.zeros_like(bslots[j])
        )
    total = aslots[0]
    for j in range(1, n_blk):
        total = total + aslots[j]
    a_ref[...] = jnp.where(sec <= n_sec - 2, total, jnp.zeros_like(total))


def _operator_scratch(n_blk, rows, width, dtype, piece, cases):
    return [
        pltpu.VMEM((n_blk, rows, width), dtype),
        pltpu.VMEM((n_blk, piece, cases), jnp.float32),
        pltpu.VMEM((n_blk, piece, cases), jnp.float32),
    ] + [pltpu.SemaphoreType.DMA((n_blk,))] * 6


def _operator_kernel(n_sec, n_blk, x_ref, up_ref, be_ref, g_ref, b_ref, a_ref, *scratch):
    sec, blk = lax.axis_index("sec"), lax.axis_index("blk")
    nxt, prv = lax.rem(sec + 1, n_sec), lax.rem(sec + n_sec - 1, n_sec)
    piece = scratch[1].shape[1]
    barrier = pltpu.get_barrier_semaphore()
    for k in range(1, n_blk):
        pl.semaphore_signal(
            barrier, inc=1, device_id={"blk": lax.rem(blk + k, n_blk)}, device_id_type=MESH
        )
    for j in range(n_blk):
        for other in (nxt, prv):
            pl.semaphore_signal(
                barrier, inc=1, device_id={"sec": other, "blk": j}, device_id_type=MESH
            )
    pl.semaphore_wait(barrier, 3 * n_blk - 1)
    mine = be_ref.at[pl.ds(pl.multiple_of(blk * piece, 8), piece)]
    _operator_phase(n_sec, n_blk, x_ref, up_ref, mine, g_ref, b_ref, a_ref, scratch)


def operator_exchange(x, up_t, be_t, n_sec, n_blk):
    rows, width = x.shape
    panel, cases = up_t.shape
    piece = panel // n_blk
    return pl.pallas_call(
        functools.partial(_operator_kernel, n_sec, n_blk),
        out_shape=(
            jax.ShapeDtypeStruct((rows, n_blk * width), x.dtype),
            jax.ShapeDtypeStruct((panel, cases), jnp.float32),
            jax.ShapeDtypeStruct((piece, cases), jnp.float32),
        ),
        in_specs=[pl.BlockSpec(memory_space=pltpu.VMEM)] * 3,
        out_specs=[pl.BlockSpec(memory_space=pltpu.VMEM)] * 3,
        scratch_shapes=_operator_scratch(n_blk, rows, width, x.dtype, piece, cases),
        compiler_params=pltpu.CompilerParams(collective_id=5, has_side_effects=True),
    )(x, up_t, be_t)


def _precondition_kernel(
    n_sec, n_blk, rounds, stages, depth, basis_ref, image_ref, inv_ref, pick_ref, u_ref,
    gain_ref, ahead_ref, h_ref, next_ref, d_ref, g_ref, b_ref, a_ref, *scratch
):
    gslots, fpiece, fslots, fmat, carry, slots, gsend, grecv, fsend, frecv, ssend, srecv = scratch[:12]
    rounded, upward, own_piece, x_ref = scratch[12:16]
    phase_scratch = scratch[16:25]
    project_scratch = scratch[25:]
    sec, blk = lax.axis_index("sec"), lax.axis_index("blk")
    first = rounds[0][1]
    offsets = len(first) + 1
    _greet_all(n_sec, n_blk, offsets, rounds, True, stages)
    _project_body(stages, depth, basis_ref, image_ref, h_ref, next_ref, project_scratch)
    x_ref[...] = next_ref[...].astype(x_ref.dtype)

    def blk_copy(k, target, slot):
        return pltpu.make_async_remote_copy(
            src_ref=x_ref,
            dst_ref=gslots.at[slot],
            send_sem=gsend.at[k],
            recv_sem=grecv.at[slot],
            device_id={"blk": target},
            device_id_type=MESH,
        )

    outgoing = [blk_copy(k, lax.rem(blk + k, n_blk), blk) for k in range(1, n_blk)]
    for copy in outgoing:
        copy.start()
    gslots[blk] = x_ref[...]
    for k in range(1, n_blk):
        sender = lax.rem(blk + k, n_blk)
        blk_copy(k, sender, sender).wait_recv()
    for copy in outgoing:
        copy.wait_send()
    width = x_ref.shape[1]
    contract = (((1,), (1,)), ((), ()))
    folded = lax.dot_general(
        gslots[0], inv_ref[:, 0:width], contract, preferred_element_type=jnp.float32
    )
    for j in range(1, n_blk):
        folded = folded + lax.dot_general(
            gslots[j],
            inv_ref[:, j * width : (j + 1) * width],
            contract,
            preferred_element_type=jnp.float32,
        )
    fpiece[...] = lax.dot_general(
        pick_ref[...], folded, contract, precision=lax.Precision.HIGHEST,
        preferred_element_type=jnp.float32,
    )
    _spread(n_sec, n_blk, offsets, fpiece, fslots, fsend, frecv)
    _assemble(n_blk, offsets, fslots, fmat)
    joined = jnp.where(sec >= 1, fmat[0], jnp.zeros_like(fmat[0]))
    for i, j in enumerate(first):
        term = jnp.dot(
            u_ref[i], fmat[j], precision=lax.Precision.HIGHEST, preferred_element_type=jnp.float32
        )
        joined = joined + jnp.where(sec >= j + 1, term, jnp.zeros_like(term))
    carry[1] = joined
    flat = len(first)
    for k in range(1, len(rounds)):
        d, js = rounds[k]
        _send_all(n_sec, sec, carry.at[k], slots, ssend, srecv, flat, d, js)
        joined = carry[k]
        for i, j in enumerate(js):
            term = jnp.dot(
                u_ref[flat + i], slots[flat + i], precision=lax.Precision.HIGHEST,
                preferred_element_type=jnp.float32,
            )
            joined = joined + jnp.where(sec >= j * d, term, jnp.zeros_like(term))
        carry[k + 1] = joined
        flat += len(js)
    before = carry[len(rounds)].T
    direction = folded - lax.dot_general(
        before, gain_ref[...], contract, precision=lax.Precision.HIGHEST,
        preferred_element_type=jnp.float32,
    )
    d_ref[...] = direction
    rounded[...] = direction.astype(rounded.dtype)
    upward[...] = jnp.dot(
        rounded[...], ahead_ref[...], preferred_element_type=jnp.float32
    ).T
    own_piece[...] = lax.dot_general(
        pick_ref[...], rounded[...].astype(jnp.float32), contract,
        precision=lax.Precision.HIGHEST, preferred_element_type=jnp.float32,
    )
    _operator_phase(n_sec, n_blk, rounded, upward, own_piece, g_ref, b_ref, a_ref, phase_scratch)


def precondition_sweep(basis, image, inverse, picks, chain, gain, ahead, mesh_shape, depth):
    n_sec, n_blk = mesh_shape["sec"], mesh_shape["blk"]
    stages = _global_stages(mesh_shape)
    cases, width = image.shape
    piece, _ = picks.shape
    panel = piece * n_blk
    plan = _plan(n_sec)
    rounds = len(plan)
    total = sum(len(js) for _, js in plan)
    offsets = len(plan[0][1]) + 1
    dtype = jnp.bfloat16
    return pl.pallas_call(
        functools.partial(_precondition_kernel, n_sec, n_blk, plan, stages, depth),
        out_shape=(
            jax.ShapeDtypeStruct((8, cases), jnp.float32),
            jax.ShapeDtypeStruct((cases, width), jnp.float32),
            jax.ShapeDtypeStruct((cases, width), jnp.float32),
            jax.ShapeDtypeStruct((cases, n_blk * width), dtype),
            jax.ShapeDtypeStruct((panel, cases), jnp.float32),
            jax.ShapeDtypeStruct((piece, cases), jnp.float32),
        ),
        in_specs=[pl.BlockSpec(memory_space=pltpu.VMEM)] * 7,
        out_specs=[pl.BlockSpec(memory_space=pltpu.VMEM)] * 6,
        scratch_shapes=[
            pltpu.VMEM((n_blk, cases, width), dtype),
            pltpu.VMEM((piece, cases), jnp.float32),
            pltpu.VMEM((offsets * n_blk, piece, cases), jnp.float32),
            pltpu.VMEM((offsets, panel, cases), jnp.float32),
            pltpu.VMEM((rounds + 1, panel, cases), jnp.float32),
            pltpu.VMEM((total, panel, cases), jnp.float32),
            pltpu.SemaphoreType.DMA((n_blk,)),
            pltpu.SemaphoreType.DMA((n_blk,)),
            pltpu.SemaphoreType.DMA((offsets * n_blk,)),
            pltpu.SemaphoreType.DMA((offsets * n_blk,)),
            pltpu.SemaphoreType.DMA((total,)),
            pltpu.SemaphoreType.DMA((total,)),
            pltpu.VMEM((cases, width), dtype),
            pltpu.VMEM((panel, cases), jnp.float32),
            pltpu.VMEM((piece, cases), jnp.float32),
            pltpu.VMEM((cases, width), dtype),
        ]
        + _operator_scratch(n_blk, cases, width, dtype, piece, cases)
        + _project_scratch(stages, cases),
        compiler_params=pltpu.CompilerParams(collective_id=10 + depth, has_side_effects=True),
    )(basis, image, inverse, picks, chain, gain, ahead)


def _exchange_sum(stages, source, slots, partial, sends, recvs, out):
    count = len(stages)
    for stage, (axis, n) in enumerate(stages):
        mine = lax.axis_index(axis)
        copies = []
        for k in range(1, n):
            copy = pltpu.make_async_remote_copy(
                src_ref=source,
                dst_ref=slots[stage].at[mine],
                send_sem=sends[stage].at[k],
                recv_sem=recvs[stage].at[mine],
                device_id={axis: lax.rem(mine + k, n)},
                device_id_type=MESH,
            )
            copy.start()
            copies.append(copy)
        slots[stage][mine] = source[...]
        for k in range(1, n):
            sender = lax.rem(mine + k, n)
            pltpu.make_async_remote_copy(
                src_ref=source,
                dst_ref=slots[stage].at[sender],
                send_sem=sends[stage].at[k],
                recv_sem=recvs[stage].at[sender],
                device_id={axis: sender},
                device_id_type=MESH,
            ).wait_recv()
        for copy in copies:
            copy.wait_send()
        total = slots[stage][0]
        for j in range(1, n):
            total = total + slots[stage][j]
        if stage == count - 1:
            out[...] = total
        else:
            partial[...] = total
            source = partial


def _project_scratch(stages, cases):
    def buffers():
        out = [pltpu.VMEM((n, 8, cases), jnp.float32) for _, n in stages]
        out.append(pltpu.VMEM((8, cases), jnp.float32))
        out += [pltpu.SemaphoreType.DMA((n,)) for _, n in stages]
        out += [pltpu.SemaphoreType.DMA((n,)) for _, n in stages]
        return out

    return buffers() + buffers() + [pltpu.VMEM((8, cases), jnp.float32)] * 2


def _project_body(stages, depth, basis_ref, image_ref, h_ref, next_ref, scratch):
    count = len(stages)
    first, second = scratch[: 3 * count + 1], scratch[3 * count + 1 : 6 * count + 2]
    rows, work = scratch[6 * count + 2 : 6 * count + 4]
    highest = lax.Precision.HIGHEST
    contract = (((1,), (1,)), ((), ()))
    image = image_ref[...]
    ones = jnp.ones((8, image.shape[1]), jnp.float32)
    eye = (
        lax.broadcasted_iota(jnp.int32, (image.shape[0],) * 2, 0)
        == lax.broadcasted_iota(jnp.int32, (image.shape[0],) * 2, 1)
    ).astype(jnp.float32)

    def run(buffers, source, out):
        slots = buffers[:count]
        partial = buffers[count]
        sends = buffers[count + 1 : 2 * count + 1]
        recvs = buffers[2 * count + 1 :]
        _exchange_sum(stages, source, slots, partial, sends, recvs, out)

    if depth > 0:
        rows[...] = jnp.zeros_like(rows)
        for i in range(depth):
            summed = lax.dot_general(
                ones, image * basis_ref[i], contract, precision=highest,
                preferred_element_type=jnp.float32,
            )
            rows[i : i + 1, :] = summed[0:1, :]
        run(first, rows, h_ref)
        columns = lax.dot_general(
            eye, h_ref[...], contract, precision=highest, preferred_element_type=jnp.float32
        )
        for i in range(depth):
            image = image - columns[:, i : i + 1] * basis_ref[i]
    else:
        h_ref[...] = jnp.zeros_like(h_ref)
    work[...] = lax.dot_general(
        ones, image * image, contract, precision=highest, preferred_element_type=jnp.float32
    )
    run(second, work, rows)
    length = jnp.sqrt(rows[...] + epsilon)
    h_ref[depth : depth + 1, :] = length[0:1, :]
    scale = lax.dot_general(
        eye, length, contract, precision=highest, preferred_element_type=jnp.float32
    )
    next_ref[...] = image / scale[:, 0:1]


def _signal_stages(barrier, stages):
    peers = 0
    for axis, n in stages:
        mine = lax.axis_index(axis)
        for k in range(1, n):
            pl.semaphore_signal(
                barrier, inc=1, device_id={axis: lax.rem(mine + k, n)}, device_id_type=MESH
            )
            peers += 1
    return peers


def _project_kernel(stages, depth, basis_ref, image_ref, h_ref, next_ref, *scratch):
    barrier = pltpu.get_barrier_semaphore()
    pl.semaphore_wait(barrier, _signal_stages(barrier, stages))
    _project_body(stages, depth, basis_ref, image_ref, h_ref, next_ref, scratch)


def _global_stages(mesh_shape):
    return tuple((axis, mesh_shape[axis]) for axis in ("blk", "sec") if mesh_shape[axis] > 1)


def project(stacked, image, mesh_shape):
    depth, cases, width = stacked.shape
    stages = _global_stages(mesh_shape)
    return pl.pallas_call(
        functools.partial(_project_kernel, stages, depth),
        out_shape=(
            jax.ShapeDtypeStruct((8, cases), jnp.float32),
            jax.ShapeDtypeStruct((cases, width), jnp.float32),
        ),
        in_specs=[pl.BlockSpec(memory_space=pltpu.VMEM)] * 2,
        out_specs=[pl.BlockSpec(memory_space=pltpu.VMEM)] * 2,
        scratch_shapes=_project_scratch(stages, cases),
        compiler_params=pltpu.CompilerParams(collective_id=6 + depth, has_side_effects=True),
    )(stacked, image)


def least_squares(columns, beta, depth):
    zero = jnp.zeros_like(beta)
    upper = [
        [columns[j][i] if i <= j + 1 else zero for j in range(depth)] for i in range(depth + 1)
    ]
    rhs = [beta] + [zero] * depth
    for column in range(depth):
        upper_row, lower_row = upper[column], upper[column + 1]
        radius = jnp.sqrt(upper_row[column] ** 2 + lower_row[column] ** 2)
        cosine = upper_row[column] / radius
        sine_term = lower_row[column] / radius
        upper[column] = [cosine * a + sine_term * b for a, b in zip(upper_row, lower_row)]
        upper[column + 1] = [-sine_term * a + cosine * b for a, b in zip(upper_row, lower_row)]
        first_rhs, second_rhs = rhs[column], rhs[column + 1]
        rhs[column] = cosine * first_rhs + sine_term * second_rhs
        rhs[column + 1] = -sine_term * first_rhs + cosine * second_rhs
    weights = [zero] * depth
    for column in reversed(range(depth)):
        remain = rhs[column]
        if column + 1 < depth:
            tail = upper[column][column + 1] * weights[column + 1]
            for k in range(column + 2, depth):
                tail = tail + upper[column][k] * weights[k]
            remain = remain - tail
        weights[column] = remain / upper[column][column]
    return weights

def local(
    mesh_shape,
    state_now, source, fan_gain, section_block, block_inverse, back_panel, ahead_panel, interface
):
    highest = lax.Precision.HIGHEST
    cases, node_rows = state_now.shape
    panel_width = back_panel.shape[1]
    indices = interface[0]
    first_row = lax.axis_index("blk") * node_rows
    selector = (indices[None, :] == first_row + jnp.arange(node_rows)[:, None]).astype(jnp.float32)
    contract = (((1,), (1,)), ((), ()))

    own_piece = panel_width // mesh_shape["blk"]
    own_picks = lax.dynamic_slice_in_dim(selector, lax.axis_index("blk") * own_piece, own_piece, 1).T

    def section_terms(dense_part, behind_vals, piece):
        width = piece.shape[1]
        dense_part = lax.dot_general(
            piece, section_block, contract, preferred_element_type=jnp.float32
        )
        picker = (indices[None, :] == jnp.arange(width)[:, None]).astype(jnp.bfloat16)
        behind_vals = jnp.dot(piece, picker, preferred_element_type=jnp.float32)
        return (dense_part, behind_vals)

    def fold_section(carry, piece):
        return section_terms(carry[0], carry[1], piece)

    n_sec, n_blk = mesh_shape["sec"], mesh_shape["blk"]
    piece = panel_width // n_blk
    local_picks = lax.dynamic_slice_in_dim(selector, lax.axis_index("blk") * piece, piece, 1)

    def finish(gathered, behind_t, ahead_piece):
        dense_part = lax.dot_general(
            gathered, section_block, contract, preferred_element_type=jnp.float32
        )
        lower_term = lax.dot_general(
            behind_t.astype(jnp.bfloat16),
            back_panel,
            (((0,), (1,)), ((), ())),
            preferred_element_type=jnp.float32,
        )
        upper_term = lax.dot_general(
            ahead_piece, local_picks, (((0,), (1,)), ((), ())), precision=highest
        )
        return dense_part + lower_term + upper_term

    def operator(vector):
        rounded = vector.astype(jnp.bfloat16)
        up_t = lax.dot_general(
            ahead_panel, rounded, (((0,), (1,)), ((), ())), preferred_element_type=jnp.float32
        )
        be_t = lax.dot_general(
            selector.astype(jnp.bfloat16),
            rounded,
            (((0,), (1,)), ((), ())),
            preferred_element_type=jnp.float32,
        )
        return finish(*operator_exchange(rounded, up_t, be_t, n_sec, n_blk))

    def compose(earlier, later):
        first_map, first_value = earlier
        second_map, second_value = later
        joined_map = jnp.dot(second_map, first_map, precision=highest)
        joined_value = jnp.dot(first_value, second_map.T, precision=highest) + second_value
        return (joined_map, joined_value)

    def lengths(vector):
        return jnp.sqrt(global_sum(jnp.sum(vector * vector, axis=1)[None], mesh_shape)[0] + epsilon)

    bent = jnp.tanh(state_now)
    state_rounded = state_now.astype(jnp.bfloat16)
    gathered, behind_t, ahead_piece, gain_panel, chain = setup_exchange(
        state_rounded,
        lax.dot_general(
            ahead_panel, state_rounded, (((0,), (1,)), ((), ())), preferred_element_type=jnp.float32
        ),
        lax.dot_general(
            selector.astype(jnp.bfloat16),
            state_rounded,
            (((0,), (1,)), ((), ())),
            preferred_element_type=jnp.float32,
        ),
        back_panel,
        block_inverse,
        own_picks,
        n_sec,
        n_blk,
    )
    residual = source - finish(gathered, behind_t, ahead_piece) - fan_gain[None, :] * bent
    jac_diag = fan_gain[None, :] * (1.0 - bent * bent)
    columns = []
    basis = []
    directions = []
    product = residual
    beta = None
    for column in range(KRYLOV):
        stacked = jnp.stack(basis) if basis else residual[None]
        sums, following, direction, gathered, behind_t, ahead_piece = precondition_sweep(
            stacked, product, block_inverse, own_picks, chain, gain_panel, ahead_panel,
            mesh_shape, len(basis),
        )
        if column == 0:
            beta = sums[0]
        else:
            columns.append(sums[: column + 1])
        basis.append(following)
        directions.append(direction)
        product = finish(gathered, behind_t, ahead_piece) + jac_diag * direction
    sums, _ = project(jnp.stack(basis), product, mesh_shape)
    columns.append(sums[: KRYLOV + 1])
    weights = least_squares(columns, beta, KRYLOV)
    update = jnp.zeros_like(state_now)
    for column in range(KRYLOV):
        update = update + weights[column][:, None] * directions[column]
    return state_now + update


def solution(mesh):
    in_specs = (
        P(None, ("sec", "blk")),
        P(None, ("sec", "blk")),
        P(("sec", "blk")),
        P(("sec", "blk"), None),
        P(("sec", "blk"), None),
        P(("sec", "blk"), None),
        P(("sec", "blk"), None),
        P("sec", None),
    )
    out_specs = P(None, ("sec", "blk"))
    return jax.shard_map(functools.partial(local, dict(mesh.shape)), mesh=mesh, in_specs=in_specs, out_specs=out_specs, check_vma=False)
```

```python
import functools

import jax
import jax.numpy as jnp
from jax import lax
from jax.experimental import pallas as pl
from jax.experimental.pallas import tpu as pltpu
from jax.sharding import PartitionSpec as P

MESH = pl.DeviceIdType.MESH

KRYLOV = 3


epsilon = 1e-06


def extended(x, sides, width):
    for axis, dim in sides:
        size, length = (lax.axis_size(axis), x.shape[dim])
        up = [(i, (i + 1) % size) for i in range(size - 1)]
        down = [(j, i) for i, j in up]
        last = lax.slice_in_dim(x, length - width, length, axis=dim)
        first = lax.slice_in_dim(x, 0, width, axis=dim)
        before = lax.ppermute(last, axis, up)
        after = lax.ppermute(first, axis, down)
        x = jnp.concatenate([before, x, after], axis=dim)
    return x


def entering(value, axis, join, neutral):
    count, mine = (lax.axis_size(axis), lax.axis_index(axis))
    pieces = jax.tree.map(lambda part: lax.all_gather(part, axis), value)
    so_far = jax.tree.map(
        lambda part, zero: jnp.full_like(part, 0) + jnp.asarray(zero, part.dtype), value, neutral
    )

    def step(position, so_far):
        longer = join(so_far, jax.tree.map(lambda part: part[position], pieces))
        return jax.tree.map(lambda new, old: jnp.where(position < mine, new, old), longer, so_far)

    return lax.fori_loop(0, count - 1, step, so_far)


def _reduce_kernel(stages, x_ref, o_ref, *scratch):
    count = len(stages)
    slots = scratch[:count]
    partial = scratch[count]
    sends = scratch[count + 1 : 2 * count + 1]
    recvs = scratch[2 * count + 1 :]
    barrier = pltpu.get_barrier_semaphore()
    peers = 0
    for axis, n in stages:
        mine = lax.axis_index(axis)
        for k in range(1, n):
            pl.semaphore_signal(
                barrier, inc=1, device_id={axis: lax.rem(mine + k, n)}, device_id_type=MESH
            )
            peers += 1
    pl.semaphore_wait(barrier, peers)
    source = x_ref
    for stage, (axis, n) in enumerate(stages):
        mine = lax.axis_index(axis)
        copies = []
        for k in range(1, n):
            copy = pltpu.make_async_remote_copy(
                src_ref=source,
                dst_ref=slots[stage].at[mine],
                send_sem=sends[stage].at[k],
                recv_sem=recvs[stage].at[mine],
                device_id={axis: lax.rem(mine + k, n)},
                device_id_type=MESH,
            )
            copy.start()
            copies.append(copy)
        slots[stage][mine] = source[...]
        for k in range(1, n):
            sender = lax.rem(mine + k, n)
            pltpu.make_async_remote_copy(
                src_ref=source,
                dst_ref=slots[stage].at[sender],
                send_sem=sends[stage].at[k],
                recv_sem=recvs[stage].at[sender],
                device_id={axis: sender},
                device_id_type=MESH,
            ).wait_recv()
        for copy in copies:
            copy.wait_send()
        total = slots[stage][0]
        for j in range(1, n):
            total = total + slots[stage][j]
        if stage == count - 1:
            o_ref[...] = total
        else:
            partial[...] = total
            source = partial


def all_sum(x, axes, mesh_shape, collective):
    stages = tuple((axis, mesh_shape[axis]) for axis in axes if mesh_shape[axis] > 1)
    rows, cols = x.shape
    scratch = [pltpu.VMEM((n, rows, cols), jnp.float32) for _, n in stages]
    scratch.append(pltpu.VMEM((rows, cols), jnp.float32))
    scratch += [pltpu.SemaphoreType.DMA((n,)) for _, n in stages]
    scratch += [pltpu.SemaphoreType.DMA((n,)) for _, n in stages]
    return pl.pallas_call(
        functools.partial(_reduce_kernel, stages),
        out_shape=jax.ShapeDtypeStruct((rows, cols), jnp.float32),
        in_specs=[pl.BlockSpec(memory_space=pltpu.VMEM)],
        out_specs=pl.BlockSpec(memory_space=pltpu.VMEM),
        scratch_shapes=scratch,
        compiler_params=pltpu.CompilerParams(collective_id=collective, has_side_effects=True),
    )(x.astype(jnp.float32))


def global_sum(rows_of_sums, mesh_shape):
    count = rows_of_sums.shape[0]
    padded = jnp.zeros((8, rows_of_sums.shape[1]), jnp.float32).at[:count].set(rows_of_sums)
    return all_sum(padded, ("blk", "sec"), mesh_shape, 0)[:count]


def _doubling(n):
    distances, d = [], 1
    while d < n:
        distances.append(d)
        d *= 2
    return tuple(distances)


def _greet(n, distances):
    barrier = pltpu.get_barrier_semaphore()
    mine = lax.axis_index("sec")
    for d in distances:
        for peer in (lax.rem(mine + d, n), lax.rem(mine + n - d, n)):
            pl.semaphore_signal(barrier, inc=1, device_id={"sec": peer}, device_id_type=MESH)
    pl.semaphore_wait(barrier, 2 * len(distances))


def _hop(n, d, source, slot, send_sem, recv_sem):
    mine = lax.axis_index("sec")
    copy = pltpu.make_async_remote_copy(
        src_ref=source,
        dst_ref=slot,
        send_sem=send_sem,
        recv_sem=recv_sem,
        device_id={"sec": lax.rem(mine + d, n)},
        device_id_type=MESH,
    )
    copy.start()
    copy.wait_recv()
    copy.wait_send()


RADIX = 4


def _plan(n):
    rounds, d = [], 1
    while d < n:
        rounds.append((d, tuple(j for j in range(1, RADIX) if j * d < n)))
        d *= RADIX
    return tuple(rounds)


def _plan_peers(rounds):
    return tuple(sorted({j * d for d, js in rounds for j in js} | {1}))


def _send_all(n, sec, sources, slots, sends, recvs, flat, d, js):
    copies = []
    for i, j in enumerate(js):
        copy = pltpu.make_async_remote_copy(
            src_ref=sources,
            dst_ref=slots.at[flat + i],
            send_sem=sends.at[flat + i],
            recv_sem=recvs.at[flat + i],
            device_id={"sec": lax.rem(sec + j * d, n)},
            device_id_type=MESH,
        )
        copy.start()
        copies.append(copy)
    for copy in copies:
        copy.wait_recv()
    for copy in copies:
        copy.wait_send()


def _spread(n_sec, n_blk, offsets, piece_ref, slots, sends, recvs):
    sec, blk = lax.axis_index("sec"), lax.axis_index("blk")

    def copy(o, j, index):
        return pltpu.make_async_remote_copy(
            src_ref=piece_ref,
            dst_ref=slots.at[index],
            send_sem=sends.at[(o - 1) * n_blk + j],
            recv_sem=recvs.at[index],
            device_id={"sec": lax.rem(sec + o, n_sec), "blk": j},
            device_id_type=MESH,
        )

    outgoing = [
        copy(o, j, (o - 1) * n_blk + blk) for o in range(1, offsets + 1) for j in range(n_blk)
    ]
    for c in outgoing:
        c.start()
    for o in range(1, offsets + 1):
        for j in range(n_blk):
            copy(o, j, (o - 1) * n_blk + j).wait_recv()
    for c in outgoing:
        c.wait_send()


def _assemble(n_blk, offsets, slots, mats):
    piece = slots.shape[1]
    for o in range(offsets):
        for j in range(n_blk):
            mats[o, j * piece : (j + 1) * piece, :] = slots[o * n_blk + j]


def _greet_all(n_sec, n_blk, offsets, rounds, blk_peers, stages=()):
    barrier = pltpu.get_barrier_semaphore()
    sec, blk = lax.axis_index("sec"), lax.axis_index("blk")
    count = _signal_stages(barrier, stages)
    if blk_peers:
        for k in range(1, n_blk):
            pl.semaphore_signal(
                barrier, inc=1, device_id={"blk": lax.rem(blk + k, n_blk)}, device_id_type=MESH
            )
            count += 1
    for o in range(1, offsets + 1):
        for j in range(n_blk):
            for peer in (lax.rem(sec + o, n_sec), lax.rem(sec + n_sec - o, n_sec)):
                pl.semaphore_signal(
                    barrier, inc=1, device_id={"sec": peer, "blk": j}, device_id_type=MESH
                )
                count += 1
    for d in sorted({j * d for d, js in rounds[1:] for j in js}):
        for peer in (lax.rem(sec + d, n_sec), lax.rem(sec + n_sec - d, n_sec)):
            pl.semaphore_signal(barrier, inc=1, device_id={"sec": peer}, device_id_type=MESH)
            count += 1
    pl.semaphore_wait(barrier, count)


def _maps_body(n, n_blk, rounds, e_ref, a_ref, eslots, emat, current, slots, esend, erecv, sends, recvs):
    sec = lax.axis_index("sec")
    first = rounds[0][1]
    offsets = len(first) + 1
    _spread(n, n_blk, offsets, e_ref, eslots, esend, erecv)
    _assemble(n_blk, offsets, eslots, emat)
    joined = emat[0]
    for i, j in enumerate(first):
        a_ref[i] = joined
        joined = jnp.dot(
            joined, emat[j], precision=lax.Precision.HIGHEST, preferred_element_type=jnp.float32
        )
    current[...] = joined
    flat = len(first)
    for k in range(1, len(rounds)):
        d, js = rounds[k]
        onward = k < len(rounds) - 1
        if onward or len(js) > 1:
            _send_all(n, sec, current, slots, sends, recvs, flat, d, js)
        joined = current[...]
        for i, j in enumerate(js):
            a_ref[flat + i] = joined
            if onward or i < len(js) - 1:
                joined = jnp.dot(
                    joined, slots[flat + i], precision=lax.Precision.HIGHEST,
                    preferred_element_type=jnp.float32,
                )
        if onward:
            current[...] = joined
        flat += len(js)


def _setup_kernel(
    n_sec, n_blk, rounds, x_ref, up_ref, be_ref, back_ref, inv_ref, pick_ref,
    g_ref, b_ref, a_ref, gain_ref, chain_ref, *scratch
):
    phase_scratch = scratch[:9]
    pslots, psend, precv, epiece = scratch[9:13]
    maps_scratch = scratch[13:]
    sec, blk = lax.axis_index("sec"), lax.axis_index("blk")
    offsets = len(rounds[0][1]) + 1
    _greet_all(n_sec, n_blk, offsets, rounds, True)
    piece = epiece.shape[0]
    mine = be_ref.at[pl.ds(pl.multiple_of(blk * piece, 8), piece)]
    _operator_phase(n_sec, n_blk, x_ref, up_ref, mine, g_ref, b_ref, a_ref, phase_scratch)

    def blk_copy(k, target, slot):
        return pltpu.make_async_remote_copy(
            src_ref=back_ref,
            dst_ref=pslots.at[slot],
            send_sem=psend.at[k],
            recv_sem=precv.at[slot],
            device_id={"blk": target},
            device_id_type=MESH,
        )

    outgoing = [blk_copy(k, lax.rem(blk + k, n_blk), blk) for k in range(1, n_blk)]
    for copy in outgoing:
        copy.start()
    pslots[blk] = back_ref[...]
    for k in range(1, n_blk):
        sender = lax.rem(blk + k, n_blk)
        blk_copy(k, sender, sender).wait_recv()
    for copy in outgoing:
        copy.wait_send()
    rows = back_ref.shape[0]
    gain = jnp.dot(inv_ref[:, 0:rows], pslots[0], preferred_element_type=jnp.float32)
    for j in range(1, n_blk):
        gain = gain + jnp.dot(
            inv_ref[:, j * rows : (j + 1) * rows], pslots[j], preferred_element_type=jnp.float32
        )
    gain_ref[...] = gain
    epiece[...] = -jnp.dot(
        pick_ref[...], gain, precision=lax.Precision.HIGHEST, preferred_element_type=jnp.float32
    )
    _maps_body(n_sec, n_blk, rounds, epiece, chain_ref, *maps_scratch)


def setup_exchange(x, up_t, be_t, back, inverse, picks, n_sec, n_blk):
    cases, width = x.shape
    panel, _ = up_t.shape
    piece = panel // n_blk
    rows, panel_width = back.shape
    rounds = _plan(n_sec)
    total = sum(len(js) for _, js in rounds)
    offsets = len(rounds[0][1]) + 1
    return pl.pallas_call(
        functools.partial(_setup_kernel, n_sec, n_blk, rounds),
        out_shape=(
            jax.ShapeDtypeStruct((cases, n_blk * width), x.dtype),
            jax.ShapeDtypeStruct((panel, cases), jnp.float32),
            jax.ShapeDtypeStruct((piece, cases), jnp.float32),
            jax.ShapeDtypeStruct((rows, panel_width), jnp.float32),
            jax.ShapeDtypeStruct((total, panel_width, panel_width), jnp.float32),
        ),
        in_specs=[pl.BlockSpec(memory_space=pltpu.VMEM)] * 6,
        out_specs=[pl.BlockSpec(memory_space=pltpu.VMEM)] * 5,
        scratch_shapes=_operator_scratch(n_blk, cases, width, x.dtype, piece, cases)
        + [
            pltpu.VMEM((n_blk, rows, panel_width), back.dtype),
            pltpu.SemaphoreType.DMA((n_blk,)),
            pltpu.SemaphoreType.DMA((n_blk,)),
            pltpu.VMEM((piece, panel_width), jnp.float32),
            pltpu.VMEM((offsets * n_blk, piece, panel_width), jnp.float32),
            pltpu.VMEM((offsets, panel_width, panel_width), jnp.float32),
            pltpu.VMEM((panel_width, panel_width), jnp.float32),
            pltpu.VMEM((total, panel_width, panel_width), jnp.float32),
            pltpu.SemaphoreType.DMA((offsets * n_blk,)),
            pltpu.SemaphoreType.DMA((offsets * n_blk,)),
            pltpu.SemaphoreType.DMA((total,)),
            pltpu.SemaphoreType.DMA((total,)),
        ],
        compiler_params=pltpu.CompilerParams(collective_id=3, has_side_effects=True),
    )(x, up_t, be_t, back, inverse, picks)


def _gather_kernel(n, x_ref, o_ref, slots, sends, recvs):
    mine = lax.axis_index("blk")
    barrier = pltpu.get_barrier_semaphore()
    for k in range(1, n):
        pl.semaphore_signal(
            barrier, inc=1, device_id={"blk": lax.rem(mine + k, n)}, device_id_type=MESH
        )
    pl.semaphore_wait(barrier, n - 1)
    copies = []
    for k in range(1, n):
        copy = pltpu.make_async_remote_copy(
            src_ref=x_ref,
            dst_ref=slots.at[mine],
            send_sem=sends.at[k],
            recv_sem=recvs.at[mine],
            device_id={"blk": lax.rem(mine + k, n)},
            device_id_type=MESH,
        )
        copy.start()
        copies.append(copy)
    slots[mine] = x_ref[...]
    for k in range(1, n):
        sender = lax.rem(mine + k, n)
        pltpu.make_async_remote_copy(
            src_ref=x_ref,
            dst_ref=slots.at[sender],
            send_sem=sends.at[k],
            recv_sem=recvs.at[sender],
            device_id={"blk": sender},
            device_id_type=MESH,
        ).wait_recv()
    for copy in copies:
        copy.wait_send()
    width = x_ref.shape[1]
    for j in range(n):
        o_ref[:, j * width : (j + 1) * width] = slots[j]


def gather_blk(x, n):
    rows, width = x.shape
    return pl.pallas_call(
        functools.partial(_gather_kernel, n),
        out_shape=jax.ShapeDtypeStruct((rows, n * width), x.dtype),
        in_specs=[pl.BlockSpec(memory_space=pltpu.VMEM)],
        out_specs=pl.BlockSpec(memory_space=pltpu.VMEM),
        scratch_shapes=[
            pltpu.VMEM((n, rows, width), x.dtype),
            pltpu.SemaphoreType.DMA((n,)),
            pltpu.SemaphoreType.DMA((n,)),
        ],
        compiler_params=pltpu.CompilerParams(collective_id=4, has_side_effects=True),
    )(x)


def _operator_phase(n_sec, n_blk, x_ref, up_ref, piece_ref, g_ref, b_ref, a_ref, scratch):
    gslots, bslots, aslots, gsend, grecv, bsend, brecv, asend, arecv = scratch
    sec, blk = lax.axis_index("sec"), lax.axis_index("blk")
    nxt, prv = lax.rem(sec + 1, n_sec), lax.rem(sec + n_sec - 1, n_sec)
    piece = bslots.shape[1]
    copies = []
    for k in range(1, n_blk):
        copies.append(
            pltpu.make_async_remote_copy(
                src_ref=x_ref,
                dst_ref=gslots.at[blk],
                send_sem=gsend.at[k],
                recv_sem=grecv.at[blk],
                device_id={"blk": lax.rem(blk + k, n_blk)},
                device_id_type=MESH,
            )
        )
    for j in range(n_blk):
        copies.append(
            pltpu.make_async_remote_copy(
                src_ref=piece_ref,
                dst_ref=bslots.at[blk],
                send_sem=bsend.at[j],
                recv_sem=brecv.at[blk],
                device_id={"sec": nxt, "blk": j},
                device_id_type=MESH,
            )
        )
        copies.append(
            pltpu.make_async_remote_copy(
                src_ref=up_ref.at[pl.ds(j * piece, piece)],
                dst_ref=aslots.at[blk],
                send_sem=asend.at[j],
                recv_sem=arecv.at[blk],
                device_id={"sec": prv, "blk": j},
                device_id_type=MESH,
            )
        )
    for copy in copies:
        copy.start()
    gslots[blk] = x_ref[...]
    for k in range(1, n_blk):
        sender = lax.rem(blk + k, n_blk)
        pltpu.make_async_remote_copy(
            src_ref=x_ref,
            dst_ref=gslots.at[sender],
            send_sem=gsend.at[k],
            recv_sem=grecv.at[sender],
            device_id={"blk": sender},
            device_id_type=MESH,
        ).wait_recv()
    for j in range(n_blk):
        pltpu.make_async_remote_copy(
            src_ref=piece_ref,
            dst_ref=bslots.at[j],
            send_sem=bsend.at[j],
            recv_sem=brecv.at[j],
            device_id={"sec": prv, "blk": j},
            device_id_type=MESH,
        ).wait_recv()
        pltpu.make_async_remote_copy(
            src_ref=up_ref.at[pl.ds(j * piece, piece)],
            dst_ref=aslots.at[j],
            send_sem=asend.at[j],
            recv_sem=arecv.at[j],
            device_id={"sec": nxt, "blk": j},
            device_id_type=MESH,
        ).wait_recv()
    for copy in copies:
        copy.wait_send()
    width = x_ref.shape[1]
    for j in range(n_blk):
        g_ref[:, j * width : (j + 1) * width] = gslots[j]
        b_ref[j * piece : (j + 1) * piece, :] = jnp.where(
            sec >= 1, bslots[j], jnp.zeros_like(bslots[j])
        )
    total = aslots[0]
    for j in range(1, n_blk):
        total = total + aslots[j]
    a_ref[...] = jnp.where(sec <= n_sec - 2, total, jnp.zeros_like(total))


def _operator_scratch(n_blk, rows, width, dtype, piece, cases):
    return [
        pltpu.VMEM((n_blk, rows, width), dtype),
        pltpu.VMEM((n_blk, piece, cases), jnp.float32),
        pltpu.VMEM((n_blk, piece, cases), jnp.float32),
    ] + [pltpu.SemaphoreType.DMA((n_blk,))] * 6


def _operator_kernel(n_sec, n_blk, x_ref, up_ref, be_ref, g_ref, b_ref, a_ref, *scratch):
    sec, blk = lax.axis_index("sec"), lax.axis_index("blk")
    nxt, prv = lax.rem(sec + 1, n_sec), lax.rem(sec + n_sec - 1, n_sec)
    piece = scratch[1].shape[1]
    barrier = pltpu.get_barrier_semaphore()
    for k in range(1, n_blk):
        pl.semaphore_signal(
            barrier, inc=1, device_id={"blk": lax.rem(blk + k, n_blk)}, device_id_type=MESH
        )
    for j in range(n_blk):
        for other in (nxt, prv):
            pl.semaphore_signal(
                barrier, inc=1, device_id={"sec": other, "blk": j}, device_id_type=MESH
            )
    pl.semaphore_wait(barrier, 3 * n_blk - 1)
    mine = be_ref.at[pl.ds(pl.multiple_of(blk * piece, 8), piece)]
    _operator_phase(n_sec, n_blk, x_ref, up_ref, mine, g_ref, b_ref, a_ref, scratch)


def operator_exchange(x, up_t, be_t, n_sec, n_blk):
    rows, width = x.shape
    panel, cases = up_t.shape
    piece = panel // n_blk
    return pl.pallas_call(
        functools.partial(_operator_kernel, n_sec, n_blk),
        out_shape=(
            jax.ShapeDtypeStruct((rows, n_blk * width), x.dtype),
            jax.ShapeDtypeStruct((panel, cases), jnp.float32),
            jax.ShapeDtypeStruct((piece, cases), jnp.float32),
        ),
        in_specs=[pl.BlockSpec(memory_space=pltpu.VMEM)] * 3,
        out_specs=[pl.BlockSpec(memory_space=pltpu.VMEM)] * 3,
        scratch_shapes=_operator_scratch(n_blk, rows, width, x.dtype, piece, cases),
        compiler_params=pltpu.CompilerParams(collective_id=5, has_side_effects=True),
    )(x, up_t, be_t)


def _precondition_kernel(
    n_sec, n_blk, rounds, stages, depth, basis_ref, image_ref, inv_ref, pick_ref, u_ref,
    gain_ref, ahead_ref, block_ref, back_ref, spread_ref, jac_ref,
    h_ref, next_ref, d_ref, p_ref, *scratch
):
    gslots, fpiece, fslots, fmat, carry, slots, gsend, grecv, fsend, frecv, ssend, srecv = scratch[:12]
    rounded, upward, own_piece, x_ref = scratch[12:16]
    g_ref, b_ref, a_ref = scratch[16:19]
    phase_scratch = scratch[19:28]
    project_scratch = scratch[28:]
    sec, blk = lax.axis_index("sec"), lax.axis_index("blk")
    first = rounds[0][1]
    offsets = len(first) + 1
    _greet_all(n_sec, n_blk, offsets, rounds, True, stages)
    _project_body(stages, depth, basis_ref, image_ref, h_ref, next_ref, project_scratch)
    x_ref[...] = next_ref[...].astype(x_ref.dtype)

    def blk_copy(k, target, slot):
        return pltpu.make_async_remote_copy(
            src_ref=x_ref,
            dst_ref=gslots.at[slot],
            send_sem=gsend.at[k],
            recv_sem=grecv.at[slot],
            device_id={"blk": target},
            device_id_type=MESH,
        )

    outgoing = [blk_copy(k, lax.rem(blk + k, n_blk), blk) for k in range(1, n_blk)]
    for copy in outgoing:
        copy.start()
    gslots[blk] = x_ref[...]
    for k in range(1, n_blk):
        sender = lax.rem(blk + k, n_blk)
        blk_copy(k, sender, sender).wait_recv()
    for copy in outgoing:
        copy.wait_send()
    width = x_ref.shape[1]
    contract = (((1,), (1,)), ((), ()))
    folded = lax.dot_general(
        gslots[0], inv_ref[:, 0:width], contract, preferred_element_type=jnp.float32
    )
    for j in range(1, n_blk):
        folded = folded + lax.dot_general(
            gslots[j],
            inv_ref[:, j * width : (j + 1) * width],
            contract,
            preferred_element_type=jnp.float32,
        )
    fpiece[...] = lax.dot_general(
        pick_ref[...], folded, contract, precision=lax.Precision.HIGHEST,
        preferred_element_type=jnp.float32,
    )
    _spread(n_sec, n_blk, offsets, fpiece, fslots, fsend, frecv)
    _assemble(n_blk, offsets, fslots, fmat)
    joined = jnp.where(sec >= 1, fmat[0], jnp.zeros_like(fmat[0]))
    for i, j in enumerate(first):
        term = jnp.dot(
            u_ref[i], fmat[j], precision=lax.Precision.HIGHEST, preferred_element_type=jnp.float32
        )
        joined = joined + jnp.where(sec >= j + 1, term, jnp.zeros_like(term))
    carry[1] = joined
    flat = len(first)
    for k in range(1, len(rounds)):
        d, js = rounds[k]
        _send_all(n_sec, sec, carry.at[k], slots, ssend, srecv, flat, d, js)
        joined = carry[k]
        for i, j in enumerate(js):
            term = jnp.dot(
                u_ref[flat + i], slots[flat + i], precision=lax.Precision.HIGHEST,
                preferred_element_type=jnp.float32,
            )
            joined = joined + jnp.where(sec >= j * d, term, jnp.zeros_like(term))
        carry[k + 1] = joined
        flat += len(js)
    before = carry[len(rounds)].T
    direction = folded - lax.dot_general(
        before, gain_ref[...], contract, precision=lax.Precision.HIGHEST,
        preferred_element_type=jnp.float32,
    )
    d_ref[...] = direction
    rounded[...] = direction.astype(rounded.dtype)
    upward[...] = jnp.dot(
        rounded[...], ahead_ref[...], preferred_element_type=jnp.float32
    ).T
    own_piece[...] = lax.dot_general(
        pick_ref[...], rounded[...].astype(jnp.float32), contract,
        precision=lax.Precision.HIGHEST, preferred_element_type=jnp.float32,
    )
    _operator_phase(n_sec, n_blk, rounded, upward, own_piece, g_ref, b_ref, a_ref, phase_scratch)
    product = jac_ref[...] * direction
    for j in range(n_blk):
        product = product + lax.dot_general(
            g_ref[:, j * width : (j + 1) * width],
            block_ref[:, j * width : (j + 1) * width],
            contract,
            preferred_element_type=jnp.float32,
        )
    product = product + lax.dot_general(
        b_ref[...].T.astype(back_ref.dtype), back_ref[...], contract,
        preferred_element_type=jnp.float32,
    )
    product = product + jnp.dot(
        spread_ref[...], a_ref[...], precision=lax.Precision.HIGHEST,
        preferred_element_type=jnp.float32,
    ).T
    p_ref[...] = product


def precondition_sweep(
    basis, image, inverse, picks, chain, gain, ahead, block, back, spread, jac, mesh_shape, depth
):
    n_sec, n_blk = mesh_shape["sec"], mesh_shape["blk"]
    stages = _global_stages(mesh_shape)
    cases, width = image.shape
    piece, _ = picks.shape
    panel = piece * n_blk
    plan = _plan(n_sec)
    rounds = len(plan)
    total = sum(len(js) for _, js in plan)
    offsets = len(plan[0][1]) + 1
    dtype = jnp.bfloat16
    return pl.pallas_call(
        functools.partial(_precondition_kernel, n_sec, n_blk, plan, stages, depth),
        out_shape=(
            jax.ShapeDtypeStruct((8, cases), jnp.float32),
            jax.ShapeDtypeStruct((cases, width), jnp.float32),
            jax.ShapeDtypeStruct((cases, width), jnp.float32),
            jax.ShapeDtypeStruct((cases, width), jnp.float32),
        ),
        in_specs=[pl.BlockSpec(memory_space=pltpu.VMEM)] * 11,
        out_specs=[pl.BlockSpec(memory_space=pltpu.VMEM)] * 4,
        scratch_shapes=[
            pltpu.VMEM((n_blk, cases, width), dtype),
            pltpu.VMEM((piece, cases), jnp.float32),
            pltpu.VMEM((offsets * n_blk, piece, cases), jnp.float32),
            pltpu.VMEM((offsets, panel, cases), jnp.float32),
            pltpu.VMEM((rounds + 1, panel, cases), jnp.float32),
            pltpu.VMEM((total, panel, cases), jnp.float32),
            pltpu.SemaphoreType.DMA((n_blk,)),
            pltpu.SemaphoreType.DMA((n_blk,)),
            pltpu.SemaphoreType.DMA((offsets * n_blk,)),
            pltpu.SemaphoreType.DMA((offsets * n_blk,)),
            pltpu.SemaphoreType.DMA((total,)),
            pltpu.SemaphoreType.DMA((total,)),
            pltpu.VMEM((cases, width), dtype),
            pltpu.VMEM((panel, cases), jnp.float32),
            pltpu.VMEM((piece, cases), jnp.float32),
            pltpu.VMEM((cases, width), dtype),
            pltpu.VMEM((cases, n_blk * width), dtype),
            pltpu.VMEM((panel, cases), jnp.float32),
            pltpu.VMEM((piece, cases), jnp.float32),
        ]
        + _operator_scratch(n_blk, cases, width, dtype, piece, cases)
        + _project_scratch(stages, cases),
        compiler_params=pltpu.CompilerParams(collective_id=10 + depth, has_side_effects=True),
    )(basis, image, inverse, picks, chain, gain, ahead, block, back, spread, jac)


def _exchange_sum(stages, source, slots, partial, sends, recvs, out):
    count = len(stages)
    for stage, (axis, n) in enumerate(stages):
        mine = lax.axis_index(axis)
        copies = []
        for k in range(1, n):
            copy = pltpu.make_async_remote_copy(
                src_ref=source,
                dst_ref=slots[stage].at[mine],
                send_sem=sends[stage].at[k],
                recv_sem=recvs[stage].at[mine],
                device_id={axis: lax.rem(mine + k, n)},
                device_id_type=MESH,
            )
            copy.start()
            copies.append(copy)
        slots[stage][mine] = source[...]
        for k in range(1, n):
            sender = lax.rem(mine + k, n)
            pltpu.make_async_remote_copy(
                src_ref=source,
                dst_ref=slots[stage].at[sender],
                send_sem=sends[stage].at[k],
                recv_sem=recvs[stage].at[sender],
                device_id={axis: sender},
                device_id_type=MESH,
            ).wait_recv()
        for copy in copies:
            copy.wait_send()
        total = slots[stage][0]
        for j in range(1, n):
            total = total + slots[stage][j]
        if stage == count - 1:
            out[...] = total
        else:
            partial[...] = total
            source = partial


def _project_scratch(stages, cases):
    def buffers():
        out = [pltpu.VMEM((n, 8, cases), jnp.float32) for _, n in stages]
        out.append(pltpu.VMEM((8, cases), jnp.float32))
        out += [pltpu.SemaphoreType.DMA((n,)) for _, n in stages]
        out += [pltpu.SemaphoreType.DMA((n,)) for _, n in stages]
        return out

    return buffers() + buffers() + [pltpu.VMEM((8, cases), jnp.float32)] * 2


def _project_body(stages, depth, basis_ref, image_ref, h_ref, next_ref, scratch):
    count = len(stages)
    first, second = scratch[: 3 * count + 1], scratch[3 * count + 1 : 6 * count + 2]
    rows, work = scratch[6 * count + 2 : 6 * count + 4]
    highest = lax.Precision.HIGHEST
    contract = (((1,), (1,)), ((), ()))
    image = image_ref[...]
    ones = jnp.ones((8, image.shape[1]), jnp.float32)
    eye = (
        lax.broadcasted_iota(jnp.int32, (image.shape[0],) * 2, 0)
        == lax.broadcasted_iota(jnp.int32, (image.shape[0],) * 2, 1)
    ).astype(jnp.float32)

    def run(buffers, source, out):
        slots = buffers[:count]
        partial = buffers[count]
        sends = buffers[count + 1 : 2 * count + 1]
        recvs = buffers[2 * count + 1 :]
        _exchange_sum(stages, source, slots, partial, sends, recvs, out)

    if depth > 0:
        rows[...] = jnp.zeros_like(rows)
        for i in range(depth):
            summed = lax.dot_general(
                ones, image * basis_ref[i], contract, precision=highest,
                preferred_element_type=jnp.float32,
            )
            rows[i : i + 1, :] = summed[0:1, :]
        run(first, rows, h_ref)
        columns = lax.dot_general(
            eye, h_ref[...], contract, precision=highest, preferred_element_type=jnp.float32
        )
        for i in range(depth):
            image = image - columns[:, i : i + 1] * basis_ref[i]
    else:
        h_ref[...] = jnp.zeros_like(h_ref)
    work[...] = lax.dot_general(
        ones, image * image, contract, precision=highest, preferred_element_type=jnp.float32
    )
    run(second, work, rows)
    length = jnp.sqrt(rows[...] + epsilon)
    h_ref[depth : depth + 1, :] = length[0:1, :]
    scale = lax.dot_general(
        eye, length, contract, precision=highest, preferred_element_type=jnp.float32
    )
    next_ref[...] = image / scale[:, 0:1]


def _signal_stages(barrier, stages):
    peers = 0
    for axis, n in stages:
        mine = lax.axis_index(axis)
        for k in range(1, n):
            pl.semaphore_signal(
                barrier, inc=1, device_id={axis: lax.rem(mine + k, n)}, device_id_type=MESH
            )
            peers += 1
    return peers


def _project_kernel(stages, depth, basis_ref, image_ref, h_ref, next_ref, *scratch):
    barrier = pltpu.get_barrier_semaphore()
    pl.semaphore_wait(barrier, _signal_stages(barrier, stages))
    _project_body(stages, depth, basis_ref, image_ref, h_ref, next_ref, scratch)


def _global_stages(mesh_shape):
    return tuple((axis, mesh_shape[axis]) for axis in ("blk", "sec") if mesh_shape[axis] > 1)


def project(stacked, image, mesh_shape):
    depth, cases, width = stacked.shape
    stages = _global_stages(mesh_shape)
    return pl.pallas_call(
        functools.partial(_project_kernel, stages, depth),
        out_shape=(
            jax.ShapeDtypeStruct((8, cases), jnp.float32),
            jax.ShapeDtypeStruct((cases, width), jnp.float32),
        ),
        in_specs=[pl.BlockSpec(memory_space=pltpu.VMEM)] * 2,
        out_specs=[pl.BlockSpec(memory_space=pltpu.VMEM)] * 2,
        scratch_shapes=_project_scratch(stages, cases),
        compiler_params=pltpu.CompilerParams(collective_id=6 + depth, has_side_effects=True),
    )(stacked, image)


def least_squares(columns, beta, depth):
    zero = jnp.zeros_like(beta)
    upper = [
        [columns[j][i] if i <= j + 1 else zero for j in range(depth)] for i in range(depth + 1)
    ]
    rhs = [beta] + [zero] * depth
    for column in range(depth):
        upper_row, lower_row = upper[column], upper[column + 1]
        radius = jnp.sqrt(upper_row[column] ** 2 + lower_row[column] ** 2)
        cosine = upper_row[column] / radius
        sine_term = lower_row[column] / radius
        upper[column] = [cosine * a + sine_term * b for a, b in zip(upper_row, lower_row)]
        upper[column + 1] = [-sine_term * a + cosine * b for a, b in zip(upper_row, lower_row)]
        first_rhs, second_rhs = rhs[column], rhs[column + 1]
        rhs[column] = cosine * first_rhs + sine_term * second_rhs
        rhs[column + 1] = -sine_term * first_rhs + cosine * second_rhs
    weights = [zero] * depth
    for column in reversed(range(depth)):
        remain = rhs[column]
        if column + 1 < depth:
            tail = upper[column][column + 1] * weights[column + 1]
            for k in range(column + 2, depth):
                tail = tail + upper[column][k] * weights[k]
            remain = remain - tail
        weights[column] = remain / upper[column][column]
    return weights

def local(
    mesh_shape,
    state_now, source, fan_gain, section_block, block_inverse, back_panel, ahead_panel, interface
):
    highest = lax.Precision.HIGHEST
    cases, node_rows = state_now.shape
    panel_width = back_panel.shape[1]
    indices = interface[0]
    first_row = lax.axis_index("blk") * node_rows
    selector = (indices[None, :] == first_row + jnp.arange(node_rows)[:, None]).astype(jnp.float32)
    contract = (((1,), (1,)), ((), ()))

    own_piece = panel_width // mesh_shape["blk"]
    own_picks = lax.dynamic_slice_in_dim(selector, lax.axis_index("blk") * own_piece, own_piece, 1).T

    def section_terms(dense_part, behind_vals, piece):
        width = piece.shape[1]
        dense_part = lax.dot_general(
            piece, section_block, contract, preferred_element_type=jnp.float32
        )
        picker = (indices[None, :] == jnp.arange(width)[:, None]).astype(jnp.bfloat16)
        behind_vals = jnp.dot(piece, picker, preferred_element_type=jnp.float32)
        return (dense_part, behind_vals)

    def fold_section(carry, piece):
        return section_terms(carry[0], carry[1], piece)

    n_sec, n_blk = mesh_shape["sec"], mesh_shape["blk"]
    piece = panel_width // n_blk
    local_picks = lax.dynamic_slice_in_dim(selector, lax.axis_index("blk") * piece, piece, 1)

    def finish(gathered, behind_t, ahead_piece):
        dense_part = lax.dot_general(
            gathered, section_block, contract, preferred_element_type=jnp.float32
        )
        lower_term = lax.dot_general(
            behind_t.astype(jnp.bfloat16),
            back_panel,
            (((0,), (1,)), ((), ())),
            preferred_element_type=jnp.float32,
        )
        upper_term = lax.dot_general(
            ahead_piece, local_picks, (((0,), (1,)), ((), ())), precision=highest
        )
        return dense_part + lower_term + upper_term

    def operator(vector):
        rounded = vector.astype(jnp.bfloat16)
        up_t = lax.dot_general(
            ahead_panel, rounded, (((0,), (1,)), ((), ())), preferred_element_type=jnp.float32
        )
        be_t = lax.dot_general(
            selector.astype(jnp.bfloat16),
            rounded,
            (((0,), (1,)), ((), ())),
            preferred_element_type=jnp.float32,
        )
        return finish(*operator_exchange(rounded, up_t, be_t, n_sec, n_blk))

    def compose(earlier, later):
        first_map, first_value = earlier
        second_map, second_value = later
        joined_map = jnp.dot(second_map, first_map, precision=highest)
        joined_value = jnp.dot(first_value, second_map.T, precision=highest) + second_value
        return (joined_map, joined_value)

    def lengths(vector):
        return jnp.sqrt(global_sum(jnp.sum(vector * vector, axis=1)[None], mesh_shape)[0] + epsilon)

    bent = jnp.tanh(state_now)
    state_rounded = state_now.astype(jnp.bfloat16)
    gathered, behind_t, ahead_piece, gain_panel, chain = setup_exchange(
        state_rounded,
        lax.dot_general(
            ahead_panel, state_rounded, (((0,), (1,)), ((), ())), preferred_element_type=jnp.float32
        ),
        lax.dot_general(
            selector.astype(jnp.bfloat16),
            state_rounded,
            (((0,), (1,)), ((), ())),
            preferred_element_type=jnp.float32,
        ),
        back_panel,
        block_inverse,
        own_picks,
        n_sec,
        n_blk,
    )
    residual = source - finish(gathered, behind_t, ahead_piece) - fan_gain[None, :] * bent
    jac_diag = fan_gain[None, :] * (1.0 - bent * bent)
    columns = []
    basis = []
    directions = []
    product = residual
    beta = None
    for column in range(KRYLOV):
        stacked = jnp.stack(basis) if basis else residual[None]
        sums, following, direction, product = precondition_sweep(
            stacked, product, block_inverse, own_picks, chain, gain_panel, ahead_panel,
            section_block, back_panel, local_picks, jac_diag, mesh_shape, len(basis),
        )
        if column == 0:
            beta = sums[0]
        else:
            columns.append(sums[: column + 1])
        basis.append(following)
        directions.append(direction)
    sums, _ = project(jnp.stack(basis), product, mesh_shape)
    columns.append(sums[: KRYLOV + 1])
    weights = least_squares(columns, beta, KRYLOV)
    update = jnp.zeros_like(state_now)
    for column in range(KRYLOV):
        update = update + weights[column][:, None] * directions[column]
    return state_now + update


def solution(mesh):
    in_specs = (
        P(None, ("sec", "blk")),
        P(None, ("sec", "blk")),
        P(("sec", "blk")),
        P(("sec", "blk"), None),
        P(("sec", "blk"), None),
        P(("sec", "blk"), None),
        P(("sec", "blk"), None),
        P("sec", None),
    )
    out_specs = P(None, ("sec", "blk"))
    return jax.shard_map(functools.partial(local, dict(mesh.shape)), mesh=mesh, in_specs=in_specs, out_specs=out_specs, check_vma=False)
```

```python
import functools

import jax
import jax.numpy as jnp
from jax import lax
from jax.experimental import pallas as pl
from jax.experimental.pallas import tpu as pltpu
from jax.sharding import PartitionSpec as P

MESH = pl.DeviceIdType.MESH

KRYLOV = 3


epsilon = 1e-06


def extended(x, sides, width):
    for axis, dim in sides:
        size, length = (lax.axis_size(axis), x.shape[dim])
        up = [(i, (i + 1) % size) for i in range(size - 1)]
        down = [(j, i) for i, j in up]
        last = lax.slice_in_dim(x, length - width, length, axis=dim)
        first = lax.slice_in_dim(x, 0, width, axis=dim)
        before = lax.ppermute(last, axis, up)
        after = lax.ppermute(first, axis, down)
        x = jnp.concatenate([before, x, after], axis=dim)
    return x


def entering(value, axis, join, neutral):
    count, mine = (lax.axis_size(axis), lax.axis_index(axis))
    pieces = jax.tree.map(lambda part: lax.all_gather(part, axis), value)
    so_far = jax.tree.map(
        lambda part, zero: jnp.full_like(part, 0) + jnp.asarray(zero, part.dtype), value, neutral
    )

    def step(position, so_far):
        longer = join(so_far, jax.tree.map(lambda part: part[position], pieces))
        return jax.tree.map(lambda new, old: jnp.where(position < mine, new, old), longer, so_far)

    return lax.fori_loop(0, count - 1, step, so_far)


def _reduce_kernel(stages, x_ref, o_ref, *scratch):
    count = len(stages)
    slots = scratch[:count]
    partial = scratch[count]
    sends = scratch[count + 1 : 2 * count + 1]
    recvs = scratch[2 * count + 1 :]
    barrier = pltpu.get_barrier_semaphore()
    peers = 0
    for axis, n in stages:
        mine = lax.axis_index(axis)
        for k in range(1, n):
            pl.semaphore_signal(
                barrier, inc=1, device_id={axis: lax.rem(mine + k, n)}, device_id_type=MESH
            )
            peers += 1
    pl.semaphore_wait(barrier, peers)
    source = x_ref
    for stage, (axis, n) in enumerate(stages):
        mine = lax.axis_index(axis)
        copies = []
        for k in range(1, n):
            copy = pltpu.make_async_remote_copy(
                src_ref=source,
                dst_ref=slots[stage].at[mine],
                send_sem=sends[stage].at[k],
                recv_sem=recvs[stage].at[mine],
                device_id={axis: lax.rem(mine + k, n)},
                device_id_type=MESH,
            )
            copy.start()
            copies.append(copy)
        slots[stage][mine] = source[...]
        for k in range(1, n):
            sender = lax.rem(mine + k, n)
            pltpu.make_async_remote_copy(
                src_ref=source,
                dst_ref=slots[stage].at[sender],
                send_sem=sends[stage].at[k],
                recv_sem=recvs[stage].at[sender],
                device_id={axis: sender},
                device_id_type=MESH,
            ).wait_recv()
        for copy in copies:
            copy.wait_send()
        total = slots[stage][0]
        for j in range(1, n):
            total = total + slots[stage][j]
        if stage == count - 1:
            o_ref[...] = total
        else:
            partial[...] = total
            source = partial


def all_sum(x, axes, mesh_shape, collective):
    stages = tuple((axis, mesh_shape[axis]) for axis in axes if mesh_shape[axis] > 1)
    rows, cols = x.shape
    scratch = [pltpu.VMEM((n, rows, cols), jnp.float32) for _, n in stages]
    scratch.append(pltpu.VMEM((rows, cols), jnp.float32))
    scratch += [pltpu.SemaphoreType.DMA((n,)) for _, n in stages]
    scratch += [pltpu.SemaphoreType.DMA((n,)) for _, n in stages]
    return pl.pallas_call(
        functools.partial(_reduce_kernel, stages),
        out_shape=jax.ShapeDtypeStruct((rows, cols), jnp.float32),
        in_specs=[pl.BlockSpec(memory_space=pltpu.VMEM)],
        out_specs=pl.BlockSpec(memory_space=pltpu.VMEM),
        scratch_shapes=scratch,
        compiler_params=pltpu.CompilerParams(collective_id=collective, has_side_effects=True),
    )(x.astype(jnp.float32))


def global_sum(rows_of_sums, mesh_shape):
    count = rows_of_sums.shape[0]
    padded = jnp.zeros((8, rows_of_sums.shape[1]), jnp.float32).at[:count].set(rows_of_sums)
    return all_sum(padded, ("blk", "sec"), mesh_shape, 0)[:count]


def _doubling(n):
    distances, d = [], 1
    while d < n:
        distances.append(d)
        d *= 2
    return tuple(distances)


def _greet(n, distances):
    barrier = pltpu.get_barrier_semaphore()
    mine = lax.axis_index("sec")
    for d in distances:
        for peer in (lax.rem(mine + d, n), lax.rem(mine + n - d, n)):
            pl.semaphore_signal(barrier, inc=1, device_id={"sec": peer}, device_id_type=MESH)
    pl.semaphore_wait(barrier, 2 * len(distances))


def _hop(n, d, source, slot, send_sem, recv_sem):
    mine = lax.axis_index("sec")
    copy = pltpu.make_async_remote_copy(
        src_ref=source,
        dst_ref=slot,
        send_sem=send_sem,
        recv_sem=recv_sem,
        device_id={"sec": lax.rem(mine + d, n)},
        device_id_type=MESH,
    )
    copy.start()
    copy.wait_recv()
    copy.wait_send()


RADIX = 4


def _plan(n):
    rounds, d = [], 1
    while d < n:
        rounds.append((d, tuple(j for j in range(1, RADIX) if j * d < n)))
        d *= RADIX
    return tuple(rounds)


def _plan_peers(rounds):
    return tuple(sorted({j * d for d, js in rounds for j in js} | {1}))


def _send_all(n, sec, sources, slots, sends, recvs, flat, d, js):
    copies = []
    for i, j in enumerate(js):
        copy = pltpu.make_async_remote_copy(
            src_ref=sources,
            dst_ref=slots.at[flat + i],
            send_sem=sends.at[flat + i],
            recv_sem=recvs.at[flat + i],
            device_id={"sec": lax.rem(sec + j * d, n)},
            device_id_type=MESH,
        )
        copy.start()
        copies.append(copy)
    for copy in copies:
        copy.wait_recv()
    for copy in copies:
        copy.wait_send()


def _spread(n_sec, n_blk, offsets, piece_ref, slots, sends, recvs):
    sec, blk = lax.axis_index("sec"), lax.axis_index("blk")

    def copy(o, j, index):
        return pltpu.make_async_remote_copy(
            src_ref=piece_ref,
            dst_ref=slots.at[index],
            send_sem=sends.at[(o - 1) * n_blk + j],
            recv_sem=recvs.at[index],
            device_id={"sec": lax.rem(sec + o, n_sec), "blk": j},
            device_id_type=MESH,
        )

    outgoing = [
        copy(o, j, (o - 1) * n_blk + blk) for o in range(1, offsets + 1) for j in range(n_blk)
    ]
    for c in outgoing:
        c.start()
    for o in range(1, offsets + 1):
        for j in range(n_blk):
            copy(o, j, (o - 1) * n_blk + j).wait_recv()
    for c in outgoing:
        c.wait_send()


def _assemble(n_blk, offsets, slots, mats):
    piece = slots.shape[1]
    for o in range(offsets):
        for j in range(n_blk):
            mats[o, j * piece : (j + 1) * piece, :] = slots[o * n_blk + j]


def _greet_all(n_sec, n_blk, offsets, rounds, blk_peers, stages=()):
    barrier = pltpu.get_barrier_semaphore()
    sec, blk = lax.axis_index("sec"), lax.axis_index("blk")
    count = _signal_stages(barrier, stages)
    if blk_peers:
        for k in range(1, n_blk):
            pl.semaphore_signal(
                barrier, inc=1, device_id={"blk": lax.rem(blk + k, n_blk)}, device_id_type=MESH
            )
            count += 1
    for o in range(1, offsets + 1):
        for j in range(n_blk):
            for peer in (lax.rem(sec + o, n_sec), lax.rem(sec + n_sec - o, n_sec)):
                pl.semaphore_signal(
                    barrier, inc=1, device_id={"sec": peer, "blk": j}, device_id_type=MESH
                )
                count += 1
    for d in sorted({j * d for d, js in rounds[1:] for j in js}):
        for peer in (lax.rem(sec + d, n_sec), lax.rem(sec + n_sec - d, n_sec)):
            pl.semaphore_signal(barrier, inc=1, device_id={"sec": peer}, device_id_type=MESH)
            count += 1
    pl.semaphore_wait(barrier, count)


def _maps_body(n, n_blk, rounds, e_ref, a_ref, eslots, emat, current, slots, esend, erecv, sends, recvs):
    sec = lax.axis_index("sec")
    first = rounds[0][1]
    offsets = len(first) + 1
    _spread(n, n_blk, offsets, e_ref, eslots, esend, erecv)
    _assemble(n_blk, offsets, eslots, emat)
    joined = emat[0]
    for i, j in enumerate(first):
        a_ref[i] = joined
        joined = jnp.dot(
            joined, emat[j], precision=lax.Precision.HIGHEST, preferred_element_type=jnp.float32
        )
    current[...] = joined
    flat = len(first)
    for k in range(1, len(rounds)):
        d, js = rounds[k]
        onward = k < len(rounds) - 1
        if onward or len(js) > 1:
            _send_all(n, sec, current, slots, sends, recvs, flat, d, js)
        joined = current[...]
        for i, j in enumerate(js):
            a_ref[flat + i] = joined
            if onward or i < len(js) - 1:
                joined = jnp.dot(
                    joined, slots[flat + i], precision=lax.Precision.HIGHEST,
                    preferred_element_type=jnp.float32,
                )
        if onward:
            current[...] = joined
        flat += len(js)


def _setup_kernel(
    n_sec, n_blk, rounds, x_ref, up_ref, be_ref, back_ref, inv_ref, pick_ref,
    g_ref, b_ref, a_ref, gain_ref, chain_ref, *scratch
):
    phase_scratch = scratch[:9]
    pslots, psend, precv, epiece = scratch[9:13]
    maps_scratch = scratch[13:]
    sec, blk = lax.axis_index("sec"), lax.axis_index("blk")
    offsets = len(rounds[0][1]) + 1
    _greet_all(n_sec, n_blk, offsets, rounds, True)
    piece = epiece.shape[0]
    mine = be_ref.at[pl.ds(pl.multiple_of(blk * piece, 8), piece)]
    _operator_phase(n_sec, n_blk, x_ref, up_ref, mine, g_ref, b_ref, a_ref, phase_scratch)

    def blk_copy(k, target, slot):
        return pltpu.make_async_remote_copy(
            src_ref=back_ref,
            dst_ref=pslots.at[slot],
            send_sem=psend.at[k],
            recv_sem=precv.at[slot],
            device_id={"blk": target},
            device_id_type=MESH,
        )

    outgoing = [blk_copy(k, lax.rem(blk + k, n_blk), blk) for k in range(1, n_blk)]
    for copy in outgoing:
        copy.start()
    pslots[blk] = back_ref[...]
    for k in range(1, n_blk):
        sender = lax.rem(blk + k, n_blk)
        blk_copy(k, sender, sender).wait_recv()
    for copy in outgoing:
        copy.wait_send()
    rows = back_ref.shape[0]
    gain = jnp.dot(inv_ref[:, 0:rows], pslots[0], preferred_element_type=jnp.float32)
    for j in range(1, n_blk):
        gain = gain + jnp.dot(
            inv_ref[:, j * rows : (j + 1) * rows], pslots[j], preferred_element_type=jnp.float32
        )
    gain_ref[...] = gain
    epiece[...] = -jnp.dot(
        pick_ref[...], gain, precision=lax.Precision.HIGHEST, preferred_element_type=jnp.float32
    )
    _maps_body(n_sec, n_blk, rounds, epiece, chain_ref, *maps_scratch)


def setup_exchange(x, up_t, be_t, back, inverse, picks, n_sec, n_blk):
    cases, width = x.shape
    panel, _ = up_t.shape
    piece = panel // n_blk
    rows, panel_width = back.shape
    rounds = _plan(n_sec)
    total = sum(len(js) for _, js in rounds)
    offsets = len(rounds[0][1]) + 1
    return pl.pallas_call(
        functools.partial(_setup_kernel, n_sec, n_blk, rounds),
        out_shape=(
            jax.ShapeDtypeStruct((cases, n_blk * width), x.dtype),
            jax.ShapeDtypeStruct((panel, cases), jnp.float32),
            jax.ShapeDtypeStruct((piece, cases), jnp.float32),
            jax.ShapeDtypeStruct((rows, panel_width), jnp.float32),
            jax.ShapeDtypeStruct((total, panel_width, panel_width), jnp.float32),
        ),
        in_specs=[pl.BlockSpec(memory_space=pltpu.VMEM)] * 6,
        out_specs=[pl.BlockSpec(memory_space=pltpu.VMEM)] * 5,
        scratch_shapes=_operator_scratch(n_blk, cases, width, x.dtype, piece, cases)
        + [
            pltpu.VMEM((n_blk, rows, panel_width), back.dtype),
            pltpu.SemaphoreType.DMA((n_blk,)),
            pltpu.SemaphoreType.DMA((n_blk,)),
            pltpu.VMEM((piece, panel_width), jnp.float32),
            pltpu.VMEM((offsets * n_blk, piece, panel_width), jnp.float32),
            pltpu.VMEM((offsets, panel_width, panel_width), jnp.float32),
            pltpu.VMEM((panel_width, panel_width), jnp.float32),
            pltpu.VMEM((total, panel_width, panel_width), jnp.float32),
            pltpu.SemaphoreType.DMA((offsets * n_blk,)),
            pltpu.SemaphoreType.DMA((offsets * n_blk,)),
            pltpu.SemaphoreType.DMA((total,)),
            pltpu.SemaphoreType.DMA((total,)),
        ],
        compiler_params=pltpu.CompilerParams(collective_id=3, has_side_effects=True),
    )(x, up_t, be_t, back, inverse, picks)


def _gather_kernel(n, x_ref, o_ref, slots, sends, recvs):
    mine = lax.axis_index("blk")
    barrier = pltpu.get_barrier_semaphore()
    for k in range(1, n):
        pl.semaphore_signal(
            barrier, inc=1, device_id={"blk": lax.rem(mine + k, n)}, device_id_type=MESH
        )
    pl.semaphore_wait(barrier, n - 1)
    copies = []
    for k in range(1, n):
        copy = pltpu.make_async_remote_copy(
            src_ref=x_ref,
            dst_ref=slots.at[mine],
            send_sem=sends.at[k],
            recv_sem=recvs.at[mine],
            device_id={"blk": lax.rem(mine + k, n)},
            device_id_type=MESH,
        )
        copy.start()
        copies.append(copy)
    slots[mine] = x_ref[...]
    for k in range(1, n):
        sender = lax.rem(mine + k, n)
        pltpu.make_async_remote_copy(
            src_ref=x_ref,
            dst_ref=slots.at[sender],
            send_sem=sends.at[k],
            recv_sem=recvs.at[sender],
            device_id={"blk": sender},
            device_id_type=MESH,
        ).wait_recv()
    for copy in copies:
        copy.wait_send()
    width = x_ref.shape[1]
    for j in range(n):
        o_ref[:, j * width : (j + 1) * width] = slots[j]


def gather_blk(x, n):
    rows, width = x.shape
    return pl.pallas_call(
        functools.partial(_gather_kernel, n),
        out_shape=jax.ShapeDtypeStruct((rows, n * width), x.dtype),
        in_specs=[pl.BlockSpec(memory_space=pltpu.VMEM)],
        out_specs=pl.BlockSpec(memory_space=pltpu.VMEM),
        scratch_shapes=[
            pltpu.VMEM((n, rows, width), x.dtype),
            pltpu.SemaphoreType.DMA((n,)),
            pltpu.SemaphoreType.DMA((n,)),
        ],
        compiler_params=pltpu.CompilerParams(collective_id=4, has_side_effects=True),
    )(x)


def _operator_phase(n_sec, n_blk, x_ref, up_ref, piece_ref, g_ref, b_ref, a_ref, scratch):
    gslots, bslots, aslots, gsend, grecv, bsend, brecv, asend, arecv = scratch
    sec, blk = lax.axis_index("sec"), lax.axis_index("blk")
    nxt, prv = lax.rem(sec + 1, n_sec), lax.rem(sec + n_sec - 1, n_sec)
    piece = bslots.shape[1]
    copies = []
    for k in range(1, n_blk):
        copies.append(
            pltpu.make_async_remote_copy(
                src_ref=x_ref,
                dst_ref=gslots.at[blk],
                send_sem=gsend.at[k],
                recv_sem=grecv.at[blk],
                device_id={"blk": lax.rem(blk + k, n_blk)},
                device_id_type=MESH,
            )
        )
    for j in range(n_blk):
        copies.append(
            pltpu.make_async_remote_copy(
                src_ref=piece_ref,
                dst_ref=bslots.at[blk],
                send_sem=bsend.at[j],
                recv_sem=brecv.at[blk],
                device_id={"sec": nxt, "blk": j},
                device_id_type=MESH,
            )
        )
        copies.append(
            pltpu.make_async_remote_copy(
                src_ref=up_ref.at[pl.ds(j * piece, piece)],
                dst_ref=aslots.at[blk],
                send_sem=asend.at[j],
                recv_sem=arecv.at[blk],
                device_id={"sec": prv, "blk": j},
                device_id_type=MESH,
            )
        )
    for copy in copies:
        copy.start()
    gslots[blk] = x_ref[...]
    for k in range(1, n_blk):
        sender = lax.rem(blk + k, n_blk)
        pltpu.make_async_remote_copy(
            src_ref=x_ref,
            dst_ref=gslots.at[sender],
            send_sem=gsend.at[k],
            recv_sem=grecv.at[sender],
            device_id={"blk": sender},
            device_id_type=MESH,
        ).wait_recv()
    for j in range(n_blk):
        pltpu.make_async_remote_copy(
            src_ref=piece_ref,
            dst_ref=bslots.at[j],
            send_sem=bsend.at[j],
            recv_sem=brecv.at[j],
            device_id={"sec": prv, "blk": j},
            device_id_type=MESH,
        ).wait_recv()
        pltpu.make_async_remote_copy(
            src_ref=up_ref.at[pl.ds(j * piece, piece)],
            dst_ref=aslots.at[j],
            send_sem=asend.at[j],
            recv_sem=arecv.at[j],
            device_id={"sec": nxt, "blk": j},
            device_id_type=MESH,
        ).wait_recv()
    for copy in copies:
        copy.wait_send()
    width = x_ref.shape[1]
    for j in range(n_blk):
        g_ref[:, j * width : (j + 1) * width] = gslots[j]
        b_ref[j * piece : (j + 1) * piece, :] = jnp.where(
            sec >= 1, bslots[j], jnp.zeros_like(bslots[j])
        )
    total = aslots[0]
    for j in range(1, n_blk):
        total = total + aslots[j]
    a_ref[...] = jnp.where(sec <= n_sec - 2, total, jnp.zeros_like(total))


def _operator_scratch(n_blk, rows, width, dtype, piece, cases):
    return [
        pltpu.VMEM((n_blk, rows, width), dtype),
        pltpu.VMEM((n_blk, piece, cases), jnp.float32),
        pltpu.VMEM((n_blk, piece, cases), jnp.float32),
    ] + [pltpu.SemaphoreType.DMA((n_blk,))] * 6


def _operator_kernel(n_sec, n_blk, x_ref, up_ref, be_ref, g_ref, b_ref, a_ref, *scratch):
    sec, blk = lax.axis_index("sec"), lax.axis_index("blk")
    nxt, prv = lax.rem(sec + 1, n_sec), lax.rem(sec + n_sec - 1, n_sec)
    piece = scratch[1].shape[1]
    barrier = pltpu.get_barrier_semaphore()
    for k in range(1, n_blk):
        pl.semaphore_signal(
            barrier, inc=1, device_id={"blk": lax.rem(blk + k, n_blk)}, device_id_type=MESH
        )
    for j in range(n_blk):
        for other in (nxt, prv):
            pl.semaphore_signal(
                barrier, inc=1, device_id={"sec": other, "blk": j}, device_id_type=MESH
            )
    pl.semaphore_wait(barrier, 3 * n_blk - 1)
    mine = be_ref.at[pl.ds(pl.multiple_of(blk * piece, 8), piece)]
    _operator_phase(n_sec, n_blk, x_ref, up_ref, mine, g_ref, b_ref, a_ref, scratch)


def operator_exchange(x, up_t, be_t, n_sec, n_blk):
    rows, width = x.shape
    panel, cases = up_t.shape
    piece = panel // n_blk
    return pl.pallas_call(
        functools.partial(_operator_kernel, n_sec, n_blk),
        out_shape=(
            jax.ShapeDtypeStruct((rows, n_blk * width), x.dtype),
            jax.ShapeDtypeStruct((panel, cases), jnp.float32),
            jax.ShapeDtypeStruct((piece, cases), jnp.float32),
        ),
        in_specs=[pl.BlockSpec(memory_space=pltpu.VMEM)] * 3,
        out_specs=[pl.BlockSpec(memory_space=pltpu.VMEM)] * 3,
        scratch_shapes=_operator_scratch(n_blk, rows, width, x.dtype, piece, cases),
        compiler_params=pltpu.CompilerParams(collective_id=5, has_side_effects=True),
    )(x, up_t, be_t)


def _precondition_kernel(n_sec, n_blk, rounds, stages, depth, *refs):
    basis_refs = refs[:depth]
    (image_ref, inv_ref, pick_ref, u_ref, gain_ref, ahead_ref, block_ref, back_ref, spread_ref,
     jac_ref, h_ref, next_ref, d_ref, p_ref) = refs[depth : depth + 14]
    scratch = refs[depth + 14 :]
    gslots, fpiece, fslots, fmat, carry, slots, gsend, grecv, fsend, frecv, ssend, srecv = scratch[:12]
    rounded, upward, own_piece, x_ref = scratch[12:16]
    g_ref, b_ref, a_ref = scratch[16:19]
    phase_scratch = scratch[19:28]
    project_scratch = scratch[28:]
    sec, blk = lax.axis_index("sec"), lax.axis_index("blk")
    first = rounds[0][1]
    offsets = len(first) + 1
    _greet_all(n_sec, n_blk, offsets, rounds, True, stages)
    _project_body(stages, depth, basis_refs, image_ref, h_ref, next_ref, project_scratch)
    x_ref[...] = next_ref[...].astype(x_ref.dtype)

    def blk_copy(k, target, slot):
        return pltpu.make_async_remote_copy(
            src_ref=x_ref,
            dst_ref=gslots.at[slot],
            send_sem=gsend.at[k],
            recv_sem=grecv.at[slot],
            device_id={"blk": target},
            device_id_type=MESH,
        )

    outgoing = [blk_copy(k, lax.rem(blk + k, n_blk), blk) for k in range(1, n_blk)]
    for copy in outgoing:
        copy.start()
    gslots[blk] = x_ref[...]
    for k in range(1, n_blk):
        sender = lax.rem(blk + k, n_blk)
        blk_copy(k, sender, sender).wait_recv()
    for copy in outgoing:
        copy.wait_send()
    width = x_ref.shape[1]
    contract = (((1,), (1,)), ((), ()))
    folded = lax.dot_general(
        gslots[0], inv_ref[:, 0:width], contract, preferred_element_type=jnp.float32
    )
    for j in range(1, n_blk):
        folded = folded + lax.dot_general(
            gslots[j],
            inv_ref[:, j * width : (j + 1) * width],
            contract,
            preferred_element_type=jnp.float32,
        )
    fpiece[...] = lax.dot_general(
        pick_ref[...], folded, contract, precision=lax.Precision.HIGHEST,
        preferred_element_type=jnp.float32,
    )
    _spread(n_sec, n_blk, offsets, fpiece, fslots, fsend, frecv)
    _assemble(n_blk, offsets, fslots, fmat)
    joined = jnp.where(sec >= 1, fmat[0], jnp.zeros_like(fmat[0]))
    for i, j in enumerate(first):
        term = jnp.dot(
            u_ref[i], fmat[j], precision=lax.Precision.HIGHEST, preferred_element_type=jnp.float32
        )
        joined = joined + jnp.where(sec >= j + 1, term, jnp.zeros_like(term))
    carry[1] = joined
    flat = len(first)
    for k in range(1, len(rounds)):
        d, js = rounds[k]
        _send_all(n_sec, sec, carry.at[k], slots, ssend, srecv, flat, d, js)
        joined = carry[k]
        for i, j in enumerate(js):
            term = jnp.dot(
                u_ref[flat + i], slots[flat + i], precision=lax.Precision.HIGHEST,
                preferred_element_type=jnp.float32,
            )
            joined = joined + jnp.where(sec >= j * d, term, jnp.zeros_like(term))
        carry[k + 1] = joined
        flat += len(js)
    before = carry[len(rounds)].T
    direction = folded - lax.dot_general(
        before, gain_ref[...], contract, precision=lax.Precision.HIGHEST,
        preferred_element_type=jnp.float32,
    )
    d_ref[...] = direction
    rounded[...] = direction.astype(rounded.dtype)
    upward[...] = jnp.dot(
        rounded[...], ahead_ref[...], preferred_element_type=jnp.float32
    ).T
    own_piece[...] = lax.dot_general(
        pick_ref[...], rounded[...].astype(jnp.float32), contract,
        precision=lax.Precision.HIGHEST, preferred_element_type=jnp.float32,
    )
    _operator_phase(n_sec, n_blk, rounded, upward, own_piece, g_ref, b_ref, a_ref, phase_scratch)
    product = jac_ref[...] * direction
    for j in range(n_blk):
        product = product + lax.dot_general(
            g_ref[:, j * width : (j + 1) * width],
            block_ref[:, j * width : (j + 1) * width],
            contract,
            preferred_element_type=jnp.float32,
        )
    product = product + lax.dot_general(
        b_ref[...].T.astype(back_ref.dtype), back_ref[...], contract,
        preferred_element_type=jnp.float32,
    )
    product = product + jnp.dot(
        spread_ref[...], a_ref[...], precision=lax.Precision.HIGHEST,
        preferred_element_type=jnp.float32,
    ).T
    p_ref[...] = product


def precondition_sweep(
    basis, image, inverse, picks, chain, gain, ahead, block, back, spread, jac, mesh_shape, depth
):
    n_sec, n_blk = mesh_shape["sec"], mesh_shape["blk"]
    stages = _global_stages(mesh_shape)
    cases, width = image.shape
    piece, _ = picks.shape
    panel = piece * n_blk
    plan = _plan(n_sec)
    rounds = len(plan)
    total = sum(len(js) for _, js in plan)
    offsets = len(plan[0][1]) + 1
    dtype = jnp.bfloat16
    return pl.pallas_call(
        functools.partial(_precondition_kernel, n_sec, n_blk, plan, stages, depth),
        out_shape=(
            jax.ShapeDtypeStruct((8, cases), jnp.float32),
            jax.ShapeDtypeStruct((cases, width), jnp.float32),
            jax.ShapeDtypeStruct((cases, width), jnp.float32),
            jax.ShapeDtypeStruct((cases, width), jnp.float32),
        ),
        in_specs=[pl.BlockSpec(memory_space=pltpu.VMEM)] * (depth + 10),
        out_specs=[pl.BlockSpec(memory_space=pltpu.VMEM)] * 4,
        scratch_shapes=[
            pltpu.VMEM((n_blk, cases, width), dtype),
            pltpu.VMEM((piece, cases), jnp.float32),
            pltpu.VMEM((offsets * n_blk, piece, cases), jnp.float32),
            pltpu.VMEM((offsets, panel, cases), jnp.float32),
            pltpu.VMEM((rounds + 1, panel, cases), jnp.float32),
            pltpu.VMEM((total, panel, cases), jnp.float32),
            pltpu.SemaphoreType.DMA((n_blk,)),
            pltpu.SemaphoreType.DMA((n_blk,)),
            pltpu.SemaphoreType.DMA((offsets * n_blk,)),
            pltpu.SemaphoreType.DMA((offsets * n_blk,)),
            pltpu.SemaphoreType.DMA((total,)),
            pltpu.SemaphoreType.DMA((total,)),
            pltpu.VMEM((cases, width), dtype),
            pltpu.VMEM((panel, cases), jnp.float32),
            pltpu.VMEM((piece, cases), jnp.float32),
            pltpu.VMEM((cases, width), dtype),
            pltpu.VMEM((cases, n_blk * width), dtype),
            pltpu.VMEM((panel, cases), jnp.float32),
            pltpu.VMEM((piece, cases), jnp.float32),
        ]
        + _operator_scratch(n_blk, cases, width, dtype, piece, cases)
        + _project_scratch(stages, cases),
        compiler_params=pltpu.CompilerParams(collective_id=10 + depth, has_side_effects=True),
    )(*basis, image, inverse, picks, chain, gain, ahead, block, back, spread, jac)


def _exchange_sum(stages, source, slots, partial, sends, recvs, out):
    count = len(stages)
    for stage, (axis, n) in enumerate(stages):
        mine = lax.axis_index(axis)
        copies = []
        for k in range(1, n):
            copy = pltpu.make_async_remote_copy(
                src_ref=source,
                dst_ref=slots[stage].at[mine],
                send_sem=sends[stage].at[k],
                recv_sem=recvs[stage].at[mine],
                device_id={axis: lax.rem(mine + k, n)},
                device_id_type=MESH,
            )
            copy.start()
            copies.append(copy)
        slots[stage][mine] = source[...]
        for k in range(1, n):
            sender = lax.rem(mine + k, n)
            pltpu.make_async_remote_copy(
                src_ref=source,
                dst_ref=slots[stage].at[sender],
                send_sem=sends[stage].at[k],
                recv_sem=recvs[stage].at[sender],
                device_id={axis: sender},
                device_id_type=MESH,
            ).wait_recv()
        for copy in copies:
            copy.wait_send()
        total = slots[stage][0]
        for j in range(1, n):
            total = total + slots[stage][j]
        if stage == count - 1:
            out[...] = total
        else:
            partial[...] = total
            source = partial


def _project_scratch(stages, cases):
    def buffers():
        out = [pltpu.VMEM((n, 8, cases), jnp.float32) for _, n in stages]
        out.append(pltpu.VMEM((8, cases), jnp.float32))
        out += [pltpu.SemaphoreType.DMA((n,)) for _, n in stages]
        out += [pltpu.SemaphoreType.DMA((n,)) for _, n in stages]
        return out

    return buffers() + buffers() + [pltpu.VMEM((8, cases), jnp.float32)] * 2


def _project_body(stages, depth, basis_refs, image_ref, h_ref, next_ref, scratch):
    count = len(stages)
    first, second = scratch[: 3 * count + 1], scratch[3 * count + 1 : 6 * count + 2]
    rows, work = scratch[6 * count + 2 : 6 * count + 4]
    highest = lax.Precision.HIGHEST
    contract = (((1,), (1,)), ((), ()))
    image = image_ref[...]
    ones = jnp.ones((8, image.shape[1]), jnp.float32)
    eye = (
        lax.broadcasted_iota(jnp.int32, (image.shape[0],) * 2, 0)
        == lax.broadcasted_iota(jnp.int32, (image.shape[0],) * 2, 1)
    ).astype(jnp.float32)

    def run(buffers, source, out):
        slots = buffers[:count]
        partial = buffers[count]
        sends = buffers[count + 1 : 2 * count + 1]
        recvs = buffers[2 * count + 1 :]
        _exchange_sum(stages, source, slots, partial, sends, recvs, out)

    if depth > 0:
        rows[...] = jnp.zeros_like(rows)
        for i in range(depth):
            summed = lax.dot_general(
                ones, image * basis_refs[i][...], contract, precision=highest,
                preferred_element_type=jnp.float32,
            )
            rows[i : i + 1, :] = summed[0:1, :]
        run(first, rows, h_ref)
        columns = lax.dot_general(
            eye, h_ref[...], contract, precision=highest, preferred_element_type=jnp.float32
        )
        for i in range(depth):
            image = image - columns[:, i : i + 1] * basis_refs[i][...]
    else:
        h_ref[...] = jnp.zeros_like(h_ref)
    work[...] = lax.dot_general(
        ones, image * image, contract, precision=highest, preferred_element_type=jnp.float32
    )
    run(second, work, rows)
    length = jnp.sqrt(rows[...] + epsilon)
    h_ref[depth : depth + 1, :] = length[0:1, :]
    scale = lax.dot_general(
        eye, length, contract, precision=highest, preferred_element_type=jnp.float32
    )
    next_ref[...] = image / scale[:, 0:1]


def _signal_stages(barrier, stages):
    peers = 0
    for axis, n in stages:
        mine = lax.axis_index(axis)
        for k in range(1, n):
            pl.semaphore_signal(
                barrier, inc=1, device_id={axis: lax.rem(mine + k, n)}, device_id_type=MESH
            )
            peers += 1
    return peers


def _project_kernel(stages, depth, *refs):
    basis_refs = refs[:depth]
    image_ref, h_ref, next_ref = refs[depth : depth + 3]
    barrier = pltpu.get_barrier_semaphore()
    pl.semaphore_wait(barrier, _signal_stages(barrier, stages))
    _project_body(stages, depth, basis_refs, image_ref, h_ref, next_ref, refs[depth + 3 :])


def _global_stages(mesh_shape):
    return tuple((axis, mesh_shape[axis]) for axis in ("blk", "sec") if mesh_shape[axis] > 1)


def project(basis, image, mesh_shape):
    depth = len(basis)
    cases, width = image.shape
    stages = _global_stages(mesh_shape)
    return pl.pallas_call(
        functools.partial(_project_kernel, stages, depth),
        out_shape=(
            jax.ShapeDtypeStruct((8, cases), jnp.float32),
            jax.ShapeDtypeStruct((cases, width), jnp.float32),
        ),
        in_specs=[pl.BlockSpec(memory_space=pltpu.VMEM)] * (depth + 1),
        out_specs=[pl.BlockSpec(memory_space=pltpu.VMEM)] * 2,
        scratch_shapes=_project_scratch(stages, cases),
        compiler_params=pltpu.CompilerParams(collective_id=6 + depth, has_side_effects=True),
    )(*basis, image)


def least_squares(columns, beta, depth):
    zero = jnp.zeros_like(beta)
    upper = [
        [columns[j][i] if i <= j + 1 else zero for j in range(depth)] for i in range(depth + 1)
    ]
    rhs = [beta] + [zero] * depth
    for column in range(depth):
        upper_row, lower_row = upper[column], upper[column + 1]
        radius = jnp.sqrt(upper_row[column] ** 2 + lower_row[column] ** 2)
        cosine = upper_row[column] / radius
        sine_term = lower_row[column] / radius
        upper[column] = [cosine * a + sine_term * b for a, b in zip(upper_row, lower_row)]
        upper[column + 1] = [-sine_term * a + cosine * b for a, b in zip(upper_row, lower_row)]
        first_rhs, second_rhs = rhs[column], rhs[column + 1]
        rhs[column] = cosine * first_rhs + sine_term * second_rhs
        rhs[column + 1] = -sine_term * first_rhs + cosine * second_rhs
    weights = [zero] * depth
    for column in reversed(range(depth)):
        remain = rhs[column]
        if column + 1 < depth:
            tail = upper[column][column + 1] * weights[column + 1]
            for k in range(column + 2, depth):
                tail = tail + upper[column][k] * weights[k]
            remain = remain - tail
        weights[column] = remain / upper[column][column]
    return weights

def local(
    mesh_shape,
    state_now, source, fan_gain, section_block, block_inverse, back_panel, ahead_panel, interface
):
    highest = lax.Precision.HIGHEST
    cases, node_rows = state_now.shape
    panel_width = back_panel.shape[1]
    indices = interface[0]
    first_row = lax.axis_index("blk") * node_rows
    selector = (indices[None, :] == first_row + jnp.arange(node_rows)[:, None]).astype(jnp.float32)
    contract = (((1,), (1,)), ((), ()))

    own_piece = panel_width // mesh_shape["blk"]
    own_picks = lax.dynamic_slice_in_dim(selector, lax.axis_index("blk") * own_piece, own_piece, 1).T

    def section_terms(dense_part, behind_vals, piece):
        width = piece.shape[1]
        dense_part = lax.dot_general(
            piece, section_block, contract, preferred_element_type=jnp.float32
        )
        picker = (indices[None, :] == jnp.arange(width)[:, None]).astype(jnp.bfloat16)
        behind_vals = jnp.dot(piece, picker, preferred_element_type=jnp.float32)
        return (dense_part, behind_vals)

    def fold_section(carry, piece):
        return section_terms(carry[0], carry[1], piece)

    n_sec, n_blk = mesh_shape["sec"], mesh_shape["blk"]
    piece = panel_width // n_blk
    local_picks = lax.dynamic_slice_in_dim(selector, lax.axis_index("blk") * piece, piece, 1)

    def finish(gathered, behind_t, ahead_piece):
        dense_part = lax.dot_general(
            gathered, section_block, contract, preferred_element_type=jnp.float32
        )
        lower_term = lax.dot_general(
            behind_t.astype(jnp.bfloat16),
            back_panel,
            (((0,), (1,)), ((), ())),
            preferred_element_type=jnp.float32,
        )
        upper_term = lax.dot_general(
            ahead_piece, local_picks, (((0,), (1,)), ((), ())), precision=highest
        )
        return dense_part + lower_term + upper_term

    def operator(vector):
        rounded = vector.astype(jnp.bfloat16)
        up_t = lax.dot_general(
            ahead_panel, rounded, (((0,), (1,)), ((), ())), preferred_element_type=jnp.float32
        )
        be_t = lax.dot_general(
            selector.astype(jnp.bfloat16),
            rounded,
            (((0,), (1,)), ((), ())),
            preferred_element_type=jnp.float32,
        )
        return finish(*operator_exchange(rounded, up_t, be_t, n_sec, n_blk))

    def compose(earlier, later):
        first_map, first_value = earlier
        second_map, second_value = later
        joined_map = jnp.dot(second_map, first_map, precision=highest)
        joined_value = jnp.dot(first_value, second_map.T, precision=highest) + second_value
        return (joined_map, joined_value)

    def lengths(vector):
        return jnp.sqrt(global_sum(jnp.sum(vector * vector, axis=1)[None], mesh_shape)[0] + epsilon)

    bent = jnp.tanh(state_now)
    state_rounded = state_now.astype(jnp.bfloat16)
    gathered, behind_t, ahead_piece, gain_panel, chain = setup_exchange(
        state_rounded,
        lax.dot_general(
            ahead_panel, state_rounded, (((0,), (1,)), ((), ())), preferred_element_type=jnp.float32
        ),
        lax.dot_general(
            selector.astype(jnp.bfloat16),
            state_rounded,
            (((0,), (1,)), ((), ())),
            preferred_element_type=jnp.float32,
        ),
        back_panel,
        block_inverse,
        own_picks,
        n_sec,
        n_blk,
    )
    residual = source - finish(gathered, behind_t, ahead_piece) - fan_gain[None, :] * bent
    jac_diag = fan_gain[None, :] * (1.0 - bent * bent)
    columns = []
    basis = []
    directions = []
    product = residual
    beta = None
    for column in range(KRYLOV):
        sums, following, direction, product = precondition_sweep(
            list(basis), product, block_inverse, own_picks, chain, gain_panel, ahead_panel,
            section_block, back_panel, local_picks, jac_diag, mesh_shape, len(basis),
        )
        if column == 0:
            beta = sums[0]
        else:
            columns.append(sums[: column + 1])
        basis.append(following)
        directions.append(direction)
    sums, _ = project(basis, product, mesh_shape)
    columns.append(sums[: KRYLOV + 1])
    weights = least_squares(columns, beta, KRYLOV)
    update = jnp.zeros_like(state_now)
    for column in range(KRYLOV):
        update = update + weights[column][:, None] * directions[column]
    return state_now + update


def solution(mesh):
    in_specs = (
        P(None, ("sec", "blk")),
        P(None, ("sec", "blk")),
        P(("sec", "blk")),
        P(("sec", "blk"), None),
        P(("sec", "blk"), None),
        P(("sec", "blk"), None),
        P(("sec", "blk"), None),
        P("sec", None),
    )
    out_specs = P(None, ("sec", "blk"))
    return jax.shard_map(functools.partial(local, dict(mesh.shape)), mesh=mesh, in_specs=in_specs, out_specs=out_specs, check_vma=False)
```

```python
import functools

import jax
import jax.numpy as jnp
from jax import lax
from jax.experimental import pallas as pl
from jax.experimental.pallas import tpu as pltpu
from jax.sharding import PartitionSpec as P

MESH = pl.DeviceIdType.MESH

KRYLOV = 3


epsilon = 1e-06


def extended(x, sides, width):
    for axis, dim in sides:
        size, length = (lax.axis_size(axis), x.shape[dim])
        up = [(i, (i + 1) % size) for i in range(size - 1)]
        down = [(j, i) for i, j in up]
        last = lax.slice_in_dim(x, length - width, length, axis=dim)
        first = lax.slice_in_dim(x, 0, width, axis=dim)
        before = lax.ppermute(last, axis, up)
        after = lax.ppermute(first, axis, down)
        x = jnp.concatenate([before, x, after], axis=dim)
    return x


def entering(value, axis, join, neutral):
    count, mine = (lax.axis_size(axis), lax.axis_index(axis))
    pieces = jax.tree.map(lambda part: lax.all_gather(part, axis), value)
    so_far = jax.tree.map(
        lambda part, zero: jnp.full_like(part, 0) + jnp.asarray(zero, part.dtype), value, neutral
    )

    def step(position, so_far):
        longer = join(so_far, jax.tree.map(lambda part: part[position], pieces))
        return jax.tree.map(lambda new, old: jnp.where(position < mine, new, old), longer, so_far)

    return lax.fori_loop(0, count - 1, step, so_far)


def _reduce_kernel(stages, x_ref, o_ref, *scratch):
    count = len(stages)
    slots = scratch[:count]
    partial = scratch[count]
    sends = scratch[count + 1 : 2 * count + 1]
    recvs = scratch[2 * count + 1 :]
    barrier = pltpu.get_barrier_semaphore()
    peers = 0
    for axis, n in stages:
        mine = lax.axis_index(axis)
        for k in range(1, n):
            pl.semaphore_signal(
                barrier, inc=1, device_id={axis: lax.rem(mine + k, n)}, device_id_type=MESH
            )
            peers += 1
    pl.semaphore_wait(barrier, peers)
    source = x_ref
    for stage, (axis, n) in enumerate(stages):
        mine = lax.axis_index(axis)
        copies = []
        for k in range(1, n):
            copy = pltpu.make_async_remote_copy(
                src_ref=source,
                dst_ref=slots[stage].at[mine],
                send_sem=sends[stage].at[k],
                recv_sem=recvs[stage].at[mine],
                device_id={axis: lax.rem(mine + k, n)},
                device_id_type=MESH,
            )
            copy.start()
            copies.append(copy)
        slots[stage][mine] = source[...]
        for k in range(1, n):
            sender = lax.rem(mine + k, n)
            pltpu.make_async_remote_copy(
                src_ref=source,
                dst_ref=slots[stage].at[sender],
                send_sem=sends[stage].at[k],
                recv_sem=recvs[stage].at[sender],
                device_id={axis: sender},
                device_id_type=MESH,
            ).wait_recv()
        for copy in copies:
            copy.wait_send()
        total = slots[stage][0]
        for j in range(1, n):
            total = total + slots[stage][j]
        if stage == count - 1:
            o_ref[...] = total
        else:
            partial[...] = total
            source = partial


def all_sum(x, axes, mesh_shape, collective):
    stages = tuple((axis, mesh_shape[axis]) for axis in axes if mesh_shape[axis] > 1)
    rows, cols = x.shape
    scratch = [pltpu.VMEM((n, rows, cols), jnp.float32) for _, n in stages]
    scratch.append(pltpu.VMEM((rows, cols), jnp.float32))
    scratch += [pltpu.SemaphoreType.DMA((n,)) for _, n in stages]
    scratch += [pltpu.SemaphoreType.DMA((n,)) for _, n in stages]
    return pl.pallas_call(
        functools.partial(_reduce_kernel, stages),
        out_shape=jax.ShapeDtypeStruct((rows, cols), jnp.float32),
        in_specs=[pl.BlockSpec(memory_space=pltpu.VMEM)],
        out_specs=pl.BlockSpec(memory_space=pltpu.VMEM),
        scratch_shapes=scratch,
        compiler_params=pltpu.CompilerParams(collective_id=collective, has_side_effects=True),
    )(x.astype(jnp.float32))


def global_sum(rows_of_sums, mesh_shape):
    count = rows_of_sums.shape[0]
    padded = jnp.zeros((8, rows_of_sums.shape[1]), jnp.float32).at[:count].set(rows_of_sums)
    return all_sum(padded, ("blk", "sec"), mesh_shape, 0)[:count]


def _doubling(n):
    distances, d = [], 1
    while d < n:
        distances.append(d)
        d *= 2
    return tuple(distances)


def _greet(n, distances):
    barrier = pltpu.get_barrier_semaphore()
    mine = lax.axis_index("sec")
    for d in distances:
        for peer in (lax.rem(mine + d, n), lax.rem(mine + n - d, n)):
            pl.semaphore_signal(barrier, inc=1, device_id={"sec": peer}, device_id_type=MESH)
    pl.semaphore_wait(barrier, 2 * len(distances))


def _hop(n, d, source, slot, send_sem, recv_sem):
    mine = lax.axis_index("sec")
    copy = pltpu.make_async_remote_copy(
        src_ref=source,
        dst_ref=slot,
        send_sem=send_sem,
        recv_sem=recv_sem,
        device_id={"sec": lax.rem(mine + d, n)},
        device_id_type=MESH,
    )
    copy.start()
    copy.wait_recv()
    copy.wait_send()


RADIX = 4


def _plan(n):
    rounds, d = [], 1
    while d < n:
        rounds.append((d, tuple(j for j in range(1, RADIX) if j * d < n)))
        d *= RADIX
    return tuple(rounds)


def _plan_peers(rounds):
    return tuple(sorted({j * d for d, js in rounds for j in js} | {1}))


def _send_all(n, sec, sources, slots, sends, recvs, flat, d, js):
    copies = []
    for i, j in enumerate(js):
        copy = pltpu.make_async_remote_copy(
            src_ref=sources,
            dst_ref=slots.at[flat + i],
            send_sem=sends.at[flat + i],
            recv_sem=recvs.at[flat + i],
            device_id={"sec": lax.rem(sec + j * d, n)},
            device_id_type=MESH,
        )
        copy.start()
        copies.append(copy)
    for copy in copies:
        copy.wait_recv()
    for copy in copies:
        copy.wait_send()


def _spread(n_sec, n_blk, offsets, piece_ref, slots, sends, recvs):
    sec, blk = lax.axis_index("sec"), lax.axis_index("blk")

    def copy(o, j, index):
        return pltpu.make_async_remote_copy(
            src_ref=piece_ref,
            dst_ref=slots.at[index],
            send_sem=sends.at[(o - 1) * n_blk + j],
            recv_sem=recvs.at[index],
            device_id={"sec": lax.rem(sec + o, n_sec), "blk": j},
            device_id_type=MESH,
        )

    outgoing = [
        copy(o, j, (o - 1) * n_blk + blk) for o in range(1, offsets + 1) for j in range(n_blk)
    ]
    for c in outgoing:
        c.start()
    for o in range(1, offsets + 1):
        for j in range(n_blk):
            copy(o, j, (o - 1) * n_blk + j).wait_recv()
    for c in outgoing:
        c.wait_send()


def _assemble(n_blk, offsets, slots, mats):
    piece = slots.shape[1]
    for o in range(offsets):
        for j in range(n_blk):
            mats[o, j * piece : (j + 1) * piece, :] = slots[o * n_blk + j]


def _greet_all(n_sec, n_blk, offsets, rounds, blk_peers, stages=()):
    barrier = pltpu.get_barrier_semaphore()
    sec, blk = lax.axis_index("sec"), lax.axis_index("blk")
    count = _signal_stages(barrier, stages)
    if blk_peers:
        for k in range(1, n_blk):
            pl.semaphore_signal(
                barrier, inc=1, device_id={"blk": lax.rem(blk + k, n_blk)}, device_id_type=MESH
            )
            count += 1
    for o in range(1, offsets + 1):
        for j in range(n_blk):
            for peer in (lax.rem(sec + o, n_sec), lax.rem(sec + n_sec - o, n_sec)):
                pl.semaphore_signal(
                    barrier, inc=1, device_id={"sec": peer, "blk": j}, device_id_type=MESH
                )
                count += 1
    for d in sorted({j * d for d, js in rounds[1:] for j in js}):
        for peer in (lax.rem(sec + d, n_sec), lax.rem(sec + n_sec - d, n_sec)):
            pl.semaphore_signal(barrier, inc=1, device_id={"sec": peer}, device_id_type=MESH)
            count += 1
    pl.semaphore_wait(barrier, count)


def _maps_body(n, n_blk, rounds, e_ref, a_ref, eslots, emat, current, slots, esend, erecv, sends, recvs):
    sec = lax.axis_index("sec")
    first = rounds[0][1]
    offsets = len(first) + 1
    _spread(n, n_blk, offsets, e_ref, eslots, esend, erecv)
    _assemble(n_blk, offsets, eslots, emat)
    joined = emat[0]
    for i, j in enumerate(first):
        a_ref[i] = joined
        joined = jnp.dot(
            joined, emat[j], precision=lax.Precision.HIGHEST, preferred_element_type=jnp.float32
        )
    current[...] = joined
    flat = len(first)
    for k in range(1, len(rounds)):
        d, js = rounds[k]
        onward = k < len(rounds) - 1
        if onward or len(js) > 1:
            _send_all(n, sec, current, slots, sends, recvs, flat, d, js)
        joined = current[...]
        for i, j in enumerate(js):
            a_ref[flat + i] = joined
            if onward or i < len(js) - 1:
                joined = jnp.dot(
                    joined, slots[flat + i], precision=lax.Precision.HIGHEST,
                    preferred_element_type=jnp.float32,
                )
        if onward:
            current[...] = joined
        flat += len(js)


def _setup_kernel(
    n_sec, n_blk, rounds, x_ref, ahead_ref, block_ref, spread_ref, back_ref, inv_ref, pick_ref,
    k_ref, gain_ref, chain_ref, *scratch
):
    phase_scratch = scratch[:9]
    pslots, psend, precv, epiece = scratch[9:13]
    g_ref, b_ref, a_ref, upward, own_piece = scratch[13:18]
    maps_scratch = scratch[18:]
    sec, blk = lax.axis_index("sec"), lax.axis_index("blk")
    offsets = len(rounds[0][1]) + 1
    _greet_all(n_sec, n_blk, offsets, rounds, True)
    contract = (((1,), (1,)), ((), ()))
    upward[...] = jnp.dot(x_ref[...], ahead_ref[...], preferred_element_type=jnp.float32).T
    own_piece[...] = lax.dot_general(
        pick_ref[...], x_ref[...].astype(jnp.float32), contract,
        precision=lax.Precision.HIGHEST, preferred_element_type=jnp.float32,
    )
    _operator_phase(n_sec, n_blk, x_ref, upward, own_piece, g_ref, b_ref, a_ref, phase_scratch)
    width = x_ref.shape[1]
    product = lax.dot_general(
        g_ref[:, 0:width], block_ref[:, 0:width], contract, preferred_element_type=jnp.float32
    )
    for j in range(1, n_blk):
        product = product + lax.dot_general(
            g_ref[:, j * width : (j + 1) * width],
            block_ref[:, j * width : (j + 1) * width],
            contract,
            preferred_element_type=jnp.float32,
        )
    product = product + lax.dot_general(
        b_ref[...].T.astype(back_ref.dtype), back_ref[...], contract,
        preferred_element_type=jnp.float32,
    )
    product = product + jnp.dot(
        spread_ref[...], a_ref[...], precision=lax.Precision.HIGHEST,
        preferred_element_type=jnp.float32,
    ).T
    k_ref[...] = product

    def blk_copy(k, target, slot):
        return pltpu.make_async_remote_copy(
            src_ref=back_ref,
            dst_ref=pslots.at[slot],
            send_sem=psend.at[k],
            recv_sem=precv.at[slot],
            device_id={"blk": target},
            device_id_type=MESH,
        )

    outgoing = [blk_copy(k, lax.rem(blk + k, n_blk), blk) for k in range(1, n_blk)]
    for copy in outgoing:
        copy.start()
    pslots[blk] = back_ref[...]
    for k in range(1, n_blk):
        sender = lax.rem(blk + k, n_blk)
        blk_copy(k, sender, sender).wait_recv()
    for copy in outgoing:
        copy.wait_send()
    rows = back_ref.shape[0]
    gain = jnp.dot(inv_ref[:, 0:rows], pslots[0], preferred_element_type=jnp.float32)
    for j in range(1, n_blk):
        gain = gain + jnp.dot(
            inv_ref[:, j * rows : (j + 1) * rows], pslots[j], preferred_element_type=jnp.float32
        )
    gain_ref[...] = gain
    epiece[...] = -jnp.dot(
        pick_ref[...], gain, precision=lax.Precision.HIGHEST, preferred_element_type=jnp.float32
    )
    _maps_body(n_sec, n_blk, rounds, epiece, chain_ref, *maps_scratch)


def setup_exchange(x, ahead, block, spread, back, inverse, picks, n_sec, n_blk):
    cases, width = x.shape
    panel = ahead.shape[1]
    piece = panel // n_blk
    rows, panel_width = back.shape
    rounds = _plan(n_sec)
    total = sum(len(js) for _, js in rounds)
    offsets = len(rounds[0][1]) + 1
    return pl.pallas_call(
        functools.partial(_setup_kernel, n_sec, n_blk, rounds),
        out_shape=(
            jax.ShapeDtypeStruct((cases, width), jnp.float32),
            jax.ShapeDtypeStruct((rows, panel_width), jnp.float32),
            jax.ShapeDtypeStruct((total, panel_width, panel_width), jnp.float32),
        ),
        in_specs=[pl.BlockSpec(memory_space=pltpu.VMEM)] * 7,
        out_specs=[pl.BlockSpec(memory_space=pltpu.VMEM)] * 3,
        scratch_shapes=_operator_scratch(n_blk, cases, width, x.dtype, piece, cases)
        + [
            pltpu.VMEM((n_blk, rows, panel_width), back.dtype),
            pltpu.SemaphoreType.DMA((n_blk,)),
            pltpu.SemaphoreType.DMA((n_blk,)),
            pltpu.VMEM((piece, panel_width), jnp.float32),
            pltpu.VMEM((cases, n_blk * width), x.dtype),
            pltpu.VMEM((panel, cases), jnp.float32),
            pltpu.VMEM((piece, cases), jnp.float32),
            pltpu.VMEM((panel, cases), jnp.float32),
            pltpu.VMEM((piece, cases), jnp.float32),
            pltpu.VMEM((offsets * n_blk, piece, panel_width), jnp.float32),
            pltpu.VMEM((offsets, panel_width, panel_width), jnp.float32),
            pltpu.VMEM((panel_width, panel_width), jnp.float32),
            pltpu.VMEM((total, panel_width, panel_width), jnp.float32),
            pltpu.SemaphoreType.DMA((offsets * n_blk,)),
            pltpu.SemaphoreType.DMA((offsets * n_blk,)),
            pltpu.SemaphoreType.DMA((total,)),
            pltpu.SemaphoreType.DMA((total,)),
        ],
        compiler_params=pltpu.CompilerParams(collective_id=3, has_side_effects=True),
    )(x, ahead, block, spread, back, inverse, picks)


def _gather_kernel(n, x_ref, o_ref, slots, sends, recvs):
    mine = lax.axis_index("blk")
    barrier = pltpu.get_barrier_semaphore()
    for k in range(1, n):
        pl.semaphore_signal(
            barrier, inc=1, device_id={"blk": lax.rem(mine + k, n)}, device_id_type=MESH
        )
    pl.semaphore_wait(barrier, n - 1)
    copies = []
    for k in range(1, n):
        copy = pltpu.make_async_remote_copy(
            src_ref=x_ref,
            dst_ref=slots.at[mine],
            send_sem=sends.at[k],
            recv_sem=recvs.at[mine],
            device_id={"blk": lax.rem(mine + k, n)},
            device_id_type=MESH,
        )
        copy.start()
        copies.append(copy)
    slots[mine] = x_ref[...]
    for k in range(1, n):
        sender = lax.rem(mine + k, n)
        pltpu.make_async_remote_copy(
            src_ref=x_ref,
            dst_ref=slots.at[sender],
            send_sem=sends.at[k],
            recv_sem=recvs.at[sender],
            device_id={"blk": sender},
            device_id_type=MESH,
        ).wait_recv()
    for copy in copies:
        copy.wait_send()
    width = x_ref.shape[1]
    for j in range(n):
        o_ref[:, j * width : (j + 1) * width] = slots[j]


def gather_blk(x, n):
    rows, width = x.shape
    return pl.pallas_call(
        functools.partial(_gather_kernel, n),
        out_shape=jax.ShapeDtypeStruct((rows, n * width), x.dtype),
        in_specs=[pl.BlockSpec(memory_space=pltpu.VMEM)],
        out_specs=pl.BlockSpec(memory_space=pltpu.VMEM),
        scratch_shapes=[
            pltpu.VMEM((n, rows, width), x.dtype),
            pltpu.SemaphoreType.DMA((n,)),
            pltpu.SemaphoreType.DMA((n,)),
        ],
        compiler_params=pltpu.CompilerParams(collective_id=4, has_side_effects=True),
    )(x)


def _operator_phase(n_sec, n_blk, x_ref, up_ref, piece_ref, g_ref, b_ref, a_ref, scratch):
    gslots, bslots, aslots, gsend, grecv, bsend, brecv, asend, arecv = scratch
    sec, blk = lax.axis_index("sec"), lax.axis_index("blk")
    nxt, prv = lax.rem(sec + 1, n_sec), lax.rem(sec + n_sec - 1, n_sec)
    piece = bslots.shape[1]
    copies = []
    for k in range(1, n_blk):
        copies.append(
            pltpu.make_async_remote_copy(
                src_ref=x_ref,
                dst_ref=gslots.at[blk],
                send_sem=gsend.at[k],
                recv_sem=grecv.at[blk],
                device_id={"blk": lax.rem(blk + k, n_blk)},
                device_id_type=MESH,
            )
        )
    for j in range(n_blk):
        copies.append(
            pltpu.make_async_remote_copy(
                src_ref=piece_ref,
                dst_ref=bslots.at[blk],
                send_sem=bsend.at[j],
                recv_sem=brecv.at[blk],
                device_id={"sec": nxt, "blk": j},
                device_id_type=MESH,
            )
        )
        copies.append(
            pltpu.make_async_remote_copy(
                src_ref=up_ref.at[pl.ds(j * piece, piece)],
                dst_ref=aslots.at[blk],
                send_sem=asend.at[j],
                recv_sem=arecv.at[blk],
                device_id={"sec": prv, "blk": j},
                device_id_type=MESH,
            )
        )
    for copy in copies:
        copy.start()
    gslots[blk] = x_ref[...]
    for k in range(1, n_blk):
        sender = lax.rem(blk + k, n_blk)
        pltpu.make_async_remote_copy(
            src_ref=x_ref,
            dst_ref=gslots.at[sender],
            send_sem=gsend.at[k],
            recv_sem=grecv.at[sender],
            device_id={"blk": sender},
            device_id_type=MESH,
        ).wait_recv()
    for j in range(n_blk):
        pltpu.make_async_remote_copy(
            src_ref=piece_ref,
            dst_ref=bslots.at[j],
            send_sem=bsend.at[j],
            recv_sem=brecv.at[j],
            device_id={"sec": prv, "blk": j},
            device_id_type=MESH,
        ).wait_recv()
        pltpu.make_async_remote_copy(
            src_ref=up_ref.at[pl.ds(j * piece, piece)],
            dst_ref=aslots.at[j],
            send_sem=asend.at[j],
            recv_sem=arecv.at[j],
            device_id={"sec": nxt, "blk": j},
            device_id_type=MESH,
        ).wait_recv()
    for copy in copies:
        copy.wait_send()
    width = x_ref.shape[1]
    for j in range(n_blk):
        g_ref[:, j * width : (j + 1) * width] = gslots[j]
        b_ref[j * piece : (j + 1) * piece, :] = jnp.where(
            sec >= 1, bslots[j], jnp.zeros_like(bslots[j])
        )
    total = aslots[0]
    for j in range(1, n_blk):
        total = total + aslots[j]
    a_ref[...] = jnp.where(sec <= n_sec - 2, total, jnp.zeros_like(total))


def _operator_scratch(n_blk, rows, width, dtype, piece, cases):
    return [
        pltpu.VMEM((n_blk, rows, width), dtype),
        pltpu.VMEM((n_blk, piece, cases), jnp.float32),
        pltpu.VMEM((n_blk, piece, cases), jnp.float32),
    ] + [pltpu.SemaphoreType.DMA((n_blk,))] * 6


def _operator_kernel(n_sec, n_blk, x_ref, up_ref, be_ref, g_ref, b_ref, a_ref, *scratch):
    sec, blk = lax.axis_index("sec"), lax.axis_index("blk")
    nxt, prv = lax.rem(sec + 1, n_sec), lax.rem(sec + n_sec - 1, n_sec)
    piece = scratch[1].shape[1]
    barrier = pltpu.get_barrier_semaphore()
    for k in range(1, n_blk):
        pl.semaphore_signal(
            barrier, inc=1, device_id={"blk": lax.rem(blk + k, n_blk)}, device_id_type=MESH
        )
    for j in range(n_blk):
        for other in (nxt, prv):
            pl.semaphore_signal(
                barrier, inc=1, device_id={"sec": other, "blk": j}, device_id_type=MESH
            )
    pl.semaphore_wait(barrier, 3 * n_blk - 1)
    mine = be_ref.at[pl.ds(pl.multiple_of(blk * piece, 8), piece)]
    _operator_phase(n_sec, n_blk, x_ref, up_ref, mine, g_ref, b_ref, a_ref, scratch)


def operator_exchange(x, up_t, be_t, n_sec, n_blk):
    rows, width = x.shape
    panel, cases = up_t.shape
    piece = panel // n_blk
    return pl.pallas_call(
        functools.partial(_operator_kernel, n_sec, n_blk),
        out_shape=(
            jax.ShapeDtypeStruct((rows, n_blk * width), x.dtype),
            jax.ShapeDtypeStruct((panel, cases), jnp.float32),
            jax.ShapeDtypeStruct((piece, cases), jnp.float32),
        ),
        in_specs=[pl.BlockSpec(memory_space=pltpu.VMEM)] * 3,
        out_specs=[pl.BlockSpec(memory_space=pltpu.VMEM)] * 3,
        scratch_shapes=_operator_scratch(n_blk, rows, width, x.dtype, piece, cases),
        compiler_params=pltpu.CompilerParams(collective_id=5, has_side_effects=True),
    )(x, up_t, be_t)


def _precondition_kernel(n_sec, n_blk, rounds, stages, depth, *refs):
    basis_refs = refs[:depth]
    (image_ref, inv_ref, pick_ref, u_ref, gain_ref, ahead_ref, block_ref, back_ref, spread_ref,
     jac_ref, h_ref, next_ref, d_ref, p_ref) = refs[depth : depth + 14]
    scratch = refs[depth + 14 :]
    gslots, fpiece, fslots, fmat, carry, slots, gsend, grecv, fsend, frecv, ssend, srecv = scratch[:12]
    rounded, upward, own_piece, x_ref = scratch[12:16]
    g_ref, b_ref, a_ref = scratch[16:19]
    phase_scratch = scratch[19:28]
    project_scratch = scratch[28:]
    sec, blk = lax.axis_index("sec"), lax.axis_index("blk")
    first = rounds[0][1]
    offsets = len(first) + 1
    _greet_all(n_sec, n_blk, offsets, rounds, True, stages)
    _project_body(stages, depth, basis_refs, image_ref, h_ref, next_ref, project_scratch)
    x_ref[...] = next_ref[...].astype(x_ref.dtype)

    def blk_copy(k, target, slot):
        return pltpu.make_async_remote_copy(
            src_ref=x_ref,
            dst_ref=gslots.at[slot],
            send_sem=gsend.at[k],
            recv_sem=grecv.at[slot],
            device_id={"blk": target},
            device_id_type=MESH,
        )

    outgoing = [blk_copy(k, lax.rem(blk + k, n_blk), blk) for k in range(1, n_blk)]
    for copy in outgoing:
        copy.start()
    gslots[blk] = x_ref[...]
    for k in range(1, n_blk):
        sender = lax.rem(blk + k, n_blk)
        blk_copy(k, sender, sender).wait_recv()
    for copy in outgoing:
        copy.wait_send()
    width = x_ref.shape[1]
    contract = (((1,), (1,)), ((), ()))
    folded = lax.dot_general(
        gslots[0], inv_ref[:, 0:width], contract, preferred_element_type=jnp.float32
    )
    for j in range(1, n_blk):
        folded = folded + lax.dot_general(
            gslots[j],
            inv_ref[:, j * width : (j + 1) * width],
            contract,
            preferred_element_type=jnp.float32,
        )
    fpiece[...] = lax.dot_general(
        pick_ref[...], folded, contract, precision=lax.Precision.HIGHEST,
        preferred_element_type=jnp.float32,
    )
    _spread(n_sec, n_blk, offsets, fpiece, fslots, fsend, frecv)
    _assemble(n_blk, offsets, fslots, fmat)
    joined = jnp.where(sec >= 1, fmat[0], jnp.zeros_like(fmat[0]))
    for i, j in enumerate(first):
        term = jnp.dot(
            u_ref[i], fmat[j], precision=lax.Precision.HIGHEST, preferred_element_type=jnp.float32
        )
        joined = joined + jnp.where(sec >= j + 1, term, jnp.zeros_like(term))
    carry[1] = joined
    flat = len(first)
    for k in range(1, len(rounds)):
        d, js = rounds[k]
        _send_all(n_sec, sec, carry.at[k], slots, ssend, srecv, flat, d, js)
        joined = carry[k]
        for i, j in enumerate(js):
            term = jnp.dot(
                u_ref[flat + i], slots[flat + i], precision=lax.Precision.HIGHEST,
                preferred_element_type=jnp.float32,
            )
            joined = joined + jnp.where(sec >= j * d, term, jnp.zeros_like(term))
        carry[k + 1] = joined
        flat += len(js)
    before = carry[len(rounds)].T
    direction = folded - lax.dot_general(
        before, gain_ref[...], contract, precision=lax.Precision.HIGHEST,
        preferred_element_type=jnp.float32,
    )
    d_ref[...] = direction
    rounded[...] = direction.astype(rounded.dtype)
    upward[...] = jnp.dot(
        rounded[...], ahead_ref[...], preferred_element_type=jnp.float32
    ).T
    own_piece[...] = lax.dot_general(
        pick_ref[...], rounded[...].astype(jnp.float32), contract,
        precision=lax.Precision.HIGHEST, preferred_element_type=jnp.float32,
    )
    _operator_phase(n_sec, n_blk, rounded, upward, own_piece, g_ref, b_ref, a_ref, phase_scratch)
    product = jac_ref[...] * direction
    for j in range(n_blk):
        product = product + lax.dot_general(
            g_ref[:, j * width : (j + 1) * width],
            block_ref[:, j * width : (j + 1) * width],
            contract,
            preferred_element_type=jnp.float32,
        )
    product = product + lax.dot_general(
        b_ref[...].T.astype(back_ref.dtype), back_ref[...], contract,
        preferred_element_type=jnp.float32,
    )
    product = product + jnp.dot(
        spread_ref[...], a_ref[...], precision=lax.Precision.HIGHEST,
        preferred_element_type=jnp.float32,
    ).T
    p_ref[...] = product


def precondition_sweep(
    basis, image, inverse, picks, chain, gain, ahead, block, back, spread, jac, mesh_shape, depth
):
    n_sec, n_blk = mesh_shape["sec"], mesh_shape["blk"]
    stages = _global_stages(mesh_shape)
    cases, width = image.shape
    piece, _ = picks.shape
    panel = piece * n_blk
    plan = _plan(n_sec)
    rounds = len(plan)
    total = sum(len(js) for _, js in plan)
    offsets = len(plan[0][1]) + 1
    dtype = jnp.bfloat16
    return pl.pallas_call(
        functools.partial(_precondition_kernel, n_sec, n_blk, plan, stages, depth),
        out_shape=(
            jax.ShapeDtypeStruct((8, cases), jnp.float32),
            jax.ShapeDtypeStruct((cases, width), jnp.float32),
            jax.ShapeDtypeStruct((cases, width), jnp.float32),
            jax.ShapeDtypeStruct((cases, width), jnp.float32),
        ),
        in_specs=[pl.BlockSpec(memory_space=pltpu.VMEM)] * (depth + 10),
        out_specs=[pl.BlockSpec(memory_space=pltpu.VMEM)] * 4,
        scratch_shapes=[
            pltpu.VMEM((n_blk, cases, width), dtype),
            pltpu.VMEM((piece, cases), jnp.float32),
            pltpu.VMEM((offsets * n_blk, piece, cases), jnp.float32),
            pltpu.VMEM((offsets, panel, cases), jnp.float32),
            pltpu.VMEM((rounds + 1, panel, cases), jnp.float32),
            pltpu.VMEM((total, panel, cases), jnp.float32),
            pltpu.SemaphoreType.DMA((n_blk,)),
            pltpu.SemaphoreType.DMA((n_blk,)),
            pltpu.SemaphoreType.DMA((offsets * n_blk,)),
            pltpu.SemaphoreType.DMA((offsets * n_blk,)),
            pltpu.SemaphoreType.DMA((total,)),
            pltpu.SemaphoreType.DMA((total,)),
            pltpu.VMEM((cases, width), dtype),
            pltpu.VMEM((panel, cases), jnp.float32),
            pltpu.VMEM((piece, cases), jnp.float32),
            pltpu.VMEM((cases, width), dtype),
            pltpu.VMEM((cases, n_blk * width), dtype),
            pltpu.VMEM((panel, cases), jnp.float32),
            pltpu.VMEM((piece, cases), jnp.float32),
        ]
        + _operator_scratch(n_blk, cases, width, dtype, piece, cases)
        + _project_scratch(stages, cases),
        compiler_params=pltpu.CompilerParams(collective_id=10 + depth, has_side_effects=True),
    )(*basis, image, inverse, picks, chain, gain, ahead, block, back, spread, jac)


def _exchange_sum(stages, source, slots, partial, sends, recvs, out):
    count = len(stages)
    for stage, (axis, n) in enumerate(stages):
        mine = lax.axis_index(axis)
        copies = []
        for k in range(1, n):
            copy = pltpu.make_async_remote_copy(
                src_ref=source,
                dst_ref=slots[stage].at[mine],
                send_sem=sends[stage].at[k],
                recv_sem=recvs[stage].at[mine],
                device_id={axis: lax.rem(mine + k, n)},
                device_id_type=MESH,
            )
            copy.start()
            copies.append(copy)
        slots[stage][mine] = source[...]
        for k in range(1, n):
            sender = lax.rem(mine + k, n)
            pltpu.make_async_remote_copy(
                src_ref=source,
                dst_ref=slots[stage].at[sender],
                send_sem=sends[stage].at[k],
                recv_sem=recvs[stage].at[sender],
                device_id={axis: sender},
                device_id_type=MESH,
            ).wait_recv()
        for copy in copies:
            copy.wait_send()
        total = slots[stage][0]
        for j in range(1, n):
            total = total + slots[stage][j]
        if stage == count - 1:
            out[...] = total
        else:
            partial[...] = total
            source = partial


def _project_scratch(stages, cases):
    def buffers():
        out = [pltpu.VMEM((n, 8, cases), jnp.float32) for _, n in stages]
        out.append(pltpu.VMEM((8, cases), jnp.float32))
        out += [pltpu.SemaphoreType.DMA((n,)) for _, n in stages]
        out += [pltpu.SemaphoreType.DMA((n,)) for _, n in stages]
        return out

    return buffers() + buffers() + [pltpu.VMEM((8, cases), jnp.float32)] * 2


def _project_body(stages, depth, basis_refs, image_ref, h_ref, next_ref, scratch):
    count = len(stages)
    first, second = scratch[: 3 * count + 1], scratch[3 * count + 1 : 6 * count + 2]
    rows, work = scratch[6 * count + 2 : 6 * count + 4]
    highest = lax.Precision.HIGHEST
    contract = (((1,), (1,)), ((), ()))
    image = image_ref[...]
    ones = jnp.ones((8, image.shape[1]), jnp.float32)
    eye = (
        lax.broadcasted_iota(jnp.int32, (image.shape[0],) * 2, 0)
        == lax.broadcasted_iota(jnp.int32, (image.shape[0],) * 2, 1)
    ).astype(jnp.float32)

    def run(buffers, source, out):
        slots = buffers[:count]
        partial = buffers[count]
        sends = buffers[count + 1 : 2 * count + 1]
        recvs = buffers[2 * count + 1 :]
        _exchange_sum(stages, source, slots, partial, sends, recvs, out)

    if depth > 0:
        rows[...] = jnp.zeros_like(rows)
        for i in range(depth):
            summed = lax.dot_general(
                ones, image * basis_refs[i][...], contract, precision=highest,
                preferred_element_type=jnp.float32,
            )
            rows[i : i + 1, :] = summed[0:1, :]
        run(first, rows, h_ref)
        columns = lax.dot_general(
            eye, h_ref[...], contract, precision=highest, preferred_element_type=jnp.float32
        )
        for i in range(depth):
            image = image - columns[:, i : i + 1] * basis_refs[i][...]
    else:
        h_ref[...] = jnp.zeros_like(h_ref)
    work[...] = lax.dot_general(
        ones, image * image, contract, precision=highest, preferred_element_type=jnp.float32
    )
    run(second, work, rows)
    length = jnp.sqrt(rows[...] + epsilon)
    h_ref[depth : depth + 1, :] = length[0:1, :]
    scale = lax.dot_general(
        eye, length, contract, precision=highest, preferred_element_type=jnp.float32
    )
    next_ref[...] = image / scale[:, 0:1]


def _signal_stages(barrier, stages):
    peers = 0
    for axis, n in stages:
        mine = lax.axis_index(axis)
        for k in range(1, n):
            pl.semaphore_signal(
                barrier, inc=1, device_id={axis: lax.rem(mine + k, n)}, device_id_type=MESH
            )
            peers += 1
    return peers


def _project_kernel(stages, depth, *refs):
    basis_refs = refs[:depth]
    image_ref, h_ref, next_ref = refs[depth : depth + 3]
    barrier = pltpu.get_barrier_semaphore()
    pl.semaphore_wait(barrier, _signal_stages(barrier, stages))
    _project_body(stages, depth, basis_refs, image_ref, h_ref, next_ref, refs[depth + 3 :])


def _global_stages(mesh_shape):
    return tuple((axis, mesh_shape[axis]) for axis in ("blk", "sec") if mesh_shape[axis] > 1)


def project(basis, image, mesh_shape):
    depth = len(basis)
    cases, width = image.shape
    stages = _global_stages(mesh_shape)
    return pl.pallas_call(
        functools.partial(_project_kernel, stages, depth),
        out_shape=(
            jax.ShapeDtypeStruct((8, cases), jnp.float32),
            jax.ShapeDtypeStruct((cases, width), jnp.float32),
        ),
        in_specs=[pl.BlockSpec(memory_space=pltpu.VMEM)] * (depth + 1),
        out_specs=[pl.BlockSpec(memory_space=pltpu.VMEM)] * 2,
        scratch_shapes=_project_scratch(stages, cases),
        compiler_params=pltpu.CompilerParams(collective_id=6 + depth, has_side_effects=True),
    )(*basis, image)


def least_squares(columns, beta, depth):
    zero = jnp.zeros_like(beta)
    upper = [
        [columns[j][i] if i <= j + 1 else zero for j in range(depth)] for i in range(depth + 1)
    ]
    rhs = [beta] + [zero] * depth
    for column in range(depth):
        upper_row, lower_row = upper[column], upper[column + 1]
        radius = jnp.sqrt(upper_row[column] ** 2 + lower_row[column] ** 2)
        cosine = upper_row[column] / radius
        sine_term = lower_row[column] / radius
        upper[column] = [cosine * a + sine_term * b for a, b in zip(upper_row, lower_row)]
        upper[column + 1] = [-sine_term * a + cosine * b for a, b in zip(upper_row, lower_row)]
        first_rhs, second_rhs = rhs[column], rhs[column + 1]
        rhs[column] = cosine * first_rhs + sine_term * second_rhs
        rhs[column + 1] = -sine_term * first_rhs + cosine * second_rhs
    weights = [zero] * depth
    for column in reversed(range(depth)):
        remain = rhs[column]
        if column + 1 < depth:
            tail = upper[column][column + 1] * weights[column + 1]
            for k in range(column + 2, depth):
                tail = tail + upper[column][k] * weights[k]
            remain = remain - tail
        weights[column] = remain / upper[column][column]
    return weights

def local(
    mesh_shape,
    state_now, source, fan_gain, section_block, block_inverse, back_panel, ahead_panel, interface
):
    highest = lax.Precision.HIGHEST
    cases, node_rows = state_now.shape
    panel_width = back_panel.shape[1]
    indices = interface[0]
    first_row = lax.axis_index("blk") * node_rows
    selector = (indices[None, :] == first_row + jnp.arange(node_rows)[:, None]).astype(jnp.float32)
    contract = (((1,), (1,)), ((), ()))

    own_piece = panel_width // mesh_shape["blk"]
    own_picks = lax.dynamic_slice_in_dim(selector, lax.axis_index("blk") * own_piece, own_piece, 1).T

    def section_terms(dense_part, behind_vals, piece):
        width = piece.shape[1]
        dense_part = lax.dot_general(
            piece, section_block, contract, preferred_element_type=jnp.float32
        )
        picker = (indices[None, :] == jnp.arange(width)[:, None]).astype(jnp.bfloat16)
        behind_vals = jnp.dot(piece, picker, preferred_element_type=jnp.float32)
        return (dense_part, behind_vals)

    def fold_section(carry, piece):
        return section_terms(carry[0], carry[1], piece)

    n_sec, n_blk = mesh_shape["sec"], mesh_shape["blk"]
    piece = panel_width // n_blk
    local_picks = lax.dynamic_slice_in_dim(selector, lax.axis_index("blk") * piece, piece, 1)

    def finish(gathered, behind_t, ahead_piece):
        dense_part = lax.dot_general(
            gathered, section_block, contract, preferred_element_type=jnp.float32
        )
        lower_term = lax.dot_general(
            behind_t.astype(jnp.bfloat16),
            back_panel,
            (((0,), (1,)), ((), ())),
            preferred_element_type=jnp.float32,
        )
        upper_term = lax.dot_general(
            ahead_piece, local_picks, (((0,), (1,)), ((), ())), precision=highest
        )
        return dense_part + lower_term + upper_term

    def operator(vector):
        rounded = vector.astype(jnp.bfloat16)
        up_t = lax.dot_general(
            ahead_panel, rounded, (((0,), (1,)), ((), ())), preferred_element_type=jnp.float32
        )
        be_t = lax.dot_general(
            selector.astype(jnp.bfloat16),
            rounded,
            (((0,), (1,)), ((), ())),
            preferred_element_type=jnp.float32,
        )
        return finish(*operator_exchange(rounded, up_t, be_t, n_sec, n_blk))

    def compose(earlier, later):
        first_map, first_value = earlier
        second_map, second_value = later
        joined_map = jnp.dot(second_map, first_map, precision=highest)
        joined_value = jnp.dot(first_value, second_map.T, precision=highest) + second_value
        return (joined_map, joined_value)

    def lengths(vector):
        return jnp.sqrt(global_sum(jnp.sum(vector * vector, axis=1)[None], mesh_shape)[0] + epsilon)

    bent = jnp.tanh(state_now)
    state_rounded = state_now.astype(jnp.bfloat16)
    applied, gain_panel, chain = setup_exchange(
        state_rounded, ahead_panel, section_block, local_picks, back_panel, block_inverse,
        own_picks, n_sec, n_blk,
    )
    residual = source - applied - fan_gain[None, :] * bent
    jac_diag = fan_gain[None, :] * (1.0 - bent * bent)
    columns = []
    basis = []
    directions = []
    product = residual
    beta = None
    for column in range(KRYLOV):
        sums, following, direction, product = precondition_sweep(
            list(basis), product, block_inverse, own_picks, chain, gain_panel, ahead_panel,
            section_block, back_panel, local_picks, jac_diag, mesh_shape, len(basis),
        )
        if column == 0:
            beta = sums[0]
        else:
            columns.append(sums[: column + 1])
        basis.append(following)
        directions.append(direction)
    sums, _ = project(basis, product, mesh_shape)
    columns.append(sums[: KRYLOV + 1])
    weights = least_squares(columns, beta, KRYLOV)
    update = jnp.zeros_like(state_now)
    for column in range(KRYLOV):
        update = update + weights[column][:, None] * directions[column]
    return state_now + update


def solution(mesh):
    in_specs = (
        P(None, ("sec", "blk")),
        P(None, ("sec", "blk")),
        P(("sec", "blk")),
        P(("sec", "blk"), None),
        P(("sec", "blk"), None),
        P(("sec", "blk"), None),
        P(("sec", "blk"), None),
        P("sec", None),
    )
    out_specs = P(None, ("sec", "blk"))
    return jax.shard_map(functools.partial(local, dict(mesh.shape)), mesh=mesh, in_specs=in_specs, out_specs=out_specs, check_vma=False)
```

```python
import functools

import jax
import jax.numpy as jnp
from jax import lax
from jax.experimental import pallas as pl
from jax.experimental.pallas import tpu as pltpu
from jax.sharding import PartitionSpec as P

MESH = pl.DeviceIdType.MESH

KRYLOV = 3


epsilon = 1e-06


def extended(x, sides, width):
    for axis, dim in sides:
        size, length = (lax.axis_size(axis), x.shape[dim])
        up = [(i, (i + 1) % size) for i in range(size - 1)]
        down = [(j, i) for i, j in up]
        last = lax.slice_in_dim(x, length - width, length, axis=dim)
        first = lax.slice_in_dim(x, 0, width, axis=dim)
        before = lax.ppermute(last, axis, up)
        after = lax.ppermute(first, axis, down)
        x = jnp.concatenate([before, x, after], axis=dim)
    return x


def entering(value, axis, join, neutral):
    count, mine = (lax.axis_size(axis), lax.axis_index(axis))
    pieces = jax.tree.map(lambda part: lax.all_gather(part, axis), value)
    so_far = jax.tree.map(
        lambda part, zero: jnp.full_like(part, 0) + jnp.asarray(zero, part.dtype), value, neutral
    )

    def step(position, so_far):
        longer = join(so_far, jax.tree.map(lambda part: part[position], pieces))
        return jax.tree.map(lambda new, old: jnp.where(position < mine, new, old), longer, so_far)

    return lax.fori_loop(0, count - 1, step, so_far)


def _reduce_kernel(stages, x_ref, o_ref, *scratch):
    count = len(stages)
    slots = scratch[:count]
    partial = scratch[count]
    sends = scratch[count + 1 : 2 * count + 1]
    recvs = scratch[2 * count + 1 :]
    barrier = pltpu.get_barrier_semaphore()
    peers = 0
    for axis, n in stages:
        mine = lax.axis_index(axis)
        for k in range(1, n):
            pl.semaphore_signal(
                barrier, inc=1, device_id={axis: lax.rem(mine + k, n)}, device_id_type=MESH
            )
            peers += 1
    pl.semaphore_wait(barrier, peers)
    source = x_ref
    for stage, (axis, n) in enumerate(stages):
        mine = lax.axis_index(axis)
        copies = []
        for k in range(1, n):
            copy = pltpu.make_async_remote_copy(
                src_ref=source,
                dst_ref=slots[stage].at[mine],
                send_sem=sends[stage].at[k],
                recv_sem=recvs[stage].at[mine],
                device_id={axis: lax.rem(mine + k, n)},
                device_id_type=MESH,
            )
            copy.start()
            copies.append(copy)
        slots[stage][mine] = source[...]
        for k in range(1, n):
            sender = lax.rem(mine + k, n)
            pltpu.make_async_remote_copy(
                src_ref=source,
                dst_ref=slots[stage].at[sender],
                send_sem=sends[stage].at[k],
                recv_sem=recvs[stage].at[sender],
                device_id={axis: sender},
                device_id_type=MESH,
            ).wait_recv()
        for copy in copies:
            copy.wait_send()
        total = slots[stage][0]
        for j in range(1, n):
            total = total + slots[stage][j]
        if stage == count - 1:
            o_ref[...] = total
        else:
            partial[...] = total
            source = partial


def all_sum(x, axes, mesh_shape, collective):
    stages = tuple((axis, mesh_shape[axis]) for axis in axes if mesh_shape[axis] > 1)
    rows, cols = x.shape
    scratch = [pltpu.VMEM((n, rows, cols), jnp.float32) for _, n in stages]
    scratch.append(pltpu.VMEM((rows, cols), jnp.float32))
    scratch += [pltpu.SemaphoreType.DMA((n,)) for _, n in stages]
    scratch += [pltpu.SemaphoreType.DMA((n,)) for _, n in stages]
    return pl.pallas_call(
        functools.partial(_reduce_kernel, stages),
        out_shape=jax.ShapeDtypeStruct((rows, cols), jnp.float32),
        in_specs=[pl.BlockSpec(memory_space=pltpu.VMEM)],
        out_specs=pl.BlockSpec(memory_space=pltpu.VMEM),
        scratch_shapes=scratch,
        compiler_params=pltpu.CompilerParams(collective_id=collective, has_side_effects=True),
    )(x.astype(jnp.float32))


def global_sum(rows_of_sums, mesh_shape):
    count = rows_of_sums.shape[0]
    padded = jnp.zeros((8, rows_of_sums.shape[1]), jnp.float32).at[:count].set(rows_of_sums)
    return all_sum(padded, ("blk", "sec"), mesh_shape, 0)[:count]


def _doubling(n):
    distances, d = [], 1
    while d < n:
        distances.append(d)
        d *= 2
    return tuple(distances)


def _greet(n, distances):
    barrier = pltpu.get_barrier_semaphore()
    mine = lax.axis_index("sec")
    for d in distances:
        for peer in (lax.rem(mine + d, n), lax.rem(mine + n - d, n)):
            pl.semaphore_signal(barrier, inc=1, device_id={"sec": peer}, device_id_type=MESH)
    pl.semaphore_wait(barrier, 2 * len(distances))


def _hop(n, d, source, slot, send_sem, recv_sem):
    mine = lax.axis_index("sec")
    copy = pltpu.make_async_remote_copy(
        src_ref=source,
        dst_ref=slot,
        send_sem=send_sem,
        recv_sem=recv_sem,
        device_id={"sec": lax.rem(mine + d, n)},
        device_id_type=MESH,
    )
    copy.start()
    copy.wait_recv()
    copy.wait_send()


RADIX = 8


def _plan(n):
    rounds, d = [], 1
    while d < n:
        rounds.append((d, tuple(j for j in range(1, RADIX) if j * d < n)))
        d *= RADIX
    return tuple(rounds)


def _plan_peers(rounds):
    return tuple(sorted({j * d for d, js in rounds for j in js} | {1}))


def _send_all(n, sec, sources, slots, sends, recvs, flat, d, js):
    copies = []
    for i, j in enumerate(js):
        copy = pltpu.make_async_remote_copy(
            src_ref=sources,
            dst_ref=slots.at[flat + i],
            send_sem=sends.at[flat + i],
            recv_sem=recvs.at[flat + i],
            device_id={"sec": lax.rem(sec + j * d, n)},
            device_id_type=MESH,
        )
        copy.start()
        copies.append(copy)
    for copy in copies:
        copy.wait_recv()
    for copy in copies:
        copy.wait_send()


def _spread(n_sec, n_blk, offsets, piece_ref, slots, sends, recvs):
    sec, blk = lax.axis_index("sec"), lax.axis_index("blk")

    def copy(o, j, index):
        return pltpu.make_async_remote_copy(
            src_ref=piece_ref,
            dst_ref=slots.at[index],
            send_sem=sends.at[(o - 1) * n_blk + j],
            recv_sem=recvs.at[index],
            device_id={"sec": lax.rem(sec + o, n_sec), "blk": j},
            device_id_type=MESH,
        )

    outgoing = [
        copy(o, j, (o - 1) * n_blk + blk) for o in range(1, offsets + 1) for j in range(n_blk)
    ]
    for c in outgoing:
        c.start()
    for o in range(1, offsets + 1):
        for j in range(n_blk):
            copy(o, j, (o - 1) * n_blk + j).wait_recv()
    for c in outgoing:
        c.wait_send()


def _assemble(n_blk, offsets, slots, mats):
    piece = slots.shape[1]
    for o in range(offsets):
        for j in range(n_blk):
            mats[o, j * piece : (j + 1) * piece, :] = slots[o * n_blk + j]


def _greet_all(n_sec, n_blk, offsets, rounds, blk_peers, stages=()):
    barrier = pltpu.get_barrier_semaphore()
    sec, blk = lax.axis_index("sec"), lax.axis_index("blk")
    count = _signal_stages(barrier, stages)
    if blk_peers:
        for k in range(1, n_blk):
            pl.semaphore_signal(
                barrier, inc=1, device_id={"blk": lax.rem(blk + k, n_blk)}, device_id_type=MESH
            )
            count += 1
    for o in range(1, offsets + 1):
        for j in range(n_blk):
            for peer in (lax.rem(sec + o, n_sec), lax.rem(sec + n_sec - o, n_sec)):
                pl.semaphore_signal(
                    barrier, inc=1, device_id={"sec": peer, "blk": j}, device_id_type=MESH
                )
                count += 1
    for d in sorted({j * d for d, js in rounds[1:] for j in js}):
        for peer in (lax.rem(sec + d, n_sec), lax.rem(sec + n_sec - d, n_sec)):
            pl.semaphore_signal(barrier, inc=1, device_id={"sec": peer}, device_id_type=MESH)
            count += 1
    pl.semaphore_wait(barrier, count)


def _maps_body(n, n_blk, rounds, e_ref, a_ref, eslots, emat, current, slots, esend, erecv, sends, recvs):
    sec = lax.axis_index("sec")
    first = rounds[0][1]
    offsets = len(first) + 1
    _spread(n, n_blk, offsets, e_ref, eslots, esend, erecv)
    _assemble(n_blk, offsets, eslots, emat)
    joined = emat[0]
    for i, j in enumerate(first):
        a_ref[i] = joined
        joined = jnp.dot(
            joined, emat[j], precision=lax.Precision.HIGHEST, preferred_element_type=jnp.float32
        )
    current[...] = joined
    flat = len(first)
    for k in range(1, len(rounds)):
        d, js = rounds[k]
        onward = k < len(rounds) - 1
        if onward or len(js) > 1:
            _send_all(n, sec, current, slots, sends, recvs, flat, d, js)
        joined = current[...]
        for i, j in enumerate(js):
            a_ref[flat + i] = joined
            if onward or i < len(js) - 1:
                joined = jnp.dot(
                    joined, slots[flat + i], precision=lax.Precision.HIGHEST,
                    preferred_element_type=jnp.float32,
                )
        if onward:
            current[...] = joined
        flat += len(js)


def _setup_kernel(
    n_sec, n_blk, rounds, x_ref, ahead_ref, block_ref, spread_ref, back_ref, inv_ref, pick_ref,
    k_ref, gain_ref, chain_ref, *scratch
):
    phase_scratch = scratch[:9]
    pslots, psend, precv, epiece = scratch[9:13]
    g_ref, b_ref, a_ref, upward, own_piece = scratch[13:18]
    maps_scratch = scratch[18:]
    sec, blk = lax.axis_index("sec"), lax.axis_index("blk")
    offsets = len(rounds[0][1]) + 1
    _greet_all(n_sec, n_blk, offsets, rounds, True)
    contract = (((1,), (1,)), ((), ()))
    upward[...] = jnp.dot(x_ref[...], ahead_ref[...], preferred_element_type=jnp.float32).T
    own_piece[...] = lax.dot_general(
        pick_ref[...], x_ref[...].astype(jnp.float32), contract,
        precision=lax.Precision.HIGHEST, preferred_element_type=jnp.float32,
    )
    _operator_phase(n_sec, n_blk, x_ref, upward, own_piece, g_ref, b_ref, a_ref, phase_scratch)
    width = x_ref.shape[1]
    product = lax.dot_general(
        g_ref[:, 0:width], block_ref[:, 0:width], contract, preferred_element_type=jnp.float32
    )
    for j in range(1, n_blk):
        product = product + lax.dot_general(
            g_ref[:, j * width : (j + 1) * width],
            block_ref[:, j * width : (j + 1) * width],
            contract,
            preferred_element_type=jnp.float32,
        )
    product = product + lax.dot_general(
        b_ref[...].T.astype(back_ref.dtype), back_ref[...], contract,
        preferred_element_type=jnp.float32,
    )
    product = product + jnp.dot(
        spread_ref[...], a_ref[...], precision=lax.Precision.HIGHEST,
        preferred_element_type=jnp.float32,
    ).T
    k_ref[...] = product

    def blk_copy(k, target, slot):
        return pltpu.make_async_remote_copy(
            src_ref=back_ref,
            dst_ref=pslots.at[slot],
            send_sem=psend.at[k],
            recv_sem=precv.at[slot],
            device_id={"blk": target},
            device_id_type=MESH,
        )

    outgoing = [blk_copy(k, lax.rem(blk + k, n_blk), blk) for k in range(1, n_blk)]
    for copy in outgoing:
        copy.start()
    pslots[blk] = back_ref[...]
    for k in range(1, n_blk):
        sender = lax.rem(blk + k, n_blk)
        blk_copy(k, sender, sender).wait_recv()
    for copy in outgoing:
        copy.wait_send()
    rows = back_ref.shape[0]
    gain = jnp.dot(inv_ref[:, 0:rows], pslots[0], preferred_element_type=jnp.float32)
    for j in range(1, n_blk):
        gain = gain + jnp.dot(
            inv_ref[:, j * rows : (j + 1) * rows], pslots[j], preferred_element_type=jnp.float32
        )
    gain_ref[...] = gain
    epiece[...] = -jnp.dot(
        pick_ref[...], gain, precision=lax.Precision.HIGHEST, preferred_element_type=jnp.float32
    )
    _maps_body(n_sec, n_blk, rounds, epiece, chain_ref, *maps_scratch)


def setup_exchange(x, ahead, block, spread, back, inverse, picks, n_sec, n_blk):
    cases, width = x.shape
    panel = ahead.shape[1]
    piece = panel // n_blk
    rows, panel_width = back.shape
    rounds = _plan(n_sec)
    total = sum(len(js) for _, js in rounds)
    offsets = len(rounds[0][1]) + 1
    return pl.pallas_call(
        functools.partial(_setup_kernel, n_sec, n_blk, rounds),
        out_shape=(
            jax.ShapeDtypeStruct((cases, width), jnp.float32),
            jax.ShapeDtypeStruct((rows, panel_width), jnp.float32),
            jax.ShapeDtypeStruct((total, panel_width, panel_width), jnp.float32),
        ),
        in_specs=[pl.BlockSpec(memory_space=pltpu.VMEM)] * 7,
        out_specs=[pl.BlockSpec(memory_space=pltpu.VMEM)] * 3,
        scratch_shapes=_operator_scratch(n_blk, cases, width, x.dtype, piece, cases)
        + [
            pltpu.VMEM((n_blk, rows, panel_width), back.dtype),
            pltpu.SemaphoreType.DMA((n_blk,)),
            pltpu.SemaphoreType.DMA((n_blk,)),
            pltpu.VMEM((piece, panel_width), jnp.float32),
            pltpu.VMEM((cases, n_blk * width), x.dtype),
            pltpu.VMEM((panel, cases), jnp.float32),
            pltpu.VMEM((piece, cases), jnp.float32),
            pltpu.VMEM((panel, cases), jnp.float32),
            pltpu.VMEM((piece, cases), jnp.float32),
            pltpu.VMEM((offsets * n_blk, piece, panel_width), jnp.float32),
            pltpu.VMEM((offsets, panel_width, panel_width), jnp.float32),
            pltpu.VMEM((panel_width, panel_width), jnp.float32),
            pltpu.VMEM((total, panel_width, panel_width), jnp.float32),
            pltpu.SemaphoreType.DMA((offsets * n_blk,)),
            pltpu.SemaphoreType.DMA((offsets * n_blk,)),
            pltpu.SemaphoreType.DMA((total,)),
            pltpu.SemaphoreType.DMA((total,)),
        ],
        compiler_params=pltpu.CompilerParams(collective_id=3, has_side_effects=True),
    )(x, ahead, block, spread, back, inverse, picks)


def _gather_kernel(n, x_ref, o_ref, slots, sends, recvs):
    mine = lax.axis_index("blk")
    barrier = pltpu.get_barrier_semaphore()
    for k in range(1, n):
        pl.semaphore_signal(
            barrier, inc=1, device_id={"blk": lax.rem(mine + k, n)}, device_id_type=MESH
        )
    pl.semaphore_wait(barrier, n - 1)
    copies = []
    for k in range(1, n):
        copy = pltpu.make_async_remote_copy(
            src_ref=x_ref,
            dst_ref=slots.at[mine],
            send_sem=sends.at[k],
            recv_sem=recvs.at[mine],
            device_id={"blk": lax.rem(mine + k, n)},
            device_id_type=MESH,
        )
        copy.start()
        copies.append(copy)
    slots[mine] = x_ref[...]
    for k in range(1, n):
        sender = lax.rem(mine + k, n)
        pltpu.make_async_remote_copy(
            src_ref=x_ref,
            dst_ref=slots.at[sender],
            send_sem=sends.at[k],
            recv_sem=recvs.at[sender],
            device_id={"blk": sender},
            device_id_type=MESH,
        ).wait_recv()
    for copy in copies:
        copy.wait_send()
    width = x_ref.shape[1]
    for j in range(n):
        o_ref[:, j * width : (j + 1) * width] = slots[j]


def gather_blk(x, n):
    rows, width = x.shape
    return pl.pallas_call(
        functools.partial(_gather_kernel, n),
        out_shape=jax.ShapeDtypeStruct((rows, n * width), x.dtype),
        in_specs=[pl.BlockSpec(memory_space=pltpu.VMEM)],
        out_specs=pl.BlockSpec(memory_space=pltpu.VMEM),
        scratch_shapes=[
            pltpu.VMEM((n, rows, width), x.dtype),
            pltpu.SemaphoreType.DMA((n,)),
            pltpu.SemaphoreType.DMA((n,)),
        ],
        compiler_params=pltpu.CompilerParams(collective_id=4, has_side_effects=True),
    )(x)


def _operator_phase(n_sec, n_blk, x_ref, up_ref, piece_ref, g_ref, b_ref, a_ref, scratch):
    gslots, bslots, aslots, gsend, grecv, bsend, brecv, asend, arecv = scratch
    sec, blk = lax.axis_index("sec"), lax.axis_index("blk")
    nxt, prv = lax.rem(sec + 1, n_sec), lax.rem(sec + n_sec - 1, n_sec)
    piece = bslots.shape[1]
    copies = []
    for k in range(1, n_blk):
        copies.append(
            pltpu.make_async_remote_copy(
                src_ref=x_ref,
                dst_ref=gslots.at[blk],
                send_sem=gsend.at[k],
                recv_sem=grecv.at[blk],
                device_id={"blk": lax.rem(blk + k, n_blk)},
                device_id_type=MESH,
            )
        )
    for j in range(n_blk):
        copies.append(
            pltpu.make_async_remote_copy(
                src_ref=piece_ref,
                dst_ref=bslots.at[blk],
                send_sem=bsend.at[j],
                recv_sem=brecv.at[blk],
                device_id={"sec": nxt, "blk": j},
                device_id_type=MESH,
            )
        )
        copies.append(
            pltpu.make_async_remote_copy(
                src_ref=up_ref.at[pl.ds(j * piece, piece)],
                dst_ref=aslots.at[blk],
                send_sem=asend.at[j],
                recv_sem=arecv.at[blk],
                device_id={"sec": prv, "blk": j},
                device_id_type=MESH,
            )
        )
    for copy in copies:
        copy.start()
    gslots[blk] = x_ref[...]
    for k in range(1, n_blk):
        sender = lax.rem(blk + k, n_blk)
        pltpu.make_async_remote_copy(
            src_ref=x_ref,
            dst_ref=gslots.at[sender],
            send_sem=gsend.at[k],
            recv_sem=grecv.at[sender],
            device_id={"blk": sender},
            device_id_type=MESH,
        ).wait_recv()
    for j in range(n_blk):
        pltpu.make_async_remote_copy(
            src_ref=piece_ref,
            dst_ref=bslots.at[j],
            send_sem=bsend.at[j],
            recv_sem=brecv.at[j],
            device_id={"sec": prv, "blk": j},
            device_id_type=MESH,
        ).wait_recv()
        pltpu.make_async_remote_copy(
            src_ref=up_ref.at[pl.ds(j * piece, piece)],
            dst_ref=aslots.at[j],
            send_sem=asend.at[j],
            recv_sem=arecv.at[j],
            device_id={"sec": nxt, "blk": j},
            device_id_type=MESH,
        ).wait_recv()
    for copy in copies:
        copy.wait_send()
    width = x_ref.shape[1]
    for j in range(n_blk):
        g_ref[:, j * width : (j + 1) * width] = gslots[j]
        b_ref[j * piece : (j + 1) * piece, :] = jnp.where(
            sec >= 1, bslots[j], jnp.zeros_like(bslots[j])
        )
    total = aslots[0]
    for j in range(1, n_blk):
        total = total + aslots[j]
    a_ref[...] = jnp.where(sec <= n_sec - 2, total, jnp.zeros_like(total))


def _operator_scratch(n_blk, rows, width, dtype, piece, cases):
    return [
        pltpu.VMEM((n_blk, rows, width), dtype),
        pltpu.VMEM((n_blk, piece, cases), jnp.float32),
        pltpu.VMEM((n_blk, piece, cases), jnp.float32),
    ] + [pltpu.SemaphoreType.DMA((n_blk,))] * 6


def _operator_kernel(n_sec, n_blk, x_ref, up_ref, be_ref, g_ref, b_ref, a_ref, *scratch):
    sec, blk = lax.axis_index("sec"), lax.axis_index("blk")
    nxt, prv = lax.rem(sec + 1, n_sec), lax.rem(sec + n_sec - 1, n_sec)
    piece = scratch[1].shape[1]
    barrier = pltpu.get_barrier_semaphore()
    for k in range(1, n_blk):
        pl.semaphore_signal(
            barrier, inc=1, device_id={"blk": lax.rem(blk + k, n_blk)}, device_id_type=MESH
        )
    for j in range(n_blk):
        for other in (nxt, prv):
            pl.semaphore_signal(
                barrier, inc=1, device_id={"sec": other, "blk": j}, device_id_type=MESH
            )
    pl.semaphore_wait(barrier, 3 * n_blk - 1)
    mine = be_ref.at[pl.ds(pl.multiple_of(blk * piece, 8), piece)]
    _operator_phase(n_sec, n_blk, x_ref, up_ref, mine, g_ref, b_ref, a_ref, scratch)


def operator_exchange(x, up_t, be_t, n_sec, n_blk):
    rows, width = x.shape
    panel, cases = up_t.shape
    piece = panel // n_blk
    return pl.pallas_call(
        functools.partial(_operator_kernel, n_sec, n_blk),
        out_shape=(
            jax.ShapeDtypeStruct((rows, n_blk * width), x.dtype),
            jax.ShapeDtypeStruct((panel, cases), jnp.float32),
            jax.ShapeDtypeStruct((piece, cases), jnp.float32),
        ),
        in_specs=[pl.BlockSpec(memory_space=pltpu.VMEM)] * 3,
        out_specs=[pl.BlockSpec(memory_space=pltpu.VMEM)] * 3,
        scratch_shapes=_operator_scratch(n_blk, rows, width, x.dtype, piece, cases),
        compiler_params=pltpu.CompilerParams(collective_id=5, has_side_effects=True),
    )(x, up_t, be_t)


def _precondition_kernel(n_sec, n_blk, rounds, stages, depth, *refs):
    basis_refs = refs[:depth]
    (image_ref, inv_ref, pick_ref, u_ref, gain_ref, ahead_ref, block_ref, back_ref, spread_ref,
     jac_ref, h_ref, next_ref, d_ref, p_ref) = refs[depth : depth + 14]
    scratch = refs[depth + 14 :]
    gslots, fpiece, fslots, fmat, carry, slots, gsend, grecv, fsend, frecv, ssend, srecv = scratch[:12]
    rounded, upward, own_piece, x_ref = scratch[12:16]
    g_ref, b_ref, a_ref = scratch[16:19]
    phase_scratch = scratch[19:28]
    project_scratch = scratch[28:]
    sec, blk = lax.axis_index("sec"), lax.axis_index("blk")
    first = rounds[0][1]
    offsets = len(first) + 1
    _greet_all(n_sec, n_blk, offsets, rounds, True, stages)
    _project_body(stages, depth, basis_refs, image_ref, h_ref, next_ref, project_scratch)
    x_ref[...] = next_ref[...].astype(x_ref.dtype)

    def blk_copy(k, target, slot):
        return pltpu.make_async_remote_copy(
            src_ref=x_ref,
            dst_ref=gslots.at[slot],
            send_sem=gsend.at[k],
            recv_sem=grecv.at[slot],
            device_id={"blk": target},
            device_id_type=MESH,
        )

    outgoing = [blk_copy(k, lax.rem(blk + k, n_blk), blk) for k in range(1, n_blk)]
    for copy in outgoing:
        copy.start()
    gslots[blk] = x_ref[...]
    for k in range(1, n_blk):
        sender = lax.rem(blk + k, n_blk)
        blk_copy(k, sender, sender).wait_recv()
    for copy in outgoing:
        copy.wait_send()
    width = x_ref.shape[1]
    contract = (((1,), (1,)), ((), ()))
    folded = lax.dot_general(
        gslots[0], inv_ref[:, 0:width], contract, preferred_element_type=jnp.float32
    )
    for j in range(1, n_blk):
        folded = folded + lax.dot_general(
            gslots[j],
            inv_ref[:, j * width : (j + 1) * width],
            contract,
            preferred_element_type=jnp.float32,
        )
    fpiece[...] = lax.dot_general(
        pick_ref[...], folded, contract, precision=lax.Precision.HIGHEST,
        preferred_element_type=jnp.float32,
    )
    _spread(n_sec, n_blk, offsets, fpiece, fslots, fsend, frecv)
    _assemble(n_blk, offsets, fslots, fmat)
    joined = jnp.where(sec >= 1, fmat[0], jnp.zeros_like(fmat[0]))
    for i, j in enumerate(first):
        term = jnp.dot(
            u_ref[i], fmat[j], precision=lax.Precision.HIGHEST, preferred_element_type=jnp.float32
        )
        joined = joined + jnp.where(sec >= j + 1, term, jnp.zeros_like(term))
    carry[1] = joined
    flat = len(first)
    for k in range(1, len(rounds)):
        d, js = rounds[k]
        _send_all(n_sec, sec, carry.at[k], slots, ssend, srecv, flat, d, js)
        joined = carry[k]
        for i, j in enumerate(js):
            term = jnp.dot(
                u_ref[flat + i], slots[flat + i], precision=lax.Precision.HIGHEST,
                preferred_element_type=jnp.float32,
            )
            joined = joined + jnp.where(sec >= j * d, term, jnp.zeros_like(term))
        carry[k + 1] = joined
        flat += len(js)
    before = carry[len(rounds)].T
    direction = folded - lax.dot_general(
        before, gain_ref[...], contract, precision=lax.Precision.HIGHEST,
        preferred_element_type=jnp.float32,
    )
    d_ref[...] = direction
    rounded[...] = direction.astype(rounded.dtype)
    upward[...] = jnp.dot(
        rounded[...], ahead_ref[...], preferred_element_type=jnp.float32
    ).T
    own_piece[...] = lax.dot_general(
        pick_ref[...], rounded[...].astype(jnp.float32), contract,
        precision=lax.Precision.HIGHEST, preferred_element_type=jnp.float32,
    )
    _operator_phase(n_sec, n_blk, rounded, upward, own_piece, g_ref, b_ref, a_ref, phase_scratch)
    product = jac_ref[...] * direction
    for j in range(n_blk):
        product = product + lax.dot_general(
            g_ref[:, j * width : (j + 1) * width],
            block_ref[:, j * width : (j + 1) * width],
            contract,
            preferred_element_type=jnp.float32,
        )
    product = product + lax.dot_general(
        b_ref[...].T.astype(back_ref.dtype), back_ref[...], contract,
        preferred_element_type=jnp.float32,
    )
    product = product + jnp.dot(
        spread_ref[...], a_ref[...], precision=lax.Precision.HIGHEST,
        preferred_element_type=jnp.float32,
    ).T
    p_ref[...] = product


def precondition_sweep(
    basis, image, inverse, picks, chain, gain, ahead, block, back, spread, jac, mesh_shape, depth
):
    n_sec, n_blk = mesh_shape["sec"], mesh_shape["blk"]
    stages = _global_stages(mesh_shape)
    cases, width = image.shape
    piece, _ = picks.shape
    panel = piece * n_blk
    plan = _plan(n_sec)
    rounds = len(plan)
    total = sum(len(js) for _, js in plan)
    offsets = len(plan[0][1]) + 1
    dtype = jnp.bfloat16
    return pl.pallas_call(
        functools.partial(_precondition_kernel, n_sec, n_blk, plan, stages, depth),
        out_shape=(
            jax.ShapeDtypeStruct((8, cases), jnp.float32),
            jax.ShapeDtypeStruct((cases, width), jnp.float32),
            jax.ShapeDtypeStruct((cases, width), jnp.float32),
            jax.ShapeDtypeStruct((cases, width), jnp.float32),
        ),
        in_specs=[pl.BlockSpec(memory_space=pltpu.VMEM)] * (depth + 10),
        out_specs=[pl.BlockSpec(memory_space=pltpu.VMEM)] * 4,
        scratch_shapes=[
            pltpu.VMEM((n_blk, cases, width), dtype),
            pltpu.VMEM((piece, cases), jnp.float32),
            pltpu.VMEM((offsets * n_blk, piece, cases), jnp.float32),
            pltpu.VMEM((offsets, panel, cases), jnp.float32),
            pltpu.VMEM((rounds + 1, panel, cases), jnp.float32),
            pltpu.VMEM((total, panel, cases), jnp.float32),
            pltpu.SemaphoreType.DMA((n_blk,)),
            pltpu.SemaphoreType.DMA((n_blk,)),
            pltpu.SemaphoreType.DMA((offsets * n_blk,)),
            pltpu.SemaphoreType.DMA((offsets * n_blk,)),
            pltpu.SemaphoreType.DMA((total,)),
            pltpu.SemaphoreType.DMA((total,)),
            pltpu.VMEM((cases, width), dtype),
            pltpu.VMEM((panel, cases), jnp.float32),
            pltpu.VMEM((piece, cases), jnp.float32),
            pltpu.VMEM((cases, width), dtype),
            pltpu.VMEM((cases, n_blk * width), dtype),
            pltpu.VMEM((panel, cases), jnp.float32),
            pltpu.VMEM((piece, cases), jnp.float32),
        ]
        + _operator_scratch(n_blk, cases, width, dtype, piece, cases)
        + _project_scratch(stages, cases),
        compiler_params=pltpu.CompilerParams(collective_id=10 + depth, has_side_effects=True),
    )(*basis, image, inverse, picks, chain, gain, ahead, block, back, spread, jac)


def _exchange_sum(stages, source, slots, partial, sends, recvs, out):
    count = len(stages)
    for stage, (axis, n) in enumerate(stages):
        mine = lax.axis_index(axis)
        copies = []
        for k in range(1, n):
            copy = pltpu.make_async_remote_copy(
                src_ref=source,
                dst_ref=slots[stage].at[mine],
                send_sem=sends[stage].at[k],
                recv_sem=recvs[stage].at[mine],
                device_id={axis: lax.rem(mine + k, n)},
                device_id_type=MESH,
            )
            copy.start()
            copies.append(copy)
        slots[stage][mine] = source[...]
        for k in range(1, n):
            sender = lax.rem(mine + k, n)
            pltpu.make_async_remote_copy(
                src_ref=source,
                dst_ref=slots[stage].at[sender],
                send_sem=sends[stage].at[k],
                recv_sem=recvs[stage].at[sender],
                device_id={axis: sender},
                device_id_type=MESH,
            ).wait_recv()
        for copy in copies:
            copy.wait_send()
        total = slots[stage][0]
        for j in range(1, n):
            total = total + slots[stage][j]
        if stage == count - 1:
            out[...] = total
        else:
            partial[...] = total
            source = partial


def _project_scratch(stages, cases):
    def buffers():
        out = [pltpu.VMEM((n, 8, cases), jnp.float32) for _, n in stages]
        out.append(pltpu.VMEM((8, cases), jnp.float32))
        out += [pltpu.SemaphoreType.DMA((n,)) for _, n in stages]
        out += [pltpu.SemaphoreType.DMA((n,)) for _, n in stages]
        return out

    return buffers() + buffers() + [pltpu.VMEM((8, cases), jnp.float32)] * 2


def _project_body(stages, depth, basis_refs, image_ref, h_ref, next_ref, scratch):
    count = len(stages)
    first, second = scratch[: 3 * count + 1], scratch[3 * count + 1 : 6 * count + 2]
    rows, work = scratch[6 * count + 2 : 6 * count + 4]
    highest = lax.Precision.HIGHEST
    contract = (((1,), (1,)), ((), ()))
    image = image_ref[...]
    ones = jnp.ones((8, image.shape[1]), jnp.float32)
    eye = (
        lax.broadcasted_iota(jnp.int32, (image.shape[0],) * 2, 0)
        == lax.broadcasted_iota(jnp.int32, (image.shape[0],) * 2, 1)
    ).astype(jnp.float32)

    def run(buffers, source, out):
        slots = buffers[:count]
        partial = buffers[count]
        sends = buffers[count + 1 : 2 * count + 1]
        recvs = buffers[2 * count + 1 :]
        _exchange_sum(stages, source, slots, partial, sends, recvs, out)

    if depth > 0:
        rows[...] = jnp.zeros_like(rows)
        for i in range(depth):
            summed = lax.dot_general(
                ones, image * basis_refs[i][...], contract, precision=highest,
                preferred_element_type=jnp.float32,
            )
            rows[i : i + 1, :] = summed[0:1, :]
        run(first, rows, h_ref)
        columns = lax.dot_general(
            eye, h_ref[...], contract, precision=highest, preferred_element_type=jnp.float32
        )
        for i in range(depth):
            image = image - columns[:, i : i + 1] * basis_refs[i][...]
    else:
        h_ref[...] = jnp.zeros_like(h_ref)
    work[...] = lax.dot_general(
        ones, image * image, contract, precision=highest, preferred_element_type=jnp.float32
    )
    run(second, work, rows)
    length = jnp.sqrt(rows[...] + epsilon)
    h_ref[depth : depth + 1, :] = length[0:1, :]
    scale = lax.dot_general(
        eye, length, contract, precision=highest, preferred_element_type=jnp.float32
    )
    next_ref[...] = image / scale[:, 0:1]


def _signal_stages(barrier, stages):
    peers = 0
    for axis, n in stages:
        mine = lax.axis_index(axis)
        for k in range(1, n):
            pl.semaphore_signal(
                barrier, inc=1, device_id={axis: lax.rem(mine + k, n)}, device_id_type=MESH
            )
            peers += 1
    return peers


def _project_kernel(stages, depth, *refs):
    basis_refs = refs[:depth]
    image_ref, h_ref, next_ref = refs[depth : depth + 3]
    barrier = pltpu.get_barrier_semaphore()
    pl.semaphore_wait(barrier, _signal_stages(barrier, stages))
    _project_body(stages, depth, basis_refs, image_ref, h_ref, next_ref, refs[depth + 3 :])


def _global_stages(mesh_shape):
    return tuple((axis, mesh_shape[axis]) for axis in ("blk", "sec") if mesh_shape[axis] > 1)


def project(basis, image, mesh_shape):
    depth = len(basis)
    cases, width = image.shape
    stages = _global_stages(mesh_shape)
    return pl.pallas_call(
        functools.partial(_project_kernel, stages, depth),
        out_shape=(
            jax.ShapeDtypeStruct((8, cases), jnp.float32),
            jax.ShapeDtypeStruct((cases, width), jnp.float32),
        ),
        in_specs=[pl.BlockSpec(memory_space=pltpu.VMEM)] * (depth + 1),
        out_specs=[pl.BlockSpec(memory_space=pltpu.VMEM)] * 2,
        scratch_shapes=_project_scratch(stages, cases),
        compiler_params=pltpu.CompilerParams(collective_id=6 + depth, has_side_effects=True),
    )(*basis, image)


def least_squares(columns, beta, depth):
    zero = jnp.zeros_like(beta)
    upper = [
        [columns[j][i] if i <= j + 1 else zero for j in range(depth)] for i in range(depth + 1)
    ]
    rhs = [beta] + [zero] * depth
    for column in range(depth):
        upper_row, lower_row = upper[column], upper[column + 1]
        radius = jnp.sqrt(upper_row[column] ** 2 + lower_row[column] ** 2)
        cosine = upper_row[column] / radius
        sine_term = lower_row[column] / radius
        upper[column] = [cosine * a + sine_term * b for a, b in zip(upper_row, lower_row)]
        upper[column + 1] = [-sine_term * a + cosine * b for a, b in zip(upper_row, lower_row)]
        first_rhs, second_rhs = rhs[column], rhs[column + 1]
        rhs[column] = cosine * first_rhs + sine_term * second_rhs
        rhs[column + 1] = -sine_term * first_rhs + cosine * second_rhs
    weights = [zero] * depth
    for column in reversed(range(depth)):
        remain = rhs[column]
        if column + 1 < depth:
            tail = upper[column][column + 1] * weights[column + 1]
            for k in range(column + 2, depth):
                tail = tail + upper[column][k] * weights[k]
            remain = remain - tail
        weights[column] = remain / upper[column][column]
    return weights

def local(
    mesh_shape,
    state_now, source, fan_gain, section_block, block_inverse, back_panel, ahead_panel, interface
):
    highest = lax.Precision.HIGHEST
    cases, node_rows = state_now.shape
    panel_width = back_panel.shape[1]
    indices = interface[0]
    first_row = lax.axis_index("blk") * node_rows
    selector = (indices[None, :] == first_row + jnp.arange(node_rows)[:, None]).astype(jnp.float32)
    contract = (((1,), (1,)), ((), ()))

    own_piece = panel_width // mesh_shape["blk"]
    own_picks = lax.dynamic_slice_in_dim(selector, lax.axis_index("blk") * own_piece, own_piece, 1).T

    def section_terms(dense_part, behind_vals, piece):
        width = piece.shape[1]
        dense_part = lax.dot_general(
            piece, section_block, contract, preferred_element_type=jnp.float32
        )
        picker = (indices[None, :] == jnp.arange(width)[:, None]).astype(jnp.bfloat16)
        behind_vals = jnp.dot(piece, picker, preferred_element_type=jnp.float32)
        return (dense_part, behind_vals)

    def fold_section(carry, piece):
        return section_terms(carry[0], carry[1], piece)

    n_sec, n_blk = mesh_shape["sec"], mesh_shape["blk"]
    piece = panel_width // n_blk
    local_picks = lax.dynamic_slice_in_dim(selector, lax.axis_index("blk") * piece, piece, 1)

    def finish(gathered, behind_t, ahead_piece):
        dense_part = lax.dot_general(
            gathered, section_block, contract, preferred_element_type=jnp.float32
        )
        lower_term = lax.dot_general(
            behind_t.astype(jnp.bfloat16),
            back_panel,
            (((0,), (1,)), ((), ())),
            preferred_element_type=jnp.float32,
        )
        upper_term = lax.dot_general(
            ahead_piece, local_picks, (((0,), (1,)), ((), ())), precision=highest
        )
        return dense_part + lower_term + upper_term

    def operator(vector):
        rounded = vector.astype(jnp.bfloat16)
        up_t = lax.dot_general(
            ahead_panel, rounded, (((0,), (1,)), ((), ())), preferred_element_type=jnp.float32
        )
        be_t = lax.dot_general(
            selector.astype(jnp.bfloat16),
            rounded,
            (((0,), (1,)), ((), ())),
            preferred_element_type=jnp.float32,
        )
        return finish(*operator_exchange(rounded, up_t, be_t, n_sec, n_blk))

    def compose(earlier, later):
        first_map, first_value = earlier
        second_map, second_value = later
        joined_map = jnp.dot(second_map, first_map, precision=highest)
        joined_value = jnp.dot(first_value, second_map.T, precision=highest) + second_value
        return (joined_map, joined_value)

    def lengths(vector):
        return jnp.sqrt(global_sum(jnp.sum(vector * vector, axis=1)[None], mesh_shape)[0] + epsilon)

    bent = jnp.tanh(state_now)
    state_rounded = state_now.astype(jnp.bfloat16)
    applied, gain_panel, chain = setup_exchange(
        state_rounded, ahead_panel, section_block, local_picks, back_panel, block_inverse,
        own_picks, n_sec, n_blk,
    )
    residual = source - applied - fan_gain[None, :] * bent
    jac_diag = fan_gain[None, :] * (1.0 - bent * bent)
    columns = []
    basis = []
    directions = []
    product = residual
    beta = None
    for column in range(KRYLOV):
        sums, following, direction, product = precondition_sweep(
            list(basis), product, block_inverse, own_picks, chain, gain_panel, ahead_panel,
            section_block, back_panel, local_picks, jac_diag, mesh_shape, len(basis),
        )
        if column == 0:
            beta = sums[0]
        else:
            columns.append(sums[: column + 1])
        basis.append(following)
        directions.append(direction)
    sums, _ = project(basis, product, mesh_shape)
    columns.append(sums[: KRYLOV + 1])
    weights = least_squares(columns, beta, KRYLOV)
    update = jnp.zeros_like(state_now)
    for column in range(KRYLOV):
        update = update + weights[column][:, None] * directions[column]
    return state_now + update


def solution(mesh):
    in_specs = (
        P(None, ("sec", "blk")),
        P(None, ("sec", "blk")),
        P(("sec", "blk")),
        P(("sec", "blk"), None),
        P(("sec", "blk"), None),
        P(("sec", "blk"), None),
        P(("sec", "blk"), None),
        P("sec", None),
    )
    out_specs = P(None, ("sec", "blk"))
    return jax.shard_map(functools.partial(local, dict(mesh.shape)), mesh=mesh, in_specs=in_specs, out_specs=out_specs, check_vma=False)
```

```python
import functools

import jax
import jax.numpy as jnp
from jax import lax
from jax.experimental import pallas as pl
from jax.experimental.pallas import tpu as pltpu
from jax.sharding import PartitionSpec as P

MESH = pl.DeviceIdType.MESH

KRYLOV = 3


epsilon = 1e-06


def extended(x, sides, width):
    for axis, dim in sides:
        size, length = (lax.axis_size(axis), x.shape[dim])
        up = [(i, (i + 1) % size) for i in range(size - 1)]
        down = [(j, i) for i, j in up]
        last = lax.slice_in_dim(x, length - width, length, axis=dim)
        first = lax.slice_in_dim(x, 0, width, axis=dim)
        before = lax.ppermute(last, axis, up)
        after = lax.ppermute(first, axis, down)
        x = jnp.concatenate([before, x, after], axis=dim)
    return x


def entering(value, axis, join, neutral):
    count, mine = (lax.axis_size(axis), lax.axis_index(axis))
    pieces = jax.tree.map(lambda part: lax.all_gather(part, axis), value)
    so_far = jax.tree.map(
        lambda part, zero: jnp.full_like(part, 0) + jnp.asarray(zero, part.dtype), value, neutral
    )

    def step(position, so_far):
        longer = join(so_far, jax.tree.map(lambda part: part[position], pieces))
        return jax.tree.map(lambda new, old: jnp.where(position < mine, new, old), longer, so_far)

    return lax.fori_loop(0, count - 1, step, so_far)


def _reduce_kernel(stages, x_ref, o_ref, *scratch):
    count = len(stages)
    slots = scratch[:count]
    partial = scratch[count]
    sends = scratch[count + 1 : 2 * count + 1]
    recvs = scratch[2 * count + 1 :]
    barrier = pltpu.get_barrier_semaphore()
    peers = 0
    for axis, n in stages:
        mine = lax.axis_index(axis)
        for k in range(1, n):
            pl.semaphore_signal(
                barrier, inc=1, device_id={axis: lax.rem(mine + k, n)}, device_id_type=MESH
            )
            peers += 1
    pl.semaphore_wait(barrier, peers)
    source = x_ref
    for stage, (axis, n) in enumerate(stages):
        mine = lax.axis_index(axis)
        copies = []
        for k in range(1, n):
            copy = pltpu.make_async_remote_copy(
                src_ref=source,
                dst_ref=slots[stage].at[mine],
                send_sem=sends[stage].at[k],
                recv_sem=recvs[stage].at[mine],
                device_id={axis: lax.rem(mine + k, n)},
                device_id_type=MESH,
            )
            copy.start()
            copies.append(copy)
        slots[stage][mine] = source[...]
        for k in range(1, n):
            sender = lax.rem(mine + k, n)
            pltpu.make_async_remote_copy(
                src_ref=source,
                dst_ref=slots[stage].at[sender],
                send_sem=sends[stage].at[k],
                recv_sem=recvs[stage].at[sender],
                device_id={axis: sender},
                device_id_type=MESH,
            ).wait_recv()
        for copy in copies:
            copy.wait_send()
        total = slots[stage][0]
        for j in range(1, n):
            total = total + slots[stage][j]
        if stage == count - 1:
            o_ref[...] = total
        else:
            partial[...] = total
            source = partial


def all_sum(x, axes, mesh_shape, collective):
    stages = tuple((axis, mesh_shape[axis]) for axis in axes if mesh_shape[axis] > 1)
    rows, cols = x.shape
    scratch = [pltpu.VMEM((n, rows, cols), jnp.float32) for _, n in stages]
    scratch.append(pltpu.VMEM((rows, cols), jnp.float32))
    scratch += [pltpu.SemaphoreType.DMA((n,)) for _, n in stages]
    scratch += [pltpu.SemaphoreType.DMA((n,)) for _, n in stages]
    return pl.pallas_call(
        functools.partial(_reduce_kernel, stages),
        out_shape=jax.ShapeDtypeStruct((rows, cols), jnp.float32),
        in_specs=[pl.BlockSpec(memory_space=pltpu.VMEM)],
        out_specs=pl.BlockSpec(memory_space=pltpu.VMEM),
        scratch_shapes=scratch,
        compiler_params=pltpu.CompilerParams(collective_id=collective, has_side_effects=True),
    )(x.astype(jnp.float32))


def global_sum(rows_of_sums, mesh_shape):
    count = rows_of_sums.shape[0]
    padded = jnp.zeros((8, rows_of_sums.shape[1]), jnp.float32).at[:count].set(rows_of_sums)
    return all_sum(padded, ("blk", "sec"), mesh_shape, 0)[:count]


def _doubling(n):
    distances, d = [], 1
    while d < n:
        distances.append(d)
        d *= 2
    return tuple(distances)


def _greet(n, distances):
    barrier = pltpu.get_barrier_semaphore()
    mine = lax.axis_index("sec")
    for d in distances:
        for peer in (lax.rem(mine + d, n), lax.rem(mine + n - d, n)):
            pl.semaphore_signal(barrier, inc=1, device_id={"sec": peer}, device_id_type=MESH)
    pl.semaphore_wait(barrier, 2 * len(distances))


def _hop(n, d, source, slot, send_sem, recv_sem):
    mine = lax.axis_index("sec")
    copy = pltpu.make_async_remote_copy(
        src_ref=source,
        dst_ref=slot,
        send_sem=send_sem,
        recv_sem=recv_sem,
        device_id={"sec": lax.rem(mine + d, n)},
        device_id_type=MESH,
    )
    copy.start()
    copy.wait_recv()
    copy.wait_send()


RADIX = 4


def _plan(n):
    rounds, d = [], 1
    while d < n:
        rounds.append((d, tuple(j for j in range(1, RADIX) if j * d < n)))
        d *= RADIX
    return tuple(rounds)


def _plan_peers(rounds):
    return tuple(sorted({j * d for d, js in rounds for j in js} | {1}))


def _send_all(n, sec, sources, slots, sends, recvs, flat, d, js):
    copies = []
    for i, j in enumerate(js):
        copy = pltpu.make_async_remote_copy(
            src_ref=sources,
            dst_ref=slots.at[flat + i],
            send_sem=sends.at[flat + i],
            recv_sem=recvs.at[flat + i],
            device_id={"sec": lax.rem(sec + j * d, n)},
            device_id_type=MESH,
        )
        copy.start()
        copies.append(copy)
    for copy in copies:
        copy.wait_recv()
    for copy in copies:
        copy.wait_send()


def _spread(n_sec, n_blk, offsets, piece_ref, slots, sends, recvs):
    sec, blk = lax.axis_index("sec"), lax.axis_index("blk")

    def copy(o, j, index):
        return pltpu.make_async_remote_copy(
            src_ref=piece_ref,
            dst_ref=slots.at[index],
            send_sem=sends.at[(o - 1) * n_blk + j],
            recv_sem=recvs.at[index],
            device_id={"sec": lax.rem(sec + o, n_sec), "blk": j},
            device_id_type=MESH,
        )

    outgoing = [
        copy(o, j, (o - 1) * n_blk + blk) for o in range(1, offsets + 1) for j in range(n_blk)
    ]
    for c in outgoing:
        c.start()
    for o in range(1, offsets + 1):
        for j in range(n_blk):
            copy(o, j, (o - 1) * n_blk + j).wait_recv()
    for c in outgoing:
        c.wait_send()


def _assemble(n_blk, offsets, slots, mats):
    piece = slots.shape[1]
    for o in range(offsets):
        for j in range(n_blk):
            mats[o, j * piece : (j + 1) * piece, :] = slots[o * n_blk + j]


def _greet_all(n_sec, n_blk, offsets, rounds, blk_peers, stages=()):
    barrier = pltpu.get_barrier_semaphore()
    sec, blk = lax.axis_index("sec"), lax.axis_index("blk")
    count = _signal_stages(barrier, stages)
    if blk_peers:
        for k in range(1, n_blk):
            pl.semaphore_signal(
                barrier, inc=1, device_id={"blk": lax.rem(blk + k, n_blk)}, device_id_type=MESH
            )
            count += 1
    covered = bool(stages)
    for o in range(1, offsets + 1):
        for k in range(1 if covered else 0, n_blk):
            for peer in (lax.rem(sec + o, n_sec), lax.rem(sec + n_sec - o, n_sec)):
                pl.semaphore_signal(
                    barrier,
                    inc=1,
                    device_id={"sec": peer, "blk": lax.rem(blk + k, n_blk)},
                    device_id_type=MESH,
                )
                count += 1
    if covered:
        pl.semaphore_wait(barrier, count)
        return
    for d in sorted({j * d for d, js in rounds[1:] for j in js}):
        for peer in (lax.rem(sec + d, n_sec), lax.rem(sec + n_sec - d, n_sec)):
            pl.semaphore_signal(barrier, inc=1, device_id={"sec": peer}, device_id_type=MESH)
            count += 1
    pl.semaphore_wait(barrier, count)


def _maps_body(n, n_blk, rounds, e_ref, a_ref, eslots, emat, current, slots, esend, erecv, sends, recvs):
    sec = lax.axis_index("sec")
    first = rounds[0][1]
    offsets = len(first) + 1
    _spread(n, n_blk, offsets, e_ref, eslots, esend, erecv)
    _assemble(n_blk, offsets, eslots, emat)
    joined = emat[0]
    for i, j in enumerate(first):
        a_ref[i] = joined
        joined = jnp.dot(
            joined, emat[j], precision=lax.Precision.HIGHEST, preferred_element_type=jnp.float32
        )
    current[...] = joined
    flat = len(first)
    for k in range(1, len(rounds)):
        d, js = rounds[k]
        onward = k < len(rounds) - 1
        if onward or len(js) > 1:
            _send_all(n, sec, current, slots, sends, recvs, flat, d, js)
        joined = current[...]
        for i, j in enumerate(js):
            a_ref[flat + i] = joined
            if onward or i < len(js) - 1:
                joined = jnp.dot(
                    joined, slots[flat + i], precision=lax.Precision.HIGHEST,
                    preferred_element_type=jnp.float32,
                )
        if onward:
            current[...] = joined
        flat += len(js)


def _setup_kernel(
    n_sec, n_blk, rounds, x_ref, ahead_ref, block_ref, spread_ref, back_ref, inv_ref, pick_ref,
    k_ref, gain_ref, chain_ref, *scratch
):
    phase_scratch = scratch[:9]
    pslots, psend, precv, epiece = scratch[9:13]
    g_ref, b_ref, a_ref, upward, own_piece = scratch[13:18]
    maps_scratch = scratch[18:]
    sec, blk = lax.axis_index("sec"), lax.axis_index("blk")
    offsets = len(rounds[0][1]) + 1
    _greet_all(n_sec, n_blk, offsets, rounds, True)
    contract = (((1,), (1,)), ((), ()))
    upward[...] = jnp.dot(x_ref[...], ahead_ref[...], preferred_element_type=jnp.float32).T
    own_piece[...] = lax.dot_general(
        pick_ref[...], x_ref[...].astype(jnp.float32), contract,
        precision=lax.Precision.HIGHEST, preferred_element_type=jnp.float32,
    )
    _operator_phase(n_sec, n_blk, x_ref, upward, own_piece, g_ref, b_ref, a_ref, phase_scratch)
    width = x_ref.shape[1]
    product = lax.dot_general(
        g_ref[:, 0:width], block_ref[:, 0:width], contract, preferred_element_type=jnp.float32
    )
    for j in range(1, n_blk):
        product = product + lax.dot_general(
            g_ref[:, j * width : (j + 1) * width],
            block_ref[:, j * width : (j + 1) * width],
            contract,
            preferred_element_type=jnp.float32,
        )
    product = product + lax.dot_general(
        b_ref[...].T.astype(back_ref.dtype), back_ref[...], contract,
        preferred_element_type=jnp.float32,
    )
    product = product + jnp.dot(
        spread_ref[...], a_ref[...], precision=lax.Precision.HIGHEST,
        preferred_element_type=jnp.float32,
    ).T
    k_ref[...] = product

    def blk_copy(k, target, slot):
        return pltpu.make_async_remote_copy(
            src_ref=back_ref,
            dst_ref=pslots.at[slot],
            send_sem=psend.at[k],
            recv_sem=precv.at[slot],
            device_id={"blk": target},
            device_id_type=MESH,
        )

    outgoing = [blk_copy(k, lax.rem(blk + k, n_blk), blk) for k in range(1, n_blk)]
    for copy in outgoing:
        copy.start()
    pslots[blk] = back_ref[...]
    for k in range(1, n_blk):
        sender = lax.rem(blk + k, n_blk)
        blk_copy(k, sender, sender).wait_recv()
    for copy in outgoing:
        copy.wait_send()
    rows = back_ref.shape[0]
    gain = jnp.dot(inv_ref[:, 0:rows], pslots[0], preferred_element_type=jnp.float32)
    for j in range(1, n_blk):
        gain = gain + jnp.dot(
            inv_ref[:, j * rows : (j + 1) * rows], pslots[j], preferred_element_type=jnp.float32
        )
    gain_ref[...] = gain
    epiece[...] = -jnp.dot(
        pick_ref[...], gain, precision=lax.Precision.HIGHEST, preferred_element_type=jnp.float32
    )
    _maps_body(n_sec, n_blk, rounds, epiece, chain_ref, *maps_scratch)


def setup_exchange(x, ahead, block, spread, back, inverse, picks, n_sec, n_blk):
    cases, width = x.shape
    panel = ahead.shape[1]
    piece = panel // n_blk
    rows, panel_width = back.shape
    rounds = _plan(n_sec)
    total = sum(len(js) for _, js in rounds)
    offsets = len(rounds[0][1]) + 1
    return pl.pallas_call(
        functools.partial(_setup_kernel, n_sec, n_blk, rounds),
        out_shape=(
            jax.ShapeDtypeStruct((cases, width), jnp.float32),
            jax.ShapeDtypeStruct((rows, panel_width), jnp.float32),
            jax.ShapeDtypeStruct((total, panel_width, panel_width), jnp.float32),
        ),
        in_specs=[pl.BlockSpec(memory_space=pltpu.VMEM)] * 7,
        out_specs=[pl.BlockSpec(memory_space=pltpu.VMEM)] * 3,
        scratch_shapes=_operator_scratch(n_blk, cases, width, x.dtype, piece, cases)
        + [
            pltpu.VMEM((n_blk, rows, panel_width), back.dtype),
            pltpu.SemaphoreType.DMA((n_blk,)),
            pltpu.SemaphoreType.DMA((n_blk,)),
            pltpu.VMEM((piece, panel_width), jnp.float32),
            pltpu.VMEM((cases, n_blk * width), x.dtype),
            pltpu.VMEM((panel, cases), jnp.float32),
            pltpu.VMEM((piece, cases), jnp.float32),
            pltpu.VMEM((panel, cases), jnp.float32),
            pltpu.VMEM((piece, cases), jnp.float32),
            pltpu.VMEM((offsets * n_blk, piece, panel_width), jnp.float32),
            pltpu.VMEM((offsets, panel_width, panel_width), jnp.float32),
            pltpu.VMEM((panel_width, panel_width), jnp.float32),
            pltpu.VMEM((total, panel_width, panel_width), jnp.float32),
            pltpu.SemaphoreType.DMA((offsets * n_blk,)),
            pltpu.SemaphoreType.DMA((offsets * n_blk,)),
            pltpu.SemaphoreType.DMA((total,)),
            pltpu.SemaphoreType.DMA((total,)),
        ],
        compiler_params=pltpu.CompilerParams(collective_id=3, has_side_effects=True),
    )(x, ahead, block, spread, back, inverse, picks)


def _gather_kernel(n, x_ref, o_ref, slots, sends, recvs):
    mine = lax.axis_index("blk")
    barrier = pltpu.get_barrier_semaphore()
    for k in range(1, n):
        pl.semaphore_signal(
            barrier, inc=1, device_id={"blk": lax.rem(mine + k, n)}, device_id_type=MESH
        )
    pl.semaphore_wait(barrier, n - 1)
    copies = []
    for k in range(1, n):
        copy = pltpu.make_async_remote_copy(
            src_ref=x_ref,
            dst_ref=slots.at[mine],
            send_sem=sends.at[k],
            recv_sem=recvs.at[mine],
            device_id={"blk": lax.rem(mine + k, n)},
            device_id_type=MESH,
        )
        copy.start()
        copies.append(copy)
    slots[mine] = x_ref[...]
    for k in range(1, n):
        sender = lax.rem(mine + k, n)
        pltpu.make_async_remote_copy(
            src_ref=x_ref,
            dst_ref=slots.at[sender],
            send_sem=sends.at[k],
            recv_sem=recvs.at[sender],
            device_id={"blk": sender},
            device_id_type=MESH,
        ).wait_recv()
    for copy in copies:
        copy.wait_send()
    width = x_ref.shape[1]
    for j in range(n):
        o_ref[:, j * width : (j + 1) * width] = slots[j]


def gather_blk(x, n):
    rows, width = x.shape
    return pl.pallas_call(
        functools.partial(_gather_kernel, n),
        out_shape=jax.ShapeDtypeStruct((rows, n * width), x.dtype),
        in_specs=[pl.BlockSpec(memory_space=pltpu.VMEM)],
        out_specs=pl.BlockSpec(memory_space=pltpu.VMEM),
        scratch_shapes=[
            pltpu.VMEM((n, rows, width), x.dtype),
            pltpu.SemaphoreType.DMA((n,)),
            pltpu.SemaphoreType.DMA((n,)),
        ],
        compiler_params=pltpu.CompilerParams(collective_id=4, has_side_effects=True),
    )(x)


def _operator_phase(n_sec, n_blk, x_ref, up_ref, piece_ref, g_ref, b_ref, a_ref, scratch):
    gslots, bslots, aslots, gsend, grecv, bsend, brecv, asend, arecv = scratch
    sec, blk = lax.axis_index("sec"), lax.axis_index("blk")
    nxt, prv = lax.rem(sec + 1, n_sec), lax.rem(sec + n_sec - 1, n_sec)
    piece = bslots.shape[1]
    copies = []
    for k in range(1, n_blk):
        copies.append(
            pltpu.make_async_remote_copy(
                src_ref=x_ref,
                dst_ref=gslots.at[blk],
                send_sem=gsend.at[k],
                recv_sem=grecv.at[blk],
                device_id={"blk": lax.rem(blk + k, n_blk)},
                device_id_type=MESH,
            )
        )
    for j in range(n_blk):
        copies.append(
            pltpu.make_async_remote_copy(
                src_ref=piece_ref,
                dst_ref=bslots.at[blk],
                send_sem=bsend.at[j],
                recv_sem=brecv.at[blk],
                device_id={"sec": nxt, "blk": j},
                device_id_type=MESH,
            )
        )
        copies.append(
            pltpu.make_async_remote_copy(
                src_ref=up_ref.at[pl.ds(j * piece, piece)],
                dst_ref=aslots.at[blk],
                send_sem=asend.at[j],
                recv_sem=arecv.at[blk],
                device_id={"sec": prv, "blk": j},
                device_id_type=MESH,
            )
        )
    for copy in copies:
        copy.start()
    gslots[blk] = x_ref[...]
    for k in range(1, n_blk):
        sender = lax.rem(blk + k, n_blk)
        pltpu.make_async_remote_copy(
            src_ref=x_ref,
            dst_ref=gslots.at[sender],
            send_sem=gsend.at[k],
            recv_sem=grecv.at[sender],
            device_id={"blk": sender},
            device_id_type=MESH,
        ).wait_recv()
    for j in range(n_blk):
        pltpu.make_async_remote_copy(
            src_ref=piece_ref,
            dst_ref=bslots.at[j],
            send_sem=bsend.at[j],
            recv_sem=brecv.at[j],
            device_id={"sec": prv, "blk": j},
            device_id_type=MESH,
        ).wait_recv()
        pltpu.make_async_remote_copy(
            src_ref=up_ref.at[pl.ds(j * piece, piece)],
            dst_ref=aslots.at[j],
            send_sem=asend.at[j],
            recv_sem=arecv.at[j],
            device_id={"sec": nxt, "blk": j},
            device_id_type=MESH,
        ).wait_recv()
    for copy in copies:
        copy.wait_send()
    width = x_ref.shape[1]
    for j in range(n_blk):
        g_ref[:, j * width : (j + 1) * width] = gslots[j]
        b_ref[j * piece : (j + 1) * piece, :] = jnp.where(
            sec >= 1, bslots[j], jnp.zeros_like(bslots[j])
        )
    total = aslots[0]
    for j in range(1, n_blk):
        total = total + aslots[j]
    a_ref[...] = jnp.where(sec <= n_sec - 2, total, jnp.zeros_like(total))


def _operator_scratch(n_blk, rows, width, dtype, piece, cases):
    return [
        pltpu.VMEM((n_blk, rows, width), dtype),
        pltpu.VMEM((n_blk, piece, cases), jnp.float32),
        pltpu.VMEM((n_blk, piece, cases), jnp.float32),
    ] + [pltpu.SemaphoreType.DMA((n_blk,))] * 6


def _operator_kernel(n_sec, n_blk, x_ref, up_ref, be_ref, g_ref, b_ref, a_ref, *scratch):
    sec, blk = lax.axis_index("sec"), lax.axis_index("blk")
    nxt, prv = lax.rem(sec + 1, n_sec), lax.rem(sec + n_sec - 1, n_sec)
    piece = scratch[1].shape[1]
    barrier = pltpu.get_barrier_semaphore()
    for k in range(1, n_blk):
        pl.semaphore_signal(
            barrier, inc=1, device_id={"blk": lax.rem(blk + k, n_blk)}, device_id_type=MESH
        )
    for j in range(n_blk):
        for other in (nxt, prv):
            pl.semaphore_signal(
                barrier, inc=1, device_id={"sec": other, "blk": j}, device_id_type=MESH
            )
    pl.semaphore_wait(barrier, 3 * n_blk - 1)
    mine = be_ref.at[pl.ds(pl.multiple_of(blk * piece, 8), piece)]
    _operator_phase(n_sec, n_blk, x_ref, up_ref, mine, g_ref, b_ref, a_ref, scratch)


def operator_exchange(x, up_t, be_t, n_sec, n_blk):
    rows, width = x.shape
    panel, cases = up_t.shape
    piece = panel // n_blk
    return pl.pallas_call(
        functools.partial(_operator_kernel, n_sec, n_blk),
        out_shape=(
            jax.ShapeDtypeStruct((rows, n_blk * width), x.dtype),
            jax.ShapeDtypeStruct((panel, cases), jnp.float32),
            jax.ShapeDtypeStruct((piece, cases), jnp.float32),
        ),
        in_specs=[pl.BlockSpec(memory_space=pltpu.VMEM)] * 3,
        out_specs=[pl.BlockSpec(memory_space=pltpu.VMEM)] * 3,
        scratch_shapes=_operator_scratch(n_blk, rows, width, x.dtype, piece, cases),
        compiler_params=pltpu.CompilerParams(collective_id=5, has_side_effects=True),
    )(x, up_t, be_t)


def _precondition_kernel(n_sec, n_blk, rounds, stages, depth, *refs):
    basis_refs = refs[:depth]
    (image_ref, inv_ref, pick_ref, u_ref, gain_ref, ahead_ref, block_ref, back_ref, spread_ref,
     jac_ref, h_ref, next_ref, d_ref, p_ref) = refs[depth : depth + 14]
    scratch = refs[depth + 14 :]
    gslots, fpiece, fslots, fmat, carry, slots, gsend, grecv, fsend, frecv, ssend, srecv = scratch[:12]
    rounded, upward, own_piece, x_ref = scratch[12:16]
    g_ref, b_ref, a_ref = scratch[16:19]
    phase_scratch = scratch[19:28]
    project_scratch = scratch[28:]
    sec, blk = lax.axis_index("sec"), lax.axis_index("blk")
    first = rounds[0][1]
    offsets = len(first) + 1
    _greet_all(n_sec, n_blk, offsets, rounds, False, stages)
    _project_body(stages, depth, basis_refs, image_ref, h_ref, next_ref, project_scratch)
    x_ref[...] = next_ref[...].astype(x_ref.dtype)

    def blk_copy(k, target, slot):
        return pltpu.make_async_remote_copy(
            src_ref=x_ref,
            dst_ref=gslots.at[slot],
            send_sem=gsend.at[k],
            recv_sem=grecv.at[slot],
            device_id={"blk": target},
            device_id_type=MESH,
        )

    outgoing = [blk_copy(k, lax.rem(blk + k, n_blk), blk) for k in range(1, n_blk)]
    for copy in outgoing:
        copy.start()
    gslots[blk] = x_ref[...]
    for k in range(1, n_blk):
        sender = lax.rem(blk + k, n_blk)
        blk_copy(k, sender, sender).wait_recv()
    for copy in outgoing:
        copy.wait_send()
    width = x_ref.shape[1]
    contract = (((1,), (1,)), ((), ()))
    folded = lax.dot_general(
        gslots[0], inv_ref[:, 0:width], contract, preferred_element_type=jnp.float32
    )
    for j in range(1, n_blk):
        folded = folded + lax.dot_general(
            gslots[j],
            inv_ref[:, j * width : (j + 1) * width],
            contract,
            preferred_element_type=jnp.float32,
        )
    fpiece[...] = lax.dot_general(
        pick_ref[...], folded, contract, precision=lax.Precision.HIGHEST,
        preferred_element_type=jnp.float32,
    )
    _spread(n_sec, n_blk, offsets, fpiece, fslots, fsend, frecv)
    _assemble(n_blk, offsets, fslots, fmat)
    joined = jnp.where(sec >= 1, fmat[0], jnp.zeros_like(fmat[0]))
    for i, j in enumerate(first):
        term = jnp.dot(
            u_ref[i], fmat[j], precision=lax.Precision.HIGHEST, preferred_element_type=jnp.float32
        )
        joined = joined + jnp.where(sec >= j + 1, term, jnp.zeros_like(term))
    carry[1] = joined
    flat = len(first)
    for k in range(1, len(rounds)):
        d, js = rounds[k]
        _send_all(n_sec, sec, carry.at[k], slots, ssend, srecv, flat, d, js)
        joined = carry[k]
        for i, j in enumerate(js):
            term = jnp.dot(
                u_ref[flat + i], slots[flat + i], precision=lax.Precision.HIGHEST,
                preferred_element_type=jnp.float32,
            )
            joined = joined + jnp.where(sec >= j * d, term, jnp.zeros_like(term))
        carry[k + 1] = joined
        flat += len(js)
    before = carry[len(rounds)].T
    direction = folded - lax.dot_general(
        before, gain_ref[...], contract, precision=lax.Precision.HIGHEST,
        preferred_element_type=jnp.float32,
    )
    d_ref[...] = direction
    rounded[...] = direction.astype(rounded.dtype)
    upward[...] = jnp.dot(
        rounded[...], ahead_ref[...], preferred_element_type=jnp.float32
    ).T
    own_piece[...] = lax.dot_general(
        pick_ref[...], rounded[...].astype(jnp.float32), contract,
        precision=lax.Precision.HIGHEST, preferred_element_type=jnp.float32,
    )
    _operator_phase(n_sec, n_blk, rounded, upward, own_piece, g_ref, b_ref, a_ref, phase_scratch)
    product = jac_ref[...] * direction
    for j in range(n_blk):
        product = product + lax.dot_general(
            g_ref[:, j * width : (j + 1) * width],
            block_ref[:, j * width : (j + 1) * width],
            contract,
            preferred_element_type=jnp.float32,
        )
    product = product + lax.dot_general(
        b_ref[...].T.astype(back_ref.dtype), back_ref[...], contract,
        preferred_element_type=jnp.float32,
    )
    product = product + jnp.dot(
        spread_ref[...], a_ref[...], precision=lax.Precision.HIGHEST,
        preferred_element_type=jnp.float32,
    ).T
    p_ref[...] = product


def precondition_sweep(
    basis, image, inverse, picks, chain, gain, ahead, block, back, spread, jac, mesh_shape, depth
):
    n_sec, n_blk = mesh_shape["sec"], mesh_shape["blk"]
    stages = _global_stages(mesh_shape)
    cases, width = image.shape
    piece, _ = picks.shape
    panel = piece * n_blk
    plan = _plan(n_sec)
    rounds = len(plan)
    total = sum(len(js) for _, js in plan)
    offsets = len(plan[0][1]) + 1
    dtype = jnp.bfloat16
    return pl.pallas_call(
        functools.partial(_precondition_kernel, n_sec, n_blk, plan, stages, depth),
        out_shape=(
            jax.ShapeDtypeStruct((8, cases), jnp.float32),
            jax.ShapeDtypeStruct((cases, width), jnp.float32),
            jax.ShapeDtypeStruct((cases, width), jnp.float32),
            jax.ShapeDtypeStruct((cases, width), jnp.float32),
        ),
        in_specs=[pl.BlockSpec(memory_space=pltpu.VMEM)] * (depth + 10),
        out_specs=[pl.BlockSpec(memory_space=pltpu.VMEM)] * 4,
        scratch_shapes=[
            pltpu.VMEM((n_blk, cases, width), dtype),
            pltpu.VMEM((piece, cases), jnp.float32),
            pltpu.VMEM((offsets * n_blk, piece, cases), jnp.float32),
            pltpu.VMEM((offsets, panel, cases), jnp.float32),
            pltpu.VMEM((rounds + 1, panel, cases), jnp.float32),
            pltpu.VMEM((total, panel, cases), jnp.float32),
            pltpu.SemaphoreType.DMA((n_blk,)),
            pltpu.SemaphoreType.DMA((n_blk,)),
            pltpu.SemaphoreType.DMA((offsets * n_blk,)),
            pltpu.SemaphoreType.DMA((offsets * n_blk,)),
            pltpu.SemaphoreType.DMA((total,)),
            pltpu.SemaphoreType.DMA((total,)),
            pltpu.VMEM((cases, width), dtype),
            pltpu.VMEM((panel, cases), jnp.float32),
            pltpu.VMEM((piece, cases), jnp.float32),
            pltpu.VMEM((cases, width), dtype),
            pltpu.VMEM((cases, n_blk * width), dtype),
            pltpu.VMEM((panel, cases), jnp.float32),
            pltpu.VMEM((piece, cases), jnp.float32),
        ]
        + _operator_scratch(n_blk, cases, width, dtype, piece, cases)
        + _project_scratch(stages, cases),
        compiler_params=pltpu.CompilerParams(collective_id=10 + depth, has_side_effects=True),
    )(*basis, image, inverse, picks, chain, gain, ahead, block, back, spread, jac)


def _exchange_sum(stages, source, slots, partial, sends, recvs, out):
    count = len(stages)
    for stage, (axis, n) in enumerate(stages):
        mine = lax.axis_index(axis)
        copies = []
        for k in range(1, n):
            copy = pltpu.make_async_remote_copy(
                src_ref=source,
                dst_ref=slots[stage].at[mine],
                send_sem=sends[stage].at[k],
                recv_sem=recvs[stage].at[mine],
                device_id={axis: lax.rem(mine + k, n)},
                device_id_type=MESH,
            )
            copy.start()
            copies.append(copy)
        slots[stage][mine] = source[...]
        for k in range(1, n):
            sender = lax.rem(mine + k, n)
            pltpu.make_async_remote_copy(
                src_ref=source,
                dst_ref=slots[stage].at[sender],
                send_sem=sends[stage].at[k],
                recv_sem=recvs[stage].at[sender],
                device_id={axis: sender},
                device_id_type=MESH,
            ).wait_recv()
        for copy in copies:
            copy.wait_send()
        total = slots[stage][0]
        for j in range(1, n):
            total = total + slots[stage][j]
        if stage == count - 1:
            out[...] = total
        else:
            partial[...] = total
            source = partial


def _project_scratch(stages, cases):
    def buffers():
        out = [pltpu.VMEM((n, 8, cases), jnp.float32) for _, n in stages]
        out.append(pltpu.VMEM((8, cases), jnp.float32))
        out += [pltpu.SemaphoreType.DMA((n,)) for _, n in stages]
        out += [pltpu.SemaphoreType.DMA((n,)) for _, n in stages]
        return out

    return buffers() + buffers() + [pltpu.VMEM((8, cases), jnp.float32)] * 2


def _project_body(stages, depth, basis_refs, image_ref, h_ref, next_ref, scratch):
    count = len(stages)
    first, second = scratch[: 3 * count + 1], scratch[3 * count + 1 : 6 * count + 2]
    rows, work = scratch[6 * count + 2 : 6 * count + 4]
    highest = lax.Precision.HIGHEST
    contract = (((1,), (1,)), ((), ()))
    image = image_ref[...]
    ones = jnp.ones((8, image.shape[1]), jnp.float32)
    eye = (
        lax.broadcasted_iota(jnp.int32, (image.shape[0],) * 2, 0)
        == lax.broadcasted_iota(jnp.int32, (image.shape[0],) * 2, 1)
    ).astype(jnp.float32)

    def run(buffers, source, out):
        slots = buffers[:count]
        partial = buffers[count]
        sends = buffers[count + 1 : 2 * count + 1]
        recvs = buffers[2 * count + 1 :]
        _exchange_sum(stages, source, slots, partial, sends, recvs, out)

    if depth > 0:
        rows[...] = jnp.zeros_like(rows)
        for i in range(depth):
            summed = lax.dot_general(
                ones, image * basis_refs[i][...], contract, precision=highest,
                preferred_element_type=jnp.float32,
            )
            rows[i : i + 1, :] = summed[0:1, :]
        run(first, rows, h_ref)
        columns = lax.dot_general(
            eye, h_ref[...], contract, precision=highest, preferred_element_type=jnp.float32
        )
        for i in range(depth):
            image = image - columns[:, i : i + 1] * basis_refs[i][...]
    else:
        h_ref[...] = jnp.zeros_like(h_ref)
    work[...] = lax.dot_general(
        ones, image * image, contract, precision=highest, preferred_element_type=jnp.float32
    )
    run(second, work, rows)
    length = jnp.sqrt(rows[...] + epsilon)
    h_ref[depth : depth + 1, :] = length[0:1, :]
    scale = lax.dot_general(
        eye, length, contract, precision=highest, preferred_element_type=jnp.float32
    )
    next_ref[...] = image / scale[:, 0:1]


def _signal_stages(barrier, stages):
    peers = 0
    for axis, n in stages:
        mine = lax.axis_index(axis)
        for k in range(1, n):
            pl.semaphore_signal(
                barrier, inc=1, device_id={axis: lax.rem(mine + k, n)}, device_id_type=MESH
            )
            peers += 1
    return peers


def _project_kernel(stages, depth, *refs):
    basis_refs = refs[:depth]
    image_ref, h_ref, next_ref = refs[depth : depth + 3]
    barrier = pltpu.get_barrier_semaphore()
    pl.semaphore_wait(barrier, _signal_stages(barrier, stages))
    _project_body(stages, depth, basis_refs, image_ref, h_ref, next_ref, refs[depth + 3 :])


def _global_stages(mesh_shape):
    return tuple((axis, mesh_shape[axis]) for axis in ("blk", "sec") if mesh_shape[axis] > 1)


def project(basis, image, mesh_shape):
    depth = len(basis)
    cases, width = image.shape
    stages = _global_stages(mesh_shape)
    return pl.pallas_call(
        functools.partial(_project_kernel, stages, depth),
        out_shape=(
            jax.ShapeDtypeStruct((8, cases), jnp.float32),
            jax.ShapeDtypeStruct((cases, width), jnp.float32),
        ),
        in_specs=[pl.BlockSpec(memory_space=pltpu.VMEM)] * (depth + 1),
        out_specs=[pl.BlockSpec(memory_space=pltpu.VMEM)] * 2,
        scratch_shapes=_project_scratch(stages, cases),
        compiler_params=pltpu.CompilerParams(collective_id=6 + depth, has_side_effects=True),
    )(*basis, image)


def least_squares(columns, beta, depth):
    zero = jnp.zeros_like(beta)
    upper = [
        [columns[j][i] if i <= j + 1 else zero for j in range(depth)] for i in range(depth + 1)
    ]
    rhs = [beta] + [zero] * depth
    for column in range(depth):
        upper_row, lower_row = upper[column], upper[column + 1]
        radius = jnp.sqrt(upper_row[column] ** 2 + lower_row[column] ** 2)
        cosine = upper_row[column] / radius
        sine_term = lower_row[column] / radius
        upper[column] = [cosine * a + sine_term * b for a, b in zip(upper_row, lower_row)]
        upper[column + 1] = [-sine_term * a + cosine * b for a, b in zip(upper_row, lower_row)]
        first_rhs, second_rhs = rhs[column], rhs[column + 1]
        rhs[column] = cosine * first_rhs + sine_term * second_rhs
        rhs[column + 1] = -sine_term * first_rhs + cosine * second_rhs
    weights = [zero] * depth
    for column in reversed(range(depth)):
        remain = rhs[column]
        if column + 1 < depth:
            tail = upper[column][column + 1] * weights[column + 1]
            for k in range(column + 2, depth):
                tail = tail + upper[column][k] * weights[k]
            remain = remain - tail
        weights[column] = remain / upper[column][column]
    return weights

def local(
    mesh_shape,
    state_now, source, fan_gain, section_block, block_inverse, back_panel, ahead_panel, interface
):
    highest = lax.Precision.HIGHEST
    cases, node_rows = state_now.shape
    panel_width = back_panel.shape[1]
    indices = interface[0]
    first_row = lax.axis_index("blk") * node_rows
    selector = (indices[None, :] == first_row + jnp.arange(node_rows)[:, None]).astype(jnp.float32)
    contract = (((1,), (1,)), ((), ()))

    own_piece = panel_width // mesh_shape["blk"]
    own_picks = lax.dynamic_slice_in_dim(selector, lax.axis_index("blk") * own_piece, own_piece, 1).T

    def section_terms(dense_part, behind_vals, piece):
        width = piece.shape[1]
        dense_part = lax.dot_general(
            piece, section_block, contract, preferred_element_type=jnp.float32
        )
        picker = (indices[None, :] == jnp.arange(width)[:, None]).astype(jnp.bfloat16)
        behind_vals = jnp.dot(piece, picker, preferred_element_type=jnp.float32)
        return (dense_part, behind_vals)

    def fold_section(carry, piece):
        return section_terms(carry[0], carry[1], piece)

    n_sec, n_blk = mesh_shape["sec"], mesh_shape["blk"]
    piece = panel_width // n_blk
    local_picks = lax.dynamic_slice_in_dim(selector, lax.axis_index("blk") * piece, piece, 1)

    def finish(gathered, behind_t, ahead_piece):
        dense_part = lax.dot_general(
            gathered, section_block, contract, preferred_element_type=jnp.float32
        )
        lower_term = lax.dot_general(
            behind_t.astype(jnp.bfloat16),
            back_panel,
            (((0,), (1,)), ((), ())),
            preferred_element_type=jnp.float32,
        )
        upper_term = lax.dot_general(
            ahead_piece, local_picks, (((0,), (1,)), ((), ())), precision=highest
        )
        return dense_part + lower_term + upper_term

    def operator(vector):
        rounded = vector.astype(jnp.bfloat16)
        up_t = lax.dot_general(
            ahead_panel, rounded, (((0,), (1,)), ((), ())), preferred_element_type=jnp.float32
        )
        be_t = lax.dot_general(
            selector.astype(jnp.bfloat16),
            rounded,
            (((0,), (1,)), ((), ())),
            preferred_element_type=jnp.float32,
        )
        return finish(*operator_exchange(rounded, up_t, be_t, n_sec, n_blk))

    def compose(earlier, later):
        first_map, first_value = earlier
        second_map, second_value = later
        joined_map = jnp.dot(second_map, first_map, precision=highest)
        joined_value = jnp.dot(first_value, second_map.T, precision=highest) + second_value
        return (joined_map, joined_value)

    def lengths(vector):
        return jnp.sqrt(global_sum(jnp.sum(vector * vector, axis=1)[None], mesh_shape)[0] + epsilon)

    bent = jnp.tanh(state_now)
    state_rounded = state_now.astype(jnp.bfloat16)
    applied, gain_panel, chain = setup_exchange(
        state_rounded, ahead_panel, section_block, local_picks, back_panel, block_inverse,
        own_picks, n_sec, n_blk,
    )
    residual = source - applied - fan_gain[None, :] * bent
    jac_diag = fan_gain[None, :] * (1.0 - bent * bent)
    columns = []
    basis = []
    directions = []
    product = residual
    beta = None
    for column in range(KRYLOV):
        sums, following, direction, product = precondition_sweep(
            list(basis), product, block_inverse, own_picks, chain, gain_panel, ahead_panel,
            section_block, back_panel, local_picks, jac_diag, mesh_shape, len(basis),
        )
        if column == 0:
            beta = sums[0]
        else:
            columns.append(sums[: column + 1])
        basis.append(following)
        directions.append(direction)
    sums, _ = project(basis, product, mesh_shape)
    columns.append(sums[: KRYLOV + 1])
    weights = least_squares(columns, beta, KRYLOV)
    update = jnp.zeros_like(state_now)
    for column in range(KRYLOV):
        update = update + weights[column][:, None] * directions[column]
    return state_now + update


def solution(mesh):
    in_specs = (
        P(None, ("sec", "blk")),
        P(None, ("sec", "blk")),
        P(("sec", "blk")),
        P(("sec", "blk"), None),
        P(("sec", "blk"), None),
        P(("sec", "blk"), None),
        P(("sec", "blk"), None),
        P("sec", None),
    )
    out_specs = P(None, ("sec", "blk"))
    return jax.shard_map(functools.partial(local, dict(mesh.shape)), mesh=mesh, in_specs=in_specs, out_specs=out_specs, check_vma=False)
```

```python
import functools

import jax
import jax.numpy as jnp
from jax import lax
from jax.experimental import pallas as pl
from jax.experimental.pallas import tpu as pltpu
from jax.sharding import PartitionSpec as P

MESH = pl.DeviceIdType.MESH

KRYLOV = 3


epsilon = 1e-06


def extended(x, sides, width):
    for axis, dim in sides:
        size, length = (lax.axis_size(axis), x.shape[dim])
        up = [(i, (i + 1) % size) for i in range(size - 1)]
        down = [(j, i) for i, j in up]
        last = lax.slice_in_dim(x, length - width, length, axis=dim)
        first = lax.slice_in_dim(x, 0, width, axis=dim)
        before = lax.ppermute(last, axis, up)
        after = lax.ppermute(first, axis, down)
        x = jnp.concatenate([before, x, after], axis=dim)
    return x


def entering(value, axis, join, neutral):
    count, mine = (lax.axis_size(axis), lax.axis_index(axis))
    pieces = jax.tree.map(lambda part: lax.all_gather(part, axis), value)
    so_far = jax.tree.map(
        lambda part, zero: jnp.full_like(part, 0) + jnp.asarray(zero, part.dtype), value, neutral
    )

    def step(position, so_far):
        longer = join(so_far, jax.tree.map(lambda part: part[position], pieces))
        return jax.tree.map(lambda new, old: jnp.where(position < mine, new, old), longer, so_far)

    return lax.fori_loop(0, count - 1, step, so_far)


def _reduce_kernel(stages, x_ref, o_ref, *scratch):
    count = len(stages)
    slots = scratch[:count]
    partial = scratch[count]
    sends = scratch[count + 1 : 2 * count + 1]
    recvs = scratch[2 * count + 1 :]
    barrier = pltpu.get_barrier_semaphore()
    peers = 0
    for axis, n in stages:
        mine = lax.axis_index(axis)
        for k in range(1, n):
            pl.semaphore_signal(
                barrier, inc=1, device_id={axis: lax.rem(mine + k, n)}, device_id_type=MESH
            )
            peers += 1
    pl.semaphore_wait(barrier, peers)
    source = x_ref
    for stage, (axis, n) in enumerate(stages):
        mine = lax.axis_index(axis)
        copies = []
        for k in range(1, n):
            copy = pltpu.make_async_remote_copy(
                src_ref=source,
                dst_ref=slots[stage].at[mine],
                send_sem=sends[stage].at[k],
                recv_sem=recvs[stage].at[mine],
                device_id={axis: lax.rem(mine + k, n)},
                device_id_type=MESH,
            )
            copy.start()
            copies.append(copy)
        slots[stage][mine] = source[...]
        for k in range(1, n):
            sender = lax.rem(mine + k, n)
            pltpu.make_async_remote_copy(
                src_ref=source,
                dst_ref=slots[stage].at[sender],
                send_sem=sends[stage].at[k],
                recv_sem=recvs[stage].at[sender],
                device_id={axis: sender},
                device_id_type=MESH,
            ).wait_recv()
        for copy in copies:
            copy.wait_send()
        total = slots[stage][0]
        for j in range(1, n):
            total = total + slots[stage][j]
        if stage == count - 1:
            o_ref[...] = total
        else:
            partial[...] = total
            source = partial


def all_sum(x, axes, mesh_shape, collective):
    stages = tuple((axis, mesh_shape[axis]) for axis in axes if mesh_shape[axis] > 1)
    rows, cols = x.shape
    scratch = [pltpu.VMEM((n, rows, cols), jnp.float32) for _, n in stages]
    scratch.append(pltpu.VMEM((rows, cols), jnp.float32))
    scratch += [pltpu.SemaphoreType.DMA((n,)) for _, n in stages]
    scratch += [pltpu.SemaphoreType.DMA((n,)) for _, n in stages]
    return pl.pallas_call(
        functools.partial(_reduce_kernel, stages),
        out_shape=jax.ShapeDtypeStruct((rows, cols), jnp.float32),
        in_specs=[pl.BlockSpec(memory_space=pltpu.VMEM)],
        out_specs=pl.BlockSpec(memory_space=pltpu.VMEM),
        scratch_shapes=scratch,
        compiler_params=pltpu.CompilerParams(collective_id=collective, has_side_effects=True),
    )(x.astype(jnp.float32))


def global_sum(rows_of_sums, mesh_shape):
    count = rows_of_sums.shape[0]
    padded = jnp.zeros((8, rows_of_sums.shape[1]), jnp.float32).at[:count].set(rows_of_sums)
    return all_sum(padded, ("blk", "sec"), mesh_shape, 0)[:count]


def _doubling(n):
    distances, d = [], 1
    while d < n:
        distances.append(d)
        d *= 2
    return tuple(distances)


def _greet(n, distances):
    barrier = pltpu.get_barrier_semaphore()
    mine = lax.axis_index("sec")
    for d in distances:
        for peer in (lax.rem(mine + d, n), lax.rem(mine + n - d, n)):
            pl.semaphore_signal(barrier, inc=1, device_id={"sec": peer}, device_id_type=MESH)
    pl.semaphore_wait(barrier, 2 * len(distances))


def _hop(n, d, source, slot, send_sem, recv_sem):
    mine = lax.axis_index("sec")
    copy = pltpu.make_async_remote_copy(
        src_ref=source,
        dst_ref=slot,
        send_sem=send_sem,
        recv_sem=recv_sem,
        device_id={"sec": lax.rem(mine + d, n)},
        device_id_type=MESH,
    )
    copy.start()
    copy.wait_recv()
    copy.wait_send()


RADIX = 4


def _plan(n):
    rounds, d = [], 1
    while d < n:
        rounds.append((d, tuple(j for j in range(1, RADIX) if j * d < n)))
        d *= RADIX
    return tuple(rounds)


def _plan_peers(rounds):
    return tuple(sorted({j * d for d, js in rounds for j in js} | {1}))


def _send_all(n, sec, sources, slots, sends, recvs, flat, d, js):
    copies = []
    for i, j in enumerate(js):
        copy = pltpu.make_async_remote_copy(
            src_ref=sources,
            dst_ref=slots.at[flat + i],
            send_sem=sends.at[flat + i],
            recv_sem=recvs.at[flat + i],
            device_id={"sec": lax.rem(sec + j * d, n)},
            device_id_type=MESH,
        )
        copy.start()
        copies.append(copy)
    for copy in copies:
        copy.wait_recv()
    for copy in copies:
        copy.wait_send()


def _spread(n_sec, n_blk, offsets, piece_ref, slots, sends, recvs):
    sec, blk = lax.axis_index("sec"), lax.axis_index("blk")

    def copy(o, j, index):
        return pltpu.make_async_remote_copy(
            src_ref=piece_ref,
            dst_ref=slots.at[index],
            send_sem=sends.at[(o - 1) * n_blk + j],
            recv_sem=recvs.at[index],
            device_id={"sec": lax.rem(sec + o, n_sec), "blk": j},
            device_id_type=MESH,
        )

    outgoing = [
        copy(o, j, (o - 1) * n_blk + blk) for o in range(1, offsets + 1) for j in range(n_blk)
    ]
    for c in outgoing:
        c.start()
    for o in range(1, offsets + 1):
        for j in range(n_blk):
            copy(o, j, (o - 1) * n_blk + j).wait_recv()
    for c in outgoing:
        c.wait_send()


def _assemble(n_blk, offsets, slots, mats):
    piece = slots.shape[1]
    for o in range(offsets):
        for j in range(n_blk):
            mats[o, j * piece : (j + 1) * piece, :] = slots[o * n_blk + j]


def _greet_all(n_sec, n_blk, offsets, rounds, blk_peers, stages=()):
    barrier = pltpu.get_barrier_semaphore()
    sec, blk = lax.axis_index("sec"), lax.axis_index("blk")
    count = _signal_stages(barrier, stages)
    if blk_peers:
        for k in range(1, n_blk):
            pl.semaphore_signal(
                barrier, inc=1, device_id={"blk": lax.rem(blk + k, n_blk)}, device_id_type=MESH
            )
            count += 1
    covered = bool(stages)
    for o in range(1, offsets + 1):
        for k in range(1 if covered else 0, n_blk):
            for peer in (lax.rem(sec + o, n_sec), lax.rem(sec + n_sec - o, n_sec)):
                pl.semaphore_signal(
                    barrier,
                    inc=1,
                    device_id={"sec": peer, "blk": lax.rem(blk + k, n_blk)},
                    device_id_type=MESH,
                )
                count += 1
    if covered:
        pl.semaphore_wait(barrier, count)
        return
    for d in sorted({j * d for d, js in rounds[1:] for j in js}):
        for peer in (lax.rem(sec + d, n_sec), lax.rem(sec + n_sec - d, n_sec)):
            pl.semaphore_signal(barrier, inc=1, device_id={"sec": peer}, device_id_type=MESH)
            count += 1
    pl.semaphore_wait(barrier, count)


def _maps_body(n, n_blk, rounds, e_ref, a_ref, eslots, emat, current, slots, esend, erecv, sends, recvs):
    sec = lax.axis_index("sec")
    first = rounds[0][1]
    offsets = len(first) + 1
    _spread(n, n_blk, offsets, e_ref, eslots, esend, erecv)
    _assemble(n_blk, offsets, eslots, emat)
    joined = emat[0]
    for i, j in enumerate(first):
        a_ref[i] = joined
        joined = jnp.dot(
            joined, emat[j], precision=lax.Precision.HIGHEST, preferred_element_type=jnp.float32
        )
    current[...] = joined
    flat = len(first)
    for k in range(1, len(rounds)):
        d, js = rounds[k]
        onward = k < len(rounds) - 1
        if onward or len(js) > 1:
            _send_all(n, sec, current, slots, sends, recvs, flat, d, js)
        joined = current[...]
        for i, j in enumerate(js):
            a_ref[flat + i] = joined
            if onward or i < len(js) - 1:
                joined = jnp.dot(
                    joined, slots[flat + i], precision=lax.Precision.HIGHEST,
                    preferred_element_type=jnp.float32,
                )
        if onward:
            current[...] = joined
        flat += len(js)


def _setup_kernel(
    n_sec, n_blk, rounds, x_ref, ahead_ref, block_ref, spread_ref, back_ref, inv_ref, pick_ref,
    k_ref, gain_ref, chain_ref, *scratch
):
    phase_scratch = scratch[:9]
    pslots, psend, precv, epiece = scratch[9:13]
    g_ref, b_ref, a_ref, upward, own_piece = scratch[13:18]
    maps_scratch = scratch[18:]
    sec, blk = lax.axis_index("sec"), lax.axis_index("blk")
    offsets = len(rounds[0][1]) + 1
    _greet_all(n_sec, n_blk, offsets, rounds, True)
    contract = (((1,), (1,)), ((), ()))
    upward[...] = jnp.dot(x_ref[...], ahead_ref[...], preferred_element_type=jnp.float32).T
    own_piece[...] = lax.dot_general(
        pick_ref[...], x_ref[...].astype(jnp.float32), contract,
        precision=lax.Precision.HIGHEST, preferred_element_type=jnp.float32,
    )

    def blk_copy(k, target, slot):
        return pltpu.make_async_remote_copy(
            src_ref=back_ref,
            dst_ref=pslots.at[slot],
            send_sem=psend.at[k],
            recv_sem=precv.at[slot],
            device_id={"blk": target},
            device_id_type=MESH,
        )

    outgoing = [blk_copy(k, lax.rem(blk + k, n_blk), blk) for k in range(1, n_blk)]
    for copy in outgoing:
        copy.start()
    _operator_phase(n_sec, n_blk, x_ref, upward, own_piece, g_ref, b_ref, a_ref, phase_scratch)
    width = x_ref.shape[1]
    product = lax.dot_general(
        g_ref[:, 0:width], block_ref[:, 0:width], contract, preferred_element_type=jnp.float32
    )
    for j in range(1, n_blk):
        product = product + lax.dot_general(
            g_ref[:, j * width : (j + 1) * width],
            block_ref[:, j * width : (j + 1) * width],
            contract,
            preferred_element_type=jnp.float32,
        )
    product = product + lax.dot_general(
        b_ref[...].T.astype(back_ref.dtype), back_ref[...], contract,
        preferred_element_type=jnp.float32,
    )
    product = product + jnp.dot(
        spread_ref[...], a_ref[...], precision=lax.Precision.HIGHEST,
        preferred_element_type=jnp.float32,
    ).T
    k_ref[...] = product
    pslots[blk] = back_ref[...]
    for k in range(1, n_blk):
        sender = lax.rem(blk + k, n_blk)
        blk_copy(k, sender, sender).wait_recv()
    for copy in outgoing:
        copy.wait_send()
    rows = back_ref.shape[0]
    gain = jnp.dot(inv_ref[:, 0:rows], pslots[0], preferred_element_type=jnp.float32)
    for j in range(1, n_blk):
        gain = gain + jnp.dot(
            inv_ref[:, j * rows : (j + 1) * rows], pslots[j], preferred_element_type=jnp.float32
        )
    gain_ref[...] = gain
    epiece[...] = -jnp.dot(
        pick_ref[...], gain, precision=lax.Precision.HIGHEST, preferred_element_type=jnp.float32
    )
    _maps_body(n_sec, n_blk, rounds, epiece, chain_ref, *maps_scratch)


def setup_exchange(x, ahead, block, spread, back, inverse, picks, n_sec, n_blk):
    cases, width = x.shape
    panel = ahead.shape[1]
    piece = panel // n_blk
    rows, panel_width = back.shape
    rounds = _plan(n_sec)
    total = sum(len(js) for _, js in rounds)
    offsets = len(rounds[0][1]) + 1
    return pl.pallas_call(
        functools.partial(_setup_kernel, n_sec, n_blk, rounds),
        out_shape=(
            jax.ShapeDtypeStruct((cases, width), jnp.float32),
            jax.ShapeDtypeStruct((rows, panel_width), jnp.float32),
            jax.ShapeDtypeStruct((total, panel_width, panel_width), jnp.float32),
        ),
        in_specs=[pl.BlockSpec(memory_space=pltpu.VMEM)] * 7,
        out_specs=[pl.BlockSpec(memory_space=pltpu.VMEM)] * 3,
        scratch_shapes=_operator_scratch(n_blk, cases, width, x.dtype, piece, cases)
        + [
            pltpu.VMEM((n_blk, rows, panel_width), back.dtype),
            pltpu.SemaphoreType.DMA((n_blk,)),
            pltpu.SemaphoreType.DMA((n_blk,)),
            pltpu.VMEM((piece, panel_width), jnp.float32),
            pltpu.VMEM((cases, n_blk * width), x.dtype),
            pltpu.VMEM((panel, cases), jnp.float32),
            pltpu.VMEM((piece, cases), jnp.float32),
            pltpu.VMEM((panel, cases), jnp.float32),
            pltpu.VMEM((piece, cases), jnp.float32),
            pltpu.VMEM((offsets * n_blk, piece, panel_width), jnp.float32),
            pltpu.VMEM((offsets, panel_width, panel_width), jnp.float32),
            pltpu.VMEM((panel_width, panel_width), jnp.float32),
            pltpu.VMEM((total, panel_width, panel_width), jnp.float32),
            pltpu.SemaphoreType.DMA((offsets * n_blk,)),
            pltpu.SemaphoreType.DMA((offsets * n_blk,)),
            pltpu.SemaphoreType.DMA((total,)),
            pltpu.SemaphoreType.DMA((total,)),
        ],
        compiler_params=pltpu.CompilerParams(collective_id=3, has_side_effects=True),
    )(x, ahead, block, spread, back, inverse, picks)


def _gather_kernel(n, x_ref, o_ref, slots, sends, recvs):
    mine = lax.axis_index("blk")
    barrier = pltpu.get_barrier_semaphore()
    for k in range(1, n):
        pl.semaphore_signal(
            barrier, inc=1, device_id={"blk": lax.rem(mine + k, n)}, device_id_type=MESH
        )
    pl.semaphore_wait(barrier, n - 1)
    copies = []
    for k in range(1, n):
        copy = pltpu.make_async_remote_copy(
            src_ref=x_ref,
            dst_ref=slots.at[mine],
            send_sem=sends.at[k],
            recv_sem=recvs.at[mine],
            device_id={"blk": lax.rem(mine + k, n)},
            device_id_type=MESH,
        )
        copy.start()
        copies.append(copy)
    slots[mine] = x_ref[...]
    for k in range(1, n):
        sender = lax.rem(mine + k, n)
        pltpu.make_async_remote_copy(
            src_ref=x_ref,
            dst_ref=slots.at[sender],
            send_sem=sends.at[k],
            recv_sem=recvs.at[sender],
            device_id={"blk": sender},
            device_id_type=MESH,
        ).wait_recv()
    for copy in copies:
        copy.wait_send()
    width = x_ref.shape[1]
    for j in range(n):
        o_ref[:, j * width : (j + 1) * width] = slots[j]


def gather_blk(x, n):
    rows, width = x.shape
    return pl.pallas_call(
        functools.partial(_gather_kernel, n),
        out_shape=jax.ShapeDtypeStruct((rows, n * width), x.dtype),
        in_specs=[pl.BlockSpec(memory_space=pltpu.VMEM)],
        out_specs=pl.BlockSpec(memory_space=pltpu.VMEM),
        scratch_shapes=[
            pltpu.VMEM((n, rows, width), x.dtype),
            pltpu.SemaphoreType.DMA((n,)),
            pltpu.SemaphoreType.DMA((n,)),
        ],
        compiler_params=pltpu.CompilerParams(collective_id=4, has_side_effects=True),
    )(x)


def _operator_phase(n_sec, n_blk, x_ref, up_ref, piece_ref, g_ref, b_ref, a_ref, scratch):
    gslots, bslots, aslots, gsend, grecv, bsend, brecv, asend, arecv = scratch
    sec, blk = lax.axis_index("sec"), lax.axis_index("blk")
    nxt, prv = lax.rem(sec + 1, n_sec), lax.rem(sec + n_sec - 1, n_sec)
    piece = bslots.shape[1]
    copies = []
    for k in range(1, n_blk):
        copies.append(
            pltpu.make_async_remote_copy(
                src_ref=x_ref,
                dst_ref=gslots.at[blk],
                send_sem=gsend.at[k],
                recv_sem=grecv.at[blk],
                device_id={"blk": lax.rem(blk + k, n_blk)},
                device_id_type=MESH,
            )
        )
    for j in range(n_blk):
        copies.append(
            pltpu.make_async_remote_copy(
                src_ref=piece_ref,
                dst_ref=bslots.at[blk],
                send_sem=bsend.at[j],
                recv_sem=brecv.at[blk],
                device_id={"sec": nxt, "blk": j},
                device_id_type=MESH,
            )
        )
        copies.append(
            pltpu.make_async_remote_copy(
                src_ref=up_ref.at[pl.ds(j * piece, piece)],
                dst_ref=aslots.at[blk],
                send_sem=asend.at[j],
                recv_sem=arecv.at[blk],
                device_id={"sec": prv, "blk": j},
                device_id_type=MESH,
            )
        )
    for copy in copies:
        copy.start()
    gslots[blk] = x_ref[...]
    for k in range(1, n_blk):
        sender = lax.rem(blk + k, n_blk)
        pltpu.make_async_remote_copy(
            src_ref=x_ref,
            dst_ref=gslots.at[sender],
            send_sem=gsend.at[k],
            recv_sem=grecv.at[sender],
            device_id={"blk": sender},
            device_id_type=MESH,
        ).wait_recv()
    for j in range(n_blk):
        pltpu.make_async_remote_copy(
            src_ref=piece_ref,
            dst_ref=bslots.at[j],
            send_sem=bsend.at[j],
            recv_sem=brecv.at[j],
            device_id={"sec": prv, "blk": j},
            device_id_type=MESH,
        ).wait_recv()
        pltpu.make_async_remote_copy(
            src_ref=up_ref.at[pl.ds(j * piece, piece)],
            dst_ref=aslots.at[j],
            send_sem=asend.at[j],
            recv_sem=arecv.at[j],
            device_id={"sec": nxt, "blk": j},
            device_id_type=MESH,
        ).wait_recv()
    for copy in copies:
        copy.wait_send()
    width = x_ref.shape[1]
    for j in range(n_blk):
        g_ref[:, j * width : (j + 1) * width] = gslots[j]
        b_ref[j * piece : (j + 1) * piece, :] = jnp.where(
            sec >= 1, bslots[j], jnp.zeros_like(bslots[j])
        )
    total = aslots[0]
    for j in range(1, n_blk):
        total = total + aslots[j]
    a_ref[...] = jnp.where(sec <= n_sec - 2, total, jnp.zeros_like(total))


def _operator_scratch(n_blk, rows, width, dtype, piece, cases):
    return [
        pltpu.VMEM((n_blk, rows, width), dtype),
        pltpu.VMEM((n_blk, piece, cases), jnp.float32),
        pltpu.VMEM((n_blk, piece, cases), jnp.float32),
    ] + [pltpu.SemaphoreType.DMA((n_blk,))] * 6


def _operator_kernel(n_sec, n_blk, x_ref, up_ref, be_ref, g_ref, b_ref, a_ref, *scratch):
    sec, blk = lax.axis_index("sec"), lax.axis_index("blk")
    nxt, prv = lax.rem(sec + 1, n_sec), lax.rem(sec + n_sec - 1, n_sec)
    piece = scratch[1].shape[1]
    barrier = pltpu.get_barrier_semaphore()
    for k in range(1, n_blk):
        pl.semaphore_signal(
            barrier, inc=1, device_id={"blk": lax.rem(blk + k, n_blk)}, device_id_type=MESH
        )
    for j in range(n_blk):
        for other in (nxt, prv):
            pl.semaphore_signal(
                barrier, inc=1, device_id={"sec": other, "blk": j}, device_id_type=MESH
            )
    pl.semaphore_wait(barrier, 3 * n_blk - 1)
    mine = be_ref.at[pl.ds(pl.multiple_of(blk * piece, 8), piece)]
    _operator_phase(n_sec, n_blk, x_ref, up_ref, mine, g_ref, b_ref, a_ref, scratch)


def operator_exchange(x, up_t, be_t, n_sec, n_blk):
    rows, width = x.shape
    panel, cases = up_t.shape
    piece = panel // n_blk
    return pl.pallas_call(
        functools.partial(_operator_kernel, n_sec, n_blk),
        out_shape=(
            jax.ShapeDtypeStruct((rows, n_blk * width), x.dtype),
            jax.ShapeDtypeStruct((panel, cases), jnp.float32),
            jax.ShapeDtypeStruct((piece, cases), jnp.float32),
        ),
        in_specs=[pl.BlockSpec(memory_space=pltpu.VMEM)] * 3,
        out_specs=[pl.BlockSpec(memory_space=pltpu.VMEM)] * 3,
        scratch_shapes=_operator_scratch(n_blk, rows, width, x.dtype, piece, cases),
        compiler_params=pltpu.CompilerParams(collective_id=5, has_side_effects=True),
    )(x, up_t, be_t)


def _precondition_kernel(n_sec, n_blk, rounds, stages, depth, *refs):
    basis_refs = refs[:depth]
    (image_ref, inv_ref, pick_ref, u_ref, gain_ref, ahead_ref, block_ref, back_ref, spread_ref,
     jac_ref, h_ref, next_ref, d_ref, p_ref) = refs[depth : depth + 14]
    scratch = refs[depth + 14 :]
    gslots, fpiece, fslots, fmat, carry, slots, gsend, grecv, fsend, frecv, ssend, srecv = scratch[:12]
    rounded, upward, own_piece, x_ref = scratch[12:16]
    g_ref, b_ref, a_ref = scratch[16:19]
    phase_scratch = scratch[19:28]
    project_scratch = scratch[28:]
    sec, blk = lax.axis_index("sec"), lax.axis_index("blk")
    first = rounds[0][1]
    offsets = len(first) + 1
    _greet_all(n_sec, n_blk, offsets, rounds, False, stages)
    _project_body(stages, depth, basis_refs, image_ref, h_ref, next_ref, project_scratch)
    x_ref[...] = next_ref[...].astype(x_ref.dtype)

    def blk_copy(k, target, slot):
        return pltpu.make_async_remote_copy(
            src_ref=x_ref,
            dst_ref=gslots.at[slot],
            send_sem=gsend.at[k],
            recv_sem=grecv.at[slot],
            device_id={"blk": target},
            device_id_type=MESH,
        )

    outgoing = [blk_copy(k, lax.rem(blk + k, n_blk), blk) for k in range(1, n_blk)]
    for copy in outgoing:
        copy.start()
    gslots[blk] = x_ref[...]
    for k in range(1, n_blk):
        sender = lax.rem(blk + k, n_blk)
        blk_copy(k, sender, sender).wait_recv()
    for copy in outgoing:
        copy.wait_send()
    width = x_ref.shape[1]
    contract = (((1,), (1,)), ((), ()))
    folded = lax.dot_general(
        gslots[0], inv_ref[:, 0:width], contract, preferred_element_type=jnp.float32
    )
    for j in range(1, n_blk):
        folded = folded + lax.dot_general(
            gslots[j],
            inv_ref[:, j * width : (j + 1) * width],
            contract,
            preferred_element_type=jnp.float32,
        )
    fpiece[...] = lax.dot_general(
        pick_ref[...], folded, contract, precision=lax.Precision.HIGHEST,
        preferred_element_type=jnp.float32,
    )
    _spread(n_sec, n_blk, offsets, fpiece, fslots, fsend, frecv)
    _assemble(n_blk, offsets, fslots, fmat)
    joined = jnp.where(sec >= 1, fmat[0], jnp.zeros_like(fmat[0]))
    for i, j in enumerate(first):
        term = jnp.dot(
            u_ref[i], fmat[j], precision=lax.Precision.HIGHEST, preferred_element_type=jnp.float32
        )
        joined = joined + jnp.where(sec >= j + 1, term, jnp.zeros_like(term))
    carry[1] = joined
    flat = len(first)
    for k in range(1, len(rounds)):
        d, js = rounds[k]
        _send_all(n_sec, sec, carry.at[k], slots, ssend, srecv, flat, d, js)
        joined = carry[k]
        for i, j in enumerate(js):
            term = jnp.dot(
                u_ref[flat + i], slots[flat + i], precision=lax.Precision.HIGHEST,
                preferred_element_type=jnp.float32,
            )
            joined = joined + jnp.where(sec >= j * d, term, jnp.zeros_like(term))
        carry[k + 1] = joined
        flat += len(js)
    before = carry[len(rounds)].T
    direction = folded - lax.dot_general(
        before, gain_ref[...], contract, precision=lax.Precision.HIGHEST,
        preferred_element_type=jnp.float32,
    )
    d_ref[...] = direction
    rounded[...] = direction.astype(rounded.dtype)
    upward[...] = jnp.dot(
        rounded[...], ahead_ref[...], preferred_element_type=jnp.float32
    ).T
    own_piece[...] = lax.dot_general(
        pick_ref[...], rounded[...].astype(jnp.float32), contract,
        precision=lax.Precision.HIGHEST, preferred_element_type=jnp.float32,
    )
    _operator_phase(n_sec, n_blk, rounded, upward, own_piece, g_ref, b_ref, a_ref, phase_scratch)
    product = jac_ref[...] * direction
    for j in range(n_blk):
        product = product + lax.dot_general(
            g_ref[:, j * width : (j + 1) * width],
            block_ref[:, j * width : (j + 1) * width],
            contract,
            preferred_element_type=jnp.float32,
        )
    product = product + lax.dot_general(
        b_ref[...].T.astype(back_ref.dtype), back_ref[...], contract,
        preferred_element_type=jnp.float32,
    )
    product = product + jnp.dot(
        spread_ref[...], a_ref[...], precision=lax.Precision.HIGHEST,
        preferred_element_type=jnp.float32,
    ).T
    p_ref[...] = product


def precondition_sweep(
    basis, image, inverse, picks, chain, gain, ahead, block, back, spread, jac, mesh_shape, depth
):
    n_sec, n_blk = mesh_shape["sec"], mesh_shape["blk"]
    stages = _global_stages(mesh_shape)
    cases, width = image.shape
    piece, _ = picks.shape
    panel = piece * n_blk
    plan = _plan(n_sec)
    rounds = len(plan)
    total = sum(len(js) for _, js in plan)
    offsets = len(plan[0][1]) + 1
    dtype = jnp.bfloat16
    return pl.pallas_call(
        functools.partial(_precondition_kernel, n_sec, n_blk, plan, stages, depth),
        out_shape=(
            jax.ShapeDtypeStruct((8, cases), jnp.float32),
            jax.ShapeDtypeStruct((cases, width), jnp.float32),
            jax.ShapeDtypeStruct((cases, width), jnp.float32),
            jax.ShapeDtypeStruct((cases, width), jnp.float32),
        ),
        in_specs=[pl.BlockSpec(memory_space=pltpu.VMEM)] * (depth + 10),
        out_specs=[pl.BlockSpec(memory_space=pltpu.VMEM)] * 4,
        scratch_shapes=[
            pltpu.VMEM((n_blk, cases, width), dtype),
            pltpu.VMEM((piece, cases), jnp.float32),
            pltpu.VMEM((offsets * n_blk, piece, cases), jnp.float32),
            pltpu.VMEM((offsets, panel, cases), jnp.float32),
            pltpu.VMEM((rounds + 1, panel, cases), jnp.float32),
            pltpu.VMEM((total, panel, cases), jnp.float32),
            pltpu.SemaphoreType.DMA((n_blk,)),
            pltpu.SemaphoreType.DMA((n_blk,)),
            pltpu.SemaphoreType.DMA((offsets * n_blk,)),
            pltpu.SemaphoreType.DMA((offsets * n_blk,)),
            pltpu.SemaphoreType.DMA((total,)),
            pltpu.SemaphoreType.DMA((total,)),
            pltpu.VMEM((cases, width), dtype),
            pltpu.VMEM((panel, cases), jnp.float32),
            pltpu.VMEM((piece, cases), jnp.float32),
            pltpu.VMEM((cases, width), dtype),
            pltpu.VMEM((cases, n_blk * width), dtype),
            pltpu.VMEM((panel, cases), jnp.float32),
            pltpu.VMEM((piece, cases), jnp.float32),
        ]
        + _operator_scratch(n_blk, cases, width, dtype, piece, cases)
        + _project_scratch(stages, cases),
        compiler_params=pltpu.CompilerParams(collective_id=10 + depth, has_side_effects=True),
    )(*basis, image, inverse, picks, chain, gain, ahead, block, back, spread, jac)


def _exchange_sum(stages, source, slots, partial, sends, recvs, out):
    count = len(stages)
    for stage, (axis, n) in enumerate(stages):
        mine = lax.axis_index(axis)
        copies = []
        for k in range(1, n):
            copy = pltpu.make_async_remote_copy(
                src_ref=source,
                dst_ref=slots[stage].at[mine],
                send_sem=sends[stage].at[k],
                recv_sem=recvs[stage].at[mine],
                device_id={axis: lax.rem(mine + k, n)},
                device_id_type=MESH,
            )
            copy.start()
            copies.append(copy)
        slots[stage][mine] = source[...]
        for k in range(1, n):
            sender = lax.rem(mine + k, n)
            pltpu.make_async_remote_copy(
                src_ref=source,
                dst_ref=slots[stage].at[sender],
                send_sem=sends[stage].at[k],
                recv_sem=recvs[stage].at[sender],
                device_id={axis: sender},
                device_id_type=MESH,
            ).wait_recv()
        for copy in copies:
            copy.wait_send()
        total = slots[stage][0]
        for j in range(1, n):
            total = total + slots[stage][j]
        if stage == count - 1:
            out[...] = total
        else:
            partial[...] = total
            source = partial


def _project_scratch(stages, cases):
    def buffers():
        out = [pltpu.VMEM((n, 8, cases), jnp.float32) for _, n in stages]
        out.append(pltpu.VMEM((8, cases), jnp.float32))
        out += [pltpu.SemaphoreType.DMA((n,)) for _, n in stages]
        out += [pltpu.SemaphoreType.DMA((n,)) for _, n in stages]
        return out

    return buffers() + buffers() + [pltpu.VMEM((8, cases), jnp.float32)] * 2


def _project_body(stages, depth, basis_refs, image_ref, h_ref, next_ref, scratch):
    count = len(stages)
    first, second = scratch[: 3 * count + 1], scratch[3 * count + 1 : 6 * count + 2]
    rows, work = scratch[6 * count + 2 : 6 * count + 4]
    highest = lax.Precision.HIGHEST
    contract = (((1,), (1,)), ((), ()))
    image = image_ref[...]
    ones = jnp.ones((8, image.shape[1]), jnp.float32)
    eye = (
        lax.broadcasted_iota(jnp.int32, (image.shape[0],) * 2, 0)
        == lax.broadcasted_iota(jnp.int32, (image.shape[0],) * 2, 1)
    ).astype(jnp.float32)

    def run(buffers, source, out):
        slots = buffers[:count]
        partial = buffers[count]
        sends = buffers[count + 1 : 2 * count + 1]
        recvs = buffers[2 * count + 1 :]
        _exchange_sum(stages, source, slots, partial, sends, recvs, out)

    if depth > 0:
        rows[...] = jnp.zeros_like(rows)
        for i in range(depth):
            summed = lax.dot_general(
                ones, image * basis_refs[i][...], contract, precision=highest,
                preferred_element_type=jnp.float32,
            )
            rows[i : i + 1, :] = summed[0:1, :]
        run(first, rows, h_ref)
        columns = lax.dot_general(
            eye, h_ref[...], contract, precision=highest, preferred_element_type=jnp.float32
        )
        for i in range(depth):
            image = image - columns[:, i : i + 1] * basis_refs[i][...]
    else:
        h_ref[...] = jnp.zeros_like(h_ref)
    work[...] = lax.dot_general(
        ones, image * image, contract, precision=highest, preferred_element_type=jnp.float32
    )
    run(second, work, rows)
    length = jnp.sqrt(rows[...] + epsilon)
    h_ref[depth : depth + 1, :] = length[0:1, :]
    scale = lax.dot_general(
        eye, length, contract, precision=highest, preferred_element_type=jnp.float32
    )
    next_ref[...] = image / scale[:, 0:1]


def _signal_stages(barrier, stages):
    peers = 0
    for axis, n in stages:
        mine = lax.axis_index(axis)
        for k in range(1, n):
            pl.semaphore_signal(
                barrier, inc=1, device_id={axis: lax.rem(mine + k, n)}, device_id_type=MESH
            )
            peers += 1
    return peers


def _project_kernel(stages, depth, *refs):
    basis_refs = refs[:depth]
    image_ref, h_ref, next_ref = refs[depth : depth + 3]
    barrier = pltpu.get_barrier_semaphore()
    pl.semaphore_wait(barrier, _signal_stages(barrier, stages))
    _project_body(stages, depth, basis_refs, image_ref, h_ref, next_ref, refs[depth + 3 :])


def _global_stages(mesh_shape):
    return tuple((axis, mesh_shape[axis]) for axis in ("blk", "sec") if mesh_shape[axis] > 1)


def project(basis, image, mesh_shape):
    depth = len(basis)
    cases, width = image.shape
    stages = _global_stages(mesh_shape)
    return pl.pallas_call(
        functools.partial(_project_kernel, stages, depth),
        out_shape=(
            jax.ShapeDtypeStruct((8, cases), jnp.float32),
            jax.ShapeDtypeStruct((cases, width), jnp.float32),
        ),
        in_specs=[pl.BlockSpec(memory_space=pltpu.VMEM)] * (depth + 1),
        out_specs=[pl.BlockSpec(memory_space=pltpu.VMEM)] * 2,
        scratch_shapes=_project_scratch(stages, cases),
        compiler_params=pltpu.CompilerParams(collective_id=6 + depth, has_side_effects=True),
    )(*basis, image)


def least_squares(columns, beta, depth):
    zero = jnp.zeros_like(beta)
    upper = [
        [columns[j][i] if i <= j + 1 else zero for j in range(depth)] for i in range(depth + 1)
    ]
    rhs = [beta] + [zero] * depth
    for column in range(depth):
        upper_row, lower_row = upper[column], upper[column + 1]
        radius = jnp.sqrt(upper_row[column] ** 2 + lower_row[column] ** 2)
        cosine = upper_row[column] / radius
        sine_term = lower_row[column] / radius
        upper[column] = [cosine * a + sine_term * b for a, b in zip(upper_row, lower_row)]
        upper[column + 1] = [-sine_term * a + cosine * b for a, b in zip(upper_row, lower_row)]
        first_rhs, second_rhs = rhs[column], rhs[column + 1]
        rhs[column] = cosine * first_rhs + sine_term * second_rhs
        rhs[column + 1] = -sine_term * first_rhs + cosine * second_rhs
    weights = [zero] * depth
    for column in reversed(range(depth)):
        remain = rhs[column]
        if column + 1 < depth:
            tail = upper[column][column + 1] * weights[column + 1]
            for k in range(column + 2, depth):
                tail = tail + upper[column][k] * weights[k]
            remain = remain - tail
        weights[column] = remain / upper[column][column]
    return weights

def local(
    mesh_shape,
    state_now, source, fan_gain, section_block, block_inverse, back_panel, ahead_panel, interface
):
    highest = lax.Precision.HIGHEST
    cases, node_rows = state_now.shape
    panel_width = back_panel.shape[1]
    indices = interface[0]
    first_row = lax.axis_index("blk") * node_rows
    selector = (indices[None, :] == first_row + jnp.arange(node_rows)[:, None]).astype(jnp.float32)
    contract = (((1,), (1,)), ((), ()))

    own_piece = panel_width // mesh_shape["blk"]
    own_picks = lax.dynamic_slice_in_dim(selector, lax.axis_index("blk") * own_piece, own_piece, 1).T

    def section_terms(dense_part, behind_vals, piece):
        width = piece.shape[1]
        dense_part = lax.dot_general(
            piece, section_block, contract, preferred_element_type=jnp.float32
        )
        picker = (indices[None, :] == jnp.arange(width)[:, None]).astype(jnp.bfloat16)
        behind_vals = jnp.dot(piece, picker, preferred_element_type=jnp.float32)
        return (dense_part, behind_vals)

    def fold_section(carry, piece):
        return section_terms(carry[0], carry[1], piece)

    n_sec, n_blk = mesh_shape["sec"], mesh_shape["blk"]
    piece = panel_width // n_blk
    local_picks = lax.dynamic_slice_in_dim(selector, lax.axis_index("blk") * piece, piece, 1)

    def finish(gathered, behind_t, ahead_piece):
        dense_part = lax.dot_general(
            gathered, section_block, contract, preferred_element_type=jnp.float32
        )
        lower_term = lax.dot_general(
            behind_t.astype(jnp.bfloat16),
            back_panel,
            (((0,), (1,)), ((), ())),
            preferred_element_type=jnp.float32,
        )
        upper_term = lax.dot_general(
            ahead_piece, local_picks, (((0,), (1,)), ((), ())), precision=highest
        )
        return dense_part + lower_term + upper_term

    def operator(vector):
        rounded = vector.astype(jnp.bfloat16)
        up_t = lax.dot_general(
            ahead_panel, rounded, (((0,), (1,)), ((), ())), preferred_element_type=jnp.float32
        )
        be_t = lax.dot_general(
            selector.astype(jnp.bfloat16),
            rounded,
            (((0,), (1,)), ((), ())),
            preferred_element_type=jnp.float32,
        )
        return finish(*operator_exchange(rounded, up_t, be_t, n_sec, n_blk))

    def compose(earlier, later):
        first_map, first_value = earlier
        second_map, second_value = later
        joined_map = jnp.dot(second_map, first_map, precision=highest)
        joined_value = jnp.dot(first_value, second_map.T, precision=highest) + second_value
        return (joined_map, joined_value)

    def lengths(vector):
        return jnp.sqrt(global_sum(jnp.sum(vector * vector, axis=1)[None], mesh_shape)[0] + epsilon)

    bent = jnp.tanh(state_now)
    state_rounded = state_now.astype(jnp.bfloat16)
    applied, gain_panel, chain = setup_exchange(
        state_rounded, ahead_panel, section_block, local_picks, back_panel, block_inverse,
        own_picks, n_sec, n_blk,
    )
    residual = source - applied - fan_gain[None, :] * bent
    jac_diag = fan_gain[None, :] * (1.0 - bent * bent)
    columns = []
    basis = []
    directions = []
    product = residual
    beta = None
    for column in range(KRYLOV):
        sums, following, direction, product = precondition_sweep(
            list(basis), product, block_inverse, own_picks, chain, gain_panel, ahead_panel,
            section_block, back_panel, local_picks, jac_diag, mesh_shape, len(basis),
        )
        if column == 0:
            beta = sums[0]
        else:
            columns.append(sums[: column + 1])
        basis.append(following)
        directions.append(direction)
    sums, _ = project(basis, product, mesh_shape)
    columns.append(sums[: KRYLOV + 1])
    weights = least_squares(columns, beta, KRYLOV)
    update = jnp.zeros_like(state_now)
    for column in range(KRYLOV):
        update = update + weights[column][:, None] * directions[column]
    return state_now + update


def solution(mesh):
    in_specs = (
        P(None, ("sec", "blk")),
        P(None, ("sec", "blk")),
        P(("sec", "blk")),
        P(("sec", "blk"), None),
        P(("sec", "blk"), None),
        P(("sec", "blk"), None),
        P(("sec", "blk"), None),
        P("sec", None),
    )
    out_specs = P(None, ("sec", "blk"))
    return jax.shard_map(functools.partial(local, dict(mesh.shape)), mesh=mesh, in_specs=in_specs, out_specs=out_specs, check_vma=False)
```

```python
import functools

import jax
import jax.numpy as jnp
from jax import lax
from jax.experimental import pallas as pl
from jax.experimental.pallas import tpu as pltpu
from jax.sharding import PartitionSpec as P

MESH = pl.DeviceIdType.MESH

KRYLOV = 3


epsilon = 1e-06


def extended(x, sides, width):
    for axis, dim in sides:
        size, length = (lax.axis_size(axis), x.shape[dim])
        up = [(i, (i + 1) % size) for i in range(size - 1)]
        down = [(j, i) for i, j in up]
        last = lax.slice_in_dim(x, length - width, length, axis=dim)
        first = lax.slice_in_dim(x, 0, width, axis=dim)
        before = lax.ppermute(last, axis, up)
        after = lax.ppermute(first, axis, down)
        x = jnp.concatenate([before, x, after], axis=dim)
    return x


def entering(value, axis, join, neutral):
    count, mine = (lax.axis_size(axis), lax.axis_index(axis))
    pieces = jax.tree.map(lambda part: lax.all_gather(part, axis), value)
    so_far = jax.tree.map(
        lambda part, zero: jnp.full_like(part, 0) + jnp.asarray(zero, part.dtype), value, neutral
    )

    def step(position, so_far):
        longer = join(so_far, jax.tree.map(lambda part: part[position], pieces))
        return jax.tree.map(lambda new, old: jnp.where(position < mine, new, old), longer, so_far)

    return lax.fori_loop(0, count - 1, step, so_far)


def _reduce_kernel(stages, x_ref, o_ref, *scratch):
    count = len(stages)
    slots = scratch[:count]
    partial = scratch[count]
    sends = scratch[count + 1 : 2 * count + 1]
    recvs = scratch[2 * count + 1 :]
    barrier = pltpu.get_barrier_semaphore()
    peers = 0
    for axis, n in stages:
        mine = lax.axis_index(axis)
        for k in range(1, n):
            pl.semaphore_signal(
                barrier, inc=1, device_id={axis: lax.rem(mine + k, n)}, device_id_type=MESH
            )
            peers += 1
    pl.semaphore_wait(barrier, peers)
    source = x_ref
    for stage, (axis, n) in enumerate(stages):
        mine = lax.axis_index(axis)
        copies = []
        for k in range(1, n):
            copy = pltpu.make_async_remote_copy(
                src_ref=source,
                dst_ref=slots[stage].at[mine],
                send_sem=sends[stage].at[k],
                recv_sem=recvs[stage].at[mine],
                device_id={axis: lax.rem(mine + k, n)},
                device_id_type=MESH,
            )
            copy.start()
            copies.append(copy)
        slots[stage][mine] = source[...]
        for k in range(1, n):
            sender = lax.rem(mine + k, n)
            pltpu.make_async_remote_copy(
                src_ref=source,
                dst_ref=slots[stage].at[sender],
                send_sem=sends[stage].at[k],
                recv_sem=recvs[stage].at[sender],
                device_id={axis: sender},
                device_id_type=MESH,
            ).wait_recv()
        for copy in copies:
            copy.wait_send()
        total = slots[stage][0]
        for j in range(1, n):
            total = total + slots[stage][j]
        if stage == count - 1:
            o_ref[...] = total
        else:
            partial[...] = total
            source = partial


def all_sum(x, axes, mesh_shape, collective):
    stages = tuple((axis, mesh_shape[axis]) for axis in axes if mesh_shape[axis] > 1)
    rows, cols = x.shape
    scratch = [pltpu.VMEM((n, rows, cols), jnp.float32) for _, n in stages]
    scratch.append(pltpu.VMEM((rows, cols), jnp.float32))
    scratch += [pltpu.SemaphoreType.DMA((n,)) for _, n in stages]
    scratch += [pltpu.SemaphoreType.DMA((n,)) for _, n in stages]
    return pl.pallas_call(
        functools.partial(_reduce_kernel, stages),
        out_shape=jax.ShapeDtypeStruct((rows, cols), jnp.float32),
        in_specs=[pl.BlockSpec(memory_space=pltpu.VMEM)],
        out_specs=pl.BlockSpec(memory_space=pltpu.VMEM),
        scratch_shapes=scratch,
        compiler_params=pltpu.CompilerParams(collective_id=collective, has_side_effects=True),
    )(x.astype(jnp.float32))


def global_sum(rows_of_sums, mesh_shape):
    count = rows_of_sums.shape[0]
    padded = jnp.zeros((8, rows_of_sums.shape[1]), jnp.float32).at[:count].set(rows_of_sums)
    return all_sum(padded, ("blk", "sec"), mesh_shape, 0)[:count]


def _doubling(n):
    distances, d = [], 1
    while d < n:
        distances.append(d)
        d *= 2
    return tuple(distances)


def _greet(n, distances):
    barrier = pltpu.get_barrier_semaphore()
    mine = lax.axis_index("sec")
    for d in distances:
        for peer in (lax.rem(mine + d, n), lax.rem(mine + n - d, n)):
            pl.semaphore_signal(barrier, inc=1, device_id={"sec": peer}, device_id_type=MESH)
    pl.semaphore_wait(barrier, 2 * len(distances))


def _hop(n, d, source, slot, send_sem, recv_sem):
    mine = lax.axis_index("sec")
    copy = pltpu.make_async_remote_copy(
        src_ref=source,
        dst_ref=slot,
        send_sem=send_sem,
        recv_sem=recv_sem,
        device_id={"sec": lax.rem(mine + d, n)},
        device_id_type=MESH,
    )
    copy.start()
    copy.wait_recv()
    copy.wait_send()


RADIX = 4


def _plan(n):
    rounds, d = [], 1
    while d < n:
        rounds.append((d, tuple(j for j in range(1, RADIX) if j * d < n)))
        d *= RADIX
    return tuple(rounds)


def _plan_peers(rounds):
    return tuple(sorted({j * d for d, js in rounds for j in js} | {1}))


def _send_all(n, sec, sources, slots, sends, recvs, flat, d, js):
    copies = []
    for i, j in enumerate(js):
        copy = pltpu.make_async_remote_copy(
            src_ref=sources,
            dst_ref=slots.at[flat + i],
            send_sem=sends.at[flat + i],
            recv_sem=recvs.at[flat + i],
            device_id={"sec": lax.rem(sec + j * d, n)},
            device_id_type=MESH,
        )
        copy.start()
        copies.append(copy)
    for copy in copies:
        copy.wait_recv()
    for copy in copies:
        copy.wait_send()


def _spread(n_sec, n_blk, offsets, piece_ref, slots, sends, recvs):
    sec, blk = lax.axis_index("sec"), lax.axis_index("blk")

    def copy(o, j, index):
        return pltpu.make_async_remote_copy(
            src_ref=piece_ref,
            dst_ref=slots.at[index],
            send_sem=sends.at[(o - 1) * n_blk + j],
            recv_sem=recvs.at[index],
            device_id={"sec": lax.rem(sec + o, n_sec), "blk": j},
            device_id_type=MESH,
        )

    outgoing = [
        copy(o, j, (o - 1) * n_blk + blk) for o in range(1, offsets + 1) for j in range(n_blk)
    ]
    for c in outgoing:
        c.start()
    for o in range(1, offsets + 1):
        for j in range(n_blk):
            copy(o, j, (o - 1) * n_blk + j).wait_recv()
    for c in outgoing:
        c.wait_send()


def _assemble(n_blk, offsets, slots, mats):
    piece = slots.shape[1]
    for o in range(offsets):
        for j in range(n_blk):
            mats[o, j * piece : (j + 1) * piece, :] = slots[o * n_blk + j]


def _greet_all(n_sec, n_blk, offsets, rounds, blk_peers, stages=()):
    barrier = pltpu.get_barrier_semaphore()
    sec, blk = lax.axis_index("sec"), lax.axis_index("blk")
    count = _signal_stages(barrier, stages)
    if blk_peers:
        for k in range(1, n_blk):
            pl.semaphore_signal(
                barrier, inc=1, device_id={"blk": lax.rem(blk + k, n_blk)}, device_id_type=MESH
            )
            count += 1
    covered = bool(stages)
    for o in range(1, offsets + 1):
        for k in range(1 if covered else 0, n_blk):
            for peer in (lax.rem(sec + o, n_sec), lax.rem(sec + n_sec - o, n_sec)):
                pl.semaphore_signal(
                    barrier,
                    inc=1,
                    device_id={"sec": peer, "blk": lax.rem(blk + k, n_blk)},
                    device_id_type=MESH,
                )
                count += 1
    if covered:
        pl.semaphore_wait(barrier, count)
        return
    for d in sorted({j * d for d, js in rounds[1:] for j in js}):
        for peer in (lax.rem(sec + d, n_sec), lax.rem(sec + n_sec - d, n_sec)):
            pl.semaphore_signal(barrier, inc=1, device_id={"sec": peer}, device_id_type=MESH)
            count += 1
    pl.semaphore_wait(barrier, count)


def _maps_body(n, n_blk, rounds, e_ref, a_ref, eslots, emat, current, slots, esend, erecv, sends, recvs):
    sec = lax.axis_index("sec")
    first = rounds[0][1]
    offsets = len(first) + 1
    _spread(n, n_blk, offsets, e_ref, eslots, esend, erecv)
    _assemble(n_blk, offsets, eslots, emat)
    joined = emat[0]
    for i, j in enumerate(first):
        a_ref[i] = joined
        joined = jnp.dot(
            joined, emat[j], precision=lax.Precision.HIGHEST, preferred_element_type=jnp.float32
        )
    current[...] = joined
    flat = len(first)
    for k in range(1, len(rounds)):
        d, js = rounds[k]
        onward = k < len(rounds) - 1
        if onward or len(js) > 1:
            _send_all(n, sec, current, slots, sends, recvs, flat, d, js)
        joined = current[...]
        for i, j in enumerate(js):
            a_ref[flat + i] = joined
            if onward or i < len(js) - 1:
                joined = jnp.dot(
                    joined, slots[flat + i], precision=lax.Precision.HIGHEST,
                    preferred_element_type=jnp.float32,
                )
        if onward:
            current[...] = joined
        flat += len(js)


def _setup_kernel(
    n_sec, n_blk, rounds, x_ref, ahead_ref, block_ref, spread_ref, back_ref, inv_ref, pick_ref,
    k_ref, gain_ref, chain_ref, *scratch
):
    phase_scratch = scratch[:9]
    pslots, psend, precv, epiece = scratch[9:13]
    g_ref, b_ref, a_ref, upward, own_piece = scratch[13:18]
    maps_scratch = scratch[18:]
    sec, blk = lax.axis_index("sec"), lax.axis_index("blk")
    offsets = len(rounds[0][1]) + 1
    _greet_all(n_sec, n_blk, offsets, rounds, True)
    contract = (((1,), (1,)), ((), ()))
    upward[...] = jnp.dot(x_ref[...], ahead_ref[...], preferred_element_type=jnp.float32).T
    own_piece[...] = lax.dot_general(
        pick_ref[...], x_ref[...].astype(jnp.float32), contract,
        precision=lax.Precision.HIGHEST, preferred_element_type=jnp.float32,
    )

    def blk_copy(k, target, slot):
        return pltpu.make_async_remote_copy(
            src_ref=back_ref,
            dst_ref=pslots.at[slot],
            send_sem=psend.at[k],
            recv_sem=precv.at[slot],
            device_id={"blk": target},
            device_id_type=MESH,
        )

    outgoing = [blk_copy(k, lax.rem(blk + k, n_blk), blk) for k in range(1, n_blk)]
    for copy in outgoing:
        copy.start()
    _operator_phase(n_sec, n_blk, x_ref, upward, own_piece, g_ref, b_ref, a_ref, phase_scratch)
    width = x_ref.shape[1]
    product = lax.dot_general(
        g_ref[:, 0:width], block_ref[:, 0:width], contract, preferred_element_type=jnp.float32
    )
    for j in range(1, n_blk):
        product = product + lax.dot_general(
            g_ref[:, j * width : (j + 1) * width],
            block_ref[:, j * width : (j + 1) * width],
            contract,
            preferred_element_type=jnp.float32,
        )
    product = product + lax.dot_general(
        b_ref[...].T.astype(back_ref.dtype), back_ref[...], contract,
        preferred_element_type=jnp.float32,
    )
    product = product + jnp.dot(
        spread_ref[...], a_ref[...], precision=lax.Precision.HIGHEST,
        preferred_element_type=jnp.float32,
    ).T
    k_ref[...] = product
    pslots[blk] = back_ref[...]
    for k in range(1, n_blk):
        sender = lax.rem(blk + k, n_blk)
        blk_copy(k, sender, sender).wait_recv()
    for copy in outgoing:
        copy.wait_send()
    rows = back_ref.shape[0]
    gain = jnp.dot(inv_ref[:, 0:rows], pslots[0], preferred_element_type=jnp.float32)
    for j in range(1, n_blk):
        gain = gain + jnp.dot(
            inv_ref[:, j * rows : (j + 1) * rows], pslots[j], preferred_element_type=jnp.float32
        )
    gain_ref[...] = gain
    epiece[...] = -jnp.dot(
        pick_ref[...], gain, precision=lax.Precision.HIGHEST, preferred_element_type=jnp.float32
    )
    _maps_body(n_sec, n_blk, rounds, epiece, chain_ref, *maps_scratch)


def setup_exchange(x, ahead, block, spread, back, inverse, picks, n_sec, n_blk):
    cases, width = x.shape
    panel = ahead.shape[1]
    piece = panel // n_blk
    rows, panel_width = back.shape
    rounds = _plan(n_sec)
    total = sum(len(js) for _, js in rounds)
    offsets = len(rounds[0][1]) + 1
    return pl.pallas_call(
        functools.partial(_setup_kernel, n_sec, n_blk, rounds),
        out_shape=(
            jax.ShapeDtypeStruct((cases, width), jnp.float32),
            jax.ShapeDtypeStruct((rows, panel_width), jnp.float32),
            jax.ShapeDtypeStruct((total, panel_width, panel_width), jnp.float32),
        ),
        in_specs=[pl.BlockSpec(memory_space=pltpu.VMEM)] * 7,
        out_specs=[pl.BlockSpec(memory_space=pltpu.VMEM)] * 3,
        scratch_shapes=_operator_scratch(n_blk, cases, width, x.dtype, piece, cases)
        + [
            pltpu.VMEM((n_blk, rows, panel_width), back.dtype),
            pltpu.SemaphoreType.DMA((n_blk,)),
            pltpu.SemaphoreType.DMA((n_blk,)),
            pltpu.VMEM((piece, panel_width), jnp.float32),
            pltpu.VMEM((cases, n_blk * width), x.dtype),
            pltpu.VMEM((panel, cases), jnp.float32),
            pltpu.VMEM((piece, cases), jnp.float32),
            pltpu.VMEM((panel, cases), jnp.float32),
            pltpu.VMEM((piece, cases), jnp.float32),
            pltpu.VMEM((offsets * n_blk, piece, panel_width), jnp.float32),
            pltpu.VMEM((offsets, panel_width, panel_width), jnp.float32),
            pltpu.VMEM((panel_width, panel_width), jnp.float32),
            pltpu.VMEM((total, panel_width, panel_width), jnp.float32),
            pltpu.SemaphoreType.DMA((offsets * n_blk,)),
            pltpu.SemaphoreType.DMA((offsets * n_blk,)),
            pltpu.SemaphoreType.DMA((total,)),
            pltpu.SemaphoreType.DMA((total,)),
        ],
        compiler_params=pltpu.CompilerParams(collective_id=3, has_side_effects=True),
    )(x, ahead, block, spread, back, inverse, picks)


def _gather_kernel(n, x_ref, o_ref, slots, sends, recvs):
    mine = lax.axis_index("blk")
    barrier = pltpu.get_barrier_semaphore()
    for k in range(1, n):
        pl.semaphore_signal(
            barrier, inc=1, device_id={"blk": lax.rem(mine + k, n)}, device_id_type=MESH
        )
    pl.semaphore_wait(barrier, n - 1)
    copies = []
    for k in range(1, n):
        copy = pltpu.make_async_remote_copy(
            src_ref=x_ref,
            dst_ref=slots.at[mine],
            send_sem=sends.at[k],
            recv_sem=recvs.at[mine],
            device_id={"blk": lax.rem(mine + k, n)},
            device_id_type=MESH,
        )
        copy.start()
        copies.append(copy)
    slots[mine] = x_ref[...]
    for k in range(1, n):
        sender = lax.rem(mine + k, n)
        pltpu.make_async_remote_copy(
            src_ref=x_ref,
            dst_ref=slots.at[sender],
            send_sem=sends.at[k],
            recv_sem=recvs.at[sender],
            device_id={"blk": sender},
            device_id_type=MESH,
        ).wait_recv()
    for copy in copies:
        copy.wait_send()
    width = x_ref.shape[1]
    for j in range(n):
        o_ref[:, j * width : (j + 1) * width] = slots[j]


def gather_blk(x, n):
    rows, width = x.shape
    return pl.pallas_call(
        functools.partial(_gather_kernel, n),
        out_shape=jax.ShapeDtypeStruct((rows, n * width), x.dtype),
        in_specs=[pl.BlockSpec(memory_space=pltpu.VMEM)],
        out_specs=pl.BlockSpec(memory_space=pltpu.VMEM),
        scratch_shapes=[
            pltpu.VMEM((n, rows, width), x.dtype),
            pltpu.SemaphoreType.DMA((n,)),
            pltpu.SemaphoreType.DMA((n,)),
        ],
        compiler_params=pltpu.CompilerParams(collective_id=4, has_side_effects=True),
    )(x)


def _operator_phase(n_sec, n_blk, x_ref, up_ref, piece_ref, g_ref, b_ref, a_ref, scratch):
    gslots, bslots, aslots, gsend, grecv, bsend, brecv, asend, arecv = scratch
    sec, blk = lax.axis_index("sec"), lax.axis_index("blk")
    nxt, prv = lax.rem(sec + 1, n_sec), lax.rem(sec + n_sec - 1, n_sec)
    piece = bslots.shape[1]
    copies = []
    for k in range(1, n_blk):
        copies.append(
            pltpu.make_async_remote_copy(
                src_ref=x_ref,
                dst_ref=gslots.at[blk],
                send_sem=gsend.at[k],
                recv_sem=grecv.at[blk],
                device_id={"blk": lax.rem(blk + k, n_blk)},
                device_id_type=MESH,
            )
        )
    for j in range(n_blk):
        copies.append(
            pltpu.make_async_remote_copy(
                src_ref=piece_ref,
                dst_ref=bslots.at[blk],
                send_sem=bsend.at[j],
                recv_sem=brecv.at[blk],
                device_id={"sec": nxt, "blk": j},
                device_id_type=MESH,
            )
        )
        copies.append(
            pltpu.make_async_remote_copy(
                src_ref=up_ref.at[pl.ds(j * piece, piece)],
                dst_ref=aslots.at[blk],
                send_sem=asend.at[j],
                recv_sem=arecv.at[blk],
                device_id={"sec": prv, "blk": j},
                device_id_type=MESH,
            )
        )
    for copy in copies:
        copy.start()
    gslots[blk] = x_ref[...]
    for k in range(1, n_blk):
        sender = lax.rem(blk + k, n_blk)
        pltpu.make_async_remote_copy(
            src_ref=x_ref,
            dst_ref=gslots.at[sender],
            send_sem=gsend.at[k],
            recv_sem=grecv.at[sender],
            device_id={"blk": sender},
            device_id_type=MESH,
        ).wait_recv()
    for j in range(n_blk):
        pltpu.make_async_remote_copy(
            src_ref=piece_ref,
            dst_ref=bslots.at[j],
            send_sem=bsend.at[j],
            recv_sem=brecv.at[j],
            device_id={"sec": prv, "blk": j},
            device_id_type=MESH,
        ).wait_recv()
        pltpu.make_async_remote_copy(
            src_ref=up_ref.at[pl.ds(j * piece, piece)],
            dst_ref=aslots.at[j],
            send_sem=asend.at[j],
            recv_sem=arecv.at[j],
            device_id={"sec": nxt, "blk": j},
            device_id_type=MESH,
        ).wait_recv()
    for copy in copies:
        copy.wait_send()
    width = x_ref.shape[1]
    for j in range(n_blk):
        g_ref[:, j * width : (j + 1) * width] = gslots[j]
        b_ref[j * piece : (j + 1) * piece, :] = jnp.where(
            sec >= 1, bslots[j], jnp.zeros_like(bslots[j])
        )
    total = aslots[0]
    for j in range(1, n_blk):
        total = total + aslots[j]
    a_ref[...] = jnp.where(sec <= n_sec - 2, total, jnp.zeros_like(total))


def _operator_scratch(n_blk, rows, width, dtype, piece, cases):
    return [
        pltpu.VMEM((n_blk, rows, width), dtype),
        pltpu.VMEM((n_blk, piece, cases), jnp.float32),
        pltpu.VMEM((n_blk, piece, cases), jnp.float32),
    ] + [pltpu.SemaphoreType.DMA((n_blk,))] * 6


def _operator_kernel(n_sec, n_blk, x_ref, up_ref, be_ref, g_ref, b_ref, a_ref, *scratch):
    sec, blk = lax.axis_index("sec"), lax.axis_index("blk")
    nxt, prv = lax.rem(sec + 1, n_sec), lax.rem(sec + n_sec - 1, n_sec)
    piece = scratch[1].shape[1]
    barrier = pltpu.get_barrier_semaphore()
    for k in range(1, n_blk):
        pl.semaphore_signal(
            barrier, inc=1, device_id={"blk": lax.rem(blk + k, n_blk)}, device_id_type=MESH
        )
    for j in range(n_blk):
        for other in (nxt, prv):
            pl.semaphore_signal(
                barrier, inc=1, device_id={"sec": other, "blk": j}, device_id_type=MESH
            )
    pl.semaphore_wait(barrier, 3 * n_blk - 1)
    mine = be_ref.at[pl.ds(pl.multiple_of(blk * piece, 8), piece)]
    _operator_phase(n_sec, n_blk, x_ref, up_ref, mine, g_ref, b_ref, a_ref, scratch)


def operator_exchange(x, up_t, be_t, n_sec, n_blk):
    rows, width = x.shape
    panel, cases = up_t.shape
    piece = panel // n_blk
    return pl.pallas_call(
        functools.partial(_operator_kernel, n_sec, n_blk),
        out_shape=(
            jax.ShapeDtypeStruct((rows, n_blk * width), x.dtype),
            jax.ShapeDtypeStruct((panel, cases), jnp.float32),
            jax.ShapeDtypeStruct((piece, cases), jnp.float32),
        ),
        in_specs=[pl.BlockSpec(memory_space=pltpu.VMEM)] * 3,
        out_specs=[pl.BlockSpec(memory_space=pltpu.VMEM)] * 3,
        scratch_shapes=_operator_scratch(n_blk, rows, width, x.dtype, piece, cases),
        compiler_params=pltpu.CompilerParams(collective_id=5, has_side_effects=True),
    )(x, up_t, be_t)


def _precondition_kernel(n_sec, n_blk, rounds, stages, depth, *refs):
    basis_refs = refs[:depth]
    (image_ref, inv_ref, pick_ref, u_ref, gain_ref, ahead_ref, block_ref, back_ref, spread_ref,
     jac_ref, h_ref, next_ref, d_ref, p_ref) = refs[depth : depth + 14]
    scratch = refs[depth + 14 :]
    gslots, fpiece, fslots, fmat, carry, slots, gsend, grecv, fsend, frecv, ssend, srecv = scratch[:12]
    rounded, upward, own_piece, x_ref = scratch[12:16]
    g_ref, b_ref, a_ref = scratch[16:19]
    phase_scratch = scratch[19:28]
    project_scratch = scratch[28:]
    sec, blk = lax.axis_index("sec"), lax.axis_index("blk")
    first = rounds[0][1]
    offsets = len(first) + 1
    _greet_all(n_sec, n_blk, offsets, rounds, False, stages)
    _project_body(stages, depth, basis_refs, image_ref, h_ref, next_ref, project_scratch)
    x_ref[...] = next_ref[...].astype(x_ref.dtype)

    def blk_copy(k, target, slot):
        return pltpu.make_async_remote_copy(
            src_ref=x_ref,
            dst_ref=gslots.at[slot],
            send_sem=gsend.at[k],
            recv_sem=grecv.at[slot],
            device_id={"blk": target},
            device_id_type=MESH,
        )

    outgoing = [blk_copy(k, lax.rem(blk + k, n_blk), blk) for k in range(1, n_blk)]
    for copy in outgoing:
        copy.start()
    width = x_ref.shape[1]
    contract = (((1,), (1,)), ((), ()))
    folded = lax.dot_general(
        x_ref[...],
        inv_ref[:, pl.ds(pl.multiple_of(blk * width, width), width)],
        contract,
        preferred_element_type=jnp.float32,
    )
    for k in range(1, n_blk):
        sender = lax.rem(blk + k, n_blk)
        blk_copy(k, sender, sender).wait_recv()
        folded = folded + lax.dot_general(
            gslots[sender],
            inv_ref[:, pl.ds(pl.multiple_of(sender * width, width), width)],
            contract,
            preferred_element_type=jnp.float32,
        )
    for copy in outgoing:
        copy.wait_send()
    fpiece[...] = lax.dot_general(
        pick_ref[...], folded, contract, precision=lax.Precision.HIGHEST,
        preferred_element_type=jnp.float32,
    )
    _spread(n_sec, n_blk, offsets, fpiece, fslots, fsend, frecv)
    _assemble(n_blk, offsets, fslots, fmat)
    joined = jnp.where(sec >= 1, fmat[0], jnp.zeros_like(fmat[0]))
    for i, j in enumerate(first):
        term = jnp.dot(
            u_ref[i], fmat[j], precision=lax.Precision.HIGHEST, preferred_element_type=jnp.float32
        )
        joined = joined + jnp.where(sec >= j + 1, term, jnp.zeros_like(term))
    carry[1] = joined
    flat = len(first)
    for k in range(1, len(rounds)):
        d, js = rounds[k]
        _send_all(n_sec, sec, carry.at[k], slots, ssend, srecv, flat, d, js)
        joined = carry[k]
        for i, j in enumerate(js):
            term = jnp.dot(
                u_ref[flat + i], slots[flat + i], precision=lax.Precision.HIGHEST,
                preferred_element_type=jnp.float32,
            )
            joined = joined + jnp.where(sec >= j * d, term, jnp.zeros_like(term))
        carry[k + 1] = joined
        flat += len(js)
    before = carry[len(rounds)].T
    direction = folded - lax.dot_general(
        before, gain_ref[...], contract, precision=lax.Precision.HIGHEST,
        preferred_element_type=jnp.float32,
    )
    d_ref[...] = direction
    rounded[...] = direction.astype(rounded.dtype)
    upward[...] = jnp.dot(
        rounded[...], ahead_ref[...], preferred_element_type=jnp.float32
    ).T
    own_piece[...] = lax.dot_general(
        pick_ref[...], rounded[...].astype(jnp.float32), contract,
        precision=lax.Precision.HIGHEST, preferred_element_type=jnp.float32,
    )
    _operator_phase(n_sec, n_blk, rounded, upward, own_piece, g_ref, b_ref, a_ref, phase_scratch)
    product = jac_ref[...] * direction
    for j in range(n_blk):
        product = product + lax.dot_general(
            g_ref[:, j * width : (j + 1) * width],
            block_ref[:, j * width : (j + 1) * width],
            contract,
            preferred_element_type=jnp.float32,
        )
    product = product + lax.dot_general(
        b_ref[...].T.astype(back_ref.dtype), back_ref[...], contract,
        preferred_element_type=jnp.float32,
    )
    product = product + jnp.dot(
        spread_ref[...], a_ref[...], precision=lax.Precision.HIGHEST,
        preferred_element_type=jnp.float32,
    ).T
    p_ref[...] = product


def precondition_sweep(
    basis, image, inverse, picks, chain, gain, ahead, block, back, spread, jac, mesh_shape, depth
):
    n_sec, n_blk = mesh_shape["sec"], mesh_shape["blk"]
    stages = _global_stages(mesh_shape)
    cases, width = image.shape
    piece, _ = picks.shape
    panel = piece * n_blk
    plan = _plan(n_sec)
    rounds = len(plan)
    total = sum(len(js) for _, js in plan)
    offsets = len(plan[0][1]) + 1
    dtype = jnp.bfloat16
    return pl.pallas_call(
        functools.partial(_precondition_kernel, n_sec, n_blk, plan, stages, depth),
        out_shape=(
            jax.ShapeDtypeStruct((8, cases), jnp.float32),
            jax.ShapeDtypeStruct((cases, width), jnp.float32),
            jax.ShapeDtypeStruct((cases, width), jnp.float32),
            jax.ShapeDtypeStruct((cases, width), jnp.float32),
        ),
        in_specs=[pl.BlockSpec(memory_space=pltpu.VMEM)] * (depth + 10),
        out_specs=[pl.BlockSpec(memory_space=pltpu.VMEM)] * 4,
        scratch_shapes=[
            pltpu.VMEM((n_blk, cases, width), dtype),
            pltpu.VMEM((piece, cases), jnp.float32),
            pltpu.VMEM((offsets * n_blk, piece, cases), jnp.float32),
            pltpu.VMEM((offsets, panel, cases), jnp.float32),
            pltpu.VMEM((rounds + 1, panel, cases), jnp.float32),
            pltpu.VMEM((total, panel, cases), jnp.float32),
            pltpu.SemaphoreType.DMA((n_blk,)),
            pltpu.SemaphoreType.DMA((n_blk,)),
            pltpu.SemaphoreType.DMA((offsets * n_blk,)),
            pltpu.SemaphoreType.DMA((offsets * n_blk,)),
            pltpu.SemaphoreType.DMA((total,)),
            pltpu.SemaphoreType.DMA((total,)),
            pltpu.VMEM((cases, width), dtype),
            pltpu.VMEM((panel, cases), jnp.float32),
            pltpu.VMEM((piece, cases), jnp.float32),
            pltpu.VMEM((cases, width), dtype),
            pltpu.VMEM((cases, n_blk * width), dtype),
            pltpu.VMEM((panel, cases), jnp.float32),
            pltpu.VMEM((piece, cases), jnp.float32),
        ]
        + _operator_scratch(n_blk, cases, width, dtype, piece, cases)
        + _project_scratch(stages, cases),
        compiler_params=pltpu.CompilerParams(collective_id=10 + depth, has_side_effects=True),
    )(*basis, image, inverse, picks, chain, gain, ahead, block, back, spread, jac)


def _exchange_sum(stages, source, slots, partial, sends, recvs, out):
    count = len(stages)
    for stage, (axis, n) in enumerate(stages):
        mine = lax.axis_index(axis)
        copies = []
        for k in range(1, n):
            copy = pltpu.make_async_remote_copy(
                src_ref=source,
                dst_ref=slots[stage].at[mine],
                send_sem=sends[stage].at[k],
                recv_sem=recvs[stage].at[mine],
                device_id={axis: lax.rem(mine + k, n)},
                device_id_type=MESH,
            )
            copy.start()
            copies.append(copy)
        slots[stage][mine] = source[...]
        for k in range(1, n):
            sender = lax.rem(mine + k, n)
            pltpu.make_async_remote_copy(
                src_ref=source,
                dst_ref=slots[stage].at[sender],
                send_sem=sends[stage].at[k],
                recv_sem=recvs[stage].at[sender],
                device_id={axis: sender},
                device_id_type=MESH,
            ).wait_recv()
        for copy in copies:
            copy.wait_send()
        total = slots[stage][0]
        for j in range(1, n):
            total = total + slots[stage][j]
        if stage == count - 1:
            out[...] = total
        else:
            partial[...] = total
            source = partial


def _project_scratch(stages, cases):
    def buffers():
        out = [pltpu.VMEM((n, 8, cases), jnp.float32) for _, n in stages]
        out.append(pltpu.VMEM((8, cases), jnp.float32))
        out += [pltpu.SemaphoreType.DMA((n,)) for _, n in stages]
        out += [pltpu.SemaphoreType.DMA((n,)) for _, n in stages]
        return out

    return buffers() + buffers() + [pltpu.VMEM((8, cases), jnp.float32)] * 2


def _project_body(stages, depth, basis_refs, image_ref, h_ref, next_ref, scratch):
    count = len(stages)
    first, second = scratch[: 3 * count + 1], scratch[3 * count + 1 : 6 * count + 2]
    rows, work = scratch[6 * count + 2 : 6 * count + 4]
    highest = lax.Precision.HIGHEST
    contract = (((1,), (1,)), ((), ()))
    image = image_ref[...]
    ones = jnp.ones((8, image.shape[1]), jnp.float32)
    eye = (
        lax.broadcasted_iota(jnp.int32, (image.shape[0],) * 2, 0)
        == lax.broadcasted_iota(jnp.int32, (image.shape[0],) * 2, 1)
    ).astype(jnp.float32)

    def run(buffers, source, out):
        slots = buffers[:count]
        partial = buffers[count]
        sends = buffers[count + 1 : 2 * count + 1]
        recvs = buffers[2 * count + 1 :]
        _exchange_sum(stages, source, slots, partial, sends, recvs, out)

    if depth > 0:
        rows[...] = jnp.zeros_like(rows)
        for i in range(depth):
            summed = lax.dot_general(
                ones, image * basis_refs[i][...], contract, precision=highest,
                preferred_element_type=jnp.float32,
            )
            rows[i : i + 1, :] = summed[0:1, :]
        run(first, rows, h_ref)
        columns = lax.dot_general(
            eye, h_ref[...], contract, precision=highest, preferred_element_type=jnp.float32
        )
        for i in range(depth):
            image = image - columns[:, i : i + 1] * basis_refs[i][...]
    else:
        h_ref[...] = jnp.zeros_like(h_ref)
    work[...] = lax.dot_general(
        ones, image * image, contract, precision=highest, preferred_element_type=jnp.float32
    )
    run(second, work, rows)
    length = jnp.sqrt(rows[...] + epsilon)
    h_ref[depth : depth + 1, :] = length[0:1, :]
    scale = lax.dot_general(
        eye, length, contract, precision=highest, preferred_element_type=jnp.float32
    )
    next_ref[...] = image / scale[:, 0:1]


def _signal_stages(barrier, stages):
    peers = 0
    for axis, n in stages:
        mine = lax.axis_index(axis)
        for k in range(1, n):
            pl.semaphore_signal(
                barrier, inc=1, device_id={axis: lax.rem(mine + k, n)}, device_id_type=MESH
            )
            peers += 1
    return peers


def _project_kernel(stages, depth, *refs):
    basis_refs = refs[:depth]
    image_ref, h_ref, next_ref = refs[depth : depth + 3]
    barrier = pltpu.get_barrier_semaphore()
    pl.semaphore_wait(barrier, _signal_stages(barrier, stages))
    _project_body(stages, depth, basis_refs, image_ref, h_ref, next_ref, refs[depth + 3 :])


def _global_stages(mesh_shape):
    return tuple((axis, mesh_shape[axis]) for axis in ("blk", "sec") if mesh_shape[axis] > 1)


def project(basis, image, mesh_shape):
    depth = len(basis)
    cases, width = image.shape
    stages = _global_stages(mesh_shape)
    return pl.pallas_call(
        functools.partial(_project_kernel, stages, depth),
        out_shape=(
            jax.ShapeDtypeStruct((8, cases), jnp.float32),
            jax.ShapeDtypeStruct((cases, width), jnp.float32),
        ),
        in_specs=[pl.BlockSpec(memory_space=pltpu.VMEM)] * (depth + 1),
        out_specs=[pl.BlockSpec(memory_space=pltpu.VMEM)] * 2,
        scratch_shapes=_project_scratch(stages, cases),
        compiler_params=pltpu.CompilerParams(collective_id=6 + depth, has_side_effects=True),
    )(*basis, image)


def least_squares(columns, beta, depth):
    zero = jnp.zeros_like(beta)
    upper = [
        [columns[j][i] if i <= j + 1 else zero for j in range(depth)] for i in range(depth + 1)
    ]
    rhs = [beta] + [zero] * depth
    for column in range(depth):
        upper_row, lower_row = upper[column], upper[column + 1]
        radius = jnp.sqrt(upper_row[column] ** 2 + lower_row[column] ** 2)
        cosine = upper_row[column] / radius
        sine_term = lower_row[column] / radius
        upper[column] = [cosine * a + sine_term * b for a, b in zip(upper_row, lower_row)]
        upper[column + 1] = [-sine_term * a + cosine * b for a, b in zip(upper_row, lower_row)]
        first_rhs, second_rhs = rhs[column], rhs[column + 1]
        rhs[column] = cosine * first_rhs + sine_term * second_rhs
        rhs[column + 1] = -sine_term * first_rhs + cosine * second_rhs
    weights = [zero] * depth
    for column in reversed(range(depth)):
        remain = rhs[column]
        if column + 1 < depth:
            tail = upper[column][column + 1] * weights[column + 1]
            for k in range(column + 2, depth):
                tail = tail + upper[column][k] * weights[k]
            remain = remain - tail
        weights[column] = remain / upper[column][column]
    return weights

def local(
    mesh_shape,
    state_now, source, fan_gain, section_block, block_inverse, back_panel, ahead_panel, interface
):
    highest = lax.Precision.HIGHEST
    cases, node_rows = state_now.shape
    panel_width = back_panel.shape[1]
    indices = interface[0]
    first_row = lax.axis_index("blk") * node_rows
    selector = (indices[None, :] == first_row + jnp.arange(node_rows)[:, None]).astype(jnp.float32)
    contract = (((1,), (1,)), ((), ()))

    own_piece = panel_width // mesh_shape["blk"]
    own_picks = lax.dynamic_slice_in_dim(selector, lax.axis_index("blk") * own_piece, own_piece, 1).T

    def section_terms(dense_part, behind_vals, piece):
        width = piece.shape[1]
        dense_part = lax.dot_general(
            piece, section_block, contract, preferred_element_type=jnp.float32
        )
        picker = (indices[None, :] == jnp.arange(width)[:, None]).astype(jnp.bfloat16)
        behind_vals = jnp.dot(piece, picker, preferred_element_type=jnp.float32)
        return (dense_part, behind_vals)

    def fold_section(carry, piece):
        return section_terms(carry[0], carry[1], piece)

    n_sec, n_blk = mesh_shape["sec"], mesh_shape["blk"]
    piece = panel_width // n_blk
    local_picks = lax.dynamic_slice_in_dim(selector, lax.axis_index("blk") * piece, piece, 1)

    def finish(gathered, behind_t, ahead_piece):
        dense_part = lax.dot_general(
            gathered, section_block, contract, preferred_element_type=jnp.float32
        )
        lower_term = lax.dot_general(
            behind_t.astype(jnp.bfloat16),
            back_panel,
            (((0,), (1,)), ((), ())),
            preferred_element_type=jnp.float32,
        )
        upper_term = lax.dot_general(
            ahead_piece, local_picks, (((0,), (1,)), ((), ())), precision=highest
        )
        return dense_part + lower_term + upper_term

    def operator(vector):
        rounded = vector.astype(jnp.bfloat16)
        up_t = lax.dot_general(
            ahead_panel, rounded, (((0,), (1,)), ((), ())), preferred_element_type=jnp.float32
        )
        be_t = lax.dot_general(
            selector.astype(jnp.bfloat16),
            rounded,
            (((0,), (1,)), ((), ())),
            preferred_element_type=jnp.float32,
        )
        return finish(*operator_exchange(rounded, up_t, be_t, n_sec, n_blk))

    def compose(earlier, later):
        first_map, first_value = earlier
        second_map, second_value = later
        joined_map = jnp.dot(second_map, first_map, precision=highest)
        joined_value = jnp.dot(first_value, second_map.T, precision=highest) + second_value
        return (joined_map, joined_value)

    def lengths(vector):
        return jnp.sqrt(global_sum(jnp.sum(vector * vector, axis=1)[None], mesh_shape)[0] + epsilon)

    bent = jnp.tanh(state_now)
    state_rounded = state_now.astype(jnp.bfloat16)
    applied, gain_panel, chain = setup_exchange(
        state_rounded, ahead_panel, section_block, local_picks, back_panel, block_inverse,
        own_picks, n_sec, n_blk,
    )
    residual = source - applied - fan_gain[None, :] * bent
    jac_diag = fan_gain[None, :] * (1.0 - bent * bent)
    columns = []
    basis = []
    directions = []
    product = residual
    beta = None
    for column in range(KRYLOV):
        sums, following, direction, product = precondition_sweep(
            list(basis), product, block_inverse, own_picks, chain, gain_panel, ahead_panel,
            section_block, back_panel, local_picks, jac_diag, mesh_shape, len(basis),
        )
        if column == 0:
            beta = sums[0]
        else:
            columns.append(sums[: column + 1])
        basis.append(following)
        directions.append(direction)
    sums, _ = project(basis, product, mesh_shape)
    columns.append(sums[: KRYLOV + 1])
    weights = least_squares(columns, beta, KRYLOV)
    update = jnp.zeros_like(state_now)
    for column in range(KRYLOV):
        update = update + weights[column][:, None] * directions[column]
    return state_now + update


def solution(mesh):
    in_specs = (
        P(None, ("sec", "blk")),
        P(None, ("sec", "blk")),
        P(("sec", "blk")),
        P(("sec", "blk"), None),
        P(("sec", "blk"), None),
        P(("sec", "blk"), None),
        P(("sec", "blk"), None),
        P("sec", None),
    )
    out_specs = P(None, ("sec", "blk"))
    return jax.shard_map(functools.partial(local, dict(mesh.shape)), mesh=mesh, in_specs=in_specs, out_specs=out_specs, check_vma=False)
```
